32 devices in a mesh: dp: 8 (over z, y), tensor: 4 (over x, core).
Axes of the slice: x: 2, y: 2, z: 4, core: 2. Of those that a mesh axis runs over, the one named last changes fastest.
Arguments:
- states: bfloat16 [32, 1024, 512], P(None, 'dp', 'tensor'), may hold values from -6 to 6
- timesteps: int32 [32], replicated, may hold values from 0 to 999
- lengths: int32 [32], replicated, may hold values from 1 to 1024, 20480 in all
- deal_order: int32 [32], replicated, may hold values from 0 to 31, each once
- w_qkv: bfloat16 [512, 3, 512], P('dp', None, 'tensor'), may hold values from -0.25 to 0.25
- w_out: bfloat16 [512, 512], P('tensor', 'dp'), may hold values from -2 to 2
- w_up: bfloat16 [512, 2048], P('dp', 'tensor'), may hold values from -0.25 to 0.25
- w_down: bfloat16 [2048, 512], P('tensor', 'dp'), may hold values from -0.125 to 0.125
- gain_attn: float32 [512], P(('dp', 'tensor')), may hold values from 0.25 to 1.75
- gain_ffn: float32 [512], P(('dp', 'tensor')), may hold values from 0.25 to 1.75
- out_grad: bfloat16 [32, 1024, 512], P(('dp', 'tensor')), may hold values from -6 to 6
Outputs:
- output: bfloat16 [32, 1024, 512], P(('dp', 'tensor'))
- states_grad: bfloat16 [32, 1024, 512], P(None, 'dp', 'tensor')
- w_qkv_grad: float32 [512, 3, 512], P('dp', None, 'tensor')
- w_out_grad: float32 [512, 512], P('tensor', 'dp')
- w_up_grad: float32 [512, 2048], P('dp', 'tensor')
- w_down_grad: float32 [2048, 512], P('tensor', 'dp')
- gain_attn_grad: float32 [512], P(('dp', 'tensor'))
- gain_ffn_grad: float32 [512], P(('dp', 'tensor'))
The draws below stay inside these ranges and needn't reach their ends.
Inputs may be any that keep to these rules, and one draw needn't show every extreme that they name: `deal_order`: every sequence number appears in exactly one slot.
All inputs are finite; a program needn't handle non-finite values.
Results may differ from the reference program's by a relative error of at most 0.017.
Values may be sent and summed in bfloat16 or wider, within the bound.
No kernel may reach another device: no remote copies, remote signals or barrier semaphores. Data moves between devices by JAX's collectives and lax.ppermute only.
A program may use at most 128 MiB of HBM per device.

```python
import math
import jax
import jax.numpy as jnp
import numpy as np
from jax import lax

D = 512
HEAD_DIM = 64
FF = 2048
LEN = 1024
STEPS = 1000
SEQS = 32


def plant(entries, stream_key, least, largest):
    longest = entries.shape.index(max(entries.shape))
    spots = []
    for shift in (0, 1):
        where = [jax.random.randint(jax.random.fold_in(stream_key, axis), (), 0, length) for axis, length in enumerate(entries.shape)]
        where[longest] = (where[longest] + shift) % entries.shape[longest]
        spots.append(tuple(where))
    return entries.at[spots[0]].set(least).at[spots[1]].set(largest)


def steps_of(stream_key, dims, pieces, smallest, largest):
    def one(dim, parts):
        steps = jax.random.uniform(jax.random.fold_in(jax.random.fold_in(stream_key, 6), dim), (parts,), jnp.float32, smallest / len(pieces), largest / len(pieces))
        return jnp.repeat(jnp.exp(steps), dims[dim] // parts).reshape((-1,) + (1,) * (len(dims) - dim - 1))

    factor_of = one(*pieces[0])
    for cut in pieces[1:]:
        factor_of = factor_of * one(*cut)
    return factor_of


def split_up(number_of, total, reach, lean):
    weights = [(1 << 20) // math.isqrt(rank ** lean) + 1 for rank in range(2, number_of + 1)]
    surplus, holding = total - reach - (number_of - 1), [1] * (number_of - 1)
    while surplus > 0:
        candidates = [i for i in range(number_of - 1) if holding[i] < reach]
        mass, remaining = sum([weights[i] for i in candidates]), surplus
        for i in candidates:
            addition = min(reach - holding[i], max(1, remaining * weights[i] // mass), surplus)
            holding[i] = holding[i] + addition
            surplus = surplus - addition
    return np.array([reach] + holding)


def uneven(stream_key, amount, total, reach, slope):
    if amount == 2:
        one = jax.random.randint(stream_key, (), max(1, total - reach), min(reach, total - 1) + 1)
        return jnp.stack([one, total - one])
    sizes = jnp.asarray(split_up(amount, total, reach, slope), jnp.int32)
    couples = (amount - 1) // 2
    giver, receiver = sizes[1:1 + 2 * couples:2], sizes[2:2 + 2 * couples:2]
    room = jnp.minimum(giver - 1, reach - receiver)
    passed = jax.random.randint(jax.random.fold_in(stream_key, 1), (couples,), 0, 1 << 20) % (room + 1)
    sizes = sizes.at[1:1 + 2 * couples:2].set(giver - passed).at[2:2 + 2 * couples:2].set(receiver + passed)
    return sizes[jax.random.permutation(jax.random.fold_in(stream_key, 2), amount)]


def centred(own_key, dims, scale, bound, split=(), kind=jnp.bfloat16):
    drawn = scale * jax.random.normal(own_key, dims, jnp.float32)
    if split:
        drawn = drawn * steps_of(own_key, dims, split, -0.22, 0.18)
    return jnp.clip(drawn, -bound, bound).astype(kind)


def setup_inputs(seed: int = 0) -> dict:
    splits = jax.random.split(jax.random.key(seed), 12)
    return {
        "states": centred(splits[0], (SEQS, LEN, D), 1.0, 6.0, ((1, 8), (2, 4))),
        "timesteps": plant(jax.random.randint(splits[1], (SEQS,), 0, STEPS), jax.random.fold_in(splits[1], 1), 0, STEPS - 1).astype(jnp.int32),
        "lengths": uneven(splits[2], SEQS, SEQS * LEN * 5 // 8, LEN, 1).astype(jnp.int32),
        "deal_order": jax.random.permutation(splits[3], SEQS).astype(jnp.int32),
        "w_qkv": centred(splits[4], (D, 3, D), D ** -0.5, 0.25, ((0, 8), (2, 4))),
        "w_out": centred(splits[5], (D, D), (D // 64) ** -0.5, 2.0, ((0, 4), (1, 8))),
        "w_up": centred(splits[6], (D, FF), D ** -0.5, 0.25, ((0, 8), (1, 4))),
        "w_down": centred(splits[7], (FF, D), FF ** -0.5, 0.125, ((0, 4), (1, 8))),
        "gain_attn": jnp.clip(1.0 + 0.15 * jax.random.normal(splits[8], (D,), jnp.float32), 0.25, 1.75),
        "gain_ffn": jnp.clip(1.0 + 0.15 * jax.random.normal(splits[9], (D,), jnp.float32), 0.25, 1.75),
        "out_grad": centred(splits[10], (SEQS, LEN, D), 1.0, 6.0, ((0, 32),)),
    }


highest = lax.Precision.HIGHEST

@jax.custom_vjp
def low(v):
    return lax.optimization_barrier(v.astype(jnp.bfloat16)).astype(jnp.float32)

@jax.custom_vjp
def low_back(v):
    return v

def low_keep(v):
    return (low(v), None)

def low_pass(kept, grad):
    return (grad,)

def back_keep(v):
    return (v, None)

def back_low(kept, grad):
    return (low(grad),)
low.defvjp(low_keep, low_pass)
low_back.defvjp(back_keep, back_low)

def clock_rows(step_ids, features):
    half_width = features // 2
    ladder = jnp.arange(half_width, dtype=jnp.float32) / half_width
    rate_rows = jnp.exp(-math.log(10000.0) * ladder)
    angles = step_ids.astype(jnp.float32)[:, None] * rate_rows[None, :]
    return jnp.concatenate([jnp.sin(angles), jnp.cos(angles)], axis=-1)

def layer_norm(values, gain_vec):
    center = values - lax.optimization_barrier(jnp.mean(values, axis=-1, keepdims=True))
    spread = lax.optimization_barrier(jnp.mean(center * center, axis=-1, keepdims=True))
    return center * lax.rsqrt(spread + 1e-05) * gain_vec

def block_forward(states_in, step_ids, limits, w_qkv, w_out, w_up, w_down, gain_attn, gain_ffn):
    batch_count, length, features = states_in.shape
    head_count = features // HEAD_DIM
    score_scale = 1.0 / math.sqrt(HEAD_DIM)
    begin_state = states_in + clock_rows(step_ids, features)[:, None, :]
    normed_one = low(layer_norm(begin_state, gain_attn))
    mixed = low(low_back(jnp.einsum('bld,dce->blce', normed_one, w_qkv, precision=highest)))
    queries = mixed[:, :, 0].reshape(batch_count, length, head_count, HEAD_DIM)
    key_rows = mixed[:, :, 1].reshape(batch_count, length, head_count, HEAD_DIM)
    values = mixed[:, :, 2].reshape(batch_count, length, head_count, HEAD_DIM)
    scores = jnp.einsum('bqhe,bkhe->bhqk', queries, key_rows, precision=highest) * score_scale
    keep_mask = jnp.arange(length)[None, :] < limits[:, None]
    scores = low_back(jnp.where(keep_mask[:, None, None, :], scores, -1e+30))
    probability = low(jax.nn.softmax(scores, axis=-1))
    context_rows = jnp.einsum('bhqk,bkhe->bqhe', probability, values, precision=highest)
    context_rows = low(low_back(context_rows.reshape(batch_count, length, features)))
    attended = low_back(jnp.einsum('bld,de->ble', context_rows, w_out, precision=highest))
    middle = begin_state + attended
    normed_two = low(layer_norm(middle, gain_ffn))
    upper_input = low_back(jnp.einsum('bld,df->blf', normed_two, w_up, precision=highest))
    active_units = low(jax.nn.gelu(upper_input, approximate=True))
    feed_out = low_back(jnp.einsum('blf,fd->bld', active_units, w_down, precision=highest))
    live_mask = keep_mask.astype(states_in.dtype)
    return (middle + feed_out) * live_mask[:, :, None]

def reference(states, timesteps, lengths, deal_order, w_qkv, w_out, w_up, w_down, gain_attn, gain_ffn, out_grad):
    blocks = SEQS // 4
    dealt_rows = states[deal_order].astype(jnp.float32).reshape(blocks, 4, LEN, D)
    times_in = timesteps[deal_order].reshape(blocks, 4)
    limits = lengths[deal_order].reshape(blocks, 4)
    cotangent = out_grad.astype(jnp.float32).reshape(blocks, 4, LEN, D)
    weights = (w_qkv.astype(jnp.float32), w_out.astype(jnp.float32), w_up.astype(jnp.float32), w_down.astype(jnp.float32), gain_attn.astype(jnp.float32), gain_ffn.astype(jnp.float32))

    def scan_step(totals, scan_item):
        piece_in, clock_in, limit_in, grad_in = scan_item

        def forward_one(piece_arg, *params):
            return block_forward(piece_arg, clock_in, limit_in, *params)
        result, pullback = jax.vjp(forward_one, piece_in, *weights)
        gradients = pullback(grad_in)
        totals = tuple((total + extra for total, extra in zip(totals, gradients[1:])))
        return (totals, (result.astype(jnp.bfloat16), gradients[0].astype(jnp.bfloat16)))
    initial = tuple((jnp.zeros_like(weight) for weight in weights))
    totals, (outputs, input_grads) = lax.scan(scan_step, initial, (dealt_rows, times_in, limits, cotangent))
    output = outputs.reshape(SEQS, LEN, D)
    inverse = jnp.zeros((SEQS,), jnp.int32).at[deal_order].set(jnp.arange(SEQS, dtype=jnp.int32))
    states_grad = input_grads.reshape(SEQS, LEN, D)[inverse]
    return (output, states_grad, totals[0], totals[1], totals[2], totals[3], totals[4], totals[5])
```

```python
import functools
import math

import jax
import jax.numpy as jnp
from jax import lax
from jax.experimental import pallas as pl
from jax.experimental.pallas import tpu as pltpu
from jax.sharding import PartitionSpec as P

HEAD_DIM = 64
PAIR = 2 * HEAD_DIM
ROWS = 256
CHUNK = 256
SCORE_SCALE = 1.0 / math.sqrt(HEAD_DIM)
LOG2E = math.log2(math.e)
F32 = jnp.float32
BF16 = jnp.bfloat16
NN = (((1,), (0,)), ((), ()))
NT = (((1,), (1,)), ((), ()))
VMEM_LIMIT = 56 * 1024 * 1024


def mul(lhs, rhs, dims=NN):
    return lax.dot_general(lhs, rhs, dims, preferred_element_type=F32)


def join_tokens(ref):
    blocks, parts, tokens, width = ref.shape
    return jnp.concatenate(
        [ref[:, part].reshape(blocks * tokens, width) for part in range(parts)], axis=-1
    ).astype(F32)


def norm_parts(values):
    center = values - jnp.mean(values, axis=-1, keepdims=True)
    spread = jnp.mean(center * center, axis=-1, keepdims=True)
    inverse = lax.rsqrt(spread + 1e-05)
    return center * inverse, inverse


def norm_back(grad, gain, unit, inverse):
    scaled = grad * gain
    mean_scaled = jnp.mean(scaled, axis=-1, keepdims=True)
    mean_along = jnp.mean(scaled * unit, axis=-1, keepdims=True)
    return inverse * (scaled - mean_scaled - unit * mean_along)


def params(**kwargs):
    return pltpu.CompilerParams(vmem_limit_bytes=VMEM_LIMIT, **kwargs)


def project_kernel(limit_ref, x_ref, clock_ref, gain_ref, *refs):
    mixed_ref, n_turn_ref, wide = refs[-3:]
    step = pl.program_id(0)

    @pl.when(step == 0)
    def _():
        for part, w_ref in enumerate(refs[:-3]):
            width = w_ref.shape[1]
            wide[:, part * width : (part + 1) * width] = w_ref[...]

    @pl.when(step * ROWS < limit_ref[0])
    def _():
        begin = join_tokens(x_ref) + clock_ref[...]
        unit, _ = norm_parts(begin)
        normed = (unit * gain_ref[...]).astype(BF16)
        n_turn_ref[...] = normed.T
        mixed_ref[...] = mul(normed, wide[...]).astype(BF16)

    @pl.when(step * ROWS >= limit_ref[0])
    def _():
        n_turn_ref[...] = jnp.zeros_like(n_turn_ref)
        mixed_ref[...] = jnp.zeros_like(mixed_ref)


def project(limit, x_blocks, clock, gain, w_parts):
    senders, feature_parts, tokens, width = x_blocks.shape
    length = senders * tokens
    features = feature_parts * width
    parts, columns = len(w_parts), w_parts[0].shape[1]
    take = ROWS // tokens
    return pl.pallas_call(
        project_kernel,
        grid_spec=pltpu.PrefetchScalarGridSpec(
            num_scalar_prefetch=1,
            grid=(length // ROWS,),
            in_specs=[
                pl.BlockSpec((take, feature_parts, tokens, width), lambda i, s: (i, 0, 0, 0)),
                pl.BlockSpec((1, features), lambda i, s: (0, 0)),
                pl.BlockSpec((1, features), lambda i, s: (0, 0)),
            ]
            + [pl.BlockSpec((features, columns), lambda i, s: (0, 0))] * parts,
            out_specs=[
                pl.BlockSpec((ROWS, parts * columns), lambda i, s: (i, 0)),
                pl.BlockSpec((features, ROWS), lambda i, s: (0, i)),
            ],
            scratch_shapes=[pltpu.VMEM((features, parts * columns), BF16)],
        ),
        out_shape=[
            jax.ShapeDtypeStruct((length, parts * columns), BF16),
            jax.ShapeDtypeStruct((features, length), BF16),
        ],
        compiler_params=params(),
        name="project",
    )(limit, x_blocks, clock, gain, *w_parts)


def head_lanes(shape, head):
    lane = lax.broadcasted_iota(jnp.int32, shape, 1)
    return (lane >= head * HEAD_DIM) & (lane < (head + 1) * HEAD_DIM)


def spare_lane(shape, head):
    lane = lax.broadcasted_iota(jnp.int32, shape, 1)
    return lane == (1 - head) * HEAD_DIM


def masked_keys(keys, head, limit):
    row = lax.broadcasted_iota(jnp.int32, keys.shape, 0)
    spare = jnp.where(
        spare_lane(keys.shape, head) & (row >= limit), jnp.asarray(-1e30, F32), jnp.asarray(0.0, F32)
    )
    return jnp.where(head_lanes(keys.shape, head), keys.astype(F32), spare).astype(BF16)


def own_lanes(values, head):
    return jnp.where(head_lanes(values.shape, head), values.astype(F32), 0.0).astype(BF16)


def masked_queries(queries, head):
    spare = jnp.where(spare_lane(queries.shape, head), jnp.asarray(1.0, F32), jnp.asarray(0.0, F32))
    return jnp.where(head_lanes(queries.shape, head), queries.astype(F32), spare).astype(BF16)


def attend_kernel(limit_ref, q_ref, k_ref, v_ref, ctx_ref, turn_ref, lse_ref, keys_s, q_s, vt_s):
    limit = limit_ref[0]
    length = q_ref.shape[0]
    vt_s[...] = v_ref[...].astype(F32).T.astype(BF16)
    for head in range(2):
        keys_s[head] = masked_keys(k_ref[...], head, limit)
        q_s[head] = masked_queries(q_ref[...], head)
    factor = SCORE_SCALE * LOG2E
    for block in range(length // CHUNK):
        span = slice(block * CHUNK, (block + 1) * CHUNK)

        @pl.when(block * CHUNK < limit)
        def _():
            for head in range(2):
                feats = slice(head * HEAD_DIM, (head + 1) * HEAD_DIM)
                scores = mul(keys_s[head], q_s[head, span, :], NT) * factor
                peak = jnp.max(scores, axis=0, keepdims=True)
                expo = jnp.exp2(scores - peak)
                total = jnp.sum(expo, axis=0, keepdims=True)
                gathered = mul(vt_s[feats, :], expo.astype(BF16))
                turn_ref[feats, span] = (gathered / total).astype(BF16)
                lse_ref[0, head : head + 1, span] = peak + jnp.log2(total)
            ctx_ref[span, :] = turn_ref[:, span].astype(F32).T.astype(BF16)

        @pl.when(block * CHUNK >= limit)
        def _():
            turn_ref[:, span] = jnp.zeros_like(turn_ref[:, span])
            ctx_ref[span, :] = jnp.zeros_like(ctx_ref[span, :])
            lse_ref[0, :, span] = jnp.zeros_like(lse_ref[0, :, span])


def attend(limit, mixed, pairs):
    length = mixed.shape[0]
    column = lambda c: pl.BlockSpec((length, PAIR), lambda i, s: (0, i * 3 + c))
    return pl.pallas_call(
        attend_kernel,
        grid_spec=pltpu.PrefetchScalarGridSpec(
            num_scalar_prefetch=1,
            grid=(pairs,),
            in_specs=[column(0), column(1), column(2)],
            out_specs=[
                pl.BlockSpec((length, PAIR), lambda i, s: (0, i)),
                pl.BlockSpec((PAIR, length), lambda i, s: (i, 0)),
                pl.BlockSpec((1, 2, length), lambda i, s: (i, 0, 0)),
            ],
            scratch_shapes=[
                pltpu.VMEM((2, length, PAIR), BF16),
                pltpu.VMEM((2, length, PAIR), BF16),
                pltpu.VMEM((PAIR, length), BF16),
            ],
        ),
        out_shape=[
            jax.ShapeDtypeStruct((length, pairs * PAIR), BF16),
            jax.ShapeDtypeStruct((pairs * PAIR, length), BF16),
            jax.ShapeDtypeStruct((pairs, 2, length), F32),
        ],
        compiler_params=params(),
        name="attend",
    )(limit, mixed, mixed, mixed)


def gelu_both(values):
    root = math.sqrt(2.0 / math.pi)
    square = values * values
    tanh = jnp.tanh(root * values * (1.0 + 0.044715 * square))
    half = 0.5 + 0.5 * tanh
    slope = half + (0.5 * root) * values * (1.0 - tanh * tanh) * (1.0 + (3 * 0.044715) * square)
    return values * half, slope


def middle_kernel(
    limit_ref, x_ref, clock_ref, gain_ref, ctx_ref, og_ref, w0, w1, w2, w3,
    out_ref, active_ref, ug_ref, n_turn_ref, fg_turn_ref, ag_turn_ref, cg_ref, mg_ref, gg_ref,
    wide,
):
    step = pl.program_id(0)
    w_refs = (w0, w1, w2, w3)
    hidden = active_ref.shape[-1]
    up = slice(PAIR, PAIR + hidden)
    down = slice(PAIR + hidden, PAIR + 2 * hidden)

    @pl.when(step == 0)
    def _():
        gg_ref[...] = jnp.zeros_like(gg_ref)
        for part, w_ref in enumerate(w_refs):
            wide[:, part * PAIR : (part + 1) * PAIR] = w_ref[:, 0:PAIR]

    @pl.when(step * ROWS < limit_ref[0])
    def _():
        gain = gain_ref[...]
        live = step * ROWS + lax.broadcasted_iota(jnp.int32, (ROWS, 1), 0) < limit_ref[0]
        begin = join_tokens(x_ref) + clock_ref[...]
        middle = begin + mul(ctx_ref[...], wide[...], NT)
        unit, inverse = norm_parts(middle)
        normed = (unit * gain).astype(BF16)
        n_turn_ref[...] = normed.T
        res_grad = jnp.where(live, og_ref[0].astype(F32), 0.0)
        feed_grad = res_grad.astype(BF16)
        fg_turn_ref[...] = feed_grad.T
        feed = jnp.zeros_like(middle)
        two_grad = jnp.zeros_like(middle)
        for part, w_ref in enumerate(w_refs):
            upper = mul(normed, w_ref[:, up])
            active, slope = gelu_both(upper)
            active = active.astype(BF16)
            active_ref[part] = active
            feed += mul(active, w_ref[:, down], NT)
            upper_grad = (mul(feed_grad, w_ref[:, down]) * slope).astype(BF16)
            ug_ref[part] = upper_grad
            two_grad += mul(upper_grad, w_ref[:, up], NT)
        out_ref[0] = jnp.where(live, middle + feed, 0.0).astype(BF16)
        gg_ref[...] += jnp.sum(two_grad * unit, axis=0, keepdims=True)
        middle_grad = res_grad + norm_back(two_grad, gain, unit, inverse)
        mg_ref[...] = middle_grad
        att_grad = middle_grad.astype(BF16)
        ag_turn_ref[...] = att_grad.T
        cg_ref[...] = mul(att_grad, wide[...]).astype(BF16)

    @pl.when(step * ROWS >= limit_ref[0])
    def _():
        for ref in (out_ref, active_ref, ug_ref, n_turn_ref, fg_turn_ref, ag_turn_ref, cg_ref, mg_ref):
            ref[...] = jnp.zeros_like(ref)


def middle_block(limit, x_blocks, clock, gain, ctx, w_parts, out_grad):
    senders, feature_parts, tokens, width = x_blocks.shape
    length = senders * tokens
    features = feature_parts * width
    parts, hidden = len(w_parts), (w_parts[0].shape[1] - PAIR) // 2
    take = ROWS // tokens
    whole = lambda array: pl.BlockSpec(array.shape, lambda i, s: (0,) * array.ndim)
    rows = lambda n: pl.BlockSpec((ROWS, n), lambda i, s: (i, 0))
    turned = pl.BlockSpec((features, ROWS), lambda i, s: (0, i))
    one = pl.BlockSpec((1, ROWS, features), lambda i, s: (0, i, 0))
    units = pl.BlockSpec((parts, ROWS, hidden), lambda i, s: (0, i, 0))
    return pl.pallas_call(
        middle_kernel,
        grid_spec=pltpu.PrefetchScalarGridSpec(
            num_scalar_prefetch=1,
            grid=(length // ROWS,),
            in_specs=[
                pl.BlockSpec((take, feature_parts, tokens, width), lambda i, s: (i, 0, 0, 0)),
                whole(clock),
                whole(gain),
                rows(features),
                one,
            ]
            + [whole(w) for w in w_parts],
            out_specs=[
                one, units, units, turned, turned, turned, rows(features), rows(features),
                pl.BlockSpec((1, features), lambda i, s: (0, 0)),
            ],
            scratch_shapes=[pltpu.VMEM((features, features), BF16)],
        ),
        out_shape=[
            jax.ShapeDtypeStruct((1, length, features), BF16),
            jax.ShapeDtypeStruct((parts, length, hidden), BF16),
            jax.ShapeDtypeStruct((parts, length, hidden), BF16),
            jax.ShapeDtypeStruct((features, length), BF16),
            jax.ShapeDtypeStruct((features, length), BF16),
            jax.ShapeDtypeStruct((features, length), BF16),
            jax.ShapeDtypeStruct((length, features), BF16),
            jax.ShapeDtypeStruct((length, features), F32),
            jax.ShapeDtypeStruct((1, features), F32),
        ],
        compiler_params=params(),
        name="middle",
    )(limit, x_blocks, clock, gain, ctx, out_grad, *w_parts)


def weight_kernel(ag_turn_ref, ctx_ref, n_turn_ref, ug_ref, fg_turn_ref, active_ref, out_ref):
    hidden = ug_ref.shape[-1]
    out_ref[:, 0:PAIR] = mul(ag_turn_ref[...], ctx_ref[...]).astype(BF16)
    out_ref[:, PAIR : PAIR + hidden] = mul(n_turn_ref[...], ug_ref[0]).astype(BF16)
    out_ref[:, PAIR + hidden :] = mul(fg_turn_ref[...], active_ref[0]).astype(BF16)


def weight_grads(ag_turn, ctx, n_turn, upper_grad, fg_turn, active, part):
    features, length = ag_turn.shape
    hidden = active.shape[-1]
    turned = pl.BlockSpec((features, length), lambda i: (0, 0))
    units = pl.BlockSpec((1, length, hidden), lambda i: (part, 0, 0))
    return pl.pallas_call(
        weight_kernel,
        grid=(1,),
        in_specs=[
            turned, pl.BlockSpec((length, PAIR), lambda i: (0, part)), turned, units, turned, units,
        ],
        out_specs=pl.BlockSpec((features, PAIR + 2 * hidden), lambda i: (0, 0)),
        out_shape=jax.ShapeDtypeStruct((features, PAIR + 2 * hidden), BF16),
        compiler_params=params(),
        name=f"weight_grads_{part}",
    )(ag_turn, ctx, n_turn, upper_grad, fg_turn, active)


def attend_back_kernel(
    limit_ref, q_ref, k_ref, v_ref, turn_ref, lse_ref, cg_ref, n_turn_ref,
    dm_ref, wg_ref, keys_s, q_s, qz_s, do_s, kt_s, delta_s, dk_s, dv_s,
):
    limit = limit_ref[0]
    length = q_ref.shape[0]
    kt_s[...] = k_ref[...].astype(F32).T.astype(BF16)
    grad_turn = cg_ref[...].astype(F32).T
    along = grad_turn * turn_ref[...].astype(F32)
    for head in range(2):
        feats = slice(head * HEAD_DIM, (head + 1) * HEAD_DIM)
        delta_s[head : head + 1, :] = jnp.sum(along[feats, :], axis=0, keepdims=True)
        keys_s[head] = masked_keys(k_ref[...], head, limit)
        q_s[head] = masked_queries(q_ref[...], head)
        qz_s[head] = own_lanes(q_ref[...], head)
        do_s[head] = own_lanes(cg_ref[...], head)
    dk_s[...] = jnp.zeros_like(dk_s)
    dv_s[...] = jnp.zeros_like(dv_s)
    factor = SCORE_SCALE * LOG2E
    for block in range(length // CHUNK):
        span = slice(block * CHUNK, (block + 1) * CHUNK)

        @pl.when(block * CHUNK < limit)
        def _():
            turned = []
            for head in range(2):
                feats = slice(head * HEAD_DIM, (head + 1) * HEAD_DIM)
                scores = mul(keys_s[head], q_s[head, span, :], NT)
                prob = jnp.exp2(scores * factor - lse_ref[0, head : head + 1, span])
                prob_grad = mul(v_ref[...], do_s[head, span, :], NT)
                score_grad = (prob * (prob_grad - delta_s[head : head + 1, span])).astype(BF16)
                dv_s[...] += mul(prob.astype(BF16), do_s[head, span, :])
                dk_s[...] += mul(score_grad, qz_s[head, span, :])
                turned.append(mul(kt_s[feats, :], score_grad))
            dq = jnp.concatenate(turned, axis=0) * SCORE_SCALE
            dm_ref[span, 0:PAIR] = dq.T.astype(BF16)

        @pl.when(block * CHUNK >= limit)
        def _():
            dm_ref[span, 0:PAIR] = jnp.zeros((CHUNK, PAIR), BF16)

    dm_ref[:, PAIR : 2 * PAIR] = (dk_s[...] * SCORE_SCALE).astype(BF16)
    dm_ref[:, 2 * PAIR : 3 * PAIR] = dv_s[...].astype(BF16)
    wg_ref[...] = mul(n_turn_ref[...], dm_ref[...]).astype(BF16)


def attend_back(limit, mixed, ctx_turn, lse, context_grad, n_turn, pair):
    length = mixed.shape[0]
    features = n_turn.shape[0]
    column = lambda c: pl.BlockSpec((length, PAIR), lambda i, s: (0, pair * 3 + c))
    return pl.pallas_call(
        attend_back_kernel,
        grid_spec=pltpu.PrefetchScalarGridSpec(
            num_scalar_prefetch=1,
            grid=(1,),
            in_specs=[
                column(0), column(1), column(2),
                pl.BlockSpec((PAIR, length), lambda i, s: (pair, 0)),
                pl.BlockSpec((1, 2, length), lambda i, s: (pair, 0, 0)),
                pl.BlockSpec((length, PAIR), lambda i, s: (0, pair)),
                pl.BlockSpec((features, length), lambda i, s: (0, 0)),
            ],
            out_specs=[
                pl.BlockSpec((length, 3 * PAIR), lambda i, s: (0, 0)),
                pl.BlockSpec((features, 3 * PAIR), lambda i, s: (0, 0)),
            ],
            scratch_shapes=[
                pltpu.VMEM((2, length, PAIR), BF16),
                pltpu.VMEM((2, length, PAIR), BF16),
                pltpu.VMEM((2, length, PAIR), BF16),
                pltpu.VMEM((2, length, PAIR), BF16),
                pltpu.VMEM((PAIR, length), BF16),
                pltpu.VMEM((8, length), F32),
                pltpu.VMEM((length, PAIR), F32),
                pltpu.VMEM((length, PAIR), F32),
            ],
        ),
        out_shape=[
            jax.ShapeDtypeStruct((length, 3 * PAIR), BF16),
            jax.ShapeDtypeStruct((features, 3 * PAIR), BF16),
        ],
        compiler_params=params(),
        name=f"attend_back_{pair}",
    )(limit, mixed, mixed, mixed, ctx_turn, lse, context_grad, n_turn)


def begin_kernel(
    limit_ref, x_ref, clock_ref, gain_ref, mg_ref, w0, w1, w2, w3, d0, d1, d2, d3, bg_ref, gg_ref
):
    step = pl.program_id(0)

    @pl.when(step == 0)
    def _():
        gg_ref[...] = jnp.zeros_like(gg_ref)

    blocks, parts, tokens, width = bg_ref.shape

    @pl.when(step * ROWS < limit_ref[0])
    def _():
        begin = join_tokens(x_ref) + clock_ref[...]
        unit, inverse = norm_parts(begin)
        one_grad = jnp.zeros_like(begin)
        for w_ref, d_ref in ((w0, d0), (w1, d1), (w2, d2), (w3, d3)):
            one_grad += mul(d_ref[...], w_ref[...], NT)
        gg_ref[...] += jnp.sum(one_grad * unit, axis=0, keepdims=True)
        total = (mg_ref[...] + norm_back(one_grad, gain_ref[...], unit, inverse)).astype(BF16)
        for part in range(parts):
            bg_ref[:, part] = total[:, part * width : (part + 1) * width].reshape(blocks, tokens, width)

    @pl.when(step * ROWS >= limit_ref[0])
    def _():
        bg_ref[...] = jnp.zeros_like(bg_ref)


def begin_block(limit, x_blocks, clock, gain, w_parts, middle_grad, mixed_grads):
    senders, feature_parts, tokens, width = x_blocks.shape
    length = senders * tokens
    features = feature_parts * width
    take = ROWS // tokens
    whole = lambda array: pl.BlockSpec(array.shape, lambda i, s: (0,) * array.ndim)
    rows = lambda n: pl.BlockSpec((ROWS, n), lambda i, s: (i, 0))
    tokens_spec = pl.BlockSpec((take, feature_parts, tokens, width), lambda i, s: (i, 0, 0, 0))
    return pl.pallas_call(
        begin_kernel,
        grid_spec=pltpu.PrefetchScalarGridSpec(
            num_scalar_prefetch=1,
            grid=(length // ROWS,),
            in_specs=[
                tokens_spec, whole(clock), whole(gain), rows(features),
            ]
            + [whole(w) for w in w_parts]
            + [rows(3 * PAIR)] * 4,
            out_specs=[tokens_spec, pl.BlockSpec((1, features), lambda i, s: (0, 0))],
        ),
        out_shape=[
            jax.ShapeDtypeStruct(x_blocks.shape, BF16),
            jax.ShapeDtypeStruct((1, features), F32),
        ],
        compiler_params=params(),
        name="begin_back",
    )(limit, x_blocks, clock, gain, middle_grad, *w_parts, *mixed_grads)


def clock_rows(step_ids, features):
    half_width = features // 2
    ladder = jnp.arange(half_width, dtype=F32) / half_width
    rate_rows = jnp.exp(-math.log(10000.0) * ladder)
    angles = step_ids.astype(F32)[:, None] * rate_rows[None, :]
    return jnp.concatenate([jnp.sin(angles), jnp.cos(angles)], axis=-1)


def swap(value, apart):
    count = lax.axis_size("tensor")
    return lax.ppermute(value, "tensor", [(i, i ^ apart) for i in range(count)])


def collect(shard):
    count = lax.axis_size("dp")
    rows = lax.all_to_all(
        jnp.broadcast_to(shard[None], (count,) + shard.shape), "dp", 0, 0, tiled=True
    )
    rows = rows.reshape(count * shard.shape[0], shard.shape[1])
    across = swap(rows, 2)
    return rows, swap(rows, 1), across, swap(across, 1)


def add_up(parts):
    count = lax.axis_size("dp")
    wide = lambda value: value.astype(F32)
    far = (wide(parts[2]) + wide(swap(parts[3], 1))).astype(BF16)
    near = wide(parts[0]) + wide(swap(parts[1], 1))
    mine = (near + wide(swap(far, 2))).astype(BF16)
    rows = mine.shape[0] // count
    spread = lax.all_to_all(mine.reshape(count, rows, -1), "dp", 0, 0, tiled=True)
    return jnp.sum(wide(spread), axis=0)


def on_device(
    states, timesteps, lengths, deal_order, w_qkv, w_out, w_up, w_down, gain_attn, gain_ffn, out_grad
):
    both = ("dp", "tensor")
    dp_count = lax.axis_size("dp")
    tensor_count = lax.axis_size("tensor")
    devices = dp_count * tensor_count
    total_seqs, tokens, width = states.shape
    assert tensor_count == 4 and total_seqs == devices
    features = width * tensor_count
    own = lax.axis_index("dp") * tensor_count + lax.axis_index("tensor")
    own_id = lax.dynamic_slice_in_dim(deal_order, own, 1)
    limit = lengths[own_id]
    clock = clock_rows(timesteps[own_id], features)

    x_blocks = lax.all_to_all(states[deal_order], both, 0, 0, tiled=True)
    x_blocks = x_blocks.reshape(dp_count, tensor_count, tokens, width)
    rows = w_qkv.shape[0]
    qkv_parts = collect(w_qkv.reshape(rows, -1))
    rest_parts = collect(jnp.concatenate([w_out.T, w_up, w_down.T], axis=1))
    gains = jnp.concatenate([gain_attn, gain_ffn])
    gains = lax.all_to_all(jnp.broadcast_to(gains[None], (devices,) + gains.shape), both, 0, 0, tiled=True)
    per = gain_attn.shape[0]
    gain_one = gains[:, :per].reshape(1, features)
    gain_two = gains[:, per:].reshape(1, features)

    mixed, n_one_turn = project(limit, x_blocks, clock, gain_one, qkv_parts)
    ctx, ctx_turn, lse = attend(limit, mixed, tensor_count)
    output, active, upper_grad, n_two_turn, fg_turn, ag_turn, context_grad, middle_grad, two_grad = (
        middle_block(limit, x_blocks, clock, gain_two, ctx, rest_parts, out_grad)
    )
    rest_grads = [
        weight_grads(ag_turn, ctx, n_two_turn, upper_grad, fg_turn, active, part)
        for part in range(tensor_count)
    ]
    backs = {
        part: attend_back(limit, mixed, ctx_turn, lse, context_grad, n_one_turn, part)
        for part in (3, 1, 2, 0)
    }
    mixed_grads = [backs[part][0] for part in range(tensor_count)]
    begin_grad, one_grad = begin_block(
        limit, x_blocks, clock, gain_one, qkv_parts, middle_grad, mixed_grads
    )
    rest_total = add_up(rest_grads)
    qkv_total = add_up([backs[part][1] for part in range(tensor_count)])
    returned = lax.all_to_all(
        begin_grad.reshape(devices, tokens, width), both, 0, 0, tiled=True
    )
    inverse = (
        jnp.zeros((total_seqs,), jnp.int32)
        .at[deal_order]
        .set(jnp.arange(total_seqs, dtype=jnp.int32))
    )
    states_grad = returned[inverse]
    gain_grads = jnp.concatenate(
        [one_grad.reshape(devices, per), two_grad.reshape(devices, per)], axis=1
    )
    gain_grads = jnp.sum(lax.all_to_all(gain_grads, both, 0, 0, tiled=True), axis=0)
    hidden = w_up.shape[1]
    return (
        output,
        states_grad,
        qkv_total.reshape(w_qkv.shape),
        rest_total[:, :PAIR].T,
        rest_total[:, PAIR : PAIR + hidden],
        rest_total[:, PAIR + hidden :].T,
        gain_grads[:per],
        gain_grads[per:],
    )


def solution(mesh):
    in_specs = (
        P(None, "dp", "tensor"),
        P(),
        P(),
        P(),
        P("dp", None, "tensor"),
        P("tensor", "dp"),
        P("dp", "tensor"),
        P("tensor", "dp"),
        P(("dp", "tensor")),
        P(("dp", "tensor")),
        P(("dp", "tensor"), None, None),
    )
    out_specs = (
        P(("dp", "tensor"), None, None),
        P(None, "dp", "tensor"),
        P("dp", None, "tensor"),
        P("tensor", "dp"),
        P("dp", "tensor"),
        P("tensor", "dp"),
        P(("dp", "tensor")),
        P(("dp", "tensor")),
    )
    return jax.shard_map(
        on_device, mesh=mesh, in_specs=in_specs, out_specs=out_specs, check_vma=False
    )
```

```python
import functools
import math

import jax
import jax.numpy as jnp
from jax import lax
from jax.experimental import pallas as pl
from jax.experimental.pallas import tpu as pltpu
from jax.sharding import PartitionSpec as P

HEAD_DIM = 64
PAIR = 2 * HEAD_DIM
ROWS = 256
CHUNK = 256
SPARE = 8
SCORE_SCALE = 1.0 / math.sqrt(HEAD_DIM)
LOG2E = math.log2(math.e)
F32 = jnp.float32
BF16 = jnp.bfloat16
NN = (((1,), (0,)), ((), ()))
NT = (((1,), (1,)), ((), ()))
VMEM_LIMIT = 56 * 1024 * 1024


def mul(lhs, rhs, dims=NN):
    return lax.dot_general(lhs, rhs, dims, preferred_element_type=F32)


def join_tokens(ref):
    blocks, parts, tall, width = ref.shape
    tokens = tall - SPARE
    return jnp.concatenate(
        [ref[:, part, 0:tokens].reshape(blocks * tokens, width) for part in range(parts)], axis=-1
    ).astype(F32)


def place_rows(order_ref, source, target, columns):
    if order_ref is None:
        target[:, columns] = source
        return
    groups = order_ref.shape[0]
    rows = source.shape[0] // groups
    for group in range(groups):
        spot = pl.ds(pl.multiple_of(order_ref[group] * rows, rows), rows)
        target[spot, columns] = source[group * rows : (group + 1) * rows]


def norm_parts(values):
    center = values - jnp.mean(values, axis=-1, keepdims=True)
    spread = jnp.mean(center * center, axis=-1, keepdims=True)
    inverse = lax.rsqrt(spread + 1e-05)
    return center * inverse, inverse


def norm_back(grad, gain, unit, inverse):
    scaled = grad * gain
    mean_scaled = jnp.mean(scaled, axis=-1, keepdims=True)
    mean_along = jnp.mean(scaled * unit, axis=-1, keepdims=True)
    return inverse * (scaled - mean_scaled - unit * mean_along)


def cost(microseconds):
    return pl.CostEstimate(
        flops=int(microseconds * 1.15e9), bytes_accessed=1 << 20, transcendentals=0
    )


def params(**kwargs):
    return pltpu.CompilerParams(vmem_limit_bytes=VMEM_LIMIT, **kwargs)


def project_kernel(ordered, limit_ref, order_ref, x_ref, clock_ref, gain_ref, *refs):
    w_refs, (mixed_ref, n_turn_ref, wide) = refs[:-3], refs[-3:]
    step = pl.program_id(0)

    @pl.when(step == 0)
    def _():
        for part, w_ref in enumerate(w_refs):
            width = w_ref.shape[1]
            columns = slice(part * width, (part + 1) * width)
            place_rows(order_ref if ordered else None, w_ref[...], wide, columns)

    @pl.when(step * ROWS < limit_ref[0])
    def _():
        begin = join_tokens(x_ref) + clock_ref[...]
        unit, _ = norm_parts(begin)
        normed = (unit * gain_ref[...]).astype(BF16)
        n_turn_ref[...] = normed.T
        mixed_ref[...] = mul(normed, wide[...]).astype(BF16)

    @pl.when(step * ROWS >= limit_ref[0])
    def _():
        n_turn_ref[...] = jnp.zeros_like(n_turn_ref)
        mixed_ref[...] = jnp.zeros_like(mixed_ref)


def project(limit, order, ordered, x_blocks, clock, gain, w_parts):
    senders, feature_parts, tall, width = x_blocks.shape
    tokens = tall - SPARE
    length = senders * tokens
    features = feature_parts * width
    parts, columns = len(w_parts), w_parts[0].shape[1]
    take = ROWS // tokens
    return pl.pallas_call(
        functools.partial(project_kernel, ordered),
        grid_spec=pltpu.PrefetchScalarGridSpec(
            num_scalar_prefetch=2,
            grid=(length // ROWS,),
            in_specs=[
                pl.BlockSpec((take, feature_parts, tall, width), lambda i, *s: (i, 0, 0, 0)),
                pl.BlockSpec((1, features), lambda i, *s: (0, 0)),
                pl.BlockSpec((1, features), lambda i, *s: (0, 0)),
            ]
            + [pl.BlockSpec((features, columns), lambda i, *s: (0, 0))] * parts,
            out_specs=[
                pl.BlockSpec((ROWS, parts * columns), lambda i, *s: (i, 0)),
                pl.BlockSpec((features, ROWS), lambda i, *s: (0, i)),
                pl.BlockSpec((features, parts * columns), lambda i, *s: (0, 0)),
            ],
        ),
        out_shape=[
            jax.ShapeDtypeStruct((length, parts * columns), BF16),
            jax.ShapeDtypeStruct((features, length), BF16),
            jax.ShapeDtypeStruct((features, parts * columns), BF16),
        ],
        compiler_params=params(),
        cost_estimate=cost(5),
        name="project",
    )(limit, order, x_blocks, clock, gain, *w_parts)


def head_lanes(shape, head):
    lane = lax.broadcasted_iota(jnp.int32, shape, 1)
    return (lane >= head * HEAD_DIM) & (lane < (head + 1) * HEAD_DIM)


def spare_lane(shape, head):
    lane = lax.broadcasted_iota(jnp.int32, shape, 1)
    return lane == (1 - head) * HEAD_DIM


def masked_keys(keys, head, limit):
    row = lax.broadcasted_iota(jnp.int32, keys.shape, 0)
    spare = jnp.where(
        spare_lane(keys.shape, head) & (row >= limit), jnp.asarray(-1e30, F32), jnp.asarray(0.0, F32)
    )
    return jnp.where(head_lanes(keys.shape, head), keys.astype(F32), spare).astype(BF16)


def own_lanes(values, head):
    return jnp.where(head_lanes(values.shape, head), values.astype(F32), 0.0).astype(BF16)


def masked_queries(queries, head):
    spare = jnp.where(spare_lane(queries.shape, head), jnp.asarray(1.0, F32), jnp.asarray(0.0, F32))
    return jnp.where(head_lanes(queries.shape, head), queries.astype(F32), spare).astype(BF16)


def attend_kernel(limit_ref, q_ref, k_ref, v_ref, ctx_ref, turn_ref, lse_ref, keys_s, q_s, vt_s):
    limit = limit_ref[0]
    length = q_ref.shape[0]
    vt_s[...] = v_ref[...].astype(F32).T.astype(BF16)
    for head in range(2):
        keys_s[head] = masked_keys(k_ref[...], head, limit)
        q_s[head] = masked_queries(q_ref[...], head)
    factor = SCORE_SCALE * LOG2E
    for block in range(length // CHUNK):
        span = slice(block * CHUNK, (block + 1) * CHUNK)

        @pl.when(block * CHUNK < limit)
        def _():
            for head in range(2):
                feats = slice(head * HEAD_DIM, (head + 1) * HEAD_DIM)
                scores = mul(keys_s[head], q_s[head, span, :], NT) * factor
                peak = jnp.max(scores, axis=0, keepdims=True)
                expo = jnp.exp2(scores - peak)
                total = jnp.sum(expo, axis=0, keepdims=True)
                gathered = mul(vt_s[feats, :], expo.astype(BF16))
                turn_ref[feats, span] = (gathered / total).astype(BF16)
                lse_ref[0, head : head + 1, span] = peak + jnp.log2(total)
            ctx_ref[span, :] = turn_ref[:, span].astype(F32).T.astype(BF16)

        @pl.when(block * CHUNK >= limit)
        def _():
            turn_ref[:, span] = jnp.zeros_like(turn_ref[:, span])
            ctx_ref[span, :] = jnp.zeros_like(ctx_ref[span, :])
            lse_ref[0, :, span] = jnp.zeros_like(lse_ref[0, :, span])


def attend(limit, mixed, pairs):
    length = mixed.shape[0]
    column = lambda c: pl.BlockSpec((length, PAIR), lambda i, s: (0, i * 3 + c))
    return pl.pallas_call(
        attend_kernel,
        grid_spec=pltpu.PrefetchScalarGridSpec(
            num_scalar_prefetch=1,
            grid=(pairs,),
            in_specs=[column(0), column(1), column(2)],
            out_specs=[
                pl.BlockSpec((length, PAIR), lambda i, s: (0, i)),
                pl.BlockSpec((PAIR, length), lambda i, s: (i, 0)),
                pl.BlockSpec((1, 2, length), lambda i, s: (i, 0, 0)),
            ],
            scratch_shapes=[
                pltpu.VMEM((2, length, PAIR), BF16),
                pltpu.VMEM((2, length, PAIR), BF16),
                pltpu.VMEM((PAIR, length), BF16),
            ],
        ),
        out_shape=[
            jax.ShapeDtypeStruct((length, pairs * PAIR), BF16),
            jax.ShapeDtypeStruct((pairs * PAIR, length), BF16),
            jax.ShapeDtypeStruct((pairs, 2, length), F32),
        ],
        compiler_params=params(),
        cost_estimate=cost(28),
        name="attend",
    )(limit, mixed, mixed, mixed)


def gelu_both(values):
    root = math.sqrt(2.0 / math.pi)
    square = values * values
    tanh = jnp.tanh(root * values * (1.0 + 0.044715 * square))
    half = 0.5 + 0.5 * tanh
    slope = half + (0.5 * root) * values * (1.0 - tanh * tanh) * (1.0 + (3 * 0.044715) * square)
    return values * half, slope


def middle_kernel(
    ordered, limit_ref, order_ref, x_ref, clock_ref, gain_ref, ctx_ref, og_ref, w0, w1, w2, w3,
    out_ref, active_ref, ug_ref, n_turn_ref, fg_turn_ref, ag_turn_ref, cg_ref, mg_ref, gg_ref,
    wide, units,
):
    step = pl.program_id(0)
    hidden = active_ref.shape[-1]

    @pl.when(step == 0)
    def _():
        gg_ref[...] = jnp.zeros_like(gg_ref)
        table = order_ref if ordered else None
        for part, w_ref in enumerate((w0, w1, w2, w3)):
            columns = slice(part * PAIR, (part + 1) * PAIR)
            place_rows(table, w_ref[:, 0:PAIR], wide, columns)
            columns = slice(part * 2 * hidden, (part + 1) * 2 * hidden)
            place_rows(table, w_ref[:, PAIR:], units, columns)

    @pl.when(step * ROWS < limit_ref[0])
    def _():
        gain = gain_ref[...]
        live = step * ROWS + lax.broadcasted_iota(jnp.int32, (ROWS, 1), 0) < limit_ref[0]
        begin = join_tokens(x_ref) + clock_ref[...]
        middle = begin + mul(ctx_ref[...], wide[...], NT)
        unit, inverse = norm_parts(middle)
        normed = (unit * gain).astype(BF16)
        n_turn_ref[...] = normed.T
        res_grad = jnp.where(live, og_ref[0].astype(F32), 0.0)
        feed_grad = res_grad.astype(BF16)
        fg_turn_ref[...] = feed_grad.T
        feed = jnp.zeros_like(middle)
        two_grad = jnp.zeros_like(middle)
        for part in range(active_ref.shape[0]):
            up = slice(2 * part * hidden, (2 * part + 1) * hidden)
            down = slice((2 * part + 1) * hidden, (2 * part + 2) * hidden)
            upper = mul(normed, units[:, up])
            active, slope = gelu_both(upper)
            active = active.astype(BF16)
            active_ref[part] = active
            feed += mul(active, units[:, down], NT)
            upper_grad = (mul(feed_grad, units[:, down]) * slope).astype(BF16)
            ug_ref[part] = upper_grad
            two_grad += mul(upper_grad, units[:, up], NT)
        out_ref[0] = jnp.where(live, middle + feed, 0.0).astype(BF16)
        gg_ref[...] += jnp.sum(two_grad * unit, axis=0, keepdims=True)
        middle_grad = res_grad + norm_back(two_grad, gain, unit, inverse)
        mg_ref[...] = middle_grad
        att_grad = middle_grad.astype(BF16)
        ag_turn_ref[...] = att_grad.T
        cg_ref[...] = mul(att_grad, wide[...]).astype(BF16)

    @pl.when(step * ROWS >= limit_ref[0])
    def _():
        for ref in (out_ref, active_ref, ug_ref, n_turn_ref, fg_turn_ref, ag_turn_ref, cg_ref, mg_ref):
            ref[...] = jnp.zeros_like(ref)


def middle_block(limit, order, ordered, x_blocks, clock, gain, ctx, w_parts, out_grad):
    senders, feature_parts, tall, width = x_blocks.shape
    tokens = tall - SPARE
    length = senders * tokens
    features = feature_parts * width
    parts, hidden = len(w_parts), (w_parts[0].shape[1] - PAIR) // 2
    take = ROWS // tokens
    whole = lambda array: pl.BlockSpec(array.shape, lambda i, *s: (0,) * array.ndim)
    rows = lambda n: pl.BlockSpec((ROWS, n), lambda i, *s: (i, 0))
    turned = pl.BlockSpec((features, ROWS), lambda i, *s: (0, i))
    one = pl.BlockSpec((1, ROWS, features), lambda i, *s: (0, i, 0))
    units = pl.BlockSpec((parts, ROWS, hidden), lambda i, *s: (0, i, 0))
    return pl.pallas_call(
        functools.partial(middle_kernel, ordered),
        grid_spec=pltpu.PrefetchScalarGridSpec(
            num_scalar_prefetch=2,
            grid=(length // ROWS,),
            in_specs=[
                pl.BlockSpec((take, feature_parts, tall, width), lambda i, *s: (i, 0, 0, 0)),
                whole(clock),
                whole(gain),
                rows(features),
                one,
            ]
            + [whole(w) for w in w_parts],
            out_specs=[
                one, units, units, turned, turned, turned, rows(features), rows(features),
                pl.BlockSpec((1, features), lambda i, *s: (0, 0)),
            ],
            scratch_shapes=[
                pltpu.VMEM((features, parts * PAIR), BF16),
                pltpu.VMEM((features, parts * 2 * hidden), BF16),
            ],
        ),
        out_shape=[
            jax.ShapeDtypeStruct((1, length, features), BF16),
            jax.ShapeDtypeStruct((parts, length, hidden), BF16),
            jax.ShapeDtypeStruct((parts, length, hidden), BF16),
            jax.ShapeDtypeStruct((features, length), BF16),
            jax.ShapeDtypeStruct((features, length), BF16),
            jax.ShapeDtypeStruct((features, length), BF16),
            jax.ShapeDtypeStruct((length, features), BF16),
            jax.ShapeDtypeStruct((length, features), F32),
            jax.ShapeDtypeStruct((1, features), F32),
        ],
        compiler_params=params(),
        cost_estimate=cost(20),
        name="middle",
    )(limit, order, x_blocks, clock, gain, ctx, out_grad, *w_parts)


def send_kernel(count, *refs):
    out_ref = refs[-1]
    at = 0
    for left, right in zip(refs[:count], refs[count : 2 * count]):
        block = right[...] if len(right.shape) == 2 else right[0]
        out_ref[0, :, at : at + block.shape[1]] = mul(left[...], block).astype(BF16)
        at += block.shape[1]


def keep_kernel(count, *refs):
    came, far_ref, near_ref = refs[-3:]
    step = pl.program_id(0)

    def into(out_ref):
        at = 0
        for left, right in zip(refs[:count], refs[count : 2 * count]):
            block = right[...] if len(right.shape) == 2 else right[0]
            columns = slice(at, at + block.shape[1])
            total = mul(left[...], block) + came[0, :, columns].astype(F32)
            out_ref[:, columns] = total.astype(BF16)
            at += block.shape[1]

    @pl.when(step == 0)
    def _():
        into(far_ref)

    @pl.when(step == 1)
    def _():
        into(near_ref)


def weight_grads(lefts, rights, came=None):
    features, length = lefts[0].shape
    first = 3 if came is None else 2
    in_specs = [pl.BlockSpec((features, length), lambda i: (0, 0)) for _ in lefts]
    total = 0
    for right in rights:
        if right.ndim == 2:
            in_specs.append(pl.BlockSpec((length, PAIR), lambda i: (0, first - 2 * i)))
            total += PAIR
        else:
            in_specs.append(
                pl.BlockSpec((1, length, right.shape[2]), lambda i: (first - 2 * i, 0, 0))
            )
            total += right.shape[2]
    pair_spec = pl.BlockSpec((1, features, total), lambda i: (i, 0, 0))
    one = jax.ShapeDtypeStruct((features, total), BF16)
    one_spec = pl.BlockSpec((features, total), lambda i: (0, 0))
    if came is None:
        return pl.pallas_call(
            functools.partial(send_kernel, len(lefts)),
            grid=(2,),
            in_specs=in_specs,
            out_specs=pair_spec,
            out_shape=jax.ShapeDtypeStruct((2, features, total), BF16),
            compiler_params=params(),
            cost_estimate=cost(4),
            name="weight_grads_send",
        )(*lefts, *rights)
    return pl.pallas_call(
        functools.partial(keep_kernel, len(lefts)),
        grid=(2,),
        in_specs=in_specs + [pair_spec],
        out_specs=[one_spec, one_spec],
        out_shape=[one, one],
        compiler_params=params(),
        cost_estimate=cost(4),
        name="weight_grads_keep",
    )(*lefts, *rights, came)


def attend_back_kernel(limit_ref, q_ref, k_ref, v_ref, turn_ref, lse_ref, cg_ref, n_turn_ref, *refs):
    dm_ref, wg_ref, keys_s, q_s, qz_s, do_s, kt_s, delta_s, dk_s, dv_s = refs[-10:]
    limit = limit_ref[0]
    length = q_ref.shape[0]
    kt_s[...] = k_ref[...].astype(F32).T.astype(BF16)
    grad_turn = cg_ref[...].astype(F32).T
    along = grad_turn * turn_ref[...].astype(F32)
    for head in range(2):
        feats = slice(head * HEAD_DIM, (head + 1) * HEAD_DIM)
        delta_s[head : head + 1, :] = jnp.sum(along[feats, :], axis=0, keepdims=True)
        keys_s[head] = masked_keys(k_ref[...], head, limit)
        q_s[head] = masked_queries(q_ref[...], head)
        qz_s[head] = own_lanes(q_ref[...], head)
        do_s[head] = own_lanes(cg_ref[...], head)
    dk_s[...] = jnp.zeros_like(dk_s)
    dv_s[...] = jnp.zeros_like(dv_s)
    factor = SCORE_SCALE * LOG2E
    for block in range(length // CHUNK):
        span = slice(block * CHUNK, (block + 1) * CHUNK)

        @pl.when(block * CHUNK < limit)
        def _():
            turned = []
            for head in range(2):
                feats = slice(head * HEAD_DIM, (head + 1) * HEAD_DIM)
                scores = mul(keys_s[head], q_s[head, span, :], NT)
                prob = jnp.exp2(scores * factor - lse_ref[0, head : head + 1, span])
                prob_grad = mul(v_ref[...], do_s[head, span, :], NT)
                score_grad = (prob * (prob_grad - delta_s[head : head + 1, span])).astype(BF16)
                dv_s[...] += mul(prob.astype(BF16), do_s[head, span, :])
                dk_s[...] += mul(score_grad, qz_s[head, span, :])
                turned.append(mul(kt_s[feats, :], score_grad))
            dq = jnp.concatenate(turned, axis=0) * SCORE_SCALE
            dm_ref[span, 0:PAIR] = dq.T.astype(BF16)

        @pl.when(block * CHUNK >= limit)
        def _():
            dm_ref[span, 0:PAIR] = jnp.zeros((CHUNK, PAIR), BF16)

    dm_ref[:, PAIR : 2 * PAIR] = (dk_s[...] * SCORE_SCALE).astype(BF16)
    dm_ref[:, 2 * PAIR : 3 * PAIR] = dv_s[...].astype(BF16)
    grad = mul(n_turn_ref[...], dm_ref[...])
    if len(refs) > 10:
        grad += refs[0][...].astype(F32)
    wg_ref[...] = grad.astype(BF16)


def attend_back(limit, mixed, ctx_turn, lse, context_grad, n_turn, pair, came=None):
    length = mixed.shape[0]
    features = n_turn.shape[0]
    column = lambda c: pl.BlockSpec((length, PAIR), lambda i, s: (0, pair * 3 + c))
    return pl.pallas_call(
        attend_back_kernel,
        grid_spec=pltpu.PrefetchScalarGridSpec(
            num_scalar_prefetch=1,
            grid=(1,),
            in_specs=[
                column(0), column(1), column(2),
                pl.BlockSpec((PAIR, length), lambda i, s: (pair, 0)),
                pl.BlockSpec((1, 2, length), lambda i, s: (pair, 0, 0)),
                pl.BlockSpec((length, PAIR), lambda i, s: (0, pair)),
                pl.BlockSpec((features, length), lambda i, s: (0, 0)),
            ]
            + [pl.BlockSpec((features, 3 * PAIR), lambda i, s: (0, 0))] * (came is not None),
            out_specs=[
                pl.BlockSpec((length, 3 * PAIR), lambda i, s: (0, 0)),
                pl.BlockSpec((features, 3 * PAIR), lambda i, s: (0, 0)),
            ],
            scratch_shapes=[
                pltpu.VMEM((2, length, PAIR), BF16),
                pltpu.VMEM((2, length, PAIR), BF16),
                pltpu.VMEM((2, length, PAIR), BF16),
                pltpu.VMEM((2, length, PAIR), BF16),
                pltpu.VMEM((PAIR, length), BF16),
                pltpu.VMEM((8, length), F32),
                pltpu.VMEM((length, PAIR), F32),
                pltpu.VMEM((length, PAIR), F32),
            ],
        ),
        out_shape=[
            jax.ShapeDtypeStruct((length, 3 * PAIR), BF16),
            jax.ShapeDtypeStruct((features, 3 * PAIR), BF16),
        ],
        compiler_params=params(),
        cost_estimate=cost(10),
        name=f"attend_back_{pair}",
    )(limit, mixed, mixed, mixed, ctx_turn, lse, context_grad, n_turn, *([] if came is None else [came]))


def begin_kernel(
    limit_ref, x_ref, clock_ref, gain_ref, gg_two_ref, mg_ref, w_ref, d0, d1, d2, d3, bg_ref, gg_s
):
    step = pl.program_id(0)
    _, parts, tall, width = bg_ref.shape
    tokens = tall - SPARE
    blocks = ROWS // tokens
    spot = pl.ds(step * blocks, blocks)

    @pl.when(step == 0)
    def _():
        gg_s[...] = jnp.zeros_like(gg_s)

    @pl.when(step * ROWS < limit_ref[0])
    def _():
        begin = join_tokens(x_ref) + clock_ref[...]
        unit, inverse = norm_parts(begin)
        one_grad = jnp.zeros_like(begin)
        for part, d_ref in enumerate((d0, d1, d2, d3)):
            columns = slice(part * 3 * PAIR, (part + 1) * 3 * PAIR)
            one_grad += mul(d_ref[...], w_ref[:, columns], NT)
        gg_s[...] += jnp.sum(one_grad * unit, axis=0, keepdims=True)
        total = (mg_ref[...] + norm_back(one_grad, gain_ref[...], unit, inverse)).astype(BF16)
        for part in range(parts):
            piece = total[:, part * width : (part + 1) * width]
            bg_ref[spot, part, 0:tokens] = piece.reshape(blocks, tokens, width)

    @pl.when(step * ROWS >= limit_ref[0])
    def _():
        bg_ref[spot] = jnp.zeros((blocks,) + bg_ref.shape[1:], BF16)

    @pl.when(step == pl.num_programs(0) - 1)
    def _():
        rows = []
        for ref in (gg_s, gg_two_ref):
            for part in range(parts):
                rows.append(ref[:, part * width : (part + 1) * width])
        bg_ref[:, :, tokens:tall] = jnp.broadcast_to(
            jnp.concatenate(rows, axis=0).astype(BF16), bg_ref.shape[:2] + (SPARE, width)
        )


def begin_block(limit, x_blocks, clock, gain, two_grad, w_wide, middle_grad, mixed_grads):
    senders, feature_parts, tall, width = x_blocks.shape
    tokens = tall - SPARE
    length = senders * tokens
    features = feature_parts * width
    take = ROWS // tokens
    whole = lambda array: pl.BlockSpec(array.shape, lambda i, s: (0,) * array.ndim)
    rows = lambda n: pl.BlockSpec((ROWS, n), lambda i, s: (i, 0))
    return pl.pallas_call(
        begin_kernel,
        grid_spec=pltpu.PrefetchScalarGridSpec(
            num_scalar_prefetch=1,
            grid=(length // ROWS,),
            in_specs=[
                pl.BlockSpec((take, feature_parts, tall, width), lambda i, s: (i, 0, 0, 0)),
                whole(clock), whole(gain), whole(two_grad), rows(features), whole(w_wide),
            ]
            + [rows(3 * PAIR)] * 4,
            out_specs=whole(x_blocks),
            scratch_shapes=[pltpu.VMEM((1, features), F32)],
        ),
        out_shape=jax.ShapeDtypeStruct(x_blocks.shape, BF16),
        compiler_params=params(),
        cost_estimate=cost(7),
        name="begin_back",
    )(limit, x_blocks, clock, gain, two_grad, middle_grad, w_wide, *mixed_grads)


DIRECT = 8


def clock_rows(step_ids, features):
    half_width = features // 2
    ladder = jnp.arange(half_width, dtype=F32) / half_width
    rate_rows = jnp.exp(-math.log(10000.0) * ladder)
    angles = step_ids.astype(F32)[:, None] * rate_rows[None, :]
    return jnp.concatenate([jnp.sin(angles), jnp.cos(angles)], axis=-1)


def swap(value, apart):
    count = lax.axis_size("tensor")
    return lax.ppermute(value, "tensor", [(i, i ^ apart) for i in range(count)])


def ahead(value, step):
    count = lax.axis_size("dp")
    return lax.ppermute(value, "dp", [(i, (i + step) % count) for i in range(count)])


def row_order():
    count = lax.axis_size("dp")
    return (lax.axis_index("dp") - jnp.arange(count, dtype=jnp.int32)) % count


def collect_rows(shard):
    count = lax.axis_size("dp")
    if count <= DIRECT:
        return jnp.concatenate([shard] + [ahead(shard, step) for step in range(1, count)], axis=0)
    rows = lax.all_to_all(
        jnp.broadcast_to(shard[None], (count,) + shard.shape), "dp", 0, 0, tiled=True
    )
    return rows.reshape(count * shard.shape[0], shard.shape[1])


def collect_columns(rows):
    across = swap(rows, 2)
    return rows, swap(rows, 1), across, swap(across, 1)


def sum_rows(value):
    count = lax.axis_size("dp")
    groups = value.reshape(count, value.shape[0] // count, value.shape[1])
    if count <= DIRECT:
        own = lax.axis_index("dp")
        total = lax.dynamic_index_in_dim(groups, own, 0, keepdims=False).astype(F32)
        for step in range(1, count):
            group = lax.dynamic_index_in_dim(groups, (own + step) % count, 0, keepdims=False)
            total += ahead(group, step).astype(F32)
        return total
    return exchange_rows(value)


def exchange_rows(value):
    count = lax.axis_size("dp")
    groups = value.reshape(count, value.shape[0] // count, value.shape[1])
    return jnp.sum(lax.all_to_all(groups, "dp", 0, 0, tiled=True).astype(F32), axis=0)


def three_terms(values):
    terms = []
    for _ in range(3):
        term = lax.reduce_precision(values, 8, 7)
        terms.append(term.astype(BF16))
        values = values - term
    return terms


def after(value, *others):
    return lax.optimization_barrier((value,) + others)[0]


def on_device(
    states, timesteps, lengths, deal_order, w_qkv, w_out, w_up, w_down, gain_attn, gain_ffn, out_grad
):
    both = ("dp", "tensor")
    dp_count = lax.axis_size("dp")
    tensor_count = lax.axis_size("tensor")
    devices = dp_count * tensor_count
    total_seqs, tokens, width = states.shape
    assert tensor_count == 4 and total_seqs == devices
    features = width * tensor_count
    own = lax.axis_index("dp") * tensor_count + lax.axis_index("tensor")
    own_id = lax.dynamic_slice_in_dim(deal_order, own, 1)
    limit = lengths[own_id]
    clock = clock_rows(timesteps[own_id], features)
    ordered = dp_count <= DIRECT
    order = row_order()
    per = gain_attn.shape[0]
    rows = w_qkv.shape[0]
    hidden = w_up.shape[1]

    spare = jnp.stack(three_terms(gain_attn) + three_terms(gain_ffn)).reshape(1, 6 * per)
    spare = jnp.pad(spare, ((0, SPARE - 1), (0, width - 6 * per)))
    arranged = jnp.concatenate(
        [states[deal_order], jnp.broadcast_to(spare[None], (devices, SPARE, width))], axis=1
    )
    x_blocks = lax.all_to_all(arranged, both, 0, 0, tiled=True)
    gains = jnp.sum(x_blocks[:, tokens, : 6 * per].reshape(devices, 2, 3, per).astype(F32), axis=2)
    gain_one = gains[:, 0].reshape(1, features)
    gain_two = gains[:, 1].reshape(1, features)
    x_blocks = x_blocks.reshape(dp_count, tensor_count, tokens + SPARE, width)

    qkv_rows = collect_rows(w_qkv.reshape(rows, -1))
    qkv_parts = collect_columns(qkv_rows)
    rest = jnp.concatenate([w_out.T, w_up, w_down.T], axis=1)
    rest_parts = collect_columns(collect_rows(after(rest, qkv_rows)))

    mixed, n_one_turn, qkv_wide = project(limit, order, ordered, x_blocks, clock, gain_one, qkv_parts)
    ctx, ctx_turn, lse = attend(limit, mixed, tensor_count)
    output, active, upper_grad, n_two_turn, fg_turn, ag_turn, context_grad, middle_grad, two_grad = (
        middle_block(limit, order, ordered, x_blocks, clock, gain_two, ctx, rest_parts, out_grad)
    )

    down = ((fg_turn,), (active,))
    up = ((n_two_turn, ag_turn), (upper_grad, ctx))
    down_far = swap(weight_grads(*down), 1)
    up_far = swap(weight_grads(*up), 1)
    down_far, down_near = weight_grads(*down, down_far)
    up_far, up_near = weight_grads(*up, up_far)
    context_grad = after(context_grad, up_far, down_far)
    down_total = exchange_rows((down_near.astype(F32) + swap(down_far, 2).astype(F32)).astype(BF16))
    up_total = exchange_rows((up_near.astype(F32) + swap(up_far, 2).astype(F32)).astype(BF16))

    back = functools.partial(attend_back, limit, mixed, ctx_turn, lse)
    mixed_three, grad_three = back(context_grad, n_one_turn, 3)
    came_three = swap(grad_three, 1)
    context_grad = after(context_grad, grad_three)
    mixed_one, grad_one = back(context_grad, n_one_turn, 1)
    came_one = swap(grad_one, 1)
    context_grad = after(context_grad, grad_one)
    mixed_two, far = back(context_grad, n_one_turn, 2, came_three)
    context_grad = after(context_grad, far)
    mixed_own, near = back(context_grad, n_one_turn, 0, came_one)
    qkv_sum = (near.astype(F32) + swap(far, 2).astype(F32)).astype(BF16)
    begin_grad = begin_block(
        limit, x_blocks, clock, gain_one, two_grad, qkv_wide, middle_grad,
        (mixed_own, mixed_one, mixed_two, mixed_three),
    )
    qkv_total = sum_rows(qkv_sum)
    returned = lax.all_to_all(
        begin_grad.reshape(devices, tokens + SPARE, width), both, 0, 0, tiled=True
    )
    inverse = (
        jnp.zeros((total_seqs,), jnp.int32)
        .at[deal_order]
        .set(jnp.arange(total_seqs, dtype=jnp.int32))
    )
    states_grad = returned[:, :tokens][inverse]
    gain_grads = jnp.sum(returned[:, tokens:].astype(F32), axis=0).reshape(2, devices, per)
    gain_grads = lax.dynamic_index_in_dim(gain_grads, own, 1, keepdims=False)
    return (
        output,
        states_grad,
        qkv_total.reshape(w_qkv.shape),
        up_total[:, hidden:].T,
        up_total[:, :hidden],
        down_total.T,
        gain_grads[0],
        gain_grads[1],
    )


def solution(mesh):
    in_specs = (
        P(None, "dp", "tensor"),
        P(),
        P(),
        P(),
        P("dp", None, "tensor"),
        P("tensor", "dp"),
        P("dp", "tensor"),
        P("tensor", "dp"),
        P(("dp", "tensor")),
        P(("dp", "tensor")),
        P(("dp", "tensor"), None, None),
    )
    out_specs = (
        P(("dp", "tensor"), None, None),
        P(None, "dp", "tensor"),
        P("dp", None, "tensor"),
        P("tensor", "dp"),
        P("dp", "tensor"),
        P("tensor", "dp"),
        P(("dp", "tensor")),
        P(("dp", "tensor")),
    )
    return jax.shard_map(
        on_device, mesh=mesh, in_specs=in_specs, out_specs=out_specs, check_vma=False
    )
```

```python
import functools
import math

import jax
import jax.numpy as jnp
from jax import lax
from jax.experimental import pallas as pl
from jax.experimental.pallas import tpu as pltpu
from jax.sharding import PartitionSpec as P

HEAD_DIM = 64
PAIR = 2 * HEAD_DIM
ROWS = 256
CHUNK = 256
SPARE = 8
SCORE_SCALE = 1.0 / math.sqrt(HEAD_DIM)
LOG2E = math.log2(math.e)
F32 = jnp.float32
BF16 = jnp.bfloat16
NN = (((1,), (0,)), ((), ()))
NT = (((1,), (1,)), ((), ()))
VMEM_LIMIT = 56 * 1024 * 1024


def mul(lhs, rhs, dims=NN):
    return lax.dot_general(lhs, rhs, dims, preferred_element_type=F32)


def join_tokens(ref):
    blocks, parts, tall, width = ref.shape
    tokens = tall - SPARE
    return jnp.concatenate(
        [ref[:, part, 0:tokens].reshape(blocks * tokens, width) for part in range(parts)], axis=-1
    ).astype(F32)


def norm_parts(values):
    center = values - jnp.mean(values, axis=-1, keepdims=True)
    spread = jnp.mean(center * center, axis=-1, keepdims=True)
    inverse = lax.rsqrt(spread + 1e-05)
    return center * inverse, inverse


def norm_back(grad, gain, unit, inverse):
    scaled = grad * gain
    mean_scaled = jnp.mean(scaled, axis=-1, keepdims=True)
    mean_along = jnp.mean(scaled * unit, axis=-1, keepdims=True)
    return inverse * (scaled - mean_scaled - unit * mean_along)


def cost(microseconds):
    return pl.CostEstimate(
        flops=int(microseconds * 1.15e9), bytes_accessed=1 << 20, transcendentals=0
    )


def params(**kwargs):
    return pltpu.CompilerParams(vmem_limit_bytes=VMEM_LIMIT, **kwargs)


def project_kernel(limit_ref, x_ref, clock_ref, gain_ref, *refs):
    w_refs, (mixed_ref, n_turn_ref, wide) = refs[:-3], refs[-3:]
    step = pl.program_id(0)

    @pl.when(step == 0)
    def _():
        for part, w_ref in enumerate(w_refs):
            width = w_ref.shape[1]
            columns = slice(part * width, (part + 1) * width)
            wide[:, columns] = w_ref[...]

    @pl.when(step * ROWS < limit_ref[0])
    def _():
        begin = join_tokens(x_ref) + clock_ref[...]
        unit, _ = norm_parts(begin)
        normed = (unit * gain_ref[...]).astype(BF16)
        n_turn_ref[...] = normed.T
        mixed_ref[...] = mul(normed, wide[...]).astype(BF16)

    @pl.when(step * ROWS >= limit_ref[0])
    def _():
        n_turn_ref[...] = jnp.zeros_like(n_turn_ref)
        mixed_ref[...] = jnp.zeros_like(mixed_ref)


def project(limit, x_blocks, clock, gain, w_parts):
    senders, feature_parts, tall, width = x_blocks.shape
    tokens = tall - SPARE
    length = senders * tokens
    features = feature_parts * width
    parts, columns = len(w_parts), w_parts[0].shape[1]
    take = ROWS // tokens
    return pl.pallas_call(
        project_kernel,
        grid_spec=pltpu.PrefetchScalarGridSpec(
            num_scalar_prefetch=1,
            grid=(length // ROWS,),
            in_specs=[
                pl.BlockSpec((take, feature_parts, tall, width), lambda i, *s: (i, 0, 0, 0)),
                pl.BlockSpec((1, features), lambda i, *s: (0, 0)),
                pl.BlockSpec((1, features), lambda i, *s: (0, 0)),
            ]
            + [pl.BlockSpec((features, columns), lambda i, *s: (0, 0))] * parts,
            out_specs=[
                pl.BlockSpec((ROWS, parts * columns), lambda i, *s: (i, 0)),
                pl.BlockSpec((features, ROWS), lambda i, *s: (0, i)),
                pl.BlockSpec((features, parts * columns), lambda i, *s: (0, 0)),
            ],
        ),
        out_shape=[
            jax.ShapeDtypeStruct((length, parts * columns), BF16),
            jax.ShapeDtypeStruct((features, length), BF16),
            jax.ShapeDtypeStruct((features, parts * columns), BF16),
        ],
        compiler_params=params(),
        cost_estimate=cost(5),
        name="project",
    )(limit, x_blocks, clock, gain, *w_parts)


def head_lanes(shape, head):
    lane = lax.broadcasted_iota(jnp.int32, shape, 1)
    return (lane >= head * HEAD_DIM) & (lane < (head + 1) * HEAD_DIM)


def spare_lane(shape, head):
    lane = lax.broadcasted_iota(jnp.int32, shape, 1)
    return lane == (1 - head) * HEAD_DIM


def masked_keys(keys, head, limit):
    row = lax.broadcasted_iota(jnp.int32, keys.shape, 0)
    spare = jnp.where(
        spare_lane(keys.shape, head) & (row >= limit), jnp.asarray(-1e30, F32), jnp.asarray(0.0, F32)
    )
    return jnp.where(head_lanes(keys.shape, head), keys.astype(F32), spare).astype(BF16)


def own_lanes(values, head):
    return jnp.where(head_lanes(values.shape, head), values.astype(F32), 0.0).astype(BF16)


def masked_queries(queries, head):
    spare = jnp.where(spare_lane(queries.shape, head), jnp.asarray(1.0, F32), jnp.asarray(0.0, F32))
    return jnp.where(head_lanes(queries.shape, head), queries.astype(F32), spare).astype(BF16)


def attend_kernel(limit_ref, q_ref, k_ref, v_ref, ctx_ref, turn_ref, lse_ref, keys_s, q_s, vt_s):
    limit = limit_ref[0]
    length = q_ref.shape[0]
    vt_s[...] = v_ref[...].astype(F32).T.astype(BF16)
    for head in range(2):
        keys_s[head] = masked_keys(k_ref[...], head, limit)
        q_s[head] = masked_queries(q_ref[...], head)
    factor = SCORE_SCALE * LOG2E
    for block in range(length // CHUNK):
        span = slice(block * CHUNK, (block + 1) * CHUNK)

        @pl.when(block * CHUNK < limit)
        def _():
            for head in range(2):
                feats = slice(head * HEAD_DIM, (head + 1) * HEAD_DIM)
                scores = mul(keys_s[head], q_s[head, span, :], NT) * factor
                peak = jnp.max(scores, axis=0, keepdims=True)
                expo = jnp.exp2(scores - peak)
                total = jnp.sum(expo, axis=0, keepdims=True)
                gathered = mul(vt_s[feats, :], expo.astype(BF16))
                turn_ref[feats, span] = (gathered / total).astype(BF16)
                lse_ref[0, head : head + 1, span] = peak + jnp.log2(total)
            ctx_ref[span, :] = turn_ref[:, span].astype(F32).T.astype(BF16)

        @pl.when(block * CHUNK >= limit)
        def _():
            turn_ref[:, span] = jnp.zeros_like(turn_ref[:, span])
            ctx_ref[span, :] = jnp.zeros_like(ctx_ref[span, :])
            lse_ref[0, :, span] = jnp.zeros_like(lse_ref[0, :, span])


def attend(limit, mixed, pairs):
    length = mixed.shape[0]
    column = lambda c: pl.BlockSpec((length, PAIR), lambda i, s: (0, i * 3 + c))
    return pl.pallas_call(
        attend_kernel,
        grid_spec=pltpu.PrefetchScalarGridSpec(
            num_scalar_prefetch=1,
            grid=(pairs,),
            in_specs=[column(0), column(1), column(2)],
            out_specs=[
                pl.BlockSpec((length, PAIR), lambda i, s: (0, i)),
                pl.BlockSpec((PAIR, length), lambda i, s: (i, 0)),
                pl.BlockSpec((1, 2, length), lambda i, s: (i, 0, 0)),
            ],
            scratch_shapes=[
                pltpu.VMEM((2, length, PAIR), BF16),
                pltpu.VMEM((2, length, PAIR), BF16),
                pltpu.VMEM((PAIR, length), BF16),
            ],
        ),
        out_shape=[
            jax.ShapeDtypeStruct((length, pairs * PAIR), BF16),
            jax.ShapeDtypeStruct((pairs * PAIR, length), BF16),
            jax.ShapeDtypeStruct((pairs, 2, length), F32),
        ],
        compiler_params=params(),
        cost_estimate=cost(28),
        name="attend",
    )(limit, mixed, mixed, mixed)


def gelu_both(values):
    root = math.sqrt(2.0 / math.pi)
    square = values * values
    tanh = jnp.tanh(root * values * (1.0 + 0.044715 * square))
    half = 0.5 + 0.5 * tanh
    slope = half + (0.5 * root) * values * (1.0 - tanh * tanh) * (1.0 + (3 * 0.044715) * square)
    return values * half, slope


def middle_kernel(
    limit_ref, rank_ref, x_ref, clock_ref, gain_ref, ctx_ref, og_ref, w_ref,
    out_ref, active_ref, ug_ref, n_turn_ref, fg_turn_ref, ag_turn_ref, cg_ref, mg_ref, gg_ref,
    wide, units,
):
    step = pl.program_id(0)
    hidden = active_ref.shape[-1]

    @pl.when(step == 0)
    def _():
        gg_ref[...] = jnp.zeros_like(gg_ref)
        parts = active_ref.shape[0]
        rows = w_ref.shape[1]
        for part in range(parts):
            for sender in range(w_ref.shape[0] // parts):
                source = w_ref.at[sender * parts + (rank_ref[0] ^ part)]
                spot = slice(sender * rows, (sender + 1) * rows)
                wide[spot, part * PAIR : (part + 1) * PAIR] = source[:, 0:PAIR]
                columns = slice(part * 2 * hidden, (part + 1) * 2 * hidden)
                units[spot, columns] = source[:, PAIR:]

    @pl.when(step * ROWS < limit_ref[0])
    def _():
        gain = gain_ref[...]
        live = step * ROWS + lax.broadcasted_iota(jnp.int32, (ROWS, 1), 0) < limit_ref[0]
        begin = join_tokens(x_ref) + clock_ref[...]
        middle = begin + mul(ctx_ref[...], wide[...], NT)
        unit, inverse = norm_parts(middle)
        normed = (unit * gain).astype(BF16)
        n_turn_ref[...] = normed.T
        res_grad = jnp.where(live, og_ref[0].astype(F32), 0.0)
        feed_grad = res_grad.astype(BF16)
        fg_turn_ref[...] = feed_grad.T
        feed = jnp.zeros_like(middle)
        two_grad = jnp.zeros_like(middle)
        for part in range(active_ref.shape[0]):
            up = slice(2 * part * hidden, (2 * part + 1) * hidden)
            down = slice((2 * part + 1) * hidden, (2 * part + 2) * hidden)
            upper = mul(normed, units[:, up])
            active, slope = gelu_both(upper)
            active = active.astype(BF16)
            active_ref[part] = active
            feed += mul(active, units[:, down], NT)
            upper_grad = (mul(feed_grad, units[:, down]) * slope).astype(BF16)
            ug_ref[part] = upper_grad
            two_grad += mul(upper_grad, units[:, up], NT)
        out_ref[0] = jnp.where(live, middle + feed, 0.0).astype(BF16)
        gg_ref[...] += jnp.sum(two_grad * unit, axis=0, keepdims=True)
        middle_grad = res_grad + norm_back(two_grad, gain, unit, inverse)
        mg_ref[...] = middle_grad
        att_grad = middle_grad.astype(BF16)
        ag_turn_ref[...] = att_grad.T
        cg_ref[...] = mul(att_grad, wide[...]).astype(BF16)

    @pl.when(step * ROWS >= limit_ref[0])
    def _():
        for ref in (out_ref, active_ref, ug_ref, n_turn_ref, fg_turn_ref, ag_turn_ref, cg_ref, mg_ref):
            ref[...] = jnp.zeros_like(ref)


def middle_block(limit, rank, x_blocks, clock, gain, ctx, w_all, parts, out_grad):
    senders, feature_parts, tall, width = x_blocks.shape
    tokens = tall - SPARE
    length = senders * tokens
    features = feature_parts * width
    hidden = (w_all.shape[2] - PAIR) // 2
    take = ROWS // tokens
    whole = lambda array: pl.BlockSpec(array.shape, lambda i, *s: (0,) * array.ndim)
    rows = lambda n: pl.BlockSpec((ROWS, n), lambda i, *s: (i, 0))
    turned = pl.BlockSpec((features, ROWS), lambda i, *s: (0, i))
    one = pl.BlockSpec((1, ROWS, features), lambda i, *s: (0, i, 0))
    units = pl.BlockSpec((parts, ROWS, hidden), lambda i, *s: (0, i, 0))
    return pl.pallas_call(
        middle_kernel,
        grid_spec=pltpu.PrefetchScalarGridSpec(
            num_scalar_prefetch=2,
            grid=(length // ROWS,),
            in_specs=[
                pl.BlockSpec((take, feature_parts, tall, width), lambda i, *s: (i, 0, 0, 0)),
                whole(clock),
                whole(gain),
                rows(features),
                one,
                whole(w_all),
            ],
            out_specs=[
                one, units, units, turned, turned, turned, rows(features), rows(features),
                pl.BlockSpec((1, features), lambda i, *s: (0, 0)),
            ],
            scratch_shapes=[
                pltpu.VMEM((features, parts * PAIR), BF16),
                pltpu.VMEM((features, parts * 2 * hidden), BF16),
            ],
        ),
        out_shape=[
            jax.ShapeDtypeStruct((1, length, features), BF16),
            jax.ShapeDtypeStruct((parts, length, hidden), BF16),
            jax.ShapeDtypeStruct((parts, length, hidden), BF16),
            jax.ShapeDtypeStruct((features, length), BF16),
            jax.ShapeDtypeStruct((features, length), BF16),
            jax.ShapeDtypeStruct((features, length), BF16),
            jax.ShapeDtypeStruct((length, features), BF16),
            jax.ShapeDtypeStruct((length, features), F32),
            jax.ShapeDtypeStruct((1, features), F32),
        ],
        compiler_params=params(),
        cost_estimate=cost(20),
        name="middle",
    )(limit, rank, x_blocks, clock, gain, ctx, out_grad, w_all)


def send_kernel(count, *refs):
    out_ref = refs[-1]
    at = 0
    for left, right in zip(refs[:count], refs[count : 2 * count]):
        block = right[...] if len(right.shape) == 2 else right[0]
        out_ref[0, :, at : at + block.shape[1]] = mul(left[...], block).astype(BF16)
        at += block.shape[1]


def keep_kernel(count, *refs):
    came, far_ref, near_ref = refs[-3:]
    step = pl.program_id(0)

    def into(out_ref):
        at = 0
        for left, right in zip(refs[:count], refs[count : 2 * count]):
            block = right[...] if len(right.shape) == 2 else right[0]
            columns = slice(at, at + block.shape[1])
            total = mul(left[...], block) + came[0, :, columns].astype(F32)
            out_ref[:, columns] = total.astype(BF16)
            at += block.shape[1]

    @pl.when(step == 0)
    def _():
        into(far_ref)

    @pl.when(step == 1)
    def _():
        into(near_ref)


def weight_grads(lefts, rights, came=None):
    features, length = lefts[0].shape
    first = 3 if came is None else 2
    in_specs = [pl.BlockSpec((features, length), lambda i: (0, 0)) for _ in lefts]
    total = 0
    for right in rights:
        if right.ndim == 2:
            in_specs.append(pl.BlockSpec((length, PAIR), lambda i: (0, first - 2 * i)))
            total += PAIR
        else:
            in_specs.append(
                pl.BlockSpec((1, length, right.shape[2]), lambda i: (first - 2 * i, 0, 0))
            )
            total += right.shape[2]
    pair_spec = pl.BlockSpec((1, features, total), lambda i: (i, 0, 0))
    one = jax.ShapeDtypeStruct((features, total), BF16)
    one_spec = pl.BlockSpec((features, total), lambda i: (0, 0))
    if came is None:
        return pl.pallas_call(
            functools.partial(send_kernel, len(lefts)),
            grid=(2,),
            in_specs=in_specs,
            out_specs=pair_spec,
            out_shape=jax.ShapeDtypeStruct((2, features, total), BF16),
            compiler_params=params(),
            cost_estimate=cost(4),
            name="weight_grads_send",
        )(*lefts, *rights)
    return pl.pallas_call(
        functools.partial(keep_kernel, len(lefts)),
        grid=(2,),
        in_specs=in_specs + [pair_spec],
        out_specs=[one_spec, one_spec],
        out_shape=[one, one],
        compiler_params=params(),
        cost_estimate=cost(4),
        name="weight_grads_keep",
    )(*lefts, *rights, came)


def attend_back_kernel(limit_ref, q_ref, k_ref, v_ref, turn_ref, lse_ref, cg_ref, n_turn_ref, *refs):
    dm_ref, wg_ref, keys_s, q_s, qz_s, do_s, kt_s, delta_s, dk_s, dv_s = refs[-10:]
    limit = limit_ref[0]
    length = q_ref.shape[0]
    kt_s[...] = k_ref[...].astype(F32).T.astype(BF16)
    grad_turn = cg_ref[...].astype(F32).T
    along = grad_turn * turn_ref[...].astype(F32)
    for head in range(2):
        feats = slice(head * HEAD_DIM, (head + 1) * HEAD_DIM)
        delta_s[head : head + 1, :] = jnp.sum(along[feats, :], axis=0, keepdims=True)
        keys_s[head] = masked_keys(k_ref[...], head, limit)
        q_s[head] = masked_queries(q_ref[...], head)
        qz_s[head] = own_lanes(q_ref[...], head)
        do_s[head] = own_lanes(cg_ref[...], head)
    dk_s[...] = jnp.zeros_like(dk_s)
    dv_s[...] = jnp.zeros_like(dv_s)
    factor = SCORE_SCALE * LOG2E
    for block in range(length // CHUNK):
        span = slice(block * CHUNK, (block + 1) * CHUNK)

        @pl.when(block * CHUNK < limit)
        def _():
            turned = []
            for head in range(2):
                feats = slice(head * HEAD_DIM, (head + 1) * HEAD_DIM)
                scores = mul(keys_s[head], q_s[head, span, :], NT)
                prob = jnp.exp2(scores * factor - lse_ref[0, head : head + 1, span])
                prob_grad = mul(v_ref[...], do_s[head, span, :], NT)
                score_grad = (prob * (prob_grad - delta_s[head : head + 1, span])).astype(BF16)
                dv_s[...] += mul(prob.astype(BF16), do_s[head, span, :])
                dk_s[...] += mul(score_grad, qz_s[head, span, :])
                turned.append(mul(kt_s[feats, :], score_grad))
            dq = jnp.concatenate(turned, axis=0) * SCORE_SCALE
            dm_ref[span, 0:PAIR] = dq.T.astype(BF16)

        @pl.when(block * CHUNK >= limit)
        def _():
            dm_ref[span, 0:PAIR] = jnp.zeros((CHUNK, PAIR), BF16)

    dm_ref[:, PAIR : 2 * PAIR] = (dk_s[...] * SCORE_SCALE).astype(BF16)
    dm_ref[:, 2 * PAIR : 3 * PAIR] = dv_s[...].astype(BF16)
    grad = mul(n_turn_ref[...], dm_ref[...])
    if len(refs) > 10:
        grad += refs[0][...].astype(F32)
    wg_ref[...] = grad.astype(BF16)


def attend_back(limit, mixed, ctx_turn, lse, context_grad, n_turn, pair, came=None):
    length = mixed.shape[0]
    features = n_turn.shape[0]
    column = lambda c: pl.BlockSpec((length, PAIR), lambda i, s: (0, pair * 3 + c))
    return pl.pallas_call(
        attend_back_kernel,
        grid_spec=pltpu.PrefetchScalarGridSpec(
            num_scalar_prefetch=1,
            grid=(1,),
            in_specs=[
                column(0), column(1), column(2),
                pl.BlockSpec((PAIR, length), lambda i, s: (pair, 0)),
                pl.BlockSpec((1, 2, length), lambda i, s: (pair, 0, 0)),
                pl.BlockSpec((length, PAIR), lambda i, s: (0, pair)),
                pl.BlockSpec((features, length), lambda i, s: (0, 0)),
            ]
            + [pl.BlockSpec((features, 3 * PAIR), lambda i, s: (0, 0))] * (came is not None),
            out_specs=[
                pl.BlockSpec((length, 3 * PAIR), lambda i, s: (0, 0)),
                pl.BlockSpec((features, 3 * PAIR), lambda i, s: (0, 0)),
            ],
            scratch_shapes=[
                pltpu.VMEM((2, length, PAIR), BF16),
                pltpu.VMEM((2, length, PAIR), BF16),
                pltpu.VMEM((2, length, PAIR), BF16),
                pltpu.VMEM((2, length, PAIR), BF16),
                pltpu.VMEM((PAIR, length), BF16),
                pltpu.VMEM((8, length), F32),
                pltpu.VMEM((length, PAIR), F32),
                pltpu.VMEM((length, PAIR), F32),
            ],
        ),
        out_shape=[
            jax.ShapeDtypeStruct((length, 3 * PAIR), BF16),
            jax.ShapeDtypeStruct((features, 3 * PAIR), BF16),
        ],
        compiler_params=params(),
        cost_estimate=cost(10),
        name=f"attend_back_{pair}",
    )(limit, mixed, mixed, mixed, ctx_turn, lse, context_grad, n_turn, *([] if came is None else [came]))


def begin_kernel(
    limit_ref, x_ref, clock_ref, gain_ref, gg_two_ref, mg_ref, w_ref, d0, d1, d2, d3, bg_ref, gg_s
):
    step = pl.program_id(0)
    _, parts, tall, width = bg_ref.shape
    tokens = tall - SPARE
    blocks = ROWS // tokens
    spot = pl.ds(step * blocks, blocks)

    @pl.when(step == 0)
    def _():
        gg_s[...] = jnp.zeros_like(gg_s)

    @pl.when(step * ROWS < limit_ref[0])
    def _():
        begin = join_tokens(x_ref) + clock_ref[...]
        unit, inverse = norm_parts(begin)
        one_grad = jnp.zeros_like(begin)
        for part, d_ref in enumerate((d0, d1, d2, d3)):
            columns = slice(part * 3 * PAIR, (part + 1) * 3 * PAIR)
            one_grad += mul(d_ref[...], w_ref[:, columns], NT)
        gg_s[...] += jnp.sum(one_grad * unit, axis=0, keepdims=True)
        total = (mg_ref[...] + norm_back(one_grad, gain_ref[...], unit, inverse)).astype(BF16)
        for part in range(parts):
            piece = total[:, part * width : (part + 1) * width]
            bg_ref[spot, part, 0:tokens] = piece.reshape(blocks, tokens, width)

    @pl.when(step * ROWS >= limit_ref[0])
    def _():
        bg_ref[spot] = jnp.zeros((blocks,) + bg_ref.shape[1:], BF16)

    @pl.when(step == pl.num_programs(0) - 1)
    def _():
        rows = []
        for ref in (gg_s, gg_two_ref):
            for part in range(parts):
                rows.append(ref[:, part * width : (part + 1) * width])
        bg_ref[:, :, tokens:tall] = jnp.broadcast_to(
            jnp.concatenate(rows, axis=0).astype(BF16), bg_ref.shape[:2] + (SPARE, width)
        )


def begin_block(limit, x_blocks, clock, gain, two_grad, w_wide, middle_grad, mixed_grads):
    senders, feature_parts, tall, width = x_blocks.shape
    tokens = tall - SPARE
    length = senders * tokens
    features = feature_parts * width
    take = ROWS // tokens
    whole = lambda array: pl.BlockSpec(array.shape, lambda i, s: (0,) * array.ndim)
    rows = lambda n: pl.BlockSpec((ROWS, n), lambda i, s: (i, 0))
    return pl.pallas_call(
        begin_kernel,
        grid_spec=pltpu.PrefetchScalarGridSpec(
            num_scalar_prefetch=1,
            grid=(length // ROWS,),
            in_specs=[
                pl.BlockSpec((take, feature_parts, tall, width), lambda i, s: (i, 0, 0, 0)),
                whole(clock), whole(gain), whole(two_grad), rows(features), whole(w_wide),
            ]
            + [rows(3 * PAIR)] * 4,
            out_specs=whole(x_blocks),
            scratch_shapes=[pltpu.VMEM((1, features), F32)],
        ),
        out_shape=jax.ShapeDtypeStruct(x_blocks.shape, BF16),
        compiler_params=params(),
        cost_estimate=cost(7),
        name="begin_back",
    )(limit, x_blocks, clock, gain, two_grad, middle_grad, w_wide, *mixed_grads)


DIRECT = 8


def clock_rows(step_ids, features):
    half_width = features // 2
    ladder = jnp.arange(half_width, dtype=F32) / half_width
    rate_rows = jnp.exp(-math.log(10000.0) * ladder)
    angles = step_ids.astype(F32)[:, None] * rate_rows[None, :]
    return jnp.concatenate([jnp.sin(angles), jnp.cos(angles)], axis=-1)


def swap(value, apart):
    count = lax.axis_size("tensor")
    return lax.ppermute(value, "tensor", [(i, i ^ apart) for i in range(count)])


def ahead(value, step):
    count = lax.axis_size("dp")
    return lax.ppermute(value, "dp", [(i, (i + step) % count) for i in range(count)])


def collect_rows(shard):
    count = lax.axis_size("dp")
    rows = lax.all_to_all(
        jnp.broadcast_to(shard[None], (count,) + shard.shape), "dp", 0, 0, tiled=True
    )
    return rows.reshape(count * shard.shape[0], shard.shape[1])


def collect_columns(rows):
    across = swap(rows, 2)
    return rows, swap(rows, 1), across, swap(across, 1)


def sum_rows(value):
    count = lax.axis_size("dp")
    groups = value.reshape(count, value.shape[0] // count, value.shape[1])
    if count <= DIRECT:
        own = lax.axis_index("dp")
        total = lax.dynamic_index_in_dim(groups, own, 0, keepdims=False).astype(F32)
        for step in range(1, count):
            group = lax.dynamic_index_in_dim(groups, (own + step) % count, 0, keepdims=False)
            total += ahead(group, step).astype(F32)
        return total
    return exchange_rows(value)


def exchange_rows(value):
    count = lax.axis_size("dp")
    groups = value.reshape(count, value.shape[0] // count, value.shape[1])
    return jnp.sum(lax.all_to_all(groups, "dp", 0, 0, tiled=True).astype(F32), axis=0)


def three_terms(values):
    terms = []
    for _ in range(3):
        term = lax.reduce_precision(values, 8, 7)
        terms.append(term.astype(BF16))
        values = values - term
    return terms


def after(value, *others):
    return lax.optimization_barrier((value,) + others)[0]


def on_device(
    states, timesteps, lengths, deal_order, w_qkv, w_out, w_up, w_down, gain_attn, gain_ffn, out_grad
):
    both = ("dp", "tensor")
    dp_count = lax.axis_size("dp")
    tensor_count = lax.axis_size("tensor")
    devices = dp_count * tensor_count
    total_seqs, tokens, width = states.shape
    assert tensor_count == 4 and total_seqs == devices
    features = width * tensor_count
    own = lax.axis_index("dp") * tensor_count + lax.axis_index("tensor")
    rank = jnp.full((1,), lax.axis_index("tensor"), jnp.int32)
    own_id = lax.dynamic_slice_in_dim(deal_order, own, 1)
    limit = lengths[own_id]
    clock = clock_rows(timesteps[own_id], features)
    per = gain_attn.shape[0]
    rows = w_qkv.shape[0]
    hidden = w_up.shape[1]

    rest = jnp.concatenate([w_out.T, w_up, w_down.T], axis=1)
    rest_all = lax.all_gather(rest, both, axis=0)
    qkv_rows = collect_rows(w_qkv.reshape(rows, -1))
    qkv_parts = collect_columns(qkv_rows)

    spare = jnp.stack(three_terms(gain_attn) + three_terms(gain_ffn)).reshape(1, 6 * per)
    spare = jnp.pad(spare, ((0, SPARE - 1), (0, width - 6 * per)))
    arranged = jnp.concatenate(
        [states[deal_order], jnp.broadcast_to(spare[None], (devices, SPARE, width))], axis=1
    )
    x_blocks = lax.all_to_all(after(arranged, qkv_rows), both, 0, 0, tiled=True)
    gains = jnp.sum(x_blocks[:, tokens, : 6 * per].reshape(devices, 2, 3, per).astype(F32), axis=2)
    gain_one = gains[:, 0].reshape(1, features)
    gain_two = gains[:, 1].reshape(1, features)
    x_blocks = x_blocks.reshape(dp_count, tensor_count, tokens + SPARE, width)

    mixed, n_one_turn, qkv_wide = project(limit, x_blocks, clock, gain_one, qkv_parts)
    ctx, ctx_turn, lse = attend(limit, mixed, tensor_count)
    output, active, upper_grad, n_two_turn, fg_turn, ag_turn, context_grad, middle_grad, two_grad = (
        middle_block(
            limit, rank, x_blocks, clock, gain_two, ctx, rest_all, tensor_count, out_grad
        )
    )

    down = ((fg_turn,), (active,))
    up = ((n_two_turn, ag_turn), (upper_grad, ctx))
    down_far = swap(weight_grads(*down), 1)
    up_far = swap(weight_grads(*up), 1)
    down_far, down_near = weight_grads(*down, down_far)
    up_far, up_near = weight_grads(*up, up_far)
    context_grad = after(context_grad, up_far, down_far)
    down_total = exchange_rows((down_near.astype(F32) + swap(down_far, 2).astype(F32)).astype(BF16))
    up_total = exchange_rows((up_near.astype(F32) + swap(up_far, 2).astype(F32)).astype(BF16))

    back = functools.partial(attend_back, limit, mixed, ctx_turn, lse)
    mixed_three, grad_three = back(context_grad, n_one_turn, 3)
    came_three = swap(grad_three, 1)
    context_grad = after(context_grad, grad_three)
    mixed_two, grad_two = back(context_grad, n_one_turn, 2)
    far = (grad_two.astype(F32) + came_three.astype(F32)).astype(BF16)
    context_grad = after(context_grad, far)
    mixed_one, grad_one = back(context_grad, n_one_turn, 1)
    came_one = swap(grad_one, 1)
    context_grad = after(context_grad, grad_one)
    mixed_own, near = back(context_grad, n_one_turn, 0, came_one)
    qkv_sum = (near.astype(F32) + swap(far, 2).astype(F32)).astype(BF16)
    begin_grad = begin_block(
        limit, x_blocks, clock, gain_one, two_grad, qkv_wide, after(middle_grad, qkv_sum),
        (mixed_own, mixed_one, mixed_two, mixed_three),
    )
    qkv_total = sum_rows(qkv_sum)
    returned = lax.all_to_all(
        begin_grad.reshape(devices, tokens + SPARE, width), both, 0, 0, tiled=True
    )
    inverse = (
        jnp.zeros((total_seqs,), jnp.int32)
        .at[deal_order]
        .set(jnp.arange(total_seqs, dtype=jnp.int32))
    )
    states_grad = returned[:, :tokens][inverse]
    gain_grads = jnp.sum(returned[:, tokens:].astype(F32), axis=0).reshape(2, devices, per)
    gain_grads = lax.dynamic_index_in_dim(gain_grads, own, 1, keepdims=False)
    return (
        output,
        states_grad,
        qkv_total.reshape(w_qkv.shape),
        up_total[:, hidden:].T,
        up_total[:, :hidden],
        down_total.T,
        gain_grads[0],
        gain_grads[1],
    )


def solution(mesh):
    in_specs = (
        P(None, "dp", "tensor"),
        P(),
        P(),
        P(),
        P("dp", None, "tensor"),
        P("tensor", "dp"),
        P("dp", "tensor"),
        P("tensor", "dp"),
        P(("dp", "tensor")),
        P(("dp", "tensor")),
        P(("dp", "tensor"), None, None),
    )
    out_specs = (
        P(("dp", "tensor"), None, None),
        P(None, "dp", "tensor"),
        P("dp", None, "tensor"),
        P("tensor", "dp"),
        P("dp", "tensor"),
        P("tensor", "dp"),
        P(("dp", "tensor")),
        P(("dp", "tensor")),
    )
    return jax.shard_map(
        on_device, mesh=mesh, in_specs=in_specs, out_specs=out_specs, check_vma=False
    )
```

```python
import functools
import math

import jax
import jax.numpy as jnp
from jax import lax
from jax.experimental import pallas as pl
from jax.experimental.pallas import tpu as pltpu
from jax.sharding import PartitionSpec as P

HEAD_DIM = 64
PAIR = 2 * HEAD_DIM
ROWS = 256
KEYS = 256
BACK_KEYS = 512
SPARE = 8
SCORE_SCALE = 1.0 / math.sqrt(HEAD_DIM)
LOG2E = math.log2(math.e)
F32 = jnp.float32
BF16 = jnp.bfloat16
NN = (((1,), (0,)), ((), ()))
NT = (((1,), (1,)), ((), ()))
VMEM_LIMIT = 56 * 1024 * 1024


def mul(lhs, rhs, dims=NN):
    return lax.dot_general(lhs, rhs, dims, preferred_element_type=F32)


def join_tokens(ref):
    blocks, parts, tall, width = ref.shape
    tokens = tall - SPARE
    return jnp.concatenate(
        [ref[:, part, 0:tokens].reshape(blocks * tokens, width) for part in range(parts)], axis=-1
    ).astype(F32)


def norm_parts(values):
    center = values - jnp.mean(values, axis=-1, keepdims=True)
    spread = jnp.mean(center * center, axis=-1, keepdims=True)
    inverse = lax.rsqrt(spread + 1e-05)
    return center * inverse, inverse


def norm_back(grad, gain, unit, inverse):
    scaled = grad * gain
    mean_scaled = jnp.mean(scaled, axis=-1, keepdims=True)
    mean_along = jnp.mean(scaled * unit, axis=-1, keepdims=True)
    return inverse * (scaled - mean_scaled - unit * mean_along)


def cost(microseconds):
    return pl.CostEstimate(
        flops=int(microseconds * 1.15e9), bytes_accessed=1 << 20, transcendentals=0
    )


def params(**kwargs):
    return pltpu.CompilerParams(vmem_limit_bytes=VMEM_LIMIT, **kwargs)


def project_kernel(limit_ref, x_ref, clock_ref, gain_ref, *refs):
    w_refs, (mixed_ref, n_turn_ref, wide) = refs[:-3], refs[-3:]
    step = pl.program_id(0)

    @pl.when(step == 0)
    def _():
        for part, w_ref in enumerate(w_refs):
            width = w_ref.shape[1]
            columns = slice(part * width, (part + 1) * width)
            wide[:, columns] = w_ref[...]

    @pl.when(step * ROWS < limit_ref[0])
    def _():
        begin = join_tokens(x_ref) + clock_ref[...]
        unit, _ = norm_parts(begin)
        normed = (unit * gain_ref[...]).astype(BF16)
        n_turn_ref[...] = normed.T
        mixed_ref[...] = mul(normed, wide[...]).astype(BF16)

    @pl.when(step * ROWS >= limit_ref[0])
    def _():
        n_turn_ref[...] = jnp.zeros_like(n_turn_ref)
        mixed_ref[...] = jnp.zeros_like(mixed_ref)


def project(limit, x_blocks, clock, gain, w_parts):
    senders, feature_parts, tall, width = x_blocks.shape
    tokens = tall - SPARE
    length = senders * tokens
    features = feature_parts * width
    parts, columns = len(w_parts), w_parts[0].shape[1]
    take = ROWS // tokens
    return pl.pallas_call(
        project_kernel,
        grid_spec=pltpu.PrefetchScalarGridSpec(
            num_scalar_prefetch=1,
            grid=(length // ROWS,),
            in_specs=[
                pl.BlockSpec((take, feature_parts, tall, width), lambda i, *s: (i, 0, 0, 0)),
                pl.BlockSpec((1, features), lambda i, *s: (0, 0)),
                pl.BlockSpec((1, features), lambda i, *s: (0, 0)),
            ]
            + [pl.BlockSpec((features, columns), lambda i, *s: (0, 0))] * parts,
            out_specs=[
                pl.BlockSpec((ROWS, parts * columns), lambda i, *s: (i, 0)),
                pl.BlockSpec((features, ROWS), lambda i, *s: (0, i)),
                pl.BlockSpec((features, parts * columns), lambda i, *s: (0, 0)),
            ],
        ),
        out_shape=[
            jax.ShapeDtypeStruct((length, parts * columns), BF16),
            jax.ShapeDtypeStruct((features, length), BF16),
            jax.ShapeDtypeStruct((features, parts * columns), BF16),
        ],
        compiler_params=params(),
        cost_estimate=cost(5),
        name="project",
    )(limit, x_blocks, clock, gain, *w_parts)


def head_lanes(shape, head):
    lane = lax.broadcasted_iota(jnp.int32, shape, 1)
    return (lane >= head * HEAD_DIM) & (lane < (head + 1) * HEAD_DIM)


def spare_lane(shape, head):
    lane = lax.broadcasted_iota(jnp.int32, shape, 1)
    return lane == (1 - head) * HEAD_DIM


def masked_keys(keys, head, limit):
    row = lax.broadcasted_iota(jnp.int32, keys.shape, 0)
    spare = jnp.where(
        spare_lane(keys.shape, head) & (row >= limit), jnp.asarray(-1e30, F32), jnp.asarray(0.0, F32)
    )
    return jnp.where(head_lanes(keys.shape, head), keys.astype(F32), spare).astype(BF16)


def own_lanes(values, head):
    return jnp.where(head_lanes(values.shape, head), values.astype(F32), 0.0).astype(BF16)


def masked_queries(queries, head):
    spare = jnp.where(spare_lane(queries.shape, head), jnp.asarray(1.0, F32), jnp.asarray(0.0, F32))
    return jnp.where(head_lanes(queries.shape, head), queries.astype(F32), spare).astype(BF16)


def attend_kernel(limit_ref, q_ref, k_ref, v_ref, ctx_ref, turn_ref, lse_ref, keys_s, q_s, vt_s, sc_s):
    length = q_ref.shape[0]
    vt_s[...] = v_ref[...].astype(F32).T.astype(BF16)
    for head in range(2):
        keys_s[head] = masked_keys(k_ref[...], head, limit_ref[0])
        q_s[head] = masked_queries(q_ref[...], head)
    factor = SCORE_SCALE * LOG2E
    spans = [slice(at, at + KEYS) for at in range(0, length, KEYS)]
    outs = []
    for head in range(2):
        feats = slice(head * HEAD_DIM, (head + 1) * HEAD_DIM)
        peak = None
        for span in spans:
            scores = mul(keys_s[head, span], q_s[head], NT)
            sc_s[head, span] = scores
            high = jnp.max(scores, axis=0, keepdims=True)
            peak = high if peak is None else jnp.maximum(peak, high)
        peak = peak * factor
        total = jnp.zeros_like(peak)
        gathered = jnp.zeros((HEAD_DIM, length), F32)
        for span in spans:
            expo = jnp.exp2(sc_s[head, span] * factor - peak)
            total += jnp.sum(expo, axis=0, keepdims=True)
            gathered += mul(vt_s[feats, span], expo.astype(BF16))
        outs.append(gathered / total)
        lse_ref[0, head : head + 1, :] = peak + jnp.log2(total)
    both = jnp.concatenate(outs, axis=0)
    turn_ref[...] = both.astype(BF16)
    ctx_ref[...] = both.T.astype(BF16)


def attend(limit, mixed, pairs):
    length = mixed.shape[0]
    column = lambda c: pl.BlockSpec((length, PAIR), lambda i, s: (0, i * 3 + c))
    return pl.pallas_call(
        attend_kernel,
        grid_spec=pltpu.PrefetchScalarGridSpec(
            num_scalar_prefetch=1,
            grid=(pairs,),
            in_specs=[column(0), column(1), column(2)],
            out_specs=[
                pl.BlockSpec((length, PAIR), lambda i, s: (0, i)),
                pl.BlockSpec((PAIR, length), lambda i, s: (i, 0)),
                pl.BlockSpec((1, 2, length), lambda i, s: (i, 0, 0)),
            ],
            scratch_shapes=[
                pltpu.VMEM((2, length, PAIR), BF16),
                pltpu.VMEM((2, length, PAIR), BF16),
                pltpu.VMEM((PAIR, length), BF16),
                pltpu.VMEM((2, length, length), F32),
            ],
        ),
        out_shape=[
            jax.ShapeDtypeStruct((length, pairs * PAIR), BF16),
            jax.ShapeDtypeStruct((pairs * PAIR, length), BF16),
            jax.ShapeDtypeStruct((pairs, 2, length), F32),
        ],
        compiler_params=params(),
        cost_estimate=cost(15),
        name="attend",
    )(limit, mixed, mixed, mixed)


def gelu_both(values):
    root = math.sqrt(2.0 / math.pi)
    square = values * values
    tanh = jnp.tanh(root * values * (1.0 + 0.044715 * square))
    half = 0.5 + 0.5 * tanh
    slope = half + (0.5 * root) * values * (1.0 - tanh * tanh) * (1.0 + (3 * 0.044715) * square)
    return values * half, slope


def middle_kernel(
    groups, limit_ref, place_ref, x_ref, clock_ref, gain_ref, ctx_ref, og_ref, *refs
):
    weight_refs, refs = refs[:-14], refs[-14:]
    out_ref, cg_ref, mg_ref, gg_ref, send_ref, keep_ref = refs[:6]
    wide, units, active_s, ug_s, n_turn, fg_turn, ag_turn, ctx_s = refs[6:]
    step = pl.program_id(0)
    parts, _, hidden = active_s.shape
    blocks = pl.num_programs(0) - parts

    @pl.when(step == 0)
    def _():
        gg_ref[...] = jnp.zeros_like(gg_ref)
        each = len(weight_refs) // parts
        for part in range(parts):
            thin = slice(part * PAIR, (part + 1) * PAIR)
            thick = slice(part * 2 * hidden, (part + 1) * 2 * hidden)
            for at, w_ref in enumerate(weight_refs[part * each : (part + 1) * each]):
                if groups is None:
                    wide[:, thin] = w_ref[:, 0:PAIR]
                    units[:, thick] = w_ref[:, PAIR:]
                    continue
                count = groups // each
                rows = w_ref.shape[0] // count
                for group in range(count):
                    spot = place_ref[at * count + group] * rows
                    spot = pl.ds(pl.multiple_of(spot, rows), rows)
                    source = w_ref[group * rows : (group + 1) * rows]
                    wide[spot, thin] = source[:, 0:PAIR]
                    units[spot, thick] = source[:, PAIR:]

    dead = (step < blocks) & (step * ROWS >= limit_ref[0])

    @pl.when((step < blocks) & jnp.logical_not(dead))
    def _():
        spot = pl.ds(pl.multiple_of(step * ROWS, ROWS), ROWS)
        gain = gain_ref[...]
        live = step * ROWS + lax.broadcasted_iota(jnp.int32, (ROWS, 1), 0) < limit_ref[0]
        begin = join_tokens(x_ref) + clock_ref[...]
        middle = begin + mul(ctx_ref[...], wide[...], NT)
        unit, inverse = norm_parts(middle)
        normed = (unit * gain).astype(BF16)
        n_turn[:, spot] = normed.T
        res_grad = jnp.where(live, og_ref[0].astype(F32), 0.0)
        feed_grad = res_grad.astype(BF16)
        fg_turn[:, spot] = feed_grad.T
        feed = jnp.zeros_like(middle)
        two_grad = jnp.zeros_like(middle)
        for part in range(parts):
            up = slice(2 * part * hidden, (2 * part + 1) * hidden)
            down = slice((2 * part + 1) * hidden, (2 * part + 2) * hidden)
            upper = mul(normed, units[:, up])
            active, slope = gelu_both(upper)
            active = active.astype(BF16)
            active_s[part, spot] = active
            feed += mul(active, units[:, down], NT)
            upper_grad = (mul(feed_grad, units[:, down]) * slope).astype(BF16)
            ug_s[part, spot] = upper_grad
            two_grad += mul(upper_grad, units[:, up], NT)
        out_ref[0] = jnp.where(live, middle + feed, 0.0).astype(BF16)
        gg_ref[...] += jnp.sum(two_grad * unit, axis=0, keepdims=True)
        middle_grad = res_grad + norm_back(two_grad, gain, unit, inverse)
        mg_ref[...] = middle_grad
        att_grad = middle_grad.astype(BF16)
        ag_turn[:, spot] = att_grad.T
        cg_ref[...] = mul(att_grad, wide[...]).astype(BF16)
        for part in range(parts):
            ctx_s[part, spot] = ctx_ref[:, part * PAIR : (part + 1) * PAIR]

    @pl.when(dead)
    def _():
        spot = pl.ds(pl.multiple_of(step * ROWS, ROWS), ROWS)
        for ref in (out_ref, cg_ref, mg_ref):
            ref[...] = jnp.zeros_like(ref)
        for ref in (active_s, ug_s, ctx_s):
            ref[:, spot] = jnp.zeros((ref.shape[0], ROWS, ref.shape[2]), BF16)
        for ref in (n_turn, fg_turn, ag_turn):
            ref[:, spot] = jnp.zeros((ref.shape[0], ROWS), BF16)

    @pl.when(step >= blocks)
    def _():
        turn = step - blocks
        part = jnp.where(turn < 2, 3 - 2 * turn, 6 - 2 * turn)
        grads = (
            mul(ag_turn[...], ctx_s[part]).astype(BF16),
            mul(n_turn[...], ug_s[part]).astype(BF16),
            mul(fg_turn[...], active_s[part]).astype(BF16),
        )

        def into(ref):
            ref[0, :, 0:PAIR], ref[0, :, PAIR : PAIR + hidden], ref[0, :, PAIR + hidden :] = grads

        pl.when(turn < 2)(lambda: into(send_ref))
        pl.when(turn >= 2)(lambda: into(keep_ref))


def middle_block(limit, place, groups, x_blocks, clock, gain, ctx, w_parts, out_grad):
    senders, feature_parts, tall, width = x_blocks.shape
    tokens = tall - SPARE
    length = senders * tokens
    features = feature_parts * width
    parts = len(w_parts)
    weights = [w for part in w_parts for w in part]
    columns = weights[0].shape[1]
    hidden = (columns - PAIR) // 2
    take = ROWS // tokens
    blocks = length // ROWS
    row = lambda i: jnp.minimum(i, blocks - 1)
    whole = lambda array: pl.BlockSpec(
        array.shape, lambda i, *s: (0,) * array.ndim, pipeline_mode=pl.Buffered(1)
    )
    rows = lambda n: pl.BlockSpec((ROWS, n), lambda i, *s: (row(i), 0))
    one = pl.BlockSpec((1, ROWS, features), lambda i, *s: (0, row(i), 0))
    grads = lambda first: pl.BlockSpec(
        (1, features, columns), lambda i, *s: (jnp.clip(i - blocks - first, 0, 1), 0, 0)
    )
    grads_shape = jax.ShapeDtypeStruct((2, features, columns), BF16)
    return pl.pallas_call(
        functools.partial(middle_kernel, groups),
        grid_spec=pltpu.PrefetchScalarGridSpec(
            num_scalar_prefetch=2,
            grid=(blocks + parts,),
            in_specs=[
                pl.BlockSpec(
                    (take, feature_parts, tall, width), lambda i, *s: (row(i), 0, 0, 0)
                ),
                whole(clock),
                whole(gain),
                rows(features),
                one,
            ]
            + [whole(w) for w in weights],
            out_specs=[
                one, rows(features), rows(features),
                pl.BlockSpec((1, features), lambda i, *s: (0, 0)),
                grads(0), grads(2),
            ],
            scratch_shapes=[
                pltpu.VMEM((features, parts * PAIR), BF16),
                pltpu.VMEM((features, parts * 2 * hidden), BF16),
                pltpu.VMEM((parts, length, hidden), BF16),
                pltpu.VMEM((parts, length, hidden), BF16),
                pltpu.VMEM((features, length), BF16),
                pltpu.VMEM((features, length), BF16),
                pltpu.VMEM((features, length), BF16),
                pltpu.VMEM((parts, length, PAIR), BF16),
            ],
        ),
        out_shape=[
            jax.ShapeDtypeStruct((1, length, features), BF16),
            jax.ShapeDtypeStruct((length, features), BF16),
            jax.ShapeDtypeStruct((length, features), F32),
            jax.ShapeDtypeStruct((1, features), F32),
            grads_shape,
            grads_shape,
        ],
        compiler_params=params(),
        cost_estimate=cost(25),
        name="middle",
    )(limit, place, x_blocks, clock, gain, ctx, out_grad, *weights)


def attend_back_kernel(
    limit_ref, q_ref, k_ref, v_ref, turn_ref, lse_ref, cg_ref, n_turn_ref,
    dm_ref, wg_ref, keys_s, q_s, qz_s, do_s, kt_s, delta_s,
):
    limit = limit_ref[0]
    length = q_ref.shape[0]
    kt_s[...] = k_ref[...].astype(F32).T.astype(BF16)
    along = cg_ref[...].astype(F32).T * turn_ref[...].astype(F32)
    for head in range(2):
        feats = slice(head * HEAD_DIM, (head + 1) * HEAD_DIM)
        delta_s[head : head + 1, :] = jnp.sum(along[feats, :], axis=0, keepdims=True)
        keys_s[head] = masked_keys(k_ref[...], head, limit)
        q_s[head] = masked_queries(q_ref[...], head)
        qz_s[head] = own_lanes(q_ref[...], head)
        do_s[head] = own_lanes(cg_ref[...], head)
    factor = SCORE_SCALE * LOG2E
    turned = [jnp.zeros((HEAD_DIM, length), F32)] * 2
    for at in range(0, length, BACK_KEYS):
        span = slice(at, at + BACK_KEYS)
        key_grad = jnp.zeros((BACK_KEYS, PAIR), F32)
        value_grad = jnp.zeros((BACK_KEYS, PAIR), F32)
        for head in range(2):
            feats = slice(head * HEAD_DIM, (head + 1) * HEAD_DIM)
            scores = mul(keys_s[head, span], q_s[head], NT)
            prob = jnp.exp2(scores * factor - lse_ref[0, head : head + 1, :])
            prob_grad = mul(v_ref[span, :], do_s[head], NT)
            score_grad = (prob * (prob_grad - delta_s[head : head + 1, :])).astype(BF16)
            value_grad += mul(prob.astype(BF16), do_s[head])
            key_grad += mul(score_grad, qz_s[head])
            turned[head] += mul(kt_s[feats, span], score_grad)
        dm_ref[span, PAIR : 2 * PAIR] = (key_grad * SCORE_SCALE).astype(BF16)
        dm_ref[span, 2 * PAIR : 3 * PAIR] = value_grad.astype(BF16)
    query_grad = jnp.concatenate(turned, axis=0) * SCORE_SCALE
    dm_ref[:, 0:PAIR] = query_grad.T.astype(BF16)
    wg_ref[0] = mul(n_turn_ref[...], dm_ref[...]).astype(BF16)


def attend_back(limit, mixed, ctx_turn, lse, context_grad, n_turn, first):
    length = mixed.shape[0]
    features = n_turn.shape[0]
    pair = lambda i: first - 2 * i
    column = lambda c: pl.BlockSpec((length, PAIR), lambda i, s: (0, pair(i) * 3 + c))
    return pl.pallas_call(
        attend_back_kernel,
        grid_spec=pltpu.PrefetchScalarGridSpec(
            num_scalar_prefetch=1,
            grid=(2,),
            in_specs=[
                column(0), column(1), column(2),
                pl.BlockSpec((PAIR, length), lambda i, s: (pair(i), 0)),
                pl.BlockSpec((1, 2, length), lambda i, s: (pair(i), 0, 0)),
                pl.BlockSpec((length, PAIR), lambda i, s: (0, pair(i))),
                pl.BlockSpec((features, length), lambda i, s: (0, 0)),
            ],
            out_specs=[
                pl.BlockSpec((length, 3 * PAIR), lambda i, s: (0, i)),
                pl.BlockSpec((1, features, 3 * PAIR), lambda i, s: (i, 0, 0)),
            ],
            scratch_shapes=[
                pltpu.VMEM((2, length, PAIR), BF16),
                pltpu.VMEM((2, length, PAIR), BF16),
                pltpu.VMEM((2, length, PAIR), BF16),
                pltpu.VMEM((2, length, PAIR), BF16),
                pltpu.VMEM((PAIR, length), BF16),
                pltpu.VMEM((8, length), F32),
            ],
        ),
        out_shape=[
            jax.ShapeDtypeStruct((length, 2 * 3 * PAIR), BF16),
            jax.ShapeDtypeStruct((2, features, 3 * PAIR), BF16),
        ],
        compiler_params=params(),
        cost_estimate=cost(16),
        name="attend_back",
    )(limit, mixed, mixed, mixed, ctx_turn, lse, context_grad, n_turn)


def begin_kernel(
    limit_ref, x_ref, clock_ref, gain_ref, gg_two_ref, mg_ref, w_ref, odd_ref, even_ref, bg_ref, gg_s
):
    step = pl.program_id(0)
    _, parts, tall, width = bg_ref.shape
    tokens = tall - SPARE
    blocks = ROWS // tokens
    spot = pl.ds(step * blocks, blocks)

    @pl.when(step == 0)
    def _():
        gg_s[...] = jnp.zeros_like(gg_s)

    @pl.when(step * ROWS < limit_ref[0])
    def _():
        begin = join_tokens(x_ref) + clock_ref[...]
        unit, inverse = norm_parts(begin)
        one_grad = jnp.zeros_like(begin)
        for part, (d_ref, at) in enumerate(((even_ref, 1), (odd_ref, 1), (even_ref, 0), (odd_ref, 0))):
            columns = slice(part * 3 * PAIR, (part + 1) * 3 * PAIR)
            own = slice(at * 3 * PAIR, (at + 1) * 3 * PAIR)
            one_grad += mul(d_ref[:, own], w_ref[:, columns], NT)
        gg_s[...] += jnp.sum(one_grad * unit, axis=0, keepdims=True)
        total = (mg_ref[...] + norm_back(one_grad, gain_ref[...], unit, inverse)).astype(BF16)
        for part in range(parts):
            piece = total[:, part * width : (part + 1) * width]
            bg_ref[spot, part, 0:tokens] = piece.reshape(blocks, tokens, width)

    @pl.when(step * ROWS >= limit_ref[0])
    def _():
        bg_ref[spot] = jnp.zeros((blocks,) + bg_ref.shape[1:], BF16)

    @pl.when(step == pl.num_programs(0) - 1)
    def _():
        rows = []
        for ref in (gg_s, gg_two_ref):
            for part in range(parts):
                rows.append(ref[:, part * width : (part + 1) * width])
        bg_ref[:, :, tokens:tall] = jnp.broadcast_to(
            jnp.concatenate(rows, axis=0).astype(BF16), bg_ref.shape[:2] + (SPARE, width)
        )


def begin_block(limit, x_blocks, clock, gain, two_grad, w_wide, middle_grad, odd, even):
    senders, feature_parts, tall, width = x_blocks.shape
    tokens = tall - SPARE
    length = senders * tokens
    features = feature_parts * width
    take = ROWS // tokens
    whole = lambda array: pl.BlockSpec(array.shape, lambda i, s: (0,) * array.ndim)
    rows = lambda n: pl.BlockSpec((ROWS, n), lambda i, s: (i, 0))
    return pl.pallas_call(
        begin_kernel,
        grid_spec=pltpu.PrefetchScalarGridSpec(
            num_scalar_prefetch=1,
            grid=(length // ROWS,),
            in_specs=[
                pl.BlockSpec((take, feature_parts, tall, width), lambda i, s: (i, 0, 0, 0)),
                whole(clock), whole(gain), whole(two_grad), rows(features), whole(w_wide),
            ]
            + [rows(6 * PAIR)] * 2,
            out_specs=whole(x_blocks),
            scratch_shapes=[pltpu.VMEM((1, features), F32)],
        ),
        out_shape=jax.ShapeDtypeStruct(x_blocks.shape, BF16),
        compiler_params=params(),
        cost_estimate=cost(7),
        name="begin_back",
    )(limit, x_blocks, clock, gain, two_grad, middle_grad, w_wide, odd, even)


DIRECT = 8


def clock_rows(step_ids, features):
    half_width = features // 2
    ladder = jnp.arange(half_width, dtype=F32) / half_width
    rate_rows = jnp.exp(-math.log(10000.0) * ladder)
    angles = step_ids.astype(F32)[:, None] * rate_rows[None, :]
    return jnp.concatenate([jnp.sin(angles), jnp.cos(angles)], axis=-1)


def swap(value, apart):
    count = lax.axis_size("tensor")
    return lax.ppermute(value, "tensor", [(i, i ^ apart) for i in range(count)])


def along_dp(value, move):
    count = lax.axis_size("dp")
    return lax.ppermute(value, "dp", [(i, move(i)) for i in range(count)])


def across(value):
    return along_dp(value, lambda i: i ^ 1)


def ahead(value, step):
    count = lax.axis_size("dp") // 2
    return along_dp(value, lambda i: (i // 2 + step) % count * 2 + i % 2)


def places():
    count = lax.axis_size("dp") // 2
    own = lax.axis_index("dp")
    coarse = (own // 2 - jnp.arange(count, dtype=jnp.int32)) % count
    return jnp.concatenate([coarse * 2 + own % 2, coarse * 2 + 1 - own % 2])


def collect_pieces(shard, gate):
    count = lax.axis_size("dp") // 2
    mine = jnp.concatenate([shard] + [ahead(shard, step) for step in range(1, count)], axis=0)
    other = across(mine)
    far_mine = swap(after(mine, gate), 2)
    far_other = swap(other, 2)
    return (
        (mine, other),
        (swap(mine, 1), swap(other, 1)),
        (far_mine, far_other),
        (swap(far_mine, 1), swap(far_other, 1)),
    )


def collect_rows(shard):
    count = lax.axis_size("dp")
    rows = lax.all_to_all(
        jnp.broadcast_to(shard[None], (count,) + shard.shape), "dp", 0, 0, tiled=True
    )
    return rows.reshape(count * shard.shape[0], shard.shape[1])


def collect_columns(rows):
    far = swap(rows, 2)
    return rows, swap(rows, 1), far, swap(far, 1)


def add(*values):
    total = values[0].astype(F32)
    for value in values[1:]:
        total += value.astype(F32)
    return total.astype(BF16)


def fold_pair(values):
    own = lax.axis_index("dp") % 2
    pick = lambda value, which: lax.dynamic_index_in_dim(value, which, value.ndim - 3, keepdims=False)
    sent = add(*[pick(value, 1 - own) for value in values])
    return sent, lambda: [pick(value, own) for value in values] + [across(sent)]


def fold_far(values):
    sent = add(*[value[0] for value in values])
    return sent, lambda: [value[1] for value in values] + [swap(sent, 2)]


def fold_coarse(values):
    count = lax.axis_size("dp") // 2
    own = lax.axis_index("dp") // 2
    pick = lambda value, which: lax.dynamic_index_in_dim(value, which % count, 0, keepdims=False)
    value = add(*values)
    total = pick(value, own).astype(F32)
    for step in range(1, count):
        total += ahead(pick(value, own + step), step).astype(F32)
    return total


def grouped(value):
    count = lax.axis_size("dp")
    two, rows, columns = value.shape
    return value.reshape(two, count // 2, 2, rows // count, columns)


def exchange_rows(value):
    count = lax.axis_size("dp")
    groups = value.reshape(count, value.shape[0] // count, value.shape[1])
    return jnp.sum(lax.all_to_all(groups, "dp", 0, 0, tiled=True).astype(F32), axis=0)


def three_terms(values):
    terms = []
    for _ in range(3):
        term = lax.reduce_precision(values, 8, 7)
        terms.append(term.astype(BF16))
        values = values - term
    return terms


def after(value, *others):
    return lax.optimization_barrier((value,) + others)[0]


def on_device(
    states, timesteps, lengths, deal_order, w_qkv, w_out, w_up, w_down, gain_attn, gain_ffn, out_grad
):
    both = ("dp", "tensor")
    dp_count = lax.axis_size("dp")
    tensor_count = lax.axis_size("tensor")
    devices = dp_count * tensor_count
    total_seqs, tokens, width = states.shape
    assert tensor_count == 4 and total_seqs == devices
    features = width * tensor_count
    own = lax.axis_index("dp") * tensor_count + lax.axis_index("tensor")
    own_id = lax.dynamic_slice_in_dim(deal_order, own, 1)
    limit = lengths[own_id]
    clock = clock_rows(timesteps[own_id], features)
    per = gain_attn.shape[0]
    rows = w_qkv.shape[0]
    hidden = w_up.shape[1]

    rest = jnp.concatenate([w_out.T, w_up, w_down.T], axis=1)
    qkv_rows = collect_rows(w_qkv.reshape(rows, -1))
    qkv_parts = collect_columns(qkv_rows)

    direct = dp_count <= DIRECT
    rest = after(rest, qkv_rows)
    if direct:
        place, groups = places(), dp_count
        rest_parts = collect_pieces(rest, qkv_parts[2])
    else:
        place, groups = jnp.zeros((1,), jnp.int32), None
        rest_parts = [(part,) for part in collect_columns(collect_rows(rest))]

    spare = jnp.stack(three_terms(gain_attn) + three_terms(gain_ffn)).reshape(1, 6 * per)
    spare = jnp.pad(spare, ((0, SPARE - 1), (0, width - 6 * per)))
    arranged = jnp.concatenate(
        [states[deal_order], jnp.broadcast_to(spare[None], (devices, SPARE, width))], axis=1
    )
    x_blocks = lax.all_to_all(after(arranged, qkv_rows), both, 0, 0, tiled=True)
    gains = jnp.sum(x_blocks[:, tokens, : 6 * per].reshape(devices, 2, 3, per).astype(F32), axis=2)
    gain_one = gains[:, 0].reshape(1, features)
    gain_two = gains[:, 1].reshape(1, features)
    x_blocks = x_blocks.reshape(dp_count, tensor_count, tokens + SPARE, width)

    mixed, n_one_turn, qkv_wide = project(limit, x_blocks, clock, gain_one, qkv_parts)
    ctx, ctx_turn, lse = attend(limit, mixed, tensor_count)
    output, context_grad, middle_grad, two_grad, rest_send, rest_keep = middle_block(
        limit, place, groups, x_blocks, clock, gain_two, ctx, rest_parts, out_grad
    )
    rest_came = swap(rest_send, 1)

    back = functools.partial(attend_back, limit, mixed, ctx_turn, lse)
    context_grad = after(context_grad, rest_send)
    odd, qkv_send = back(context_grad, n_one_turn, 3)
    qkv_came = swap(qkv_send, 1)
    split = PAIR + hidden
    if direct:
        rest_values = [grouped(value) for value in (rest_keep, rest_came)]
        down_sent, down_rest = fold_pair([value[..., split:] for value in rest_values])
        up_sent, up_rest = fold_far([value[..., :split] for value in rest_values])
        even, qkv_keep = back(after(context_grad, odd, down_sent, up_sent), n_one_turn, 2)
        down_value, up_value = add(*down_rest()), add(*up_rest())
        down_sent, down_rest = fold_far([down_value])
        up_sent, up_rest = fold_pair([up_value])
        qkv_keep = after(qkv_keep, down_value, up_value)
        qkv_values = [grouped(value) for value in (qkv_keep, qkv_came)]
        qkv_sent, qkv_rest = fold_pair(qkv_values)
        middle_grad = after(middle_grad, down_sent, up_sent, qkv_sent)
        down_total = fold_coarse(down_rest())
        up_total = fold_coarse(up_rest())
        qkv_sent, qkv_rest = fold_far([add(*qkv_rest())])
        qkv_total = fold_coarse(qkv_rest())
    else:
        even, qkv_keep = back(after(context_grad, odd), n_one_turn, 2)
        rest_sent, rest_rest = fold_far([rest_keep, rest_came])
        rest_total = exchange_rows(add(*rest_rest()))
        up_total, down_total = rest_total[:, :split], rest_total[:, split:]
        qkv_sent, qkv_rest = fold_far([qkv_keep, qkv_came])
        qkv_total = exchange_rows(add(*qkv_rest()))
    begin_grad = begin_block(
        limit, x_blocks, clock, gain_one, two_grad, qkv_wide, middle_grad, odd, even
    )
    returned = lax.all_to_all(
        begin_grad.reshape(devices, tokens + SPARE, width), both, 0, 0, tiled=True
    )
    inverse = (
        jnp.zeros((total_seqs,), jnp.int32)
        .at[deal_order]
        .set(jnp.arange(total_seqs, dtype=jnp.int32))
    )
    states_grad = returned[:, :tokens][inverse]
    gain_grads = jnp.sum(returned[:, tokens:].astype(F32), axis=0).reshape(2, devices, per)
    gain_grads = lax.dynamic_index_in_dim(gain_grads, own, 1, keepdims=False)
    return (
        output,
        states_grad,
        qkv_total.reshape(w_qkv.shape),
        up_total[:, :PAIR].T,
        up_total[:, PAIR:],
        down_total.T,
        gain_grads[0],
        gain_grads[1],
    )


def solution(mesh):
    in_specs = (
        P(None, "dp", "tensor"),
        P(),
        P(),
        P(),
        P("dp", None, "tensor"),
        P("tensor", "dp"),
        P("dp", "tensor"),
        P("tensor", "dp"),
        P(("dp", "tensor")),
        P(("dp", "tensor")),
        P(("dp", "tensor"), None, None),
    )
    out_specs = (
        P(("dp", "tensor"), None, None),
        P(None, "dp", "tensor"),
        P("dp", None, "tensor"),
        P("tensor", "dp"),
        P("dp", "tensor"),
        P("tensor", "dp"),
        P(("dp", "tensor")),
        P(("dp", "tensor")),
    )
    return jax.shard_map(
        on_device, mesh=mesh, in_specs=in_specs, out_specs=out_specs, check_vma=False
    )
```

```python
import functools
import math

import jax
import jax.numpy as jnp
from jax import lax
from jax.experimental import pallas as pl
from jax.experimental.pallas import tpu as pltpu
from jax.sharding import PartitionSpec as P

HEAD_DIM = 64
PAIR = 2 * HEAD_DIM
ROWS = 256
KEYS = 256
BACK_KEYS = 512
SPARE = 8
SCORE_SCALE = 1.0 / math.sqrt(HEAD_DIM)
LOG2E = math.log2(math.e)
F32 = jnp.float32
BF16 = jnp.bfloat16
NN = (((1,), (0,)), ((), ()))
NT = (((1,), (1,)), ((), ()))
VMEM_LIMIT = 56 * 1024 * 1024


def mul(lhs, rhs, dims=NN):
    return lax.dot_general(lhs, rhs, dims, preferred_element_type=F32)


def join_tokens(ref):
    blocks, parts, tall, width = ref.shape
    tokens = tall - SPARE
    return jnp.concatenate(
        [ref[:, part, 0:tokens].reshape(blocks * tokens, width) for part in range(parts)], axis=-1
    ).astype(F32)


def norm_parts(values):
    center = values - jnp.mean(values, axis=-1, keepdims=True)
    spread = jnp.mean(center * center, axis=-1, keepdims=True)
    inverse = lax.rsqrt(spread + 1e-05)
    return center * inverse, inverse


def norm_back(grad, gain, unit, inverse):
    scaled = grad * gain
    mean_scaled = jnp.mean(scaled, axis=-1, keepdims=True)
    mean_along = jnp.mean(scaled * unit, axis=-1, keepdims=True)
    return inverse * (scaled - mean_scaled - unit * mean_along)


def cost(microseconds):
    return pl.CostEstimate(
        flops=int(microseconds * 1.15e9), bytes_accessed=1 << 20, transcendentals=0
    )


def params(**kwargs):
    return pltpu.CompilerParams(vmem_limit_bytes=VMEM_LIMIT, **kwargs)


def project_kernel(limit_ref, x_ref, clock_ref, gain_ref, *refs):
    w_refs, (mixed_ref, n_turn_ref, wide) = refs[:-3], refs[-3:]
    step = pl.program_id(0)

    @pl.when(step == 0)
    def _():
        for part, w_ref in enumerate(w_refs):
            width = w_ref.shape[1]
            columns = slice(part * width, (part + 1) * width)
            wide[:, columns] = w_ref[...]

    @pl.when(step * ROWS < limit_ref[0])
    def _():
        begin = join_tokens(x_ref) + clock_ref[...]
        unit, _ = norm_parts(begin)
        normed = (unit * gain_ref[...]).astype(BF16)
        n_turn_ref[...] = normed.T
        mixed_ref[...] = mul(normed, wide[...]).astype(BF16)

    @pl.when(step * ROWS >= limit_ref[0])
    def _():
        n_turn_ref[...] = jnp.zeros_like(n_turn_ref)
        mixed_ref[...] = jnp.zeros_like(mixed_ref)


def project(limit, x_blocks, clock, gain, w_parts):
    senders, feature_parts, tall, width = x_blocks.shape
    tokens = tall - SPARE
    length = senders * tokens
    features = feature_parts * width
    parts, columns = len(w_parts), w_parts[0].shape[1]
    take = ROWS // tokens
    return pl.pallas_call(
        project_kernel,
        grid_spec=pltpu.PrefetchScalarGridSpec(
            num_scalar_prefetch=1,
            grid=(length // ROWS,),
            in_specs=[
                pl.BlockSpec((take, feature_parts, tall, width), lambda i, *s: (i, 0, 0, 0)),
                pl.BlockSpec((1, features), lambda i, *s: (0, 0)),
                pl.BlockSpec((1, features), lambda i, *s: (0, 0)),
            ]
            + [pl.BlockSpec((features, columns), lambda i, *s: (0, 0))] * parts,
            out_specs=[
                pl.BlockSpec((ROWS, parts * columns), lambda i, *s: (i, 0)),
                pl.BlockSpec((features, ROWS), lambda i, *s: (0, i)),
                pl.BlockSpec((features, parts * columns), lambda i, *s: (0, 0)),
            ],
        ),
        out_shape=[
            jax.ShapeDtypeStruct((length, parts * columns), BF16),
            jax.ShapeDtypeStruct((features, length), BF16),
            jax.ShapeDtypeStruct((features, parts * columns), BF16),
        ],
        compiler_params=params(),
        cost_estimate=cost(5),
        name="project",
    )(limit, x_blocks, clock, gain, *w_parts)


def head_lanes(shape, head):
    lane = lax.broadcasted_iota(jnp.int32, shape, 1)
    return (lane >= head * HEAD_DIM) & (lane < (head + 1) * HEAD_DIM)


def spare_lane(shape, head):
    lane = lax.broadcasted_iota(jnp.int32, shape, 1)
    return lane == (1 - head) * HEAD_DIM


def masked_keys(keys, head, limit):
    row = lax.broadcasted_iota(jnp.int32, keys.shape, 0)
    spare = jnp.where(
        spare_lane(keys.shape, head) & (row >= limit), jnp.asarray(-1e30, F32), jnp.asarray(0.0, F32)
    )
    return jnp.where(head_lanes(keys.shape, head), keys.astype(F32), spare).astype(BF16)


def own_lanes(values, head):
    return jnp.where(head_lanes(values.shape, head), values.astype(F32), 0.0).astype(BF16)


def masked_queries(queries, head):
    spare = jnp.where(spare_lane(queries.shape, head), jnp.asarray(1.0, F32), jnp.asarray(0.0, F32))
    return jnp.where(head_lanes(queries.shape, head), queries.astype(F32), spare).astype(BF16)


def attend_kernel(limit_ref, q_ref, k_ref, v_ref, ctx_ref, turn_ref, lse_ref, keys_s, q_s, vt_s, sc_s):
    length = q_ref.shape[0]
    vt_s[...] = v_ref[...].astype(F32).T.astype(BF16)
    for head in range(2):
        keys_s[head] = masked_keys(k_ref[...], head, limit_ref[0])
        q_s[head] = masked_queries(q_ref[...], head)
    factor = SCORE_SCALE * LOG2E
    spans = [slice(at, at + KEYS) for at in range(0, length, KEYS)]
    outs = []
    for head in range(2):
        feats = slice(head * HEAD_DIM, (head + 1) * HEAD_DIM)
        peak = None
        for span in spans:
            scores = mul(keys_s[head, span], q_s[head], NT)
            sc_s[head, span] = scores
            high = jnp.max(scores, axis=0, keepdims=True)
            peak = high if peak is None else jnp.maximum(peak, high)
        peak = peak * factor
        total = jnp.zeros_like(peak)
        gathered = jnp.zeros((HEAD_DIM, length), F32)
        for span in spans:
            expo = jnp.exp2(sc_s[head, span] * factor - peak)
            total += jnp.sum(expo, axis=0, keepdims=True)
            gathered += mul(vt_s[feats, span], expo.astype(BF16))
        outs.append(gathered / total)
        lse_ref[0, head : head + 1, :] = peak + jnp.log2(total)
    both = jnp.concatenate(outs, axis=0)
    turn_ref[...] = both.astype(BF16)
    ctx_ref[...] = both.T.astype(BF16)


def attend(limit, mixed, pairs):
    length = mixed.shape[0]
    column = lambda c: pl.BlockSpec((length, PAIR), lambda i, s: (0, i * 3 + c))
    return pl.pallas_call(
        attend_kernel,
        grid_spec=pltpu.PrefetchScalarGridSpec(
            num_scalar_prefetch=1,
            grid=(pairs,),
            in_specs=[column(0), column(1), column(2)],
            out_specs=[
                pl.BlockSpec((length, PAIR), lambda i, s: (0, i)),
                pl.BlockSpec((PAIR, length), lambda i, s: (i, 0)),
                pl.BlockSpec((1, 2, length), lambda i, s: (i, 0, 0)),
            ],
            scratch_shapes=[
                pltpu.VMEM((2, length, PAIR), BF16),
                pltpu.VMEM((2, length, PAIR), BF16),
                pltpu.VMEM((PAIR, length), BF16),
                pltpu.VMEM((2, length, length), F32),
            ],
        ),
        out_shape=[
            jax.ShapeDtypeStruct((length, pairs * PAIR), BF16),
            jax.ShapeDtypeStruct((pairs * PAIR, length), BF16),
            jax.ShapeDtypeStruct((pairs, 2, length), F32),
        ],
        compiler_params=params(),
        cost_estimate=cost(15),
        name="attend",
    )(limit, mixed, mixed, mixed)


def gelu_both(values):
    root = math.sqrt(2.0 / math.pi)
    scaled = root * values
    inner = scaled * (1.0 + 0.044715 * (values * values))
    tanh = jnp.tanh(inner)
    half = 0.5 + 0.5 * tanh
    slope = half + (1.0 - tanh * tanh) * (1.5 * inner - scaled)
    return values * half, slope


def middle_kernel(
    groups, limit_ref, place_ref, x_ref, clock_ref, gain_ref, ctx_ref, og_ref, *refs
):
    weight_refs, refs = refs[:-16], refs[-16:]
    out_ref, cg_ref, mg_ref, gg_ref, up_send, down_send, up_keep, down_keep = refs[:8]
    wide, units, active_s, ug_s, n_turn, fg_turn, ag_turn, ctx_s = refs[8:]
    step = pl.program_id(0)
    parts, _, hidden = active_s.shape
    blocks = pl.num_programs(0) - parts

    @pl.when(step == 0)
    def _():
        gg_ref[...] = jnp.zeros_like(gg_ref)
        each = len(weight_refs) // parts
        for part in range(parts):
            thin = slice(part * PAIR, (part + 1) * PAIR)
            thick = slice(part * 2 * hidden, (part + 1) * 2 * hidden)
            for at, w_ref in enumerate(weight_refs[part * each : (part + 1) * each]):
                if groups is None:
                    wide[:, thin] = w_ref[:, 0:PAIR]
                    units[:, thick] = w_ref[:, PAIR:]
                    continue
                count = groups // each
                rows = w_ref.shape[0] // count
                for group in range(count):
                    spot = place_ref[at * count + group] * rows
                    spot = pl.ds(pl.multiple_of(spot, rows), rows)
                    source = w_ref[group * rows : (group + 1) * rows]
                    wide[spot, thin] = source[:, 0:PAIR]
                    units[spot, thick] = source[:, PAIR:]

    dead = (step < blocks) & (step * ROWS >= limit_ref[0])

    @pl.when((step < blocks) & jnp.logical_not(dead))
    def _():
        spot = pl.ds(pl.multiple_of(step * ROWS, ROWS), ROWS)
        gain = gain_ref[...]
        live = step * ROWS + lax.broadcasted_iota(jnp.int32, (ROWS, 1), 0) < limit_ref[0]
        begin = join_tokens(x_ref) + clock_ref[...]
        middle = begin + mul(ctx_ref[...], wide[...], NT)
        unit, inverse = norm_parts(middle)
        normed = (unit * gain).astype(BF16)
        n_turn[:, spot] = normed.T
        res_grad = jnp.where(live, og_ref[0].astype(F32), 0.0)
        feed_grad = res_grad.astype(BF16)
        fg_turn[:, spot] = feed_grad.T
        feed = jnp.zeros_like(middle)
        two_grad = jnp.zeros_like(middle)
        for part in range(parts):
            up = slice(2 * part * hidden, (2 * part + 1) * hidden)
            down = slice((2 * part + 1) * hidden, (2 * part + 2) * hidden)
            upper = mul(normed, units[:, up])
            active, slope = gelu_both(upper)
            active = active.astype(BF16)
            active_s[part, spot] = active
            feed += mul(active, units[:, down], NT)
            upper_grad = (mul(feed_grad, units[:, down]) * slope).astype(BF16)
            ug_s[part, spot] = upper_grad
            two_grad += mul(upper_grad, units[:, up], NT)
        out_ref[0] = jnp.where(live, middle + feed, 0.0).astype(BF16)
        gg_ref[...] += jnp.sum(two_grad * unit, axis=0, keepdims=True)
        middle_grad = res_grad + norm_back(two_grad, gain, unit, inverse)
        mg_ref[...] = middle_grad
        att_grad = middle_grad.astype(BF16)
        ag_turn[:, spot] = att_grad.T
        cg_ref[...] = mul(att_grad, wide[...]).astype(BF16)
        for part in range(parts):
            ctx_s[part, spot] = ctx_ref[:, part * PAIR : (part + 1) * PAIR]

    @pl.when(dead)
    def _():
        spot = pl.ds(pl.multiple_of(step * ROWS, ROWS), ROWS)
        for ref in (out_ref, cg_ref, mg_ref):
            ref[...] = jnp.zeros_like(ref)
        for ref in (active_s, ug_s, ctx_s):
            ref[:, spot] = jnp.zeros((ref.shape[0], ROWS, ref.shape[2]), BF16)
        for ref in (n_turn, fg_turn, ag_turn):
            ref[:, spot] = jnp.zeros((ref.shape[0], ROWS), BF16)

    @pl.when(step >= blocks)
    def _():
        turn = step - blocks
        part = jnp.where(turn < 2, 3 - 2 * turn, 6 - 2 * turn)
        grads = (
            mul(ag_turn[...], ctx_s[part]).astype(BF16),
            mul(n_turn[...], ug_s[part]).astype(BF16),
            mul(fg_turn[...], active_s[part]).astype(BF16),
        )

        def into(up_ref, down_ref):
            up_ref[0, :, 0:PAIR], up_ref[0, :, PAIR:], down_ref[0] = grads

        pl.when(turn < 2)(lambda: into(up_send, down_send))
        pl.when(turn >= 2)(lambda: into(up_keep, down_keep))


def middle_block(limit, place, groups, x_blocks, clock, gain, ctx, w_parts, out_grad):
    senders, feature_parts, tall, width = x_blocks.shape
    tokens = tall - SPARE
    length = senders * tokens
    features = feature_parts * width
    parts = len(w_parts)
    weights = [w for part in w_parts for w in part]
    columns = weights[0].shape[1]
    hidden = (columns - PAIR) // 2
    take = ROWS // tokens
    blocks = length // ROWS
    row = lambda i: jnp.minimum(i, blocks - 1)
    whole = lambda array: pl.BlockSpec(
        array.shape, lambda i, *s: (0,) * array.ndim, pipeline_mode=pl.Buffered(1)
    )
    rows = lambda n: pl.BlockSpec((ROWS, n), lambda i, *s: (row(i), 0))
    one = pl.BlockSpec((1, ROWS, features), lambda i, *s: (0, row(i), 0))
    grads = lambda first, n: pl.BlockSpec(
        (1, features, n), lambda i, *s: (jnp.clip(i - blocks - first, 0, 1), 0, 0)
    )
    up_shape = jax.ShapeDtypeStruct((2, features, PAIR + hidden), BF16)
    down_shape = jax.ShapeDtypeStruct((2, features, hidden), BF16)
    return pl.pallas_call(
        functools.partial(middle_kernel, groups),
        grid_spec=pltpu.PrefetchScalarGridSpec(
            num_scalar_prefetch=2,
            grid=(blocks + parts,),
            in_specs=[
                pl.BlockSpec(
                    (take, feature_parts, tall, width), lambda i, *s: (row(i), 0, 0, 0)
                ),
                whole(clock),
                whole(gain),
                rows(features),
                one,
            ]
            + [whole(w) for w in weights],
            out_specs=[
                one, rows(features), rows(features),
                pl.BlockSpec((1, features), lambda i, *s: (0, 0)),
                grads(0, PAIR + hidden), grads(0, hidden), grads(2, PAIR + hidden), grads(2, hidden),
            ],
            scratch_shapes=[
                pltpu.VMEM((features, parts * PAIR), BF16),
                pltpu.VMEM((features, parts * 2 * hidden), BF16),
                pltpu.VMEM((parts, length, hidden), BF16),
                pltpu.VMEM((parts, length, hidden), BF16),
                pltpu.VMEM((features, length), BF16),
                pltpu.VMEM((features, length), BF16),
                pltpu.VMEM((features, length), BF16),
                pltpu.VMEM((parts, length, PAIR), BF16),
            ],
        ),
        out_shape=[
            jax.ShapeDtypeStruct((1, length, features), BF16),
            jax.ShapeDtypeStruct((length, features), BF16),
            jax.ShapeDtypeStruct((length, features), F32),
            jax.ShapeDtypeStruct((1, features), F32),
            up_shape, down_shape, up_shape, down_shape,
        ],
        compiler_params=params(),
        cost_estimate=cost(25),
        name="middle",
    )(limit, place, x_blocks, clock, gain, ctx, out_grad, *weights)


def attend_back_kernel(
    limit_ref, q_ref, k_ref, v_ref, turn_ref, lse_ref, cg_ref, n_turn_ref,
    dm_ref, wg_ref, keys_s, q_s, qz_s, do_s, kt_s, delta_s,
):
    limit = limit_ref[0]
    length = q_ref.shape[0]
    kt_s[...] = k_ref[...].astype(F32).T.astype(BF16)
    along = cg_ref[...].astype(F32).T * turn_ref[...].astype(F32)
    for head in range(2):
        feats = slice(head * HEAD_DIM, (head + 1) * HEAD_DIM)
        delta_s[head : head + 1, :] = jnp.sum(along[feats, :], axis=0, keepdims=True)
        keys_s[head] = masked_keys(k_ref[...], head, limit)
        q_s[head] = masked_queries(q_ref[...], head)
        qz_s[head] = own_lanes(q_ref[...], head)
        do_s[head] = own_lanes(cg_ref[...], head)
    factor = SCORE_SCALE * LOG2E
    turned = [jnp.zeros((HEAD_DIM, length), F32)] * 2
    for at in range(0, length, BACK_KEYS):
        span = slice(at, at + BACK_KEYS)
        key_grad = jnp.zeros((BACK_KEYS, PAIR), F32)
        value_grad = jnp.zeros((BACK_KEYS, PAIR), F32)
        for head in range(2):
            feats = slice(head * HEAD_DIM, (head + 1) * HEAD_DIM)
            scores = mul(keys_s[head, span], q_s[head], NT)
            prob = jnp.exp2(scores * factor - lse_ref[0, head : head + 1, :])
            prob_grad = mul(v_ref[span, :], do_s[head], NT)
            score_grad = (prob * (prob_grad - delta_s[head : head + 1, :])).astype(BF16)
            value_grad += mul(prob.astype(BF16), do_s[head])
            key_grad += mul(score_grad, qz_s[head])
            turned[head] += mul(kt_s[feats, span], score_grad)
        dm_ref[span, PAIR : 2 * PAIR] = (key_grad * SCORE_SCALE).astype(BF16)
        dm_ref[span, 2 * PAIR : 3 * PAIR] = value_grad.astype(BF16)
    query_grad = jnp.concatenate(turned, axis=0) * SCORE_SCALE
    dm_ref[:, 0:PAIR] = query_grad.T.astype(BF16)
    wg_ref[0] = mul(n_turn_ref[...], dm_ref[...]).astype(BF16)


def attend_back(limit, mixed, ctx_turn, lse, context_grad, n_turn, first):
    length = mixed.shape[0]
    features = n_turn.shape[0]
    pair = lambda i: first - 2 * i
    column = lambda c: pl.BlockSpec((length, PAIR), lambda i, s: (0, pair(i) * 3 + c))
    return pl.pallas_call(
        attend_back_kernel,
        grid_spec=pltpu.PrefetchScalarGridSpec(
            num_scalar_prefetch=1,
            grid=(2,),
            in_specs=[
                column(0), column(1), column(2),
                pl.BlockSpec((PAIR, length), lambda i, s: (pair(i), 0)),
                pl.BlockSpec((1, 2, length), lambda i, s: (pair(i), 0, 0)),
                pl.BlockSpec((length, PAIR), lambda i, s: (0, pair(i))),
                pl.BlockSpec((features, length), lambda i, s: (0, 0)),
            ],
            out_specs=[
                pl.BlockSpec((length, 3 * PAIR), lambda i, s: (0, i)),
                pl.BlockSpec((1, features, 3 * PAIR), lambda i, s: (i, 0, 0)),
            ],
            scratch_shapes=[
                pltpu.VMEM((2, length, PAIR), BF16),
                pltpu.VMEM((2, length, PAIR), BF16),
                pltpu.VMEM((2, length, PAIR), BF16),
                pltpu.VMEM((2, length, PAIR), BF16),
                pltpu.VMEM((PAIR, length), BF16),
                pltpu.VMEM((8, length), F32),
            ],
        ),
        out_shape=[
            jax.ShapeDtypeStruct((length, 2 * 3 * PAIR), BF16),
            jax.ShapeDtypeStruct((2, features, 3 * PAIR), BF16),
        ],
        compiler_params=params(),
        cost_estimate=cost(16),
        name="attend_back",
    )(limit, mixed, mixed, mixed, ctx_turn, lse, context_grad, n_turn)


def begin_kernel(
    limit_ref, x_ref, clock_ref, gain_ref, gg_two_ref, mg_ref, w_ref, odd_ref, even_ref, bg_ref, gg_s
):
    step = pl.program_id(0)
    _, parts, tall, width = bg_ref.shape
    tokens = tall - SPARE
    blocks = ROWS // tokens
    spot = pl.ds(step * blocks, blocks)

    @pl.when(step == 0)
    def _():
        gg_s[...] = jnp.zeros_like(gg_s)

    @pl.when(step * ROWS < limit_ref[0])
    def _():
        begin = join_tokens(x_ref) + clock_ref[...]
        unit, inverse = norm_parts(begin)
        one_grad = jnp.zeros_like(begin)
        for part, (d_ref, at) in enumerate(((even_ref, 1), (odd_ref, 1), (even_ref, 0), (odd_ref, 0))):
            columns = slice(part * 3 * PAIR, (part + 1) * 3 * PAIR)
            own = slice(at * 3 * PAIR, (at + 1) * 3 * PAIR)
            one_grad += mul(d_ref[:, own], w_ref[:, columns], NT)
        gg_s[...] += jnp.sum(one_grad * unit, axis=0, keepdims=True)
        total = (mg_ref[...] + norm_back(one_grad, gain_ref[...], unit, inverse)).astype(BF16)
        for part in range(parts):
            piece = total[:, part * width : (part + 1) * width]
            bg_ref[spot, part, 0:tokens] = piece.reshape(blocks, tokens, width)

    @pl.when(step * ROWS >= limit_ref[0])
    def _():
        bg_ref[spot] = jnp.zeros((blocks,) + bg_ref.shape[1:], BF16)

    @pl.when(step == pl.num_programs(0) - 1)
    def _():
        rows = []
        for ref in (gg_s, gg_two_ref):
            for part in range(parts):
                rows.append(ref[:, part * width : (part + 1) * width])
        bg_ref[:, :, tokens:tall] = jnp.broadcast_to(
            jnp.concatenate(rows, axis=0).astype(BF16), bg_ref.shape[:2] + (SPARE, width)
        )


def begin_block(limit, x_blocks, clock, gain, two_grad, w_wide, middle_grad, odd, even):
    senders, feature_parts, tall, width = x_blocks.shape
    tokens = tall - SPARE
    length = senders * tokens
    features = feature_parts * width
    take = ROWS // tokens
    whole = lambda array: pl.BlockSpec(array.shape, lambda i, s: (0,) * array.ndim)
    rows = lambda n: pl.BlockSpec((ROWS, n), lambda i, s: (i, 0))
    return pl.pallas_call(
        begin_kernel,
        grid_spec=pltpu.PrefetchScalarGridSpec(
            num_scalar_prefetch=1,
            grid=(length // ROWS,),
            in_specs=[
                pl.BlockSpec((take, feature_parts, tall, width), lambda i, s: (i, 0, 0, 0)),
                whole(clock), whole(gain), whole(two_grad), rows(features), whole(w_wide),
            ]
            + [rows(6 * PAIR)] * 2,
            out_specs=whole(x_blocks),
            scratch_shapes=[pltpu.VMEM((1, features), F32)],
        ),
        out_shape=jax.ShapeDtypeStruct(x_blocks.shape, BF16),
        compiler_params=params(),
        cost_estimate=cost(7),
        name="begin_back",
    )(limit, x_blocks, clock, gain, two_grad, middle_grad, w_wide, odd, even)


DIRECT = 8


def clock_rows(step_ids, features):
    half_width = features // 2
    ladder = jnp.arange(half_width, dtype=F32) / half_width
    rate_rows = jnp.exp(-math.log(10000.0) * ladder)
    angles = step_ids.astype(F32)[:, None] * rate_rows[None, :]
    return jnp.concatenate([jnp.sin(angles), jnp.cos(angles)], axis=-1)


def swap(value, apart):
    count = lax.axis_size("tensor")
    return lax.ppermute(value, "tensor", [(i, i ^ apart) for i in range(count)])


def along_dp(value, move):
    count = lax.axis_size("dp")
    return lax.ppermute(value, "dp", [(i, move(i)) for i in range(count)])


def across(value):
    return along_dp(value, lambda i: i ^ 1)


def ahead(value, step):
    count = lax.axis_size("dp") // 2
    return along_dp(value, lambda i: (i // 2 + step) % count * 2 + i % 2)


def places():
    count = lax.axis_size("dp") // 2
    own = lax.axis_index("dp")
    coarse = (own // 2 - jnp.arange(count, dtype=jnp.int32)) % count
    return jnp.concatenate([coarse * 2 + own % 2, coarse * 2 + 1 - own % 2])


def collect_pieces(shard, gate):
    count = lax.axis_size("dp") // 2
    mine = jnp.concatenate([shard] + [ahead(shard, step) for step in range(1, count)], axis=0)
    mine = after(mine, gate)
    other = across(mine)
    return mine, other, swap(mine, 2), swap(other, 2)


def collect_rows(shard):
    count = lax.axis_size("dp")
    rows = lax.all_to_all(
        jnp.broadcast_to(shard[None], (count,) + shard.shape), "dp", 0, 0, tiled=True
    )
    return rows.reshape(count * shard.shape[0], shard.shape[1])


def collect_columns(rows):
    far = swap(rows, 2)
    return rows, swap(rows, 1), far, swap(far, 1)


def add(*values):
    total = values[0].astype(F32)
    for value in values[1:]:
        total += value.astype(F32)
    return total.astype(BF16)


def fold_pair(values):
    own = lax.axis_index("dp") % 2
    pick = lambda value, which: lax.dynamic_index_in_dim(value, which, value.ndim - 3, keepdims=False)
    sent = add(*[pick(value, 1 - own) for value in values])
    return sent, lambda: [pick(value, own) for value in values] + [across(sent)]


def fold_far(values):
    sent = add(*[value[0] for value in values])
    return sent, lambda: [value[1] for value in values] + [swap(sent, 2)]


def fold_coarse(values):
    count = lax.axis_size("dp") // 2
    own = lax.axis_index("dp") // 2
    pick = lambda value, which: lax.dynamic_index_in_dim(value, which % count, 0, keepdims=False)
    value = add(*values)
    total = pick(value, own).astype(F32)
    for step in range(1, count):
        total += ahead(pick(value, own + step), step).astype(F32)
    return total


def grouped(value):
    count = lax.axis_size("dp")
    two, rows, columns = value.shape
    return value.reshape(two, count // 2, 2, rows // count, columns)


def exchange_rows(value):
    count = lax.axis_size("dp")
    groups = value.reshape(count, value.shape[0] // count, value.shape[1])
    return jnp.sum(lax.all_to_all(groups, "dp", 0, 0, tiled=True).astype(F32), axis=0)


def three_terms(values):
    terms = []
    for _ in range(3):
        term = lax.reduce_precision(values, 8, 7)
        terms.append(term.astype(BF16))
        values = values - term
    return terms


def after(value, *others):
    return lax.optimization_barrier((value,) + others)[0]


def on_device(
    states, timesteps, lengths, deal_order, w_qkv, w_out, w_up, w_down, gain_attn, gain_ffn, out_grad
):
    both = ("dp", "tensor")
    dp_count = lax.axis_size("dp")
    tensor_count = lax.axis_size("tensor")
    devices = dp_count * tensor_count
    total_seqs, tokens, width = states.shape
    assert tensor_count == 4 and total_seqs == devices
    features = width * tensor_count
    own = lax.axis_index("dp") * tensor_count + lax.axis_index("tensor")
    own_id = lax.dynamic_slice_in_dim(deal_order, own, 1)
    limit = lengths[own_id]
    clock = clock_rows(timesteps[own_id], features)
    per = gain_attn.shape[0]
    rows = w_qkv.shape[0]
    hidden = w_up.shape[1]

    rest = jnp.concatenate([w_out.T, w_up, w_down.T], axis=1)
    qkv_rows = collect_rows(w_qkv.reshape(rows, -1))
    qkv_parts = collect_columns(qkv_rows)

    direct = dp_count <= DIRECT
    if direct:
        place, groups = places(), dp_count
        pieces = collect_pieces(rest, qkv_parts[2])
    else:
        place, groups = jnp.zeros((1,), jnp.int32), None
        rest_parts = [(part,) for part in collect_columns(collect_rows(rest))]

    spare = jnp.stack(three_terms(gain_attn) + three_terms(gain_ffn)).reshape(1, 6 * per)
    spare = jnp.pad(spare, ((0, SPARE - 1), (0, width - 6 * per)))
    arranged = jnp.concatenate(
        [states[deal_order], jnp.broadcast_to(spare[None], (devices, SPARE, width))], axis=1
    )
    x_blocks = lax.all_to_all(after(arranged, qkv_rows), both, 0, 0, tiled=True)
    gains = jnp.sum(x_blocks[:, tokens, : 6 * per].reshape(devices, 2, 3, per).astype(F32), axis=2)
    gain_one = gains[:, 0].reshape(1, features)
    gain_two = gains[:, 1].reshape(1, features)
    x_blocks = x_blocks.reshape(dp_count, tensor_count, tokens + SPARE, width)

    mixed, n_one_turn, qkv_wide = project(limit, x_blocks, clock, gain_one, qkv_parts)
    if direct:
        mine, other, far_mine, far_other = pieces
        near_mine, near_other, last_mine = swap(mine, 1), swap(other, 1), swap(far_mine, 1)
        mixed = after(mixed, near_mine, near_other, last_mine)
    ctx, ctx_turn, lse = attend(limit, mixed, tensor_count)
    if direct:
        last_other = swap(after(far_other, ctx), 1)
        rest_parts = (
            (mine, other), (near_mine, near_other), (far_mine, far_other), (last_mine, last_other)
        )
    output, context_grad, middle_grad, two_grad, up_send, down_send, up_keep, down_keep = middle_block(
        limit, place, groups, x_blocks, clock, gain_two, ctx, rest_parts, out_grad
    )
    up_came, down_came = swap(up_send, 1), swap(down_send, 1)

    back = functools.partial(attend_back, limit, mixed, ctx_turn, lse)
    context_grad = after(context_grad, up_send, down_send)
    odd, qkv_send = back(context_grad, n_one_turn, 3)
    qkv_came = swap(qkv_send, 1)
    if direct:
        down_sent, down_rest = fold_pair([grouped(value) for value in (down_keep, down_came)])
        up_sent, up_rest = fold_far([grouped(value) for value in (up_keep, up_came)])
        even, qkv_keep = back(after(context_grad, odd, down_sent, up_sent), n_one_turn, 2)
        down_value, up_value = add(*down_rest()), add(*up_rest())
        down_sent, down_rest = fold_far([down_value])
        up_sent, up_rest = fold_pair([up_value])
        qkv_keep = after(qkv_keep, down_value, up_value)
        qkv_sent, qkv_rest = fold_pair([grouped(value) for value in (qkv_keep, qkv_came)])
        middle_grad = after(middle_grad, down_sent, up_sent, qkv_sent)
        down_total = fold_coarse(down_rest())
        up_total = fold_coarse(up_rest())
        qkv_sent, qkv_rest = fold_far([add(*qkv_rest())])
        qkv_total = fold_coarse(qkv_rest())
    else:
        even, qkv_keep = back(after(context_grad, odd), n_one_turn, 2)
        totals = []
        for pair in ((up_keep, up_came), (down_keep, down_came), (qkv_keep, qkv_came)):
            totals.append(exchange_rows(add(*fold_far(pair)[1]())))
        up_total, down_total, qkv_total = totals
    begin_grad = begin_block(
        limit, x_blocks, clock, gain_one, two_grad, qkv_wide, middle_grad, odd, even
    )
    returned = lax.all_to_all(
        begin_grad.reshape(devices, tokens + SPARE, width), both, 0, 0, tiled=True
    )
    inverse = (
        jnp.zeros((total_seqs,), jnp.int32)
        .at[deal_order]
        .set(jnp.arange(total_seqs, dtype=jnp.int32))
    )
    states_grad = returned[:, :tokens][inverse]
    gain_grads = jnp.sum(returned[:, tokens:].astype(F32), axis=0).reshape(2, devices, per)
    gain_grads = lax.dynamic_index_in_dim(gain_grads, own, 1, keepdims=False)
    return (
        output,
        states_grad,
        qkv_total.reshape(w_qkv.shape),
        up_total[:, :PAIR].T,
        up_total[:, PAIR:],
        down_total.T,
        gain_grads[0],
        gain_grads[1],
    )


def solution(mesh):
    in_specs = (
        P(None, "dp", "tensor"),
        P(),
        P(),
        P(),
        P("dp", None, "tensor"),
        P("tensor", "dp"),
        P("dp", "tensor"),
        P("tensor", "dp"),
        P(("dp", "tensor")),
        P(("dp", "tensor")),
        P(("dp", "tensor"), None, None),
    )
    out_specs = (
        P(("dp", "tensor"), None, None),
        P(None, "dp", "tensor"),
        P("dp", None, "tensor"),
        P("tensor", "dp"),
        P("dp", "tensor"),
        P("tensor", "dp"),
        P(("dp", "tensor")),
        P(("dp", "tensor")),
    )
    return jax.shard_map(
        on_device, mesh=mesh, in_specs=in_specs, out_specs=out_specs, check_vma=False
    )
```

```python
import functools
import math

import jax
import jax.numpy as jnp
from jax import lax
from jax.experimental import pallas as pl
from jax.experimental.pallas import tpu as pltpu
from jax.sharding import PartitionSpec as P

HEAD_DIM = 64
PAIR = 2 * HEAD_DIM
ROWS = 256
KEYS = 256
BACK_KEYS = 512
SPARE = 8
SCORE_SCALE = 1.0 / math.sqrt(HEAD_DIM)
LOG2E = math.log2(math.e)
F32 = jnp.float32
BF16 = jnp.bfloat16
NN = (((1,), (0,)), ((), ()))
NT = (((1,), (1,)), ((), ()))
VMEM_LIMIT = 56 * 1024 * 1024


def mul(lhs, rhs, dims=NN):
    return lax.dot_general(lhs, rhs, dims, preferred_element_type=F32)


def join_tokens(ref):
    blocks, parts, tall, width = ref.shape
    tokens = tall - SPARE
    return jnp.concatenate(
        [ref[:, part, 0:tokens].reshape(blocks * tokens, width) for part in range(parts)], axis=-1
    ).astype(F32)


def place_rows(groups, place_ref, first, source, targets):
    if groups is None:
        for target, columns, own in targets:
            target[:, columns] = source[:, own]
        return
    rows = source.shape[0] // groups
    for group in range(groups):
        spot = pl.ds(pl.multiple_of(place_ref[first + group] * rows, rows), rows)
        for target, columns, own in targets:
            target[spot, columns] = source[group * rows : (group + 1) * rows, own]


def norm_parts(values):
    center = values - jnp.mean(values, axis=-1, keepdims=True)
    spread = jnp.mean(center * center, axis=-1, keepdims=True)
    inverse = lax.rsqrt(spread + 1e-05)
    return center * inverse, inverse


def norm_back(grad, gain, unit, inverse):
    scaled = grad * gain
    mean_scaled = jnp.mean(scaled, axis=-1, keepdims=True)
    mean_along = jnp.mean(scaled * unit, axis=-1, keepdims=True)
    return inverse * (scaled - mean_scaled - unit * mean_along)


def cost(microseconds):
    return pl.CostEstimate(
        flops=int(microseconds * 1.15e9), bytes_accessed=1 << 20, transcendentals=0
    )


def params(**kwargs):
    return pltpu.CompilerParams(vmem_limit_bytes=VMEM_LIMIT, **kwargs)


def project_kernel(groups, limit_ref, place_ref, x_ref, clock_ref, gain_ref, *refs):
    w_refs, (mixed_ref, n_turn_ref, wide) = refs[:-3], refs[-3:]
    step = pl.program_id(0)

    @pl.when(step == 0)
    def _():
        for part, w_ref in enumerate(w_refs):
            width = w_ref.shape[1]
            columns = slice(part * width, (part + 1) * width)
            place_rows(groups, place_ref, 0, w_ref, [(wide, columns, slice(0, width))])

    @pl.when(step * ROWS < limit_ref[0])
    def _():
        begin = join_tokens(x_ref) + clock_ref[...]
        unit, _ = norm_parts(begin)
        normed = (unit * gain_ref[...]).astype(BF16)
        n_turn_ref[...] = normed.T
        mixed_ref[...] = mul(normed, wide[...]).astype(BF16)

    @pl.when(step * ROWS >= limit_ref[0])
    def _():
        n_turn_ref[...] = jnp.zeros_like(n_turn_ref)
        mixed_ref[...] = jnp.zeros_like(mixed_ref)


def project(limit, place, groups, x_blocks, clock, gain, w_parts):
    senders, feature_parts, tall, width = x_blocks.shape
    tokens = tall - SPARE
    length = senders * tokens
    features = feature_parts * width
    parts, columns = len(w_parts), w_parts[0].shape[1]
    take = ROWS // tokens
    return pl.pallas_call(
        functools.partial(project_kernel, groups),
        grid_spec=pltpu.PrefetchScalarGridSpec(
            num_scalar_prefetch=2,
            grid=(length // ROWS,),
            in_specs=[
                pl.BlockSpec((take, feature_parts, tall, width), lambda i, *s: (i, 0, 0, 0)),
                pl.BlockSpec((1, features), lambda i, *s: (0, 0)),
                pl.BlockSpec((1, features), lambda i, *s: (0, 0)),
            ]
            + [pl.BlockSpec((features, columns), lambda i, *s: (0, 0))] * parts,
            out_specs=[
                pl.BlockSpec((ROWS, parts * columns), lambda i, *s: (i, 0)),
                pl.BlockSpec((features, ROWS), lambda i, *s: (0, i)),
                pl.BlockSpec((features, parts * columns), lambda i, *s: (0, 0)),
            ],
        ),
        out_shape=[
            jax.ShapeDtypeStruct((length, parts * columns), BF16),
            jax.ShapeDtypeStruct((features, length), BF16),
            jax.ShapeDtypeStruct((features, parts * columns), BF16),
        ],
        compiler_params=params(),
        cost_estimate=cost(5),
        name="project",
    )(limit, place, x_blocks, clock, gain, *w_parts)


def head_lanes(shape, head):
    lane = lax.broadcasted_iota(jnp.int32, shape, 1)
    return (lane >= head * HEAD_DIM) & (lane < (head + 1) * HEAD_DIM)


def spare_lane(shape, head):
    lane = lax.broadcasted_iota(jnp.int32, shape, 1)
    return lane == (1 - head) * HEAD_DIM


def masked_keys(keys, head, limit):
    row = lax.broadcasted_iota(jnp.int32, keys.shape, 0)
    spare = jnp.where(
        spare_lane(keys.shape, head) & (row >= limit), jnp.asarray(-1e30, F32), jnp.asarray(0.0, F32)
    )
    return jnp.where(head_lanes(keys.shape, head), keys.astype(F32), spare).astype(BF16)


def own_lanes(values, head):
    return jnp.where(head_lanes(values.shape, head), values.astype(F32), 0.0).astype(BF16)


def masked_queries(queries, head):
    spare = jnp.where(spare_lane(queries.shape, head), jnp.asarray(1.0, F32), jnp.asarray(0.0, F32))
    return jnp.where(head_lanes(queries.shape, head), queries.astype(F32), spare).astype(BF16)


def attend_kernel(limit_ref, q_ref, k_ref, v_ref, ctx_ref, turn_ref, lse_ref, keys_s, q_s, vt_s, sc_s):
    length = q_ref.shape[0]
    vt_s[...] = v_ref[...].astype(F32).T.astype(BF16)
    for head in range(2):
        keys_s[head] = masked_keys(k_ref[...], head, limit_ref[0])
        q_s[head] = masked_queries(q_ref[...], head)
    factor = SCORE_SCALE * LOG2E
    spans = [slice(at, at + KEYS) for at in range(0, length, KEYS)]
    outs = []
    for head in range(2):
        feats = slice(head * HEAD_DIM, (head + 1) * HEAD_DIM)
        peak = None
        for span in spans:
            scores = mul(keys_s[head, span], q_s[head], NT)
            sc_s[head, span] = scores
            high = jnp.max(scores, axis=0, keepdims=True)
            peak = high if peak is None else jnp.maximum(peak, high)
        peak = peak * factor
        total = jnp.zeros_like(peak)
        gathered = jnp.zeros((HEAD_DIM, length), F32)
        for span in spans:
            expo = jnp.exp2(sc_s[head, span] * factor - peak)
            total += jnp.sum(expo, axis=0, keepdims=True)
            gathered += mul(vt_s[feats, span], expo.astype(BF16))
        outs.append(gathered / total)
        lse_ref[0, head : head + 1, :] = peak + jnp.log2(total)
    both = jnp.concatenate(outs, axis=0)
    turn_ref[...] = both.astype(BF16)
    ctx_ref[...] = both.T.astype(BF16)


def attend(limit, mixed, pairs):
    length = mixed.shape[0]
    column = lambda c: pl.BlockSpec((length, PAIR), lambda i, s: (0, i * 3 + c))
    return pl.pallas_call(
        attend_kernel,
        grid_spec=pltpu.PrefetchScalarGridSpec(
            num_scalar_prefetch=1,
            grid=(pairs,),
            in_specs=[column(0), column(1), column(2)],
            out_specs=[
                pl.BlockSpec((length, PAIR), lambda i, s: (0, i)),
                pl.BlockSpec((PAIR, length), lambda i, s: (i, 0)),
                pl.BlockSpec((1, 2, length), lambda i, s: (i, 0, 0)),
            ],
            scratch_shapes=[
                pltpu.VMEM((2, length, PAIR), BF16),
                pltpu.VMEM((2, length, PAIR), BF16),
                pltpu.VMEM((PAIR, length), BF16),
                pltpu.VMEM((2, length, length), F32),
            ],
        ),
        out_shape=[
            jax.ShapeDtypeStruct((length, pairs * PAIR), BF16),
            jax.ShapeDtypeStruct((pairs * PAIR, length), BF16),
            jax.ShapeDtypeStruct((pairs, 2, length), F32),
        ],
        compiler_params=params(),
        cost_estimate=cost(15),
        name="attend",
    )(limit, mixed, mixed, mixed)


def gelu_both(values):
    root = math.sqrt(2.0 / math.pi)
    scaled = root * values
    inner = scaled * (1.0 + 0.044715 * (values * values))
    tanh = jnp.tanh(inner)
    half = 0.5 + 0.5 * tanh
    slope = half + (1.0 - tanh * tanh) * (1.5 * inner - scaled)
    return values * half, slope


def middle_kernel(
    groups, limit_ref, place_ref, x_ref, clock_ref, gain_ref, ctx_ref, og_ref, *refs
):
    weight_refs, refs = refs[:-16], refs[-16:]
    out_ref, cg_ref, mg_ref, gg_ref, up_send, down_send, up_keep, down_keep = refs[:8]
    wide, units, active_s, ug_s, n_turn, fg_turn, ag_turn, ctx_s = refs[8:]
    step = pl.program_id(0)
    parts, _, hidden = active_s.shape
    blocks = pl.num_programs(0) - parts

    @pl.when(step == 0)
    def _():
        gg_ref[...] = jnp.zeros_like(gg_ref)
        each = len(weight_refs) // parts
        for part in range(parts):
            thin = slice(part * PAIR, (part + 1) * PAIR)
            thick = slice(part * 2 * hidden, (part + 1) * 2 * hidden)
            for at, w_ref in enumerate(weight_refs[part * each : (part + 1) * each]):
                targets = [
                    (wide, thin, slice(0, PAIR)), (units, thick, slice(PAIR, PAIR + 2 * hidden))
                ]
                count = None if groups is None else groups // each
                place_rows(count, place_ref, at * (count or 0), w_ref, targets)

    dead = (step < blocks) & (step * ROWS >= limit_ref[0])

    @pl.when((step < blocks) & jnp.logical_not(dead))
    def _():
        spot = pl.ds(pl.multiple_of(step * ROWS, ROWS), ROWS)
        gain = gain_ref[...]
        live = step * ROWS + lax.broadcasted_iota(jnp.int32, (ROWS, 1), 0) < limit_ref[0]
        begin = join_tokens(x_ref) + clock_ref[...]
        middle = begin + mul(ctx_ref[...], wide[...], NT)
        unit, inverse = norm_parts(middle)
        normed = (unit * gain).astype(BF16)
        n_turn[:, spot] = normed.T
        res_grad = jnp.where(live, og_ref[0].astype(F32), 0.0)
        feed_grad = res_grad.astype(BF16)
        fg_turn[:, spot] = feed_grad.T
        feed = jnp.zeros_like(middle)
        two_grad = jnp.zeros_like(middle)
        for part in range(parts):
            up = slice(2 * part * hidden, (2 * part + 1) * hidden)
            down = slice((2 * part + 1) * hidden, (2 * part + 2) * hidden)
            upper = mul(normed, units[:, up])
            active, slope = gelu_both(upper)
            active = active.astype(BF16)
            active_s[part, spot] = active
            feed += mul(active, units[:, down], NT)
            upper_grad = (mul(feed_grad, units[:, down]) * slope).astype(BF16)
            ug_s[part, spot] = upper_grad
            two_grad += mul(upper_grad, units[:, up], NT)
        out_ref[0] = jnp.where(live, middle + feed, 0.0).astype(BF16)
        gg_ref[...] += jnp.sum(two_grad * unit, axis=0, keepdims=True)
        middle_grad = res_grad + norm_back(two_grad, gain, unit, inverse)
        mg_ref[...] = middle_grad
        att_grad = middle_grad.astype(BF16)
        ag_turn[:, spot] = att_grad.T
        cg_ref[...] = mul(att_grad, wide[...]).astype(BF16)
        for part in range(parts):
            ctx_s[part, spot] = ctx_ref[:, part * PAIR : (part + 1) * PAIR]

    @pl.when(dead)
    def _():
        spot = pl.ds(pl.multiple_of(step * ROWS, ROWS), ROWS)
        for ref in (out_ref, cg_ref, mg_ref):
            ref[...] = jnp.zeros_like(ref)
        for ref in (active_s, ug_s, ctx_s):
            ref[:, spot] = jnp.zeros((ref.shape[0], ROWS, ref.shape[2]), BF16)
        for ref in (n_turn, fg_turn, ag_turn):
            ref[:, spot] = jnp.zeros((ref.shape[0], ROWS), BF16)

    @pl.when(step >= blocks)
    def _():
        turn = step - blocks
        part = jnp.where(turn < 2, 3 - 2 * turn, 6 - 2 * turn)
        grads = (
            mul(ag_turn[...], ctx_s[part]).astype(BF16),
            mul(n_turn[...], ug_s[part]).astype(BF16),
            mul(fg_turn[...], active_s[part]).astype(BF16),
        )

        def into(up_ref, down_ref):
            up_ref[0, :, 0:PAIR], up_ref[0, :, PAIR:], down_ref[0] = grads

        pl.when(turn < 2)(lambda: into(up_send, down_send))
        pl.when(turn >= 2)(lambda: into(up_keep, down_keep))


def middle_block(limit, place, groups, x_blocks, clock, gain, ctx, w_parts, out_grad):
    senders, feature_parts, tall, width = x_blocks.shape
    tokens = tall - SPARE
    length = senders * tokens
    features = feature_parts * width
    parts = len(w_parts)
    weights = [w for part in w_parts for w in part]
    columns = weights[0].shape[1]
    hidden = (columns - PAIR) // 2
    take = ROWS // tokens
    blocks = length // ROWS
    row = lambda i: jnp.minimum(i, blocks - 1)
    whole = lambda array: pl.BlockSpec(
        array.shape, lambda i, *s: (0,) * array.ndim, pipeline_mode=pl.Buffered(1)
    )
    rows = lambda n: pl.BlockSpec((ROWS, n), lambda i, *s: (row(i), 0))
    one = pl.BlockSpec((1, ROWS, features), lambda i, *s: (0, row(i), 0))
    grads = lambda first, n: pl.BlockSpec(
        (1, features, n), lambda i, *s: (jnp.clip(i - blocks - first, 0, 1), 0, 0)
    )
    up_shape = jax.ShapeDtypeStruct((2, features, PAIR + hidden), BF16)
    down_shape = jax.ShapeDtypeStruct((2, features, hidden), BF16)
    return pl.pallas_call(
        functools.partial(middle_kernel, groups),
        grid_spec=pltpu.PrefetchScalarGridSpec(
            num_scalar_prefetch=2,
            grid=(blocks + parts,),
            in_specs=[
                pl.BlockSpec(
                    (take, feature_parts, tall, width), lambda i, *s: (row(i), 0, 0, 0)
                ),
                whole(clock),
                whole(gain),
                rows(features),
                one,
            ]
            + [whole(w) for w in weights],
            out_specs=[
                one, rows(features), rows(features),
                pl.BlockSpec((1, features), lambda i, *s: (0, 0)),
                grads(0, PAIR + hidden), grads(0, hidden), grads(2, PAIR + hidden), grads(2, hidden),
            ],
            scratch_shapes=[
                pltpu.VMEM((features, parts * PAIR), BF16),
                pltpu.VMEM((features, parts * 2 * hidden), BF16),
                pltpu.VMEM((parts, length, hidden), BF16),
                pltpu.VMEM((parts, length, hidden), BF16),
                pltpu.VMEM((features, length), BF16),
                pltpu.VMEM((features, length), BF16),
                pltpu.VMEM((features, length), BF16),
                pltpu.VMEM((parts, length, PAIR), BF16),
            ],
        ),
        out_shape=[
            jax.ShapeDtypeStruct((1, length, features), BF16),
            jax.ShapeDtypeStruct((length, features), BF16),
            jax.ShapeDtypeStruct((length, features), F32),
            jax.ShapeDtypeStruct((1, features), F32),
            up_shape, down_shape, up_shape, down_shape,
        ],
        compiler_params=params(),
        cost_estimate=cost(25),
        name="middle",
    )(limit, place, x_blocks, clock, gain, ctx, out_grad, *weights)


def attend_back_kernel(
    limit_ref, q_ref, k_ref, v_ref, turn_ref, lse_ref, cg_ref, n_turn_ref,
    dm_ref, first_ref, second_ref, keys_s, q_s, qz_s, do_s, kt_s, delta_s,
):
    limit = limit_ref[0]
    length = q_ref.shape[0]
    kt_s[...] = k_ref[...].astype(F32).T.astype(BF16)
    along = cg_ref[...].astype(F32).T * turn_ref[...].astype(F32)
    for head in range(2):
        feats = slice(head * HEAD_DIM, (head + 1) * HEAD_DIM)
        delta_s[head : head + 1, :] = jnp.sum(along[feats, :], axis=0, keepdims=True)
        keys_s[head] = masked_keys(k_ref[...], head, limit)
        q_s[head] = masked_queries(q_ref[...], head)
        qz_s[head] = own_lanes(q_ref[...], head)
        do_s[head] = own_lanes(cg_ref[...], head)
    factor = SCORE_SCALE * LOG2E
    turned = [jnp.zeros((HEAD_DIM, length), F32)] * 2
    for at in range(0, length, BACK_KEYS):
        span = slice(at, at + BACK_KEYS)
        key_grad = jnp.zeros((BACK_KEYS, PAIR), F32)
        value_grad = jnp.zeros((BACK_KEYS, PAIR), F32)
        for head in range(2):
            feats = slice(head * HEAD_DIM, (head + 1) * HEAD_DIM)
            scores = mul(keys_s[head, span], q_s[head], NT)
            prob = jnp.exp2(scores * factor - lse_ref[0, head : head + 1, :])
            prob_grad = mul(v_ref[span, :], do_s[head], NT)
            score_grad = (prob * (prob_grad - delta_s[head : head + 1, :])).astype(BF16)
            value_grad += mul(prob.astype(BF16), do_s[head])
            key_grad += mul(score_grad, qz_s[head])
            turned[head] += mul(kt_s[feats, span], score_grad)
        dm_ref[span, PAIR : 2 * PAIR] = (key_grad * SCORE_SCALE).astype(BF16)
        dm_ref[span, 2 * PAIR : 3 * PAIR] = value_grad.astype(BF16)
    query_grad = jnp.concatenate(turned, axis=0) * SCORE_SCALE
    dm_ref[:, 0:PAIR] = query_grad.T.astype(BF16)
    grad = mul(n_turn_ref[...], dm_ref[...]).astype(BF16)

    @pl.when(pl.program_id(0) == 0)
    def _():
        first_ref[...] = grad

    @pl.when(pl.program_id(0) == 1)
    def _():
        second_ref[...] = grad


def attend_back(limit, mixed, ctx_turn, lse, context_grad, n_turn, first):
    length = mixed.shape[0]
    features = n_turn.shape[0]
    pair = lambda i: first - i
    column = lambda c: pl.BlockSpec((length, PAIR), lambda i, s: (0, pair(i) * 3 + c))
    return pl.pallas_call(
        attend_back_kernel,
        grid_spec=pltpu.PrefetchScalarGridSpec(
            num_scalar_prefetch=1,
            grid=(2,),
            in_specs=[
                column(0), column(1), column(2),
                pl.BlockSpec((PAIR, length), lambda i, s: (pair(i), 0)),
                pl.BlockSpec((1, 2, length), lambda i, s: (pair(i), 0, 0)),
                pl.BlockSpec((length, PAIR), lambda i, s: (0, pair(i))),
                pl.BlockSpec((features, length), lambda i, s: (0, 0)),
            ],
            out_specs=[
                pl.BlockSpec((length, 3 * PAIR), lambda i, s: (0, i)),
                pl.BlockSpec((features, 3 * PAIR), lambda i, s: (0, 0)),
                pl.BlockSpec((features, 3 * PAIR), lambda i, s: (0, 0)),
            ],
            scratch_shapes=[
                pltpu.VMEM((2, length, PAIR), BF16),
                pltpu.VMEM((2, length, PAIR), BF16),
                pltpu.VMEM((2, length, PAIR), BF16),
                pltpu.VMEM((2, length, PAIR), BF16),
                pltpu.VMEM((PAIR, length), BF16),
                pltpu.VMEM((8, length), F32),
            ],
        ),
        out_shape=[
            jax.ShapeDtypeStruct((length, 2 * 3 * PAIR), BF16),
            jax.ShapeDtypeStruct((features, 3 * PAIR), BF16),
            jax.ShapeDtypeStruct((features, 3 * PAIR), BF16),
        ],
        compiler_params=params(),
        cost_estimate=cost(16),
        name="attend_back",
    )(limit, mixed, mixed, mixed, ctx_turn, lse, context_grad, n_turn)


def begin_kernel(
    limit_ref, x_ref, clock_ref, gain_ref, gg_two_ref, mg_ref, w_ref, high_ref, low_ref, bg_ref, gg_s
):
    step = pl.program_id(0)
    _, parts, tall, width = bg_ref.shape
    tokens = tall - SPARE
    blocks = ROWS // tokens
    spot = pl.ds(step * blocks, blocks)

    @pl.when(step == 0)
    def _():
        gg_s[...] = jnp.zeros_like(gg_s)

    @pl.when(step * ROWS < limit_ref[0])
    def _():
        begin = join_tokens(x_ref) + clock_ref[...]
        unit, inverse = norm_parts(begin)
        one_grad = jnp.zeros_like(begin)
        for part, (d_ref, at) in enumerate(((low_ref, 1), (low_ref, 0), (high_ref, 1), (high_ref, 0))):
            columns = slice(part * 3 * PAIR, (part + 1) * 3 * PAIR)
            own = slice(at * 3 * PAIR, (at + 1) * 3 * PAIR)
            one_grad += mul(d_ref[:, own], w_ref[:, columns], NT)
        gg_s[...] += jnp.sum(one_grad * unit, axis=0, keepdims=True)
        total = (mg_ref[...] + norm_back(one_grad, gain_ref[...], unit, inverse)).astype(BF16)
        for part in range(parts):
            piece = total[:, part * width : (part + 1) * width]
            bg_ref[spot, part, 0:tokens] = piece.reshape(blocks, tokens, width)

    @pl.when(step * ROWS >= limit_ref[0])
    def _():
        bg_ref[spot] = jnp.zeros((blocks,) + bg_ref.shape[1:], BF16)

    @pl.when(step == pl.num_programs(0) - 1)
    def _():
        rows = []
        for ref in (gg_s, gg_two_ref):
            for part in range(parts):
                rows.append(ref[:, part * width : (part + 1) * width])
        bg_ref[:, :, tokens:tall] = jnp.broadcast_to(
            jnp.concatenate(rows, axis=0).astype(BF16), bg_ref.shape[:2] + (SPARE, width)
        )


def begin_block(limit, x_blocks, clock, gain, two_grad, w_wide, middle_grad, high, low):
    senders, feature_parts, tall, width = x_blocks.shape
    tokens = tall - SPARE
    length = senders * tokens
    features = feature_parts * width
    take = ROWS // tokens
    whole = lambda array: pl.BlockSpec(array.shape, lambda i, s: (0,) * array.ndim)
    rows = lambda n: pl.BlockSpec((ROWS, n), lambda i, s: (i, 0))
    return pl.pallas_call(
        begin_kernel,
        grid_spec=pltpu.PrefetchScalarGridSpec(
            num_scalar_prefetch=1,
            grid=(length // ROWS,),
            in_specs=[
                pl.BlockSpec((take, feature_parts, tall, width), lambda i, s: (i, 0, 0, 0)),
                whole(clock), whole(gain), whole(two_grad), rows(features), whole(w_wide),
            ]
            + [rows(6 * PAIR)] * 2,
            out_specs=whole(x_blocks),
            scratch_shapes=[pltpu.VMEM((1, features), F32)],
        ),
        out_shape=jax.ShapeDtypeStruct(x_blocks.shape, BF16),
        compiler_params=params(),
        cost_estimate=cost(7),
        name="begin_back",
    )(limit, x_blocks, clock, gain, two_grad, middle_grad, w_wide, high, low)


DIRECT = 8


def clock_rows(step_ids, features):
    half_width = features // 2
    ladder = jnp.arange(half_width, dtype=F32) / half_width
    rate_rows = jnp.exp(-math.log(10000.0) * ladder)
    angles = step_ids.astype(F32)[:, None] * rate_rows[None, :]
    return jnp.concatenate([jnp.sin(angles), jnp.cos(angles)], axis=-1)


def swap(value, apart):
    count = lax.axis_size("tensor")
    return lax.ppermute(value, "tensor", [(i, i ^ apart) for i in range(count)])


def along_dp(value, move):
    count = lax.axis_size("dp")
    return lax.ppermute(value, "dp", [(i, move(i)) for i in range(count)])


def across(value):
    return along_dp(value, lambda i: i ^ 1)


def ahead(value, step):
    count = lax.axis_size("dp") // 2
    return along_dp(value, lambda i: (i // 2 + step) % count * 2 + i % 2)


def places():
    count = lax.axis_size("dp") // 2
    own = lax.axis_index("dp")
    coarse = (own // 2 - jnp.arange(count, dtype=jnp.int32)) % count
    return jnp.concatenate([coarse * 2 + own % 2, coarse * 2 + 1 - own % 2])


def collect_coarse(shard):
    count = lax.axis_size("dp") // 2
    return jnp.concatenate([shard] + [ahead(shard, step) for step in range(1, count)], axis=0)


def collect_rows(shard):
    count = lax.axis_size("dp")
    rows = lax.all_to_all(
        jnp.broadcast_to(shard[None], (count,) + shard.shape), "dp", 0, 0, tiled=True
    )
    return rows.reshape(count * shard.shape[0], shard.shape[1])


def collect_columns(rows):
    far = swap(rows, 2)
    return rows, swap(rows, 1), far, swap(far, 1)


def add(*values):
    total = values[0].astype(F32)
    for value in values[1:]:
        total += value.astype(F32)
    return total.astype(BF16)


def fold_pair(values):
    own = lax.axis_index("dp") % 2
    pick = lambda value, which: lax.dynamic_index_in_dim(value, which, value.ndim - 3, keepdims=False)
    sent = add(*[pick(value, 1 - own) for value in values])
    return sent, lambda: [pick(value, own) for value in values] + [across(sent)]


def fold_far(values):
    sent = add(*[value[0] for value in values])
    return sent, lambda: [value[1] for value in values] + [swap(sent, 2)]


def fold_coarse(values):
    count = lax.axis_size("dp") // 2
    own = lax.axis_index("dp") // 2
    pick = lambda value, which: lax.dynamic_index_in_dim(value, which % count, 0, keepdims=False)
    value = add(*values)
    came = [ahead(pick(value, own + step), step) for step in range(1, count)]

    def finish(*others):
        pieces = lax.optimization_barrier((*came, *others))[: count - 1]
        total = pick(value, own).astype(F32)
        for piece in pieces:
            total += piece.astype(F32)
        return total

    return value, finish


def grouped(value):
    count = lax.axis_size("dp")
    two, rows, columns = value.shape
    return value.reshape(two, count // 2, 2, rows // count, columns)


def exchange_rows(value):
    count = lax.axis_size("dp")
    groups = value.reshape(count, value.shape[0] // count, value.shape[1])
    return jnp.sum(lax.all_to_all(groups, "dp", 0, 0, tiled=True).astype(F32), axis=0)


def three_terms(values):
    terms = []
    for _ in range(3):
        term = lax.reduce_precision(values, 8, 7)
        terms.append(term.astype(BF16))
        values = values - term
    return terms


def after(value, *others):
    return lax.optimization_barrier((value,) + others)[0]


def on_device(
    states, timesteps, lengths, deal_order, w_qkv, w_out, w_up, w_down, gain_attn, gain_ffn, out_grad
):
    both = ("dp", "tensor")
    dp_count = lax.axis_size("dp")
    tensor_count = lax.axis_size("tensor")
    devices = dp_count * tensor_count
    total_seqs, tokens, width = states.shape
    assert tensor_count == 4 and total_seqs == devices
    features = width * tensor_count
    own = lax.axis_index("dp") * tensor_count + lax.axis_index("tensor")
    own_id = lax.dynamic_slice_in_dim(deal_order, own, 1)
    limit = lengths[own_id]
    clock = clock_rows(timesteps[own_id], features)
    per = gain_attn.shape[0]
    rows = w_qkv.shape[0]
    hidden = w_up.shape[1]

    rest = jnp.concatenate([w_out.T, w_up, w_down.T], axis=1)
    qkv = w_qkv.reshape(rows, -1)
    direct = dp_count <= DIRECT
    if direct:
        place, groups = places(), dp_count
        first = collect_coarse(jnp.concatenate([qkv, rest], axis=1))
        qkv_rows = first[:, : qkv.shape[1]]
        qkv_parts = collect_columns(jnp.concatenate([qkv_rows, across(qkv_rows)], axis=0))
        mine = after(first[:, qkv.shape[1] :], qkv_parts[2])
        other = across(mine)
        far_mine, far_other = swap(mine, 2), swap(other, 2)
    else:
        place, groups = jnp.zeros((1,), jnp.int32), None
        first = collect_rows(qkv)
        qkv_parts = collect_columns(first)
        rest_parts = [(part,) for part in collect_columns(collect_rows(rest))]

    spare = jnp.stack(three_terms(gain_attn) + three_terms(gain_ffn)).reshape(1, 6 * per)
    spare = jnp.pad(spare, ((0, SPARE - 1), (0, width - 6 * per)))
    arranged = jnp.concatenate(
        [states[deal_order], jnp.broadcast_to(spare[None], (devices, SPARE, width))], axis=1
    )
    x_blocks = lax.all_to_all(after(arranged, first), both, 0, 0, tiled=True)
    gains = jnp.sum(x_blocks[:, tokens, : 6 * per].reshape(devices, 2, 3, per).astype(F32), axis=2)
    gain_one = gains[:, 0].reshape(1, features)
    gain_two = gains[:, 1].reshape(1, features)
    x_blocks = x_blocks.reshape(dp_count, tensor_count, tokens + SPARE, width)

    mixed, n_one_turn, qkv_wide = project(
        limit, place, groups, x_blocks, clock, gain_one, qkv_parts
    )
    if direct:
        near_mine, near_other, last_mine = swap(mine, 1), swap(other, 1), swap(far_mine, 1)
        mixed = after(mixed, near_mine, near_other, last_mine)
    ctx, ctx_turn, lse = attend(limit, mixed, tensor_count)
    if direct:
        last_other = swap(after(far_other, ctx), 1)
        rest_parts = (
            (mine, other), (near_mine, near_other), (far_mine, far_other), (last_mine, last_other)
        )
    output, context_grad, middle_grad, two_grad, up_send, down_send, up_keep, down_keep = middle_block(
        limit, place, groups, x_blocks, clock, gain_two, ctx, rest_parts, out_grad
    )
    up_came, down_came = swap(up_send, 1), swap(down_send, 1)

    back = functools.partial(attend_back, limit, mixed, ctx_turn, lse)
    context_grad = after(context_grad, up_send, down_send)
    high, three, two = back(context_grad, n_one_turn, 3)
    came_three = swap(three, 1)
    far = add(two, came_three)
    came_far = swap(far, 2)
    context_grad = after(context_grad, high, far)
    if direct:
        down_sent, down_rest = fold_pair([grouped(value) for value in (down_keep, down_came)])
        up_sent, up_rest = fold_far([grouped(value) for value in (up_keep, up_came)])
        context_grad = after(context_grad, down_sent, up_sent)
    low, one, own_part = back(context_grad, n_one_turn, 1)
    came_one = swap(one, 1)
    if direct:
        down_sent, down_rest = fold_far([add(*[after(value, low) for value in down_rest()])])
        up_sent, up_rest = fold_pair([add(*[after(value, low) for value in up_rest()])])
        middle_grad = after(middle_grad, down_sent, up_sent, came_far)
    begin_grad = begin_block(
        limit, x_blocks, clock, gain_one, two_grad, qkv_wide, middle_grad, high, low
    )
    near = (own_part, came_one, came_far)
    if direct:
        down_value, down_finish = fold_coarse(down_rest())
        up_value, up_finish = fold_coarse(up_rest())
        begin_grad = after(begin_grad, down_value, up_value)
        near = [grouped(after(value, up_value)[None])[0] for value in near]
        qkv_value, qkv_finish = fold_coarse(fold_pair(near)[1]())
        down_total, up_total, qkv_total = down_finish(qkv_value), up_finish(qkv_value), qkv_finish()
    else:
        up_total = exchange_rows(add(*fold_far([up_keep, up_came])[1]()))
        down_total = exchange_rows(add(*fold_far([down_keep, down_came])[1]()))
        qkv_total = exchange_rows(add(*near))
    returned = lax.all_to_all(
        begin_grad.reshape(devices, tokens + SPARE, width), both, 0, 0, tiled=True
    )
    inverse = (
        jnp.zeros((total_seqs,), jnp.int32)
        .at[deal_order]
        .set(jnp.arange(total_seqs, dtype=jnp.int32))
    )
    states_grad = returned[:, :tokens][inverse]
    gain_grads = jnp.sum(returned[:, tokens:].astype(F32), axis=0).reshape(2, devices, per)
    gain_grads = lax.dynamic_index_in_dim(gain_grads, own, 1, keepdims=False)
    return (
        output,
        states_grad,
        qkv_total.reshape(w_qkv.shape),
        up_total[:, :PAIR].T,
        up_total[:, PAIR:],
        down_total.T,
        gain_grads[0],
        gain_grads[1],
    )


def solution(mesh):
    in_specs = (
        P(None, "dp", "tensor"),
        P(),
        P(),
        P(),
        P("dp", None, "tensor"),
        P("tensor", "dp"),
        P("dp", "tensor"),
        P("tensor", "dp"),
        P(("dp", "tensor")),
        P(("dp", "tensor")),
        P(("dp", "tensor"), None, None),
    )
    out_specs = (
        P(("dp", "tensor"), None, None),
        P(None, "dp", "tensor"),
        P("dp", None, "tensor"),
        P("tensor", "dp"),
        P("dp", "tensor"),
        P("tensor", "dp"),
        P(("dp", "tensor")),
        P(("dp", "tensor")),
    )
    return jax.shard_map(
        on_device, mesh=mesh, in_specs=in_specs, out_specs=out_specs, check_vma=False
    )
```

```python
import functools
import math

import jax
import jax.numpy as jnp
from jax import lax
from jax.experimental import pallas as pl
from jax.experimental.pallas import tpu as pltpu
from jax.sharding import PartitionSpec as P

HEAD_DIM = 64
PAIR = 2 * HEAD_DIM
ROWS = 256
KEYS = 256
BACK_KEYS = 512
SPARE = 8
SCORE_SCALE = 1.0 / math.sqrt(HEAD_DIM)
LOG2E = math.log2(math.e)
F32 = jnp.float32
BF16 = jnp.bfloat16
NN = (((1,), (0,)), ((), ()))
NT = (((1,), (1,)), ((), ()))
VMEM_LIMIT = 56 * 1024 * 1024


def mul(lhs, rhs, dims=NN):
    return lax.dot_general(lhs, rhs, dims, preferred_element_type=F32)


def join_tokens(ref):
    blocks, parts, tall, width = ref.shape
    tokens = tall - SPARE
    return jnp.concatenate(
        [ref[:, part, 0:tokens].reshape(blocks * tokens, width) for part in range(parts)], axis=-1
    ).astype(F32)


def place_rows(groups, place_ref, first, source, targets):
    if groups is None:
        for target, columns, own in targets:
            target[:, columns] = source[:, own]
        return
    rows = source.shape[0] // groups
    for group in range(groups):
        spot = pl.ds(pl.multiple_of(place_ref[first + group] * rows, rows), rows)
        for target, columns, own in targets:
            target[spot, columns] = source[group * rows : (group + 1) * rows, own]


def norm_parts(values):
    center = values - jnp.mean(values, axis=-1, keepdims=True)
    spread = jnp.mean(center * center, axis=-1, keepdims=True)
    inverse = lax.rsqrt(spread + 1e-05)
    return center * inverse, inverse


def norm_back(grad, gain, unit, inverse):
    scaled = grad * gain
    mean_scaled = jnp.mean(scaled, axis=-1, keepdims=True)
    mean_along = jnp.mean(scaled * unit, axis=-1, keepdims=True)
    return inverse * (scaled - mean_scaled - unit * mean_along)


def cost(microseconds):
    return pl.CostEstimate(
        flops=int(microseconds * 1.15e9), bytes_accessed=1 << 20, transcendentals=0
    )


def params(**kwargs):
    return pltpu.CompilerParams(vmem_limit_bytes=VMEM_LIMIT, **kwargs)


def project_kernel(groups, limit_ref, place_ref, x_ref, clock_ref, gain_ref, *refs):
    w_refs, (mixed_ref, n_turn_ref, wide) = refs[:-3], refs[-3:]
    step = pl.program_id(0)

    @pl.when(step == 0)
    def _():
        for part, w_ref in enumerate(w_refs):
            width = w_ref.shape[1]
            columns = slice(part * width, (part + 1) * width)
            place_rows(groups, place_ref, 0, w_ref, [(wide, columns, slice(0, width))])

    @pl.when(step * ROWS < limit_ref[0])
    def _():
        begin = join_tokens(x_ref) + clock_ref[...]
        unit, _ = norm_parts(begin)
        normed = (unit * gain_ref[...]).astype(BF16)
        n_turn_ref[...] = normed.T
        mixed_ref[...] = mul(normed, wide[...]).astype(BF16)

    @pl.when(step * ROWS >= limit_ref[0])
    def _():
        n_turn_ref[...] = jnp.zeros_like(n_turn_ref)
        mixed_ref[...] = jnp.zeros_like(mixed_ref)


def project(limit, place, groups, x_blocks, clock, gain, w_parts):
    senders, feature_parts, tall, width = x_blocks.shape
    tokens = tall - SPARE
    length = senders * tokens
    features = feature_parts * width
    parts, columns = len(w_parts), w_parts[0].shape[1]
    take = ROWS // tokens
    return pl.pallas_call(
        functools.partial(project_kernel, groups),
        grid_spec=pltpu.PrefetchScalarGridSpec(
            num_scalar_prefetch=2,
            grid=(length // ROWS,),
            in_specs=[
                pl.BlockSpec((take, feature_parts, tall, width), lambda i, *s: (i, 0, 0, 0)),
                pl.BlockSpec((1, features), lambda i, *s: (0, 0)),
                pl.BlockSpec((1, features), lambda i, *s: (0, 0)),
            ]
            + [pl.BlockSpec((features, columns), lambda i, *s: (0, 0))] * parts,
            out_specs=[
                pl.BlockSpec((ROWS, parts * columns), lambda i, *s: (i, 0)),
                pl.BlockSpec((features, ROWS), lambda i, *s: (0, i)),
                pl.BlockSpec((features, parts * columns), lambda i, *s: (0, 0)),
            ],
        ),
        out_shape=[
            jax.ShapeDtypeStruct((length, parts * columns), BF16),
            jax.ShapeDtypeStruct((features, length), BF16),
            jax.ShapeDtypeStruct((features, parts * columns), BF16),
        ],
        compiler_params=params(),
        cost_estimate=cost(5),
        name="project",
    )(limit, place, x_blocks, clock, gain, *w_parts)


def head_lanes(shape, head):
    lane = lax.broadcasted_iota(jnp.int32, shape, 1)
    return (lane >= head * HEAD_DIM) & (lane < (head + 1) * HEAD_DIM)


def spare_lane(shape, head):
    lane = lax.broadcasted_iota(jnp.int32, shape, 1)
    return lane == (1 - head) * HEAD_DIM


def masked_keys(keys, head, limit):
    row = lax.broadcasted_iota(jnp.int32, keys.shape, 0)
    spare = jnp.where(
        spare_lane(keys.shape, head) & (row >= limit), jnp.asarray(-1e30, F32), jnp.asarray(0.0, F32)
    )
    return jnp.where(head_lanes(keys.shape, head), keys.astype(F32), spare).astype(BF16)


def own_lanes(values, head):
    return jnp.where(head_lanes(values.shape, head), values.astype(F32), 0.0).astype(BF16)


def masked_queries(queries, head):
    spare = jnp.where(spare_lane(queries.shape, head), jnp.asarray(1.0, F32), jnp.asarray(0.0, F32))
    return jnp.where(head_lanes(queries.shape, head), queries.astype(F32), spare).astype(BF16)


def attend_kernel(limit_ref, q_ref, k_ref, v_ref, ctx_ref, turn_ref, lse_ref, keys_s, q_s, vt_s, sc_s):
    length = q_ref.shape[0]
    vt_s[...] = v_ref[...].astype(F32).T.astype(BF16)
    for head in range(2):
        keys_s[head] = masked_keys(k_ref[...], head, limit_ref[0])
        q_s[head] = masked_queries(q_ref[...], head)
    factor = SCORE_SCALE * LOG2E
    spans = [slice(at, at + KEYS) for at in range(0, length, KEYS)]
    outs = []
    for head in range(2):
        feats = slice(head * HEAD_DIM, (head + 1) * HEAD_DIM)
        peak = None
        for span in spans:
            scores = mul(keys_s[head, span], q_s[head], NT)
            sc_s[head, span] = scores
            high = jnp.max(scores, axis=0, keepdims=True)
            peak = high if peak is None else jnp.maximum(peak, high)
        peak = peak * factor
        total = jnp.zeros_like(peak)
        gathered = jnp.zeros((HEAD_DIM, length), F32)
        for span in spans:
            expo = jnp.exp2(sc_s[head, span] * factor - peak)
            total += jnp.sum(expo, axis=0, keepdims=True)
            gathered += mul(vt_s[feats, span], expo.astype(BF16))
        outs.append(gathered / total)
        lse_ref[0, head : head + 1, :] = peak + jnp.log2(total)
    both = jnp.concatenate(outs, axis=0)
    turn_ref[...] = both.astype(BF16)
    ctx_ref[...] = both.T.astype(BF16)


def attend(limit, mixed, pairs):
    length = mixed.shape[0]
    column = lambda c: pl.BlockSpec((length, PAIR), lambda i, s: (0, i * 3 + c))
    return pl.pallas_call(
        attend_kernel,
        grid_spec=pltpu.PrefetchScalarGridSpec(
            num_scalar_prefetch=1,
            grid=(pairs,),
            in_specs=[column(0), column(1), column(2)],
            out_specs=[
                pl.BlockSpec((length, PAIR), lambda i, s: (0, i)),
                pl.BlockSpec((PAIR, length), lambda i, s: (i, 0)),
                pl.BlockSpec((1, 2, length), lambda i, s: (i, 0, 0)),
            ],
            scratch_shapes=[
                pltpu.VMEM((2, length, PAIR), BF16),
                pltpu.VMEM((2, length, PAIR), BF16),
                pltpu.VMEM((PAIR, length), BF16),
                pltpu.VMEM((2, length, length), F32),
            ],
        ),
        out_shape=[
            jax.ShapeDtypeStruct((length, pairs * PAIR), BF16),
            jax.ShapeDtypeStruct((pairs * PAIR, length), BF16),
            jax.ShapeDtypeStruct((pairs, 2, length), F32),
        ],
        compiler_params=params(),
        cost_estimate=cost(15),
        name="attend",
    )(limit, mixed, mixed, mixed)


def gelu_both(values):
    root = math.sqrt(2.0 / math.pi)
    scaled = root * values
    inner = scaled * (1.0 + 0.044715 * (values * values))
    tanh = jnp.tanh(inner)
    half = 0.5 + 0.5 * tanh
    slope = half + (1.0 - tanh * tanh) * (1.5 * inner - scaled)
    return values * half, slope


def middle_kernel(
    groups, limit_ref, place_ref, x_ref, clock_ref, gain_ref, ctx_ref, og_ref, *refs
):
    weight_refs, refs = refs[:-16], refs[-16:]
    out_ref, cg_ref, mg_ref, gg_ref, up_send, down_send, up_keep, down_keep = refs[:8]
    wide, units, active_s, ug_s, n_turn, fg_turn, ag_turn, ctx_s = refs[8:]
    step = pl.program_id(0)
    parts, _, hidden = active_s.shape
    blocks = pl.num_programs(0) - parts

    @pl.when(step == 0)
    def _():
        gg_ref[...] = jnp.zeros_like(gg_ref)
        each = len(weight_refs) // parts
        for part in range(parts):
            thin = slice(part * PAIR, (part + 1) * PAIR)
            thick = slice(part * 2 * hidden, (part + 1) * 2 * hidden)
            for at, w_ref in enumerate(weight_refs[part * each : (part + 1) * each]):
                targets = [
                    (wide, thin, slice(0, PAIR)), (units, thick, slice(PAIR, PAIR + 2 * hidden))
                ]
                count = None if groups is None else groups // each
                place_rows(count, place_ref, at * (count or 0), w_ref, targets)

    dead = (step < blocks) & (step * ROWS >= limit_ref[0])

    @pl.when((step < blocks) & jnp.logical_not(dead))
    def _():
        spot = pl.ds(pl.multiple_of(step * ROWS, ROWS), ROWS)
        gain = gain_ref[...]
        live = step * ROWS + lax.broadcasted_iota(jnp.int32, (ROWS, 1), 0) < limit_ref[0]
        begin = join_tokens(x_ref) + clock_ref[...]
        middle = begin + mul(ctx_ref[...], wide[...], NT)
        unit, inverse = norm_parts(middle)
        normed = (unit * gain).astype(BF16)
        n_turn[:, spot] = normed.T
        res_grad = jnp.where(live, og_ref[0].astype(F32), 0.0)
        feed_grad = res_grad.astype(BF16)
        fg_turn[:, spot] = feed_grad.T
        feed = jnp.zeros_like(middle)
        two_grad = jnp.zeros_like(middle)
        for part in range(parts):
            up = slice(2 * part * hidden, (2 * part + 1) * hidden)
            down = slice((2 * part + 1) * hidden, (2 * part + 2) * hidden)
            upper = mul(normed, units[:, up])
            active, slope = gelu_both(upper)
            active = active.astype(BF16)
            active_s[part, spot] = active
            feed += mul(active, units[:, down], NT)
            upper_grad = (mul(feed_grad, units[:, down]) * slope).astype(BF16)
            ug_s[part, spot] = upper_grad
            two_grad += mul(upper_grad, units[:, up], NT)
        out_ref[0] = jnp.where(live, middle + feed, 0.0).astype(BF16)
        gg_ref[...] += jnp.sum(two_grad * unit, axis=0, keepdims=True)
        middle_grad = res_grad + norm_back(two_grad, gain, unit, inverse)
        mg_ref[...] = middle_grad
        att_grad = middle_grad.astype(BF16)
        ag_turn[:, spot] = att_grad.T
        cg_ref[...] = mul(att_grad, wide[...]).astype(BF16)
        for part in range(parts):
            ctx_s[part, spot] = ctx_ref[:, part * PAIR : (part + 1) * PAIR]

    @pl.when(dead)
    def _():
        spot = pl.ds(pl.multiple_of(step * ROWS, ROWS), ROWS)
        for ref in (out_ref, cg_ref, mg_ref):
            ref[...] = jnp.zeros_like(ref)
        for ref in (active_s, ug_s, ctx_s):
            ref[:, spot] = jnp.zeros((ref.shape[0], ROWS, ref.shape[2]), BF16)
        for ref in (n_turn, fg_turn, ag_turn):
            ref[:, spot] = jnp.zeros((ref.shape[0], ROWS), BF16)

    @pl.when(step >= blocks)
    def _():
        turn = step - blocks
        part = jnp.where(turn < 2, 3 - 2 * turn, 6 - 2 * turn)
        grads = (
            mul(ag_turn[...], ctx_s[part]).astype(BF16),
            mul(n_turn[...], ug_s[part]).astype(BF16),
            mul(fg_turn[...], active_s[part]).astype(BF16),
        )

        def into(up_ref, down_ref):
            up_ref[0, :, 0:PAIR], up_ref[0, :, PAIR:], down_ref[0] = grads

        pl.when(turn < 2)(lambda: into(up_send, down_send))
        pl.when(turn >= 2)(lambda: into(up_keep, down_keep))


def middle_block(limit, place, groups, x_blocks, clock, gain, ctx, w_parts, out_grad):
    senders, feature_parts, tall, width = x_blocks.shape
    tokens = tall - SPARE
    length = senders * tokens
    features = feature_parts * width
    parts = len(w_parts)
    weights = [w for part in w_parts for w in part]
    columns = weights[0].shape[1]
    hidden = (columns - PAIR) // 2
    take = ROWS // tokens
    blocks = length // ROWS
    row = lambda i: jnp.minimum(i, blocks - 1)
    whole = lambda array: pl.BlockSpec(
        array.shape, lambda i, *s: (0,) * array.ndim, pipeline_mode=pl.Buffered(1)
    )
    rows = lambda n: pl.BlockSpec((ROWS, n), lambda i, *s: (row(i), 0))
    one = pl.BlockSpec((1, ROWS, features), lambda i, *s: (0, row(i), 0))
    grads = lambda first, n: pl.BlockSpec(
        (1, features, n), lambda i, *s: (jnp.clip(i - blocks - first, 0, 1), 0, 0)
    )
    up_shape = jax.ShapeDtypeStruct((2, features, PAIR + hidden), BF16)
    down_shape = jax.ShapeDtypeStruct((2, features, hidden), BF16)
    return pl.pallas_call(
        functools.partial(middle_kernel, groups),
        grid_spec=pltpu.PrefetchScalarGridSpec(
            num_scalar_prefetch=2,
            grid=(blocks + parts,),
            in_specs=[
                pl.BlockSpec(
                    (take, feature_parts, tall, width), lambda i, *s: (row(i), 0, 0, 0)
                ),
                whole(clock),
                whole(gain),
                rows(features),
                one,
            ]
            + [whole(w) for w in weights],
            out_specs=[
                one, rows(features), rows(features),
                pl.BlockSpec((1, features), lambda i, *s: (0, 0)),
                grads(0, PAIR + hidden), grads(0, hidden), grads(2, PAIR + hidden), grads(2, hidden),
            ],
            scratch_shapes=[
                pltpu.VMEM((features, parts * PAIR), BF16),
                pltpu.VMEM((features, parts * 2 * hidden), BF16),
                pltpu.VMEM((parts, length, hidden), BF16),
                pltpu.VMEM((parts, length, hidden), BF16),
                pltpu.VMEM((features, length), BF16),
                pltpu.VMEM((features, length), BF16),
                pltpu.VMEM((features, length), BF16),
                pltpu.VMEM((parts, length, PAIR), BF16),
            ],
        ),
        out_shape=[
            jax.ShapeDtypeStruct((1, length, features), BF16),
            jax.ShapeDtypeStruct((length, features), BF16),
            jax.ShapeDtypeStruct((length, features), F32),
            jax.ShapeDtypeStruct((1, features), F32),
            up_shape, down_shape, up_shape, down_shape,
        ],
        compiler_params=params(),
        cost_estimate=cost(25),
        name="middle",
    )(limit, place, x_blocks, clock, gain, ctx, out_grad, *weights)


def attend_back_kernel(
    limit_ref, q_ref, k_ref, v_ref, turn_ref, lse_ref, cg_ref, n_turn_ref,
    dm_ref, first_ref, second_ref, keys_s, q_s, qz_s, do_s, kt_s, delta_s,
):
    limit = limit_ref[0]
    length = q_ref.shape[0]
    kt_s[...] = k_ref[...].astype(F32).T.astype(BF16)
    along = cg_ref[...].astype(F32).T * turn_ref[...].astype(F32)
    for head in range(2):
        feats = slice(head * HEAD_DIM, (head + 1) * HEAD_DIM)
        delta_s[head : head + 1, :] = jnp.sum(along[feats, :], axis=0, keepdims=True)
        keys_s[head] = masked_keys(k_ref[...], head, limit)
        q_s[head] = masked_queries(q_ref[...], head)
        qz_s[head] = own_lanes(q_ref[...], head)
        do_s[head] = own_lanes(cg_ref[...], head)
    factor = SCORE_SCALE * LOG2E
    turned = [jnp.zeros((HEAD_DIM, length), F32)] * 2
    for at in range(0, length, BACK_KEYS):
        span = slice(at, at + BACK_KEYS)
        key_grad = jnp.zeros((BACK_KEYS, PAIR), F32)
        value_grad = jnp.zeros((BACK_KEYS, PAIR), F32)
        for head in range(2):
            feats = slice(head * HEAD_DIM, (head + 1) * HEAD_DIM)
            scores = mul(keys_s[head, span], q_s[head], NT)
            prob = jnp.exp2(scores * factor - lse_ref[0, head : head + 1, :])
            prob_grad = mul(v_ref[span, :], do_s[head], NT)
            score_grad = (prob * (prob_grad - delta_s[head : head + 1, :])).astype(BF16)
            value_grad += mul(prob.astype(BF16), do_s[head])
            key_grad += mul(score_grad, qz_s[head])
            turned[head] += mul(kt_s[feats, span], score_grad)
        dm_ref[span, PAIR : 2 * PAIR] = (key_grad * SCORE_SCALE).astype(BF16)
        dm_ref[span, 2 * PAIR : 3 * PAIR] = value_grad.astype(BF16)
    query_grad = jnp.concatenate(turned, axis=0) * SCORE_SCALE
    dm_ref[:, 0:PAIR] = query_grad.T.astype(BF16)
    grad = mul(n_turn_ref[...], dm_ref[...]).astype(BF16)

    @pl.when(pl.program_id(0) == 0)
    def _():
        first_ref[...] = grad

    @pl.when(pl.program_id(0) == 1)
    def _():
        second_ref[...] = grad


def attend_back(limit, mixed, ctx_turn, lse, context_grad, n_turn, first):
    length = mixed.shape[0]
    features = n_turn.shape[0]
    pair = lambda i: first - i
    column = lambda c: pl.BlockSpec((length, PAIR), lambda i, s: (0, pair(i) * 3 + c))
    return pl.pallas_call(
        attend_back_kernel,
        grid_spec=pltpu.PrefetchScalarGridSpec(
            num_scalar_prefetch=1,
            grid=(2,),
            in_specs=[
                column(0), column(1), column(2),
                pl.BlockSpec((PAIR, length), lambda i, s: (pair(i), 0)),
                pl.BlockSpec((1, 2, length), lambda i, s: (pair(i), 0, 0)),
                pl.BlockSpec((length, PAIR), lambda i, s: (0, pair(i))),
                pl.BlockSpec((features, length), lambda i, s: (0, 0)),
            ],
            out_specs=[
                pl.BlockSpec((length, 3 * PAIR), lambda i, s: (0, i)),
                pl.BlockSpec((features, 3 * PAIR), lambda i, s: (0, 0)),
                pl.BlockSpec((features, 3 * PAIR), lambda i, s: (0, 0)),
            ],
            scratch_shapes=[
                pltpu.VMEM((2, length, PAIR), BF16),
                pltpu.VMEM((2, length, PAIR), BF16),
                pltpu.VMEM((2, length, PAIR), BF16),
                pltpu.VMEM((2, length, PAIR), BF16),
                pltpu.VMEM((PAIR, length), BF16),
                pltpu.VMEM((8, length), F32),
            ],
        ),
        out_shape=[
            jax.ShapeDtypeStruct((length, 2 * 3 * PAIR), BF16),
            jax.ShapeDtypeStruct((features, 3 * PAIR), BF16),
            jax.ShapeDtypeStruct((features, 3 * PAIR), BF16),
        ],
        compiler_params=params(),
        cost_estimate=cost(16),
        name="attend_back",
    )(limit, mixed, mixed, mixed, ctx_turn, lse, context_grad, n_turn)


def begin_kernel(
    limit_ref, x_ref, clock_ref, gain_ref, gg_two_ref, mg_ref, w_ref, high_ref, low_ref, bg_ref, gg_s
):
    step = pl.program_id(0)
    _, parts, tall, width = bg_ref.shape
    tokens = tall - SPARE
    blocks = ROWS // tokens
    spot = pl.ds(step * blocks, blocks)

    @pl.when(step == 0)
    def _():
        gg_s[...] = jnp.zeros_like(gg_s)

    @pl.when(step * ROWS < limit_ref[0])
    def _():
        begin = join_tokens(x_ref) + clock_ref[...]
        unit, inverse = norm_parts(begin)
        one_grad = jnp.zeros_like(begin)
        for part, (d_ref, at) in enumerate(((low_ref, 1), (low_ref, 0), (high_ref, 1), (high_ref, 0))):
            columns = slice(part * 3 * PAIR, (part + 1) * 3 * PAIR)
            own = slice(at * 3 * PAIR, (at + 1) * 3 * PAIR)
            one_grad += mul(d_ref[:, own], w_ref[:, columns], NT)
        gg_s[...] += jnp.sum(one_grad * unit, axis=0, keepdims=True)
        total = (mg_ref[...] + norm_back(one_grad, gain_ref[...], unit, inverse)).astype(BF16)
        for part in range(parts):
            piece = total[:, part * width : (part + 1) * width]
            bg_ref[spot, part, 0:tokens] = piece.reshape(blocks, tokens, width)

    @pl.when(step * ROWS >= limit_ref[0])
    def _():
        bg_ref[spot] = jnp.zeros((blocks,) + bg_ref.shape[1:], BF16)

    @pl.when(step == pl.num_programs(0) - 1)
    def _():
        rows = []
        for ref in (gg_s, gg_two_ref):
            for part in range(parts):
                rows.append(ref[:, part * width : (part + 1) * width])
        bg_ref[:, :, tokens:tall] = jnp.broadcast_to(
            jnp.concatenate(rows, axis=0).astype(BF16), bg_ref.shape[:2] + (SPARE, width)
        )


def begin_block(limit, x_blocks, clock, gain, two_grad, w_wide, middle_grad, high, low):
    senders, feature_parts, tall, width = x_blocks.shape
    tokens = tall - SPARE
    length = senders * tokens
    features = feature_parts * width
    take = ROWS // tokens
    whole = lambda array: pl.BlockSpec(array.shape, lambda i, s: (0,) * array.ndim)
    rows = lambda n: pl.BlockSpec((ROWS, n), lambda i, s: (i, 0))
    return pl.pallas_call(
        begin_kernel,
        grid_spec=pltpu.PrefetchScalarGridSpec(
            num_scalar_prefetch=1,
            grid=(length // ROWS,),
            in_specs=[
                pl.BlockSpec((take, feature_parts, tall, width), lambda i, s: (i, 0, 0, 0)),
                whole(clock), whole(gain), whole(two_grad), rows(features), whole(w_wide),
            ]
            + [rows(6 * PAIR)] * 2,
            out_specs=whole(x_blocks),
            scratch_shapes=[pltpu.VMEM((1, features), F32)],
        ),
        out_shape=jax.ShapeDtypeStruct(x_blocks.shape, BF16),
        compiler_params=params(),
        cost_estimate=cost(7),
        name="begin_back",
    )(limit, x_blocks, clock, gain, two_grad, middle_grad, w_wide, high, low)


DIRECT = 8


def clock_rows(step_ids, features):
    half_width = features // 2
    ladder = jnp.arange(half_width, dtype=F32) / half_width
    rate_rows = jnp.exp(-math.log(10000.0) * ladder)
    angles = step_ids.astype(F32)[:, None] * rate_rows[None, :]
    return jnp.concatenate([jnp.sin(angles), jnp.cos(angles)], axis=-1)


def swap(value, apart):
    count = lax.axis_size("tensor")
    return lax.ppermute(value, "tensor", [(i, i ^ apart) for i in range(count)])


def along_dp(value, move):
    count = lax.axis_size("dp")
    return lax.ppermute(value, "dp", [(i, move(i)) for i in range(count)])


def across(value):
    return along_dp(value, lambda i: i ^ 1)


def ahead(value, step):
    count = lax.axis_size("dp") // 2
    return along_dp(value, lambda i: (i // 2 + step) % count * 2 + i % 2)


def places():
    count = lax.axis_size("dp") // 2
    own = lax.axis_index("dp")
    coarse = (own // 2 - jnp.arange(count, dtype=jnp.int32)) % count
    return jnp.concatenate([coarse * 2 + own % 2, coarse * 2 + 1 - own % 2])


def collect_coarse(shard):
    count = lax.axis_size("dp") // 2
    return jnp.concatenate([shard] + [ahead(shard, step) for step in range(1, count)], axis=0)


def collect_rows(shard):
    count = lax.axis_size("dp")
    rows = lax.all_to_all(
        jnp.broadcast_to(shard[None], (count,) + shard.shape), "dp", 0, 0, tiled=True
    )
    return rows.reshape(count * shard.shape[0], shard.shape[1])


def collect_columns(rows):
    far = swap(rows, 2)
    return rows, swap(rows, 1), far, swap(far, 1)


def add(*values):
    total = values[0].astype(F32)
    for value in values[1:]:
        total += value.astype(F32)
    return total.astype(BF16)


def fold_pair(values):
    own = lax.axis_index("dp") % 2
    pick = lambda value, which: lax.dynamic_index_in_dim(value, which, value.ndim - 3, keepdims=False)
    sent = add(*[pick(value, 1 - own) for value in values])
    return sent, lambda: [pick(value, own) for value in values] + [across(sent)]


def fold_far(values):
    sent = add(*[value[0] for value in values])
    return sent, lambda: [value[1] for value in values] + [swap(sent, 2)]


def fold_coarse(values):
    count = lax.axis_size("dp") // 2
    own = lax.axis_index("dp") // 2
    pick = lambda value, which: lax.dynamic_index_in_dim(value, which % count, 0, keepdims=False)
    value = add(*values)
    came = [ahead(pick(value, own + step), step) for step in range(1, count)]

    def finish(*others):
        pieces = lax.optimization_barrier((*came, *others))[: count - 1]
        total = pick(value, own).astype(F32)
        for piece in pieces:
            total += piece.astype(F32)
        return total

    return value, finish


def grouped(value):
    count = lax.axis_size("dp")
    two, rows, columns = value.shape
    return value.reshape(two, count // 2, 2, rows // count, columns)


def exchange_rows(value):
    count = lax.axis_size("dp")
    groups = value.reshape(count, value.shape[0] // count, value.shape[1])
    return jnp.sum(lax.all_to_all(groups, "dp", 0, 0, tiled=True).astype(F32), axis=0)


def three_terms(values):
    terms = []
    for _ in range(3):
        term = lax.reduce_precision(values, 8, 7)
        terms.append(term.astype(BF16))
        values = values - term
    return terms


def together(*values):
    return lax.optimization_barrier(values)


def after(value, *others):
    return lax.optimization_barrier((value,) + others)[0]


def on_device(
    states, timesteps, lengths, deal_order, w_qkv, w_out, w_up, w_down, gain_attn, gain_ffn, out_grad
):
    both = ("dp", "tensor")
    dp_count = lax.axis_size("dp")
    tensor_count = lax.axis_size("tensor")
    devices = dp_count * tensor_count
    total_seqs, tokens, width = states.shape
    assert tensor_count == 4 and total_seqs == devices
    features = width * tensor_count
    own = lax.axis_index("dp") * tensor_count + lax.axis_index("tensor")
    own_id = lax.dynamic_slice_in_dim(deal_order, own, 1)
    limit = lengths[own_id]
    clock = clock_rows(timesteps[own_id], features)
    per = gain_attn.shape[0]
    rows = w_qkv.shape[0]
    hidden = w_up.shape[1]

    rest = jnp.concatenate([w_out.T, w_up, w_down.T], axis=1)
    qkv = w_qkv.reshape(rows, -1)
    direct = dp_count <= DIRECT
    if direct:
        place, groups = places(), dp_count
        first = collect_coarse(jnp.concatenate([qkv, rest], axis=1))
        qkv_rows = first[:, : qkv.shape[1]]
        qkv_parts = collect_columns(jnp.concatenate([qkv_rows, across(qkv_rows)], axis=0))
        mine = after(first[:, qkv.shape[1] :], qkv_parts[2])
        other, far_mine = across(mine), swap(mine, 2)
    else:
        place, groups = jnp.zeros((1,), jnp.int32), None
        first = collect_rows(qkv)
        qkv_parts = collect_columns(first)
        rest_parts = [(part,) for part in collect_columns(collect_rows(rest))]

    spare = jnp.stack(three_terms(gain_attn) + three_terms(gain_ffn)).reshape(1, 6 * per)
    spare = jnp.pad(spare, ((0, SPARE - 1), (0, width - 6 * per)))
    by_tensor = deal_order.reshape(dp_count, tensor_count).T.reshape(devices)
    arranged = jnp.concatenate(
        [states[by_tensor], jnp.broadcast_to(spare[None], (devices, SPARE, width))], axis=1
    )
    arranged = lax.all_to_all(arranged, "tensor", 0, 0, tiled=True)
    arranged = arranged.reshape(tensor_count, dp_count, tokens + SPARE, width).swapaxes(0, 1)
    x_blocks = lax.all_to_all(after(arranged, first), "dp", 0, 0, tiled=True)
    x_blocks = x_blocks.reshape(devices, tokens + SPARE, width)
    gains = jnp.sum(x_blocks[:, tokens, : 6 * per].reshape(devices, 2, 3, per).astype(F32), axis=2)
    gain_one = gains[:, 0].reshape(1, features)
    gain_two = gains[:, 1].reshape(1, features)
    x_blocks = x_blocks.reshape(dp_count, tensor_count, tokens + SPARE, width)

    mixed, n_one_turn, qkv_wide = project(
        limit, place, groups, x_blocks, clock, gain_one, qkv_parts
    )
    if direct:
        mixed, other, far_mine = together(mixed, other, far_mine)
        near_mine, near_other = swap(after(mine, mixed), 1), swap(other, 1)
        last_mine, far_other = swap(far_mine, 1), swap(other, 2)
    ctx, ctx_turn, lse = attend(limit, mixed, tensor_count)
    if direct:
        ctx, near_mine, near_other, last_mine, far_other = together(
            ctx, near_mine, near_other, last_mine, far_other
        )
        last_other = swap(far_other, 1)
        rest_parts = (
            (mine, other), (near_mine, near_other), (far_mine, far_other), (last_mine, last_other)
        )
    output, context_grad, middle_grad, two_grad, up_send, down_send, up_keep, down_keep = middle_block(
        limit, place, groups, x_blocks, clock, gain_two, ctx, rest_parts, out_grad
    )
    up_came, down_came = swap(up_send, 1), swap(down_send, 1)

    back = functools.partial(attend_back, limit, mixed, ctx_turn, lse)
    if direct:
        down_sent, down_rest = fold_pair([grouped(value) for value in (down_keep, down_came)])
        up_sent, up_rest = fold_far([grouped(value) for value in (up_keep, up_came)])
        context_grad = after(context_grad, down_sent, up_sent)
    high, three, two = back(context_grad, n_one_turn, 3)
    if direct:
        *down_rest, down_came = down_rest()
        *up_rest, up_came = up_rest()
        high, three, two, down_came, up_came = together(high, three, two, down_came, up_came)
        down_sent, down_rest = fold_far([add(*down_rest, down_came)])
        up_sent, up_rest = fold_pair([add(*up_rest, up_came)])
        context_grad = after(context_grad, down_sent, up_sent)
    far = add(two, swap(three, 1))
    came_far = swap(far, 2)
    low, one, own_part = back(after(context_grad, high, far), n_one_turn, 1)
    if direct:
        *down_rest, down_came = down_rest()
        *up_rest, up_came = up_rest()
        low, one, own_part, down_came, up_came, came_far = together(
            low, one, own_part, down_came, up_came, came_far
        )
        down_value, down_finish = fold_coarse([*down_rest, down_came])
        up_value, up_finish = fold_coarse([*up_rest, up_came])
        middle_grad = after(middle_grad, down_value, up_value)
    came_one = swap(one, 1)
    begin_grad = begin_block(
        limit, x_blocks, clock, gain_one, two_grad, qkv_wide, middle_grad, high, low
    )
    if direct:
        begin_grad, came_one = together(begin_grad, came_one)
        near = [grouped(value[None])[0] for value in (own_part, came_one, came_far)]
        qkv_value, qkv_finish = fold_coarse(fold_pair(near)[1]())
        down_total, up_total, qkv_total = down_finish(qkv_value), up_finish(qkv_value), qkv_finish()
    else:
        up_total = exchange_rows(add(*fold_far([up_keep, up_came])[1]()))
        down_total = exchange_rows(add(*fold_far([down_keep, down_came])[1]()))
        qkv_total = exchange_rows(add(own_part, came_one, came_far))
    returned = lax.all_to_all(
        begin_grad.reshape(devices, tokens + SPARE, width), both, 0, 0, tiled=True
    )
    inverse = (
        jnp.zeros((total_seqs,), jnp.int32)
        .at[deal_order]
        .set(jnp.arange(total_seqs, dtype=jnp.int32))
    )
    states_grad = returned[:, :tokens][inverse]
    gain_grads = jnp.sum(returned[:, tokens:].astype(F32), axis=0).reshape(2, devices, per)
    gain_grads = lax.dynamic_index_in_dim(gain_grads, own, 1, keepdims=False)
    return (
        output,
        states_grad,
        qkv_total.reshape(w_qkv.shape),
        up_total[:, :PAIR].T,
        up_total[:, PAIR:],
        down_total.T,
        gain_grads[0],
        gain_grads[1],
    )


def solution(mesh):
    in_specs = (
        P(None, "dp", "tensor"),
        P(),
        P(),
        P(),
        P("dp", None, "tensor"),
        P("tensor", "dp"),
        P("dp", "tensor"),
        P("tensor", "dp"),
        P(("dp", "tensor")),
        P(("dp", "tensor")),
        P(("dp", "tensor"), None, None),
    )
    out_specs = (
        P(("dp", "tensor"), None, None),
        P(None, "dp", "tensor"),
        P("dp", None, "tensor"),
        P("tensor", "dp"),
        P("dp", "tensor"),
        P("tensor", "dp"),
        P(("dp", "tensor")),
        P(("dp", "tensor")),
    )
    return jax.shard_map(
        on_device, mesh=mesh, in_specs=in_specs, out_specs=out_specs, check_vma=False
    )
```

```python
import functools
import math

import jax
import jax.numpy as jnp
from jax import lax
from jax.experimental import pallas as pl
from jax.experimental.pallas import tpu as pltpu
from jax.sharding import PartitionSpec as P

HEAD_DIM = 64
PAIR = 2 * HEAD_DIM
ROWS = 512
KEYS = 256
BACK_KEYS = 512
SPARE = 8
SCORE_SCALE = 1.0 / math.sqrt(HEAD_DIM)
LOG2E = math.log2(math.e)
F32 = jnp.float32
BF16 = jnp.bfloat16
NN = (((1,), (0,)), ((), ()))
NT = (((1,), (1,)), ((), ()))
MIB = 1024 * 1024


def mul(lhs, rhs, dims=NN):
    return lax.dot_general(lhs, rhs, dims, preferred_element_type=F32)


def join_tokens(ref):
    blocks, parts, tall, width = ref.shape
    tokens = tall - SPARE
    return jnp.concatenate(
        [ref[:, part, 0:tokens].reshape(blocks * tokens, width) for part in range(parts)], axis=-1
    ).astype(F32)


def place_rows(groups, place_ref, first, source, targets):
    if groups is None:
        for target, columns, own in targets:
            target[:, columns] = source[:, own]
        return
    rows = source.shape[0] // groups
    for group in range(groups):
        spot = pl.ds(pl.multiple_of(place_ref[first + group] * rows, rows), rows)
        for target, columns, own in targets:
            target[spot, columns] = source[group * rows : (group + 1) * rows, own]


def norm_parts(values):
    center = values - jnp.mean(values, axis=-1, keepdims=True)
    spread = jnp.mean(center * center, axis=-1, keepdims=True)
    inverse = lax.rsqrt(spread + 1e-05)
    return center * inverse, inverse


def norm_back(grad, gain, unit, inverse):
    scaled = grad * gain
    mean_scaled = jnp.mean(scaled, axis=-1, keepdims=True)
    mean_along = jnp.mean(scaled * unit, axis=-1, keepdims=True)
    return inverse * (scaled - mean_scaled - unit * mean_along)


def cost(microseconds):
    return pl.CostEstimate(
        flops=int(microseconds * 1.15e9), bytes_accessed=1 << 20, transcendentals=0
    )


def params(mebibytes):
    return pltpu.CompilerParams(vmem_limit_bytes=mebibytes * MIB)


def project_kernel(groups, limit_ref, place_ref, x_ref, clock_ref, gain_ref, *refs):
    w_refs, (mixed_ref, n_turn_ref, wide) = refs[:-3], refs[-3:]
    step = pl.program_id(0)

    @pl.when(step == 0)
    def _():
        for part, w_ref in enumerate(w_refs):
            width = w_ref.shape[1]
            columns = slice(part * width, (part + 1) * width)
            place_rows(groups, place_ref, 0, w_ref, [(wide, columns, slice(0, width))])

    @pl.when(step * ROWS < limit_ref[0])
    def _():
        begin = join_tokens(x_ref) + clock_ref[...]
        unit, _ = norm_parts(begin)
        normed = (unit * gain_ref[...]).astype(BF16)
        n_turn_ref[...] = normed.T
        mixed_ref[...] = mul(normed, wide[...]).astype(BF16)

    @pl.when(step * ROWS >= limit_ref[0])
    def _():
        n_turn_ref[...] = jnp.zeros_like(n_turn_ref)
        mixed_ref[...] = jnp.zeros_like(mixed_ref)


def project(limit, place, groups, x_blocks, clock, gain, w_parts):
    senders, feature_parts, tall, width = x_blocks.shape
    tokens = tall - SPARE
    length = senders * tokens
    features = feature_parts * width
    parts, columns = len(w_parts), w_parts[0].shape[1]
    take = ROWS // tokens
    return pl.pallas_call(
        functools.partial(project_kernel, groups),
        grid_spec=pltpu.PrefetchScalarGridSpec(
            num_scalar_prefetch=2,
            grid=(length // ROWS,),
            in_specs=[
                pl.BlockSpec((take, feature_parts, tall, width), lambda i, *s: (i, 0, 0, 0)),
                pl.BlockSpec((1, features), lambda i, *s: (0, 0)),
                pl.BlockSpec((1, features), lambda i, *s: (0, 0)),
            ]
            + [pl.BlockSpec((features, columns), lambda i, *s: (0, 0))] * parts,
            out_specs=[
                pl.BlockSpec((ROWS, parts * columns), lambda i, *s: (i, 0)),
                pl.BlockSpec((features, ROWS), lambda i, *s: (0, i)),
                pl.BlockSpec((features, parts * columns), lambda i, *s: (0, 0)),
            ],
        ),
        out_shape=[
            jax.ShapeDtypeStruct((length, parts * columns), BF16),
            jax.ShapeDtypeStruct((features, length), BF16),
            jax.ShapeDtypeStruct((features, parts * columns), BF16),
        ],
        compiler_params=params(20),
        cost_estimate=cost(5),
        name="project",
    )(limit, place, x_blocks, clock, gain, *w_parts)


def head_lanes(shape, head):
    lane = lax.broadcasted_iota(jnp.int32, shape, 1)
    return (lane >= head * HEAD_DIM) & (lane < (head + 1) * HEAD_DIM)


def spare_lane(shape, head):
    lane = lax.broadcasted_iota(jnp.int32, shape, 1)
    return lane == (1 - head) * HEAD_DIM


def masked_keys(keys, head, limit):
    row = lax.broadcasted_iota(jnp.int32, keys.shape, 0)
    spare = jnp.where(
        spare_lane(keys.shape, head) & (row >= limit), jnp.asarray(-1e30, F32), jnp.asarray(0.0, F32)
    )
    return jnp.where(head_lanes(keys.shape, head), keys.astype(F32), spare).astype(BF16)


def own_lanes(values, head):
    return jnp.where(head_lanes(values.shape, head), values.astype(F32), 0.0).astype(BF16)


def masked_queries(queries, head):
    spare = jnp.where(spare_lane(queries.shape, head), jnp.asarray(1.0, F32), jnp.asarray(0.0, F32))
    return jnp.where(head_lanes(queries.shape, head), queries.astype(F32), spare).astype(BF16)


def attend_kernel(limit_ref, q_ref, k_ref, v_ref, ctx_ref, turn_ref, lse_ref, keys_s, q_s, vt_s, sc_s):
    length = q_ref.shape[0]
    vt_s[...] = v_ref[...].astype(F32).T.astype(BF16)
    for head in range(2):
        keys_s[head] = masked_keys(k_ref[...], head, limit_ref[0])
        q_s[head] = masked_queries(q_ref[...], head)
    factor = SCORE_SCALE * LOG2E
    spans = [slice(at, at + KEYS) for at in range(0, length, KEYS)]
    outs = []
    for head in range(2):
        feats = slice(head * HEAD_DIM, (head + 1) * HEAD_DIM)
        peak = None
        for span in spans:
            scores = mul(keys_s[head, span], q_s[head], NT)
            sc_s[head, span] = scores
            high = jnp.max(scores, axis=0, keepdims=True)
            peak = high if peak is None else jnp.maximum(peak, high)
        peak = peak * factor
        total = jnp.zeros_like(peak)
        gathered = jnp.zeros((HEAD_DIM, length), F32)
        for span in spans:
            expo = jnp.exp2(sc_s[head, span] * factor - peak)
            total += jnp.sum(expo, axis=0, keepdims=True)
            gathered += mul(vt_s[feats, span], expo.astype(BF16))
        outs.append(gathered / total)
        lse_ref[0, head : head + 1, :] = peak + jnp.log2(total)
    both = jnp.concatenate(outs, axis=0)
    turn_ref[...] = both.astype(BF16)
    ctx_ref[...] = both.T.astype(BF16)


def attend(limit, mixed, pairs):
    length = mixed.shape[0]
    column = lambda c: pl.BlockSpec((length, PAIR), lambda i, s: (0, i * 3 + c))
    return pl.pallas_call(
        attend_kernel,
        grid_spec=pltpu.PrefetchScalarGridSpec(
            num_scalar_prefetch=1,
            grid=(pairs,),
            in_specs=[column(0), column(1), column(2)],
            out_specs=[
                pl.BlockSpec((length, PAIR), lambda i, s: (0, i)),
                pl.BlockSpec((PAIR, length), lambda i, s: (i, 0)),
                pl.BlockSpec((1, 2, length), lambda i, s: (i, 0, 0)),
            ],
            scratch_shapes=[
                pltpu.VMEM((2, length, PAIR), BF16),
                pltpu.VMEM((2, length, PAIR), BF16),
                pltpu.VMEM((PAIR, length), BF16),
                pltpu.VMEM((2, length, length), F32),
            ],
        ),
        out_shape=[
            jax.ShapeDtypeStruct((length, pairs * PAIR), BF16),
            jax.ShapeDtypeStruct((pairs * PAIR, length), BF16),
            jax.ShapeDtypeStruct((pairs, 2, length), F32),
        ],
        compiler_params=params(28),
        cost_estimate=cost(15),
        name="attend",
    )(limit, mixed, mixed, mixed)


def gelu_both(values):
    root = math.sqrt(2.0 / math.pi)
    scaled = root * values
    inner = scaled * (1.0 + 0.044715 * (values * values))
    tanh = jnp.tanh(inner)
    half = 0.5 + 0.5 * tanh
    slope = half + (1.0 - tanh * tanh) * (1.5 * inner - scaled)
    return values * half, slope


def middle_kernel(
    groups, limit_ref, place_ref, x_ref, clock_ref, gain_ref, ctx_ref, og_ref, *refs
):
    weight_refs, refs = refs[:-16], refs[-16:]
    out_ref, cg_ref, mg_ref, gg_ref, up_send, down_send, up_keep, down_keep = refs[:8]
    wide, units, active_s, ug_s, n_turn, fg_turn, ag_turn, ctx_s = refs[8:]
    step = pl.program_id(0)
    parts, _, hidden = active_s.shape
    blocks = pl.num_programs(0) - parts

    @pl.when(step == 0)
    def _():
        gg_ref[...] = jnp.zeros_like(gg_ref)
        each = len(weight_refs) // parts
        for part in range(parts):
            thin = slice(part * PAIR, (part + 1) * PAIR)
            thick = slice(part * 2 * hidden, (part + 1) * 2 * hidden)
            for at, w_ref in enumerate(weight_refs[part * each : (part + 1) * each]):
                targets = [
                    (wide, thin, slice(0, PAIR)), (units, thick, slice(PAIR, PAIR + 2 * hidden))
                ]
                count = None if groups is None else groups // each
                place_rows(count, place_ref, at * (count or 0), w_ref, targets)

    dead = (step < blocks) & (step * ROWS >= limit_ref[0])

    @pl.when((step < blocks) & jnp.logical_not(dead))
    def _():
        spot = pl.ds(pl.multiple_of(step * ROWS, ROWS), ROWS)
        gain = gain_ref[...]
        live = step * ROWS + lax.broadcasted_iota(jnp.int32, (ROWS, 1), 0) < limit_ref[0]
        begin = join_tokens(x_ref) + clock_ref[...]
        middle = begin + mul(ctx_ref[...], wide[...], NT)
        unit, inverse = norm_parts(middle)
        normed = (unit * gain).astype(BF16)
        n_turn[:, spot] = normed.T
        res_grad = jnp.where(live, og_ref[0].astype(F32), 0.0)
        feed_grad = res_grad.astype(BF16)
        fg_turn[:, spot] = feed_grad.T
        feed = jnp.zeros_like(middle)
        two_grad = jnp.zeros_like(middle)
        for part in range(parts):
            up = slice(2 * part * hidden, (2 * part + 1) * hidden)
            down = slice((2 * part + 1) * hidden, (2 * part + 2) * hidden)
            upper = mul(normed, units[:, up])
            active, slope = gelu_both(upper)
            active = active.astype(BF16)
            active_s[part, spot] = active
            feed += mul(active, units[:, down], NT)
            upper_grad = (mul(feed_grad, units[:, down]) * slope).astype(BF16)
            ug_s[part, spot] = upper_grad
            two_grad += mul(upper_grad, units[:, up], NT)
        out_ref[0] = jnp.where(live, middle + feed, 0.0).astype(BF16)
        gg_ref[...] += jnp.sum(two_grad * unit, axis=0, keepdims=True)
        middle_grad = res_grad + norm_back(two_grad, gain, unit, inverse)
        mg_ref[...] = middle_grad
        att_grad = middle_grad.astype(BF16)
        ag_turn[:, spot] = att_grad.T
        cg_ref[...] = mul(att_grad, wide[...]).astype(BF16)
        for part in range(parts):
            ctx_s[part, spot] = ctx_ref[:, part * PAIR : (part + 1) * PAIR]

    @pl.when(dead)
    def _():
        spot = pl.ds(pl.multiple_of(step * ROWS, ROWS), ROWS)
        for ref in (out_ref, cg_ref, mg_ref):
            ref[...] = jnp.zeros_like(ref)
        for ref in (active_s, ug_s, ctx_s):
            ref[:, spot] = jnp.zeros((ref.shape[0], ROWS, ref.shape[2]), BF16)
        for ref in (n_turn, fg_turn, ag_turn):
            ref[:, spot] = jnp.zeros((ref.shape[0], ROWS), BF16)

    @pl.when(step >= blocks)
    def _():
        turn = step - blocks
        part = jnp.where(turn < 2, 3 - 2 * turn, 6 - 2 * turn)
        grads = (
            mul(ag_turn[...], ctx_s[part]).astype(BF16),
            mul(n_turn[...], ug_s[part]).astype(BF16),
            mul(fg_turn[...], active_s[part]).astype(BF16),
        )

        def into(up_ref, down_ref):
            up_ref[0, :, 0:PAIR], up_ref[0, :, PAIR:], down_ref[0] = grads

        pl.when(turn < 2)(lambda: into(up_send, down_send))
        pl.when(turn >= 2)(lambda: into(up_keep, down_keep))


def middle_block(limit, place, groups, x_blocks, clock, gain, ctx, w_parts, out_grad):
    senders, feature_parts, tall, width = x_blocks.shape
    tokens = tall - SPARE
    length = senders * tokens
    features = feature_parts * width
    parts = len(w_parts)
    weights = [w for part in w_parts for w in part]
    columns = weights[0].shape[1]
    hidden = (columns - PAIR) // 2
    take = ROWS // tokens
    blocks = length // ROWS
    row = lambda i: jnp.minimum(i, blocks - 1)
    whole = lambda array: pl.BlockSpec(
        array.shape, lambda i, *s: (0,) * array.ndim, pipeline_mode=pl.Buffered(1)
    )
    rows = lambda n: pl.BlockSpec((ROWS, n), lambda i, *s: (row(i), 0))
    one = pl.BlockSpec((1, ROWS, features), lambda i, *s: (0, row(i), 0))
    grads = lambda first, n: pl.BlockSpec(
        (1, features, n), lambda i, *s: (jnp.clip(i - blocks - first, 0, 1), 0, 0)
    )
    up_shape = jax.ShapeDtypeStruct((2, features, PAIR + hidden), BF16)
    down_shape = jax.ShapeDtypeStruct((2, features, hidden), BF16)
    return pl.pallas_call(
        functools.partial(middle_kernel, groups),
        grid_spec=pltpu.PrefetchScalarGridSpec(
            num_scalar_prefetch=2,
            grid=(blocks + parts,),
            in_specs=[
                pl.BlockSpec(
                    (take, feature_parts, tall, width), lambda i, *s: (row(i), 0, 0, 0)
                ),
                whole(clock),
                whole(gain),
                rows(features),
                one,
            ]
            + [whole(w) for w in weights],
            out_specs=[
                one, rows(features), rows(features),
                pl.BlockSpec((1, features), lambda i, *s: (0, 0)),
                grads(0, PAIR + hidden), grads(0, hidden), grads(2, PAIR + hidden), grads(2, hidden),
            ],
            scratch_shapes=[
                pltpu.VMEM((features, parts * PAIR), BF16),
                pltpu.VMEM((features, parts * 2 * hidden), BF16),
                pltpu.VMEM((parts, length, hidden), BF16),
                pltpu.VMEM((parts, length, hidden), BF16),
                pltpu.VMEM((features, length), BF16),
                pltpu.VMEM((features, length), BF16),
                pltpu.VMEM((features, length), BF16),
                pltpu.VMEM((parts, length, PAIR), BF16),
            ],
        ),
        out_shape=[
            jax.ShapeDtypeStruct((1, length, features), BF16),
            jax.ShapeDtypeStruct((length, features), BF16),
            jax.ShapeDtypeStruct((length, features), F32),
            jax.ShapeDtypeStruct((1, features), F32),
            up_shape, down_shape, up_shape, down_shape,
        ],
        compiler_params=params(40),
        cost_estimate=cost(25),
        name="middle",
    )(limit, place, x_blocks, clock, gain, ctx, out_grad, *weights)


def attend_back_kernel(
    limit_ref, q_ref, k_ref, v_ref, turn_ref, lse_ref, cg_ref, n_turn_ref,
    dm_ref, first_ref, second_ref, keys_s, q_s, qz_s, do_s, kt_s, delta_s,
):
    limit = limit_ref[0]
    length = q_ref.shape[0]
    kt_s[...] = k_ref[...].astype(F32).T.astype(BF16)
    along = cg_ref[...].astype(F32).T * turn_ref[...].astype(F32)
    for head in range(2):
        feats = slice(head * HEAD_DIM, (head + 1) * HEAD_DIM)
        delta_s[head : head + 1, :] = jnp.sum(along[feats, :], axis=0, keepdims=True)
        keys_s[head] = masked_keys(k_ref[...], head, limit)
        q_s[head] = masked_queries(q_ref[...], head)
        qz_s[head] = own_lanes(q_ref[...], head)
        do_s[head] = own_lanes(cg_ref[...], head)
    factor = SCORE_SCALE * LOG2E
    turned = [jnp.zeros((HEAD_DIM, length), F32)] * 2
    for at in range(0, length, BACK_KEYS):
        span = slice(at, at + BACK_KEYS)
        key_grad = jnp.zeros((BACK_KEYS, PAIR), F32)
        value_grad = jnp.zeros((BACK_KEYS, PAIR), F32)
        for head in range(2):
            feats = slice(head * HEAD_DIM, (head + 1) * HEAD_DIM)
            scores = mul(keys_s[head, span], q_s[head], NT)
            prob = jnp.exp2(scores * factor - lse_ref[0, head : head + 1, :])
            prob_grad = mul(v_ref[span, :], do_s[head], NT)
            score_grad = (prob * (prob_grad - delta_s[head : head + 1, :])).astype(BF16)
            value_grad += mul(prob.astype(BF16), do_s[head])
            key_grad += mul(score_grad, qz_s[head])
            turned[head] += mul(kt_s[feats, span], score_grad)
        dm_ref[span, PAIR : 2 * PAIR] = (key_grad * SCORE_SCALE).astype(BF16)
        dm_ref[span, 2 * PAIR : 3 * PAIR] = value_grad.astype(BF16)
    query_grad = jnp.concatenate(turned, axis=0) * SCORE_SCALE
    dm_ref[:, 0:PAIR] = query_grad.T.astype(BF16)
    grad = mul(n_turn_ref[...], dm_ref[...]).astype(BF16)

    @pl.when(pl.program_id(0) == 0)
    def _():
        first_ref[...] = grad

    @pl.when(pl.program_id(0) == 1)
    def _():
        second_ref[...] = grad


def attend_back(limit, mixed, ctx_turn, lse, context_grad, n_turn, first):
    length = mixed.shape[0]
    features = n_turn.shape[0]
    pair = lambda i: first - i
    column = lambda c: pl.BlockSpec((length, PAIR), lambda i, s: (0, pair(i) * 3 + c))
    return pl.pallas_call(
        attend_back_kernel,
        grid_spec=pltpu.PrefetchScalarGridSpec(
            num_scalar_prefetch=1,
            grid=(2,),
            in_specs=[
                column(0), column(1), column(2),
                pl.BlockSpec((PAIR, length), lambda i, s: (pair(i), 0)),
                pl.BlockSpec((1, 2, length), lambda i, s: (pair(i), 0, 0)),
                pl.BlockSpec((length, PAIR), lambda i, s: (0, pair(i))),
                pl.BlockSpec((features, length), lambda i, s: (0, 0)),
            ],
            out_specs=[
                pl.BlockSpec((length, 3 * PAIR), lambda i, s: (0, i)),
                pl.BlockSpec((features, 3 * PAIR), lambda i, s: (0, 0)),
                pl.BlockSpec((features, 3 * PAIR), lambda i, s: (0, 0)),
            ],
            scratch_shapes=[
                pltpu.VMEM((2, length, PAIR), BF16),
                pltpu.VMEM((2, length, PAIR), BF16),
                pltpu.VMEM((2, length, PAIR), BF16),
                pltpu.VMEM((2, length, PAIR), BF16),
                pltpu.VMEM((PAIR, length), BF16),
                pltpu.VMEM((8, length), F32),
            ],
        ),
        out_shape=[
            jax.ShapeDtypeStruct((length, 2 * 3 * PAIR), BF16),
            jax.ShapeDtypeStruct((features, 3 * PAIR), BF16),
            jax.ShapeDtypeStruct((features, 3 * PAIR), BF16),
        ],
        compiler_params=params(28),
        cost_estimate=cost(16),
        name="attend_back",
    )(limit, mixed, mixed, mixed, ctx_turn, lse, context_grad, n_turn)


def begin_kernel(
    limit_ref, x_ref, clock_ref, gain_ref, gg_two_ref, mg_ref, w_ref, high_ref, low_ref, bg_ref, gg_s
):
    step = pl.program_id(0)
    _, parts, tall, width = bg_ref.shape
    tokens = tall - SPARE
    blocks = ROWS // tokens
    spot = pl.ds(step * blocks, blocks)

    @pl.when(step == 0)
    def _():
        gg_s[...] = jnp.zeros_like(gg_s)

    @pl.when(step * ROWS < limit_ref[0])
    def _():
        begin = join_tokens(x_ref) + clock_ref[...]
        unit, inverse = norm_parts(begin)
        one_grad = jnp.zeros_like(begin)
        for part, (d_ref, at) in enumerate(((low_ref, 1), (low_ref, 0), (high_ref, 1), (high_ref, 0))):
            columns = slice(part * 3 * PAIR, (part + 1) * 3 * PAIR)
            own = slice(at * 3 * PAIR, (at + 1) * 3 * PAIR)
            one_grad += mul(d_ref[:, own], w_ref[:, columns], NT)
        gg_s[...] += jnp.sum(one_grad * unit, axis=0, keepdims=True)
        total = (mg_ref[...] + norm_back(one_grad, gain_ref[...], unit, inverse)).astype(BF16)
        for part in range(parts):
            piece = total[:, part * width : (part + 1) * width]
            bg_ref[spot, part, 0:tokens] = piece.reshape(blocks, tokens, width)

    @pl.when(step * ROWS >= limit_ref[0])
    def _():
        bg_ref[spot] = jnp.zeros((blocks,) + bg_ref.shape[1:], BF16)

    @pl.when(step == pl.num_programs(0) - 1)
    def _():
        rows = []
        for ref in (gg_s, gg_two_ref):
            for part in range(parts):
                rows.append(ref[:, part * width : (part + 1) * width])
        bg_ref[:, :, tokens:tall] = jnp.broadcast_to(
            jnp.concatenate(rows, axis=0).astype(BF16), bg_ref.shape[:2] + (SPARE, width)
        )


def begin_block(limit, x_blocks, clock, gain, two_grad, w_wide, middle_grad, high, low):
    senders, feature_parts, tall, width = x_blocks.shape
    tokens = tall - SPARE
    length = senders * tokens
    features = feature_parts * width
    take = ROWS // tokens
    whole = lambda array: pl.BlockSpec(array.shape, lambda i, s: (0,) * array.ndim)
    rows = lambda n: pl.BlockSpec((ROWS, n), lambda i, s: (i, 0))
    return pl.pallas_call(
        begin_kernel,
        grid_spec=pltpu.PrefetchScalarGridSpec(
            num_scalar_prefetch=1,
            grid=(length // ROWS,),
            in_specs=[
                pl.BlockSpec((take, feature_parts, tall, width), lambda i, s: (i, 0, 0, 0)),
                whole(clock), whole(gain), whole(two_grad), rows(features), whole(w_wide),
            ]
            + [rows(6 * PAIR)] * 2,
            out_specs=whole(x_blocks),
            scratch_shapes=[pltpu.VMEM((1, features), F32)],
        ),
        out_shape=jax.ShapeDtypeStruct(x_blocks.shape, BF16),
        compiler_params=params(20),
        cost_estimate=cost(7),
        name="begin_back",
    )(limit, x_blocks, clock, gain, two_grad, middle_grad, w_wide, high, low)


DIRECT = 8


def clock_rows(step_ids, features):
    half_width = features // 2
    ladder = jnp.arange(half_width, dtype=F32) / half_width
    rate_rows = jnp.exp(-math.log(10000.0) * ladder)
    angles = step_ids.astype(F32)[:, None] * rate_rows[None, :]
    return jnp.concatenate([jnp.sin(angles), jnp.cos(angles)], axis=-1)


def swap(value, apart):
    count = lax.axis_size("tensor")
    return lax.ppermute(value, "tensor", [(i, i ^ apart) for i in range(count)])


def along_dp(value, move):
    count = lax.axis_size("dp")
    return lax.ppermute(value, "dp", [(i, move(i)) for i in range(count)])


def across(value):
    return along_dp(value, lambda i: i ^ 1)


def ahead(value, step):
    count = lax.axis_size("dp") // 2
    return along_dp(value, lambda i: (i // 2 + step) % count * 2 + i % 2)


def places():
    count = lax.axis_size("dp") // 2
    own = lax.axis_index("dp")
    coarse = (own // 2 - jnp.arange(count, dtype=jnp.int32)) % count
    return jnp.concatenate([coarse * 2 + own % 2, coarse * 2 + 1 - own % 2])


def collect_coarse(shard):
    count = lax.axis_size("dp") // 2
    return jnp.concatenate([shard] + [ahead(shard, step) for step in range(1, count)], axis=0)


def collect_rows(shard):
    count = lax.axis_size("dp")
    rows = lax.all_to_all(
        jnp.broadcast_to(shard[None], (count,) + shard.shape), "dp", 0, 0, tiled=True
    )
    return rows.reshape(count * shard.shape[0], shard.shape[1])


def collect_columns(rows):
    far = swap(rows, 2)
    return rows, swap(rows, 1), far, swap(far, 1)


def add(*values):
    total = values[0].astype(F32)
    for value in values[1:]:
        total += value.astype(F32)
    return total.astype(BF16)


def fold_pair(values):
    own = lax.axis_index("dp") % 2
    pick = lambda value, which: lax.dynamic_index_in_dim(value, which, value.ndim - 3, keepdims=False)
    sent = add(*[pick(value, 1 - own) for value in values])
    return sent, lambda: [pick(value, own) for value in values] + [across(sent)]


def fold_far(values):
    sent = add(*[value[0] for value in values])
    return sent, lambda: [value[1] for value in values] + [swap(sent, 2)]


def fold_coarse(values):
    count = lax.axis_size("dp") // 2
    own = lax.axis_index("dp") // 2
    pick = lambda value, which: lax.dynamic_index_in_dim(value, which % count, 0, keepdims=False)
    value = add(*values)
    came = [ahead(pick(value, own + step), step) for step in range(1, count)]

    def finish(*others):
        pieces = lax.optimization_barrier((*came, *others))[: count - 1]
        total = pick(value, own).astype(F32)
        for piece in pieces:
            total += piece.astype(F32)
        return total

    return value, finish


def grouped(value):
    count = lax.axis_size("dp")
    two, rows, columns = value.shape
    return value.reshape(two, count // 2, 2, rows // count, columns)


def exchange_rows(value):
    count = lax.axis_size("dp")
    groups = value.reshape(count, value.shape[0] // count, value.shape[1])
    return jnp.sum(lax.all_to_all(groups, "dp", 0, 0, tiled=True).astype(F32), axis=0)


def three_terms(values):
    terms = []
    for _ in range(3):
        term = lax.reduce_precision(values, 8, 7)
        terms.append(term.astype(BF16))
        values = values - term
    return terms


def together(*values):
    return lax.optimization_barrier(values)


def after(value, *others):
    return lax.optimization_barrier((value,) + others)[0]


def on_device(
    states, timesteps, lengths, deal_order, w_qkv, w_out, w_up, w_down, gain_attn, gain_ffn, out_grad
):
    both = ("dp", "tensor")
    dp_count = lax.axis_size("dp")
    tensor_count = lax.axis_size("tensor")
    devices = dp_count * tensor_count
    total_seqs, tokens, width = states.shape
    assert tensor_count == 4 and total_seqs == devices
    features = width * tensor_count
    own = lax.axis_index("dp") * tensor_count + lax.axis_index("tensor")
    own_id = lax.dynamic_slice_in_dim(deal_order, own, 1)
    limit = lengths[own_id]
    clock = clock_rows(timesteps[own_id], features)
    per = gain_attn.shape[0]
    rows = w_qkv.shape[0]
    hidden = w_up.shape[1]

    rest = jnp.concatenate([w_out.T, w_up, w_down.T], axis=1)
    qkv = w_qkv.reshape(rows, -1)
    direct = dp_count <= DIRECT
    if direct:
        place, groups = places(), dp_count
        first = collect_coarse(jnp.concatenate([qkv, rest], axis=1))
        qkv_rows = first[:, : qkv.shape[1]]
        qkv_other = across(qkv_rows)
        qkv_parts = collect_columns(jnp.concatenate([qkv_rows, qkv_other], axis=0))
        mine = after(first[:, qkv.shape[1] :], qkv_other)
        other, far_mine = across(mine), swap(after(mine, qkv_parts[2]), 2)
    else:
        place, groups = jnp.zeros((1,), jnp.int32), None
        first = collect_rows(qkv)
        qkv_parts = collect_columns(first)
        rest_parts = [(part,) for part in collect_columns(collect_rows(rest))]

    spare = jnp.stack(three_terms(gain_attn) + three_terms(gain_ffn)).reshape(1, 6 * per)
    spare = jnp.pad(spare, ((0, SPARE - 1), (0, width - 6 * per)))
    by_tensor = deal_order.reshape(dp_count, tensor_count).T.reshape(devices)
    arranged = jnp.concatenate(
        [states[by_tensor], jnp.broadcast_to(spare[None], (devices, SPARE, width))], axis=1
    )
    arranged = lax.all_to_all(arranged, "tensor", 0, 0, tiled=True)
    arranged = arranged.reshape(tensor_count, dp_count, tokens + SPARE, width).swapaxes(0, 1)
    x_blocks = lax.all_to_all(after(arranged, first), "dp", 0, 0, tiled=True)
    x_blocks = x_blocks.reshape(devices, tokens + SPARE, width)
    gains = jnp.sum(x_blocks[:, tokens, : 6 * per].reshape(devices, 2, 3, per).astype(F32), axis=2)
    gain_one = gains[:, 0].reshape(1, features)
    gain_two = gains[:, 1].reshape(1, features)
    x_blocks = x_blocks.reshape(dp_count, tensor_count, tokens + SPARE, width)

    mixed, n_one_turn, qkv_wide = project(
        limit, place, groups, x_blocks, clock, gain_one, qkv_parts
    )
    if direct:
        mixed, other = together(mixed, other)
        near_mine, near_other = swap(after(mine, mixed), 1), swap(other, 1)
        far_other = swap(other, 2)
    ctx, ctx_turn, lse = attend(limit, mixed, tensor_count)
    if direct:
        ctx, near_mine, near_other, far_mine, far_other = together(
            ctx, near_mine, near_other, far_mine, far_other
        )
        last_mine, last_other = swap(far_mine, 1), swap(far_other, 1)
        rest_parts = (
            (mine, other), (near_mine, near_other), (far_mine, far_other), (last_mine, last_other)
        )
    output, context_grad, middle_grad, two_grad, up_send, down_send, up_keep, down_keep = middle_block(
        limit, place, groups, x_blocks, clock, gain_two, ctx, rest_parts, out_grad
    )
    up_came, down_came = swap(up_send, 1), swap(down_send, 1)

    back = functools.partial(attend_back, limit, mixed, ctx_turn, lse)
    if direct:
        down_sent, down_rest = fold_pair([grouped(value) for value in (down_keep, down_came)])
        up_sent, up_rest = fold_far([grouped(value) for value in (up_keep, up_came)])
        context_grad = after(context_grad, down_sent, up_sent)
    high, three, two = back(context_grad, n_one_turn, 3)
    if direct:
        *down_rest, down_came = down_rest()
        *up_rest, up_came = up_rest()
        high, three, two, down_came, up_came = together(high, three, two, down_came, up_came)
        down_sent, down_rest = fold_far([add(*down_rest, down_came)])
        up_sent, up_rest = fold_pair([add(*up_rest, up_came)])
        context_grad = after(context_grad, down_sent, up_sent)
    far = add(two, swap(three, 1))
    came_far = swap(far, 2)
    low, one, own_part = back(after(context_grad, high, far), n_one_turn, 1)
    if direct:
        *down_rest, down_came = down_rest()
        *up_rest, up_came = up_rest()
        low, one, own_part, down_came, up_came, came_far = together(
            low, one, own_part, down_came, up_came, came_far
        )
        rest_sum = [add(*up_rest, up_came), add(*down_rest, down_came)]
        rest_value, rest_finish = fold_coarse([jnp.concatenate(rest_sum, axis=-1)])
        middle_grad = after(middle_grad, rest_value)
    came_one = swap(one, 1)
    begin_grad = begin_block(
        limit, x_blocks, clock, gain_one, two_grad, qkv_wide, middle_grad, high, low
    )
    if direct:
        begin_grad, came_one = together(begin_grad, came_one)
        near = [grouped(value[None])[0] for value in (own_part, came_one, came_far)]
        qkv_value, qkv_finish = fold_coarse(fold_pair(near)[1]())
        rest_total, qkv_total = rest_finish(qkv_value), qkv_finish()
        up_total, down_total = rest_total[:, : PAIR + hidden], rest_total[:, PAIR + hidden :]
    else:
        up_total = exchange_rows(add(*fold_far([up_keep, up_came])[1]()))
        down_total = exchange_rows(add(*fold_far([down_keep, down_came])[1]()))
        qkv_total = exchange_rows(add(own_part, came_one, came_far))
    returned = lax.all_to_all(
        begin_grad.reshape(devices, tokens + SPARE, width), both, 0, 0, tiled=True
    )
    inverse = (
        jnp.zeros((total_seqs,), jnp.int32)
        .at[deal_order]
        .set(jnp.arange(total_seqs, dtype=jnp.int32))
    )
    states_grad = returned[inverse][:, :tokens]
    gain_grads = jnp.sum(returned[:, tokens:].astype(F32), axis=0).reshape(2, devices, per)
    gain_grads = lax.dynamic_index_in_dim(gain_grads, own, 1, keepdims=False)
    return (
        output,
        states_grad,
        qkv_total.reshape(w_qkv.shape),
        up_total[:, :PAIR].T,
        up_total[:, PAIR:],
        down_total.T,
        gain_grads[0],
        gain_grads[1],
    )


def solution(mesh):
    in_specs = (
        P(None, "dp", "tensor"),
        P(),
        P(),
        P(),
        P("dp", None, "tensor"),
        P("tensor", "dp"),
        P("dp", "tensor"),
        P("tensor", "dp"),
        P(("dp", "tensor")),
        P(("dp", "tensor")),
        P(("dp", "tensor"), None, None),
    )
    out_specs = (
        P(("dp", "tensor"), None, None),
        P(None, "dp", "tensor"),
        P("dp", None, "tensor"),
        P("tensor", "dp"),
        P("dp", "tensor"),
        P("tensor", "dp"),
        P(("dp", "tensor")),
        P(("dp", "tensor")),
    )
    return jax.shard_map(
        on_device, mesh=mesh, in_specs=in_specs, out_specs=out_specs, check_vma=False
    )
```

```python
import functools
import math

import jax
import jax.numpy as jnp
from jax import lax
from jax.experimental import pallas as pl
from jax.experimental.pallas import tpu as pltpu
from jax.sharding import PartitionSpec as P

HEAD_DIM = 64
PAIR = 2 * HEAD_DIM
ROWS = 512
KEYS = 256
BACK_KEYS = 512
SPARE = 8
SCORE_SCALE = 1.0 / math.sqrt(HEAD_DIM)
LOG2E = math.log2(math.e)
F32 = jnp.float32
BF16 = jnp.bfloat16
NN = (((1,), (0,)), ((), ()))
NT = (((1,), (1,)), ((), ()))
MIB = 1024 * 1024


def mul(lhs, rhs, dims=NN):
    return lax.dot_general(lhs, rhs, dims, preferred_element_type=F32)


def join_tokens(ref):
    blocks, parts, tall, width = ref.shape
    tokens = tall - SPARE
    return jnp.concatenate(
        [ref[:, part, 0:tokens].reshape(blocks * tokens, width) for part in range(parts)], axis=-1
    ).astype(F32)


def place_rows(groups, place_ref, first, source, targets):
    if groups is None:
        for target, columns, own in targets:
            target[:, columns] = source[:, own]
        return
    rows = source.shape[0] // groups
    for group in range(groups):
        spot = pl.ds(pl.multiple_of(place_ref[first + group] * rows, rows), rows)
        for target, columns, own in targets:
            target[spot, columns] = source[group * rows : (group + 1) * rows, own]


def norm_parts(values):
    center = values - jnp.mean(values, axis=-1, keepdims=True)
    spread = jnp.mean(center * center, axis=-1, keepdims=True)
    inverse = lax.rsqrt(spread + 1e-05)
    return center * inverse, inverse


def norm_back(grad, gain, unit, inverse):
    scaled = grad * gain
    mean_scaled = jnp.mean(scaled, axis=-1, keepdims=True)
    mean_along = jnp.mean(scaled * unit, axis=-1, keepdims=True)
    return inverse * (scaled - mean_scaled - unit * mean_along)


def cost(microseconds):
    return pl.CostEstimate(
        flops=int(microseconds * 1.15e9), bytes_accessed=1 << 20, transcendentals=0
    )


def params(mebibytes):
    return pltpu.CompilerParams(vmem_limit_bytes=mebibytes * MIB)


def project_kernel(groups, limit_ref, place_ref, x_ref, clock_ref, gain_ref, *refs):
    w_refs, (mixed_ref, n_turn_ref, wide) = refs[:-3], refs[-3:]
    step = pl.program_id(0)

    @pl.when(step == 0)
    def _():
        for part, w_ref in enumerate(w_refs):
            width = w_ref.shape[1]
            columns = slice(part * width, (part + 1) * width)
            place_rows(groups, place_ref, 0, w_ref, [(wide, columns, slice(0, width))])

    @pl.when(step * ROWS < limit_ref[0])
    def _():
        begin = join_tokens(x_ref) + clock_ref[...]
        unit, _ = norm_parts(begin)
        normed = (unit * gain_ref[...]).astype(BF16)
        n_turn_ref[...] = normed.T
        mixed_ref[...] = mul(normed, wide[...]).astype(BF16)

    @pl.when(step * ROWS >= limit_ref[0])
    def _():
        n_turn_ref[...] = jnp.zeros_like(n_turn_ref)
        mixed_ref[...] = jnp.zeros_like(mixed_ref)


def project(limit, place, groups, x_blocks, clock, gain, w_parts):
    senders, feature_parts, tall, width = x_blocks.shape
    tokens = tall - SPARE
    length = senders * tokens
    features = feature_parts * width
    parts, columns = len(w_parts), w_parts[0].shape[1]
    take = ROWS // tokens
    return pl.pallas_call(
        functools.partial(project_kernel, groups),
        grid_spec=pltpu.PrefetchScalarGridSpec(
            num_scalar_prefetch=2,
            grid=(length // ROWS,),
            in_specs=[
                pl.BlockSpec((take, feature_parts, tall, width), lambda i, *s: (i, 0, 0, 0)),
                pl.BlockSpec((1, features), lambda i, *s: (0, 0)),
                pl.BlockSpec((1, features), lambda i, *s: (0, 0)),
            ]
            + [pl.BlockSpec((features, columns), lambda i, *s: (0, 0))] * parts,
            out_specs=[
                pl.BlockSpec((ROWS, parts * columns), lambda i, *s: (i, 0)),
                pl.BlockSpec((features, ROWS), lambda i, *s: (0, i)),
                pl.BlockSpec((features, parts * columns), lambda i, *s: (0, 0)),
            ],
        ),
        out_shape=[
            jax.ShapeDtypeStruct((length, parts * columns), BF16),
            jax.ShapeDtypeStruct((features, length), BF16),
            jax.ShapeDtypeStruct((features, parts * columns), BF16),
        ],
        compiler_params=params(20),
        cost_estimate=cost(5),
        name="project",
    )(limit, place, x_blocks, clock, gain, *w_parts)


def head_lanes(shape, head):
    lane = lax.broadcasted_iota(jnp.int32, shape, 1)
    return (lane >= head * HEAD_DIM) & (lane < (head + 1) * HEAD_DIM)


def spare_lane(shape, head):
    lane = lax.broadcasted_iota(jnp.int32, shape, 1)
    return lane == (1 - head) * HEAD_DIM


def masked_keys(keys, head, limit):
    row = lax.broadcasted_iota(jnp.int32, keys.shape, 0)
    spare = jnp.where(
        spare_lane(keys.shape, head) & (row >= limit), jnp.asarray(-1e30, F32), jnp.asarray(0.0, F32)
    )
    return jnp.where(head_lanes(keys.shape, head), keys.astype(F32), spare).astype(BF16)


def own_lanes(values, head):
    return jnp.where(head_lanes(values.shape, head), values.astype(F32), 0.0).astype(BF16)


def masked_queries(queries, head):
    spare = jnp.where(spare_lane(queries.shape, head), jnp.asarray(1.0, F32), jnp.asarray(0.0, F32))
    return jnp.where(head_lanes(queries.shape, head), queries.astype(F32), spare).astype(BF16)


def attend_kernel(limit_ref, q_ref, k_ref, v_ref, ctx_ref, turn_ref, lse_ref, keys_s, q_s, vt_s, sc_s):
    length = q_ref.shape[0]
    vt_s[...] = v_ref[...].astype(F32).T.astype(BF16)
    for head in range(2):
        keys_s[head] = masked_keys(k_ref[...], head, limit_ref[0])
        q_s[head] = masked_queries(q_ref[...], head)
    factor = SCORE_SCALE * LOG2E
    spans = [slice(at, at + KEYS) for at in range(0, length, KEYS)]
    outs = []
    for head in range(2):
        feats = slice(head * HEAD_DIM, (head + 1) * HEAD_DIM)
        peak = None
        for span in spans:
            scores = mul(keys_s[head, span], q_s[head], NT)
            sc_s[head, span] = scores
            high = jnp.max(scores, axis=0, keepdims=True)
            peak = high if peak is None else jnp.maximum(peak, high)
        peak = peak * factor
        total = jnp.zeros_like(peak)
        gathered = jnp.zeros((HEAD_DIM, length), F32)
        for span in spans:
            expo = jnp.exp2(sc_s[head, span] * factor - peak)
            total += jnp.sum(expo, axis=0, keepdims=True)
            gathered += mul(vt_s[feats, span], expo.astype(BF16))
        outs.append(gathered / total)
        lse_ref[0, head : head + 1, :] = peak + jnp.log2(total)
    both = jnp.concatenate(outs, axis=0)
    turn_ref[...] = both.astype(BF16)
    ctx_ref[...] = both.T.astype(BF16)


def attend(limit, mixed, pairs):
    length = mixed.shape[0]
    column = lambda c: pl.BlockSpec((length, PAIR), lambda i, s: (0, i * 3 + c))
    return pl.pallas_call(
        attend_kernel,
        grid_spec=pltpu.PrefetchScalarGridSpec(
            num_scalar_prefetch=1,
            grid=(pairs,),
            in_specs=[column(0), column(1), column(2)],
            out_specs=[
                pl.BlockSpec((length, PAIR), lambda i, s: (0, i)),
                pl.BlockSpec((PAIR, length), lambda i, s: (i, 0)),
                pl.BlockSpec((1, 2, length), lambda i, s: (i, 0, 0)),
            ],
            scratch_shapes=[
                pltpu.VMEM((2, length, PAIR), BF16),
                pltpu.VMEM((2, length, PAIR), BF16),
                pltpu.VMEM((PAIR, length), BF16),
                pltpu.VMEM((2, length, length), F32),
            ],
        ),
        out_shape=[
            jax.ShapeDtypeStruct((length, pairs * PAIR), BF16),
            jax.ShapeDtypeStruct((pairs * PAIR, length), BF16),
            jax.ShapeDtypeStruct((pairs, 2, length), F32),
        ],
        compiler_params=params(28),
        cost_estimate=cost(15),
        name="attend",
    )(limit, mixed, mixed, mixed)


def gelu_both(values):
    root = math.sqrt(2.0 / math.pi)
    scaled = root * values
    inner = scaled * (1.0 + 0.044715 * (values * values))
    tanh = jnp.tanh(inner)
    half = 0.5 + 0.5 * tanh
    slope = half + (1.0 - tanh * tanh) * (1.5 * inner - scaled)
    return values * half, slope


def middle_kernel(
    groups, limit_ref, place_ref, x_ref, clock_ref, gain_ref, ctx_ref, og_ref, *refs
):
    weight_refs, refs = refs[:-17], refs[-17:]
    out_ref, cg_ref, mg_ref, gg_ref, up_send, down_send, up_keep, down_keep = refs[:8]
    wide, units, active_s, ug_s, n_turn, fg_turn, ag_turn, ctx_s, sems = refs[8:]
    step = pl.program_id(0)
    parts, _, hidden = active_s.shape
    blocks = pl.num_programs(0) - parts
    each = len(weight_refs) // parts

    def fetch(part, kind):
        target, wide_, own = (
            (wide, PAIR, slice(0, PAIR)),
            (units, 2 * hidden, slice(PAIR, PAIR + 2 * hidden)),
        )[kind]
        columns = slice(part * wide_, (part + 1) * wide_)
        copies = []
        for at, w_ref in enumerate(weight_refs[part * each : (part + 1) * each]):
            count = 1 if groups is None else groups // each
            rows = w_ref.shape[0] // count
            for group in range(count):
                index = at * count + group
                spot = pl.ds(0, rows)
                if groups is not None:
                    spot = pl.ds(pl.multiple_of(place_ref[index] * rows, rows), rows)
                copies.append(
                    pltpu.make_async_copy(
                        w_ref.at[pl.ds(group * rows, rows), own],
                        target.at[spot, columns],
                        sems.at[kind, part, index],
                    )
                )
        return copies

    @pl.when(step == 0)
    def _():
        gg_ref[...] = jnp.zeros_like(gg_ref)
        for part in range(parts):
            for copy in fetch(part, 0) + fetch(part, 1):
                copy.start()
        for part in range(parts):
            for copy in fetch(part, 0) + fetch(part, 1):
                copy.wait()

    dead = (step < blocks) & (step * ROWS >= limit_ref[0])

    @pl.when((step < blocks) & jnp.logical_not(dead))
    def _():
        spot = pl.ds(pl.multiple_of(step * ROWS, ROWS), ROWS)
        gain = gain_ref[...]
        live = step * ROWS + lax.broadcasted_iota(jnp.int32, (ROWS, 1), 0) < limit_ref[0]
        begin = join_tokens(x_ref) + clock_ref[...]
        middle = begin + mul(ctx_ref[...], wide[...], NT)
        unit, inverse = norm_parts(middle)
        normed = (unit * gain).astype(BF16)
        n_turn[:, spot] = normed.T
        res_grad = jnp.where(live, og_ref[0].astype(F32), 0.0)
        feed_grad = res_grad.astype(BF16)
        fg_turn[:, spot] = feed_grad.T
        feed = jnp.zeros_like(middle)
        two_grad = jnp.zeros_like(middle)
        for part in range(parts):
            up = slice(2 * part * hidden, (2 * part + 1) * hidden)
            down = slice((2 * part + 1) * hidden, (2 * part + 2) * hidden)
            upper = mul(normed, units[:, up])
            active, slope = gelu_both(upper)
            active = active.astype(BF16)
            active_s[part, spot] = active
            feed += mul(active, units[:, down], NT)
            upper_grad = (mul(feed_grad, units[:, down]) * slope).astype(BF16)
            ug_s[part, spot] = upper_grad
            two_grad += mul(upper_grad, units[:, up], NT)
        out_ref[0] = jnp.where(live, middle + feed, 0.0).astype(BF16)
        gg_ref[...] += jnp.sum(two_grad * unit, axis=0, keepdims=True)
        middle_grad = res_grad + norm_back(two_grad, gain, unit, inverse)
        mg_ref[...] = middle_grad
        att_grad = middle_grad.astype(BF16)
        ag_turn[:, spot] = att_grad.T
        cg_ref[...] = mul(att_grad, wide[...]).astype(BF16)
        for part in range(parts):
            ctx_s[part, spot] = ctx_ref[:, part * PAIR : (part + 1) * PAIR]

    @pl.when(dead)
    def _():
        spot = pl.ds(pl.multiple_of(step * ROWS, ROWS), ROWS)
        for ref in (out_ref, cg_ref, mg_ref):
            ref[...] = jnp.zeros_like(ref)
        for ref in (active_s, ug_s, ctx_s):
            ref[:, spot] = jnp.zeros((ref.shape[0], ROWS, ref.shape[2]), BF16)
        for ref in (n_turn, fg_turn, ag_turn):
            ref[:, spot] = jnp.zeros((ref.shape[0], ROWS), BF16)

    @pl.when(step >= blocks)
    def _():
        turn = step - blocks
        part = jnp.where(turn < 2, 3 - 2 * turn, 6 - 2 * turn)
        grads = (
            mul(ag_turn[...], ctx_s[part]).astype(BF16),
            mul(n_turn[...], ug_s[part]).astype(BF16),
            mul(fg_turn[...], active_s[part]).astype(BF16),
        )

        def into(up_ref, down_ref):
            up_ref[0, :, 0:PAIR], up_ref[0, :, PAIR:], down_ref[0] = grads

        pl.when(turn < 2)(lambda: into(up_send, down_send))
        pl.when(turn >= 2)(lambda: into(up_keep, down_keep))


def middle_block(limit, place, groups, x_blocks, clock, gain, ctx, w_parts, out_grad):
    senders, feature_parts, tall, width = x_blocks.shape
    tokens = tall - SPARE
    length = senders * tokens
    features = feature_parts * width
    parts = len(w_parts)
    weights = [w for part in w_parts for w in part]
    columns = weights[0].shape[1]
    hidden = (columns - PAIR) // 2
    take = ROWS // tokens
    blocks = length // ROWS
    row = lambda i: jnp.minimum(i, blocks - 1)
    whole = lambda array: pl.BlockSpec(
        array.shape, lambda i, *s: (0,) * array.ndim, pipeline_mode=pl.Buffered(1)
    )
    rows = lambda n: pl.BlockSpec((ROWS, n), lambda i, *s: (row(i), 0))
    one = pl.BlockSpec((1, ROWS, features), lambda i, *s: (0, row(i), 0))
    grads = lambda first, n: pl.BlockSpec(
        (1, features, n), lambda i, *s: (jnp.clip(i - blocks - first, 0, 1), 0, 0)
    )
    up_shape = jax.ShapeDtypeStruct((2, features, PAIR + hidden), BF16)
    down_shape = jax.ShapeDtypeStruct((2, features, hidden), BF16)
    return pl.pallas_call(
        functools.partial(middle_kernel, groups),
        grid_spec=pltpu.PrefetchScalarGridSpec(
            num_scalar_prefetch=2,
            grid=(blocks + parts,),
            in_specs=[
                pl.BlockSpec(
                    (take, feature_parts, tall, width), lambda i, *s: (row(i), 0, 0, 0)
                ),
                whole(clock),
                whole(gain),
                rows(features),
                one,
            ]
            + [pl.BlockSpec(memory_space=pltpu.HBM)] * len(weights),
            out_specs=[
                one, rows(features), rows(features),
                pl.BlockSpec((1, features), lambda i, *s: (0, 0)),
                grads(0, PAIR + hidden), grads(0, hidden), grads(2, PAIR + hidden), grads(2, hidden),
            ],
            scratch_shapes=[
                pltpu.VMEM((features, parts * PAIR), BF16),
                pltpu.VMEM((features, parts * 2 * hidden), BF16),
                pltpu.VMEM((parts, length, hidden), BF16),
                pltpu.VMEM((parts, length, hidden), BF16),
                pltpu.VMEM((features, length), BF16),
                pltpu.VMEM((features, length), BF16),
                pltpu.VMEM((features, length), BF16),
                pltpu.VMEM((parts, length, PAIR), BF16),
                pltpu.SemaphoreType.DMA((2, parts, groups or 1)),
            ],
        ),
        out_shape=[
            jax.ShapeDtypeStruct((1, length, features), BF16),
            jax.ShapeDtypeStruct((length, features), BF16),
            jax.ShapeDtypeStruct((length, features), F32),
            jax.ShapeDtypeStruct((1, features), F32),
            up_shape, down_shape, up_shape, down_shape,
        ],
        compiler_params=params(40),
        cost_estimate=cost(25),
        name="middle",
    )(limit, place, x_blocks, clock, gain, ctx, out_grad, *weights)


def attend_back_kernel(
    limit_ref, q_ref, k_ref, v_ref, turn_ref, lse_ref, cg_ref, n_turn_ref,
    dm_ref, first_ref, second_ref, keys_s, q_s, qz_s, do_s, kt_s, delta_s,
):
    limit = limit_ref[0]
    length = q_ref.shape[0]
    kt_s[...] = k_ref[...].astype(F32).T.astype(BF16)
    along = cg_ref[...].astype(F32).T * turn_ref[...].astype(F32)
    for head in range(2):
        feats = slice(head * HEAD_DIM, (head + 1) * HEAD_DIM)
        delta_s[head : head + 1, :] = jnp.sum(along[feats, :], axis=0, keepdims=True)
        keys_s[head] = masked_keys(k_ref[...], head, limit)
        q_s[head] = masked_queries(q_ref[...], head)
        qz_s[head] = own_lanes(q_ref[...], head)
        do_s[head] = own_lanes(cg_ref[...], head)
    factor = SCORE_SCALE * LOG2E
    turned = [jnp.zeros((HEAD_DIM, length), F32)] * 2
    for at in range(0, length, BACK_KEYS):
        span = slice(at, at + BACK_KEYS)
        key_grad = jnp.zeros((BACK_KEYS, PAIR), F32)
        value_grad = jnp.zeros((BACK_KEYS, PAIR), F32)
        for head in range(2):
            feats = slice(head * HEAD_DIM, (head + 1) * HEAD_DIM)
            scores = mul(keys_s[head, span], q_s[head], NT)
            prob = jnp.exp2(scores * factor - lse_ref[0, head : head + 1, :])
            prob_grad = mul(v_ref[span, :], do_s[head], NT)
            score_grad = (prob * (prob_grad - delta_s[head : head + 1, :])).astype(BF16)
            value_grad += mul(prob.astype(BF16), do_s[head])
            key_grad += mul(score_grad, qz_s[head])
            turned[head] += mul(kt_s[feats, span], score_grad)
        dm_ref[span, PAIR : 2 * PAIR] = (key_grad * SCORE_SCALE).astype(BF16)
        dm_ref[span, 2 * PAIR : 3 * PAIR] = value_grad.astype(BF16)
    query_grad = jnp.concatenate(turned, axis=0) * SCORE_SCALE
    dm_ref[:, 0:PAIR] = query_grad.T.astype(BF16)
    grad = mul(n_turn_ref[...], dm_ref[...]).astype(BF16)

    @pl.when(pl.program_id(0) == 0)
    def _():
        first_ref[...] = grad

    @pl.when(pl.program_id(0) == 1)
    def _():
        second_ref[...] = grad


def attend_back(limit, mixed, ctx_turn, lse, context_grad, n_turn, first):
    length = mixed.shape[0]
    features = n_turn.shape[0]
    pair = lambda i: first - i
    column = lambda c: pl.BlockSpec((length, PAIR), lambda i, s: (0, pair(i) * 3 + c))
    return pl.pallas_call(
        attend_back_kernel,
        grid_spec=pltpu.PrefetchScalarGridSpec(
            num_scalar_prefetch=1,
            grid=(2,),
            in_specs=[
                column(0), column(1), column(2),
                pl.BlockSpec((PAIR, length), lambda i, s: (pair(i), 0)),
                pl.BlockSpec((1, 2, length), lambda i, s: (pair(i), 0, 0)),
                pl.BlockSpec((length, PAIR), lambda i, s: (0, pair(i))),
                pl.BlockSpec((features, length), lambda i, s: (0, 0)),
            ],
            out_specs=[
                pl.BlockSpec((length, 3 * PAIR), lambda i, s: (0, i)),
                pl.BlockSpec((features, 3 * PAIR), lambda i, s: (0, 0)),
                pl.BlockSpec((features, 3 * PAIR), lambda i, s: (0, 0)),
            ],
            scratch_shapes=[
                pltpu.VMEM((2, length, PAIR), BF16),
                pltpu.VMEM((2, length, PAIR), BF16),
                pltpu.VMEM((2, length, PAIR), BF16),
                pltpu.VMEM((2, length, PAIR), BF16),
                pltpu.VMEM((PAIR, length), BF16),
                pltpu.VMEM((8, length), F32),
            ],
        ),
        out_shape=[
            jax.ShapeDtypeStruct((length, 2 * 3 * PAIR), BF16),
            jax.ShapeDtypeStruct((features, 3 * PAIR), BF16),
            jax.ShapeDtypeStruct((features, 3 * PAIR), BF16),
        ],
        compiler_params=params(28),
        cost_estimate=cost(16),
        name="attend_back",
    )(limit, mixed, mixed, mixed, ctx_turn, lse, context_grad, n_turn)


def begin_kernel(
    limit_ref, x_ref, clock_ref, gain_ref, gg_two_ref, mg_ref, w_ref, high_ref, low_ref, bg_ref, gg_s
):
    step = pl.program_id(0)
    _, parts, tall, width = bg_ref.shape
    tokens = tall - SPARE
    blocks = ROWS // tokens
    spot = pl.ds(step * blocks, blocks)

    @pl.when(step == 0)
    def _():
        gg_s[...] = jnp.zeros_like(gg_s)

    @pl.when(step * ROWS < limit_ref[0])
    def _():
        begin = join_tokens(x_ref) + clock_ref[...]
        unit, inverse = norm_parts(begin)
        one_grad = jnp.zeros_like(begin)
        for part, (d_ref, at) in enumerate(((low_ref, 1), (low_ref, 0), (high_ref, 1), (high_ref, 0))):
            columns = slice(part * 3 * PAIR, (part + 1) * 3 * PAIR)
            own = slice(at * 3 * PAIR, (at + 1) * 3 * PAIR)
            one_grad += mul(d_ref[:, own], w_ref[:, columns], NT)
        gg_s[...] += jnp.sum(one_grad * unit, axis=0, keepdims=True)
        total = (mg_ref[...] + norm_back(one_grad, gain_ref[...], unit, inverse)).astype(BF16)
        for part in range(parts):
            piece = total[:, part * width : (part + 1) * width]
            bg_ref[spot, part, 0:tokens] = piece.reshape(blocks, tokens, width)

    @pl.when(step * ROWS >= limit_ref[0])
    def _():
        bg_ref[spot] = jnp.zeros((blocks,) + bg_ref.shape[1:], BF16)

    @pl.when(step == pl.num_programs(0) - 1)
    def _():
        rows = []
        for ref in (gg_s, gg_two_ref):
            for part in range(parts):
                rows.append(ref[:, part * width : (part + 1) * width])
        bg_ref[:, :, tokens:tall] = jnp.broadcast_to(
            jnp.concatenate(rows, axis=0).astype(BF16), bg_ref.shape[:2] + (SPARE, width)
        )


def begin_block(limit, x_blocks, clock, gain, two_grad, w_wide, middle_grad, high, low):
    senders, feature_parts, tall, width = x_blocks.shape
    tokens = tall - SPARE
    length = senders * tokens
    features = feature_parts * width
    take = ROWS // tokens
    whole = lambda array: pl.BlockSpec(array.shape, lambda i, s: (0,) * array.ndim)
    rows = lambda n: pl.BlockSpec((ROWS, n), lambda i, s: (i, 0))
    return pl.pallas_call(
        begin_kernel,
        grid_spec=pltpu.PrefetchScalarGridSpec(
            num_scalar_prefetch=1,
            grid=(length // ROWS,),
            in_specs=[
                pl.BlockSpec((take, feature_parts, tall, width), lambda i, s: (i, 0, 0, 0)),
                whole(clock), whole(gain), whole(two_grad), rows(features), whole(w_wide),
            ]
            + [rows(6 * PAIR)] * 2,
            out_specs=whole(x_blocks),
            scratch_shapes=[pltpu.VMEM((1, features), F32)],
        ),
        out_shape=jax.ShapeDtypeStruct(x_blocks.shape, BF16),
        compiler_params=params(20),
        cost_estimate=cost(7),
        name="begin_back",
    )(limit, x_blocks, clock, gain, two_grad, middle_grad, w_wide, high, low)


DIRECT = 8


def clock_rows(step_ids, features):
    half_width = features // 2
    ladder = jnp.arange(half_width, dtype=F32) / half_width
    rate_rows = jnp.exp(-math.log(10000.0) * ladder)
    angles = step_ids.astype(F32)[:, None] * rate_rows[None, :]
    return jnp.concatenate([jnp.sin(angles), jnp.cos(angles)], axis=-1)


def swap(value, apart):
    count = lax.axis_size("tensor")
    return lax.ppermute(value, "tensor", [(i, i ^ apart) for i in range(count)])


def along_dp(value, move):
    count = lax.axis_size("dp")
    return lax.ppermute(value, "dp", [(i, move(i)) for i in range(count)])


def across(value):
    return along_dp(value, lambda i: i ^ 1)


def ahead(value, step):
    count = lax.axis_size("dp") // 2
    return along_dp(value, lambda i: (i // 2 + step) % count * 2 + i % 2)


def places():
    count = lax.axis_size("dp") // 2
    own = lax.axis_index("dp")
    coarse = (own // 2 - jnp.arange(count, dtype=jnp.int32)) % count
    return jnp.concatenate([coarse * 2 + own % 2, coarse * 2 + 1 - own % 2])


def collect_coarse(shard):
    count = lax.axis_size("dp") // 2
    return jnp.concatenate([shard] + [ahead(shard, step) for step in range(1, count)], axis=0)


def collect_rows(shard):
    count = lax.axis_size("dp")
    rows = lax.all_to_all(
        jnp.broadcast_to(shard[None], (count,) + shard.shape), "dp", 0, 0, tiled=True
    )
    return rows.reshape(count * shard.shape[0], shard.shape[1])


def collect_columns(rows):
    far = swap(rows, 2)
    return rows, swap(rows, 1), far, swap(far, 1)


def add(*values):
    return add_wide(*values).astype(BF16)


def fold_pair(values):
    own = lax.axis_index("dp") % 2
    pick = lambda value, which: lax.dynamic_index_in_dim(value, which, value.ndim - 3, keepdims=False)
    sent = add(*[pick(value, 1 - own) for value in values])
    return sent, lambda: [pick(value, own) for value in values] + [across(sent)]


def fold_far(values):
    sent = add(*[value[0] for value in values])
    return sent, lambda: [value[1] for value in values] + [swap(sent, 2)]


def fold_coarse(values):
    count = lax.axis_size("dp") // 2
    own = lax.axis_index("dp") // 2
    pick = lambda value, which: lax.dynamic_index_in_dim(value, which % count, 0, keepdims=False)
    value = add(*values)
    came = [ahead(pick(value, own + step), step) for step in range(1, count)]
    return value, [pick(value, own)] + came


def add_wide(*values):
    total = values[0].astype(F32)
    for value in values[1:]:
        total += value.astype(F32)
    return total


def grouped(value):
    count = lax.axis_size("dp")
    two, rows, columns = value.shape
    return value.reshape(two, count // 2, 2, rows // count, columns)


def exchange_rows(value):
    count = lax.axis_size("dp")
    groups = value.reshape(count, value.shape[0] // count, value.shape[1])
    return jnp.sum(lax.all_to_all(groups, "dp", 0, 0, tiled=True).astype(F32), axis=0)


def three_terms(values):
    terms = []
    for _ in range(3):
        term = lax.reduce_precision(values, 8, 7)
        terms.append(term.astype(BF16))
        values = values - term
    return terms


def together(*values):
    return lax.optimization_barrier(values)


def after(value, *others):
    return lax.optimization_barrier((value,) + others)[0]


def on_device(
    states, timesteps, lengths, deal_order, w_qkv, w_out, w_up, w_down, gain_attn, gain_ffn, out_grad
):
    both = ("dp", "tensor")
    dp_count = lax.axis_size("dp")
    tensor_count = lax.axis_size("tensor")
    devices = dp_count * tensor_count
    total_seqs, tokens, width = states.shape
    assert tensor_count == 4 and total_seqs == devices
    features = width * tensor_count
    own = lax.axis_index("dp") * tensor_count + lax.axis_index("tensor")
    own_id = lax.dynamic_slice_in_dim(deal_order, own, 1)
    limit = lengths[own_id]
    clock = clock_rows(timesteps[own_id], features)
    per = gain_attn.shape[0]
    rows = w_qkv.shape[0]
    hidden = w_up.shape[1]

    rest = jnp.concatenate([w_out.T, w_up, w_down.T], axis=1)
    qkv = w_qkv.reshape(rows, -1)
    direct = dp_count <= DIRECT
    if direct:
        place, groups = places(), dp_count
        first = collect_coarse(jnp.concatenate([qkv, rest], axis=1))
        qkv_rows = first[:, : qkv.shape[1]]
        qkv_other = across(qkv_rows)
        qkv_parts = collect_columns(jnp.concatenate([qkv_rows, qkv_other], axis=0))
        mine = after(first[:, qkv.shape[1] :], qkv_other)
        other, far_mine = across(mine), swap(after(mine, qkv_parts[2]), 2)
    else:
        place, groups = jnp.zeros((1,), jnp.int32), None
        first = collect_rows(qkv)
        qkv_parts = collect_columns(first)
        rest_parts = [(part,) for part in collect_columns(collect_rows(rest))]

    spare = jnp.stack(three_terms(gain_attn) + three_terms(gain_ffn)).reshape(1, 6 * per)
    spare = jnp.pad(spare, ((0, SPARE - 1), (0, width - 6 * per)))
    by_tensor = deal_order.reshape(dp_count, tensor_count).T.reshape(devices)
    arranged = jnp.concatenate(
        [states[by_tensor], jnp.broadcast_to(spare[None], (devices, SPARE, width))], axis=1
    )
    arranged = lax.all_to_all(arranged, "tensor", 0, 0, tiled=True)
    arranged = arranged.reshape(tensor_count, dp_count, tokens + SPARE, width).swapaxes(0, 1)
    x_blocks = lax.all_to_all(after(arranged, first), "dp", 0, 0, tiled=True)
    x_blocks = x_blocks.reshape(devices, tokens + SPARE, width)
    gains = jnp.sum(x_blocks[:, tokens, : 6 * per].reshape(devices, 2, 3, per).astype(F32), axis=2)
    gain_one = gains[:, 0].reshape(1, features)
    gain_two = gains[:, 1].reshape(1, features)
    x_blocks = x_blocks.reshape(dp_count, tensor_count, tokens + SPARE, width)

    mixed, n_one_turn, qkv_wide = project(
        limit, place, groups, x_blocks, clock, gain_one, qkv_parts
    )
    if direct:
        mixed, other = together(mixed, other)
        near_mine, near_other = swap(after(mine, mixed), 1), swap(other, 1)
        far_other = swap(other, 2)
    ctx, ctx_turn, lse = attend(limit, mixed, tensor_count)
    if direct:
        ctx, near_mine, near_other, far_mine, far_other = together(
            ctx, near_mine, near_other, far_mine, far_other
        )
        last_mine, last_other = swap(far_mine, 1), swap(far_other, 1)
        rest_parts = (
            (mine, other), (near_mine, near_other), (far_mine, far_other), (last_mine, last_other)
        )
    output, context_grad, middle_grad, two_grad, up_send, down_send, up_keep, down_keep = middle_block(
        limit, place, groups, x_blocks, clock, gain_two, ctx, rest_parts, out_grad
    )
    up_came, down_came = swap(up_send, 1), swap(down_send, 1)

    back = functools.partial(attend_back, limit, mixed, ctx_turn, lse)
    if direct:
        down_sent, down_rest = fold_far([grouped(value) for value in (down_keep, down_came)])
        up_sent, up_rest = fold_pair([grouped(value) for value in (up_keep, up_came)])
        context_grad = after(context_grad, down_sent, up_sent)
    high, three, two = back(context_grad, n_one_turn, 3)
    if direct:
        *down_rest, down_came = down_rest()
        *up_rest, up_came = up_rest()
        high, three, two, down_came, up_came = together(high, three, two, down_came, up_came)
        down_value, down_pieces = fold_coarse([*down_rest, down_came])
        up_sent, up_rest = fold_far([add(*up_rest, up_came)])
        context_grad = after(context_grad, down_value, up_sent)
    far = add(two, swap(three, 1))
    came_far = swap(far, 2)
    low, one, own_part = back(after(context_grad, high, far), n_one_turn, 1)
    if direct:
        *up_rest, up_came = up_rest()
        low, one, own_part, up_came, came_far, *down_pieces = together(
            low, one, own_part, up_came, came_far, *down_pieces
        )
        up_value, up_pieces = fold_coarse([*up_rest, up_came])
        down_sent, down_rest = fold_pair([add_wide(*down_pieces)[..., None, :, :, :]])
        middle_grad = after(middle_grad, up_value, down_sent)
    came_one = swap(one, 1)
    begin_grad = begin_block(
        limit, x_blocks, clock, gain_one, two_grad, qkv_wide, middle_grad, high, low
    )
    if direct:
        begin_grad, came_one = together(begin_grad, came_one)
        near = [grouped(value[None])[0] for value in (own_part, came_one, came_far)]
        qkv_value, qkv_pieces = fold_coarse(fold_pair(near)[1]())
        *up_pieces, down_came, _ = together(*up_pieces, down_rest()[-1], qkv_value)
        up_total = add_wide(*up_pieces)
        down_total = add_wide(*down_rest()[:-1], down_came)[0]
        qkv_total = add_wide(*qkv_pieces)
    else:
        up_total = exchange_rows(add(*fold_far([up_keep, up_came])[1]()))
        down_total = exchange_rows(add(*fold_far([down_keep, down_came])[1]()))
        qkv_total = exchange_rows(add(own_part, came_one, came_far))
    returned = lax.all_to_all(
        begin_grad.reshape(devices, tokens + SPARE, width), both, 0, 0, tiled=True
    )
    inverse = (
        jnp.zeros((total_seqs,), jnp.int32)
        .at[deal_order]
        .set(jnp.arange(total_seqs, dtype=jnp.int32))
    )
    states_grad = returned[inverse][:, :tokens]
    gain_grads = jnp.sum(returned[:, tokens:].astype(F32), axis=0).reshape(2, devices, per)
    gain_grads = lax.dynamic_index_in_dim(gain_grads, own, 1, keepdims=False)
    return (
        output,
        states_grad,
        qkv_total.reshape(w_qkv.shape),
        up_total[:, :PAIR].T,
        up_total[:, PAIR:],
        down_total.T,
        gain_grads[0],
        gain_grads[1],
    )


def solution(mesh):
    in_specs = (
        P(None, "dp", "tensor"),
        P(),
        P(),
        P(),
        P("dp", None, "tensor"),
        P("tensor", "dp"),
        P("dp", "tensor"),
        P("tensor", "dp"),
        P(("dp", "tensor")),
        P(("dp", "tensor")),
        P(("dp", "tensor"), None, None),
    )
    out_specs = (
        P(("dp", "tensor"), None, None),
        P(None, "dp", "tensor"),
        P("dp", None, "tensor"),
        P("tensor", "dp"),
        P("dp", "tensor"),
        P("tensor", "dp"),
        P(("dp", "tensor")),
        P(("dp", "tensor")),
    )
    return jax.shard_map(
        on_device, mesh=mesh, in_specs=in_specs, out_specs=out_specs, check_vma=False
    )
```

```python
import functools
import math

import jax
import jax.numpy as jnp
from jax import lax
from jax.experimental import pallas as pl
from jax.experimental.pallas import tpu as pltpu
from jax.sharding import PartitionSpec as P

HEAD_DIM = 64
PAIR = 2 * HEAD_DIM
ROWS = 512
KEYS = 256
BACK_KEYS = 512
SPARE = 8
SCORE_SCALE = 1.0 / math.sqrt(HEAD_DIM)
LOG2E = math.log2(math.e)
F32 = jnp.float32
BF16 = jnp.bfloat16
NN = (((1,), (0,)), ((), ()))
NT = (((1,), (1,)), ((), ()))
MIB = 1024 * 1024


def mul(lhs, rhs, dims=NN):
    return lax.dot_general(lhs, rhs, dims, preferred_element_type=F32)


def join_tokens(ref):
    blocks, parts, tall, width = ref.shape
    tokens = tall - SPARE
    return jnp.concatenate(
        [ref[:, part, 0:tokens].reshape(blocks * tokens, width) for part in range(parts)], axis=-1
    ).astype(F32)


def place_rows(groups, place_ref, first, source, targets):
    if groups is None:
        for target, columns, own in targets:
            target[:, columns] = source[:, own]
        return
    rows = source.shape[0] // groups
    for group in range(groups):
        spot = pl.ds(pl.multiple_of(place_ref[first + group] * rows, rows), rows)
        for target, columns, own in targets:
            target[spot, columns] = source[group * rows : (group + 1) * rows, own]


def norm_parts(values):
    center = values - jnp.mean(values, axis=-1, keepdims=True)
    spread = jnp.mean(center * center, axis=-1, keepdims=True)
    inverse = lax.rsqrt(spread + 1e-05)
    return center * inverse, inverse


def norm_back(grad, gain, unit, inverse):
    scaled = grad * gain
    mean_scaled = jnp.mean(scaled, axis=-1, keepdims=True)
    mean_along = jnp.mean(scaled * unit, axis=-1, keepdims=True)
    return inverse * (scaled - mean_scaled - unit * mean_along)


def in_hbm(value):
    return pltpu.with_memory_space_constraint(value, pltpu.HBM)


def cost(microseconds):
    return pl.CostEstimate(
        flops=int(microseconds * 1.15e9), bytes_accessed=1 << 20, transcendentals=0
    )


def params(mebibytes):
    return pltpu.CompilerParams(vmem_limit_bytes=mebibytes * MIB)


def project_kernel(groups, limit_ref, place_ref, x_ref, clock_ref, gain_ref, *refs):
    w_refs, (mixed_ref, n_turn_ref, wide) = refs[:-3], refs[-3:]
    step = pl.program_id(0)

    @pl.when(step == 0)
    def _():
        for part, w_ref in enumerate(w_refs):
            width = w_ref.shape[1]
            columns = slice(part * width, (part + 1) * width)
            place_rows(groups, place_ref, 0, w_ref, [(wide, columns, slice(0, width))])

    @pl.when(step * ROWS < limit_ref[0])
    def _():
        begin = join_tokens(x_ref) + clock_ref[...]
        unit, _ = norm_parts(begin)
        normed = (unit * gain_ref[...]).astype(BF16)
        n_turn_ref[...] = normed.T
        mixed_ref[...] = mul(normed, wide[...]).astype(BF16)

    @pl.when(step * ROWS >= limit_ref[0])
    def _():
        n_turn_ref[...] = jnp.zeros_like(n_turn_ref)
        mixed_ref[...] = jnp.zeros_like(mixed_ref)


def project(limit, place, groups, x_blocks, clock, gain, w_parts):
    senders, feature_parts, tall, width = x_blocks.shape
    tokens = tall - SPARE
    length = senders * tokens
    features = feature_parts * width
    parts, columns = len(w_parts), w_parts[0].shape[1]
    take = ROWS // tokens
    return pl.pallas_call(
        functools.partial(project_kernel, groups),
        grid_spec=pltpu.PrefetchScalarGridSpec(
            num_scalar_prefetch=2,
            grid=(length // ROWS,),
            in_specs=[
                pl.BlockSpec((take, feature_parts, tall, width), lambda i, *s: (i, 0, 0, 0)),
                pl.BlockSpec((1, features), lambda i, *s: (0, 0)),
                pl.BlockSpec((1, features), lambda i, *s: (0, 0)),
            ]
            + [pl.BlockSpec((features, columns), lambda i, *s: (0, 0))] * parts,
            out_specs=[
                pl.BlockSpec((ROWS, parts * columns), lambda i, *s: (i, 0)),
                pl.BlockSpec((features, ROWS), lambda i, *s: (0, i)),
                pl.BlockSpec((features, parts * columns), lambda i, *s: (0, 0)),
            ],
        ),
        out_shape=[
            jax.ShapeDtypeStruct((length, parts * columns), BF16),
            pltpu.HBM((features, length), BF16),
            pltpu.HBM((features, parts * columns), BF16),
        ],
        compiler_params=params(20),
        cost_estimate=cost(5),
        name="project",
    )(limit, place, x_blocks, clock, gain, *w_parts)


def head_lanes(shape, head):
    lane = lax.broadcasted_iota(jnp.int32, shape, 1)
    return (lane >= head * HEAD_DIM) & (lane < (head + 1) * HEAD_DIM)


def spare_lane(shape, head):
    lane = lax.broadcasted_iota(jnp.int32, shape, 1)
    return lane == (1 - head) * HEAD_DIM


def masked_keys(keys, head, limit):
    row = lax.broadcasted_iota(jnp.int32, keys.shape, 0)
    spare = jnp.where(
        spare_lane(keys.shape, head) & (row >= limit), jnp.asarray(-1e30, F32), jnp.asarray(0.0, F32)
    )
    return jnp.where(head_lanes(keys.shape, head), keys.astype(F32), spare).astype(BF16)


def own_lanes(values, head):
    return jnp.where(head_lanes(values.shape, head), values.astype(F32), 0.0).astype(BF16)


def masked_queries(queries, head):
    spare = jnp.where(spare_lane(queries.shape, head), jnp.asarray(1.0, F32), jnp.asarray(0.0, F32))
    return jnp.where(head_lanes(queries.shape, head), queries.astype(F32), spare).astype(BF16)


def attend_kernel(limit_ref, q_ref, k_ref, v_ref, ctx_ref, turn_ref, lse_ref, keys_s, q_s, vt_s, sc_s):
    length = q_ref.shape[0]
    vt_s[...] = v_ref[...].astype(F32).T.astype(BF16)
    for head in range(2):
        keys_s[head] = masked_keys(k_ref[...], head, limit_ref[0])
        q_s[head] = masked_queries(q_ref[...], head)
    factor = SCORE_SCALE * LOG2E
    spans = [slice(at, at + KEYS) for at in range(0, length, KEYS)]
    outs = []
    for head in range(2):
        feats = slice(head * HEAD_DIM, (head + 1) * HEAD_DIM)
        peak = None
        for span in spans:
            scores = mul(keys_s[head, span], q_s[head], NT)
            sc_s[head, span] = scores
            high = jnp.max(scores, axis=0, keepdims=True)
            peak = high if peak is None else jnp.maximum(peak, high)
        peak = peak * factor
        total = jnp.zeros_like(peak)
        gathered = jnp.zeros((HEAD_DIM, length), F32)
        for span in spans:
            expo = jnp.exp2(sc_s[head, span] * factor - peak)
            total += jnp.sum(expo, axis=0, keepdims=True)
            gathered += mul(vt_s[feats, span], expo.astype(BF16))
        outs.append(gathered / total)
        lse_ref[0, head : head + 1, :] = peak + jnp.log2(total)
    both = jnp.concatenate(outs, axis=0)
    turn_ref[...] = both.astype(BF16)
    ctx_ref[...] = both.T.astype(BF16)


def attend(limit, mixed, pairs):
    length = mixed.shape[0]
    column = lambda c: pl.BlockSpec((length, PAIR), lambda i, s: (0, i * 3 + c))
    return pl.pallas_call(
        attend_kernel,
        grid_spec=pltpu.PrefetchScalarGridSpec(
            num_scalar_prefetch=1,
            grid=(pairs,),
            in_specs=[column(0), column(1), column(2)],
            out_specs=[
                pl.BlockSpec((length, PAIR), lambda i, s: (0, i)),
                pl.BlockSpec((PAIR, length), lambda i, s: (i, 0)),
                pl.BlockSpec((1, 2, length), lambda i, s: (i, 0, 0)),
            ],
            scratch_shapes=[
                pltpu.VMEM((2, length, PAIR), BF16),
                pltpu.VMEM((2, length, PAIR), BF16),
                pltpu.VMEM((PAIR, length), BF16),
                pltpu.VMEM((2, length, length), F32),
            ],
        ),
        out_shape=[
            pltpu.HBM((length, pairs * PAIR), BF16),
            pltpu.HBM((pairs * PAIR, length), BF16),
            jax.ShapeDtypeStruct((pairs, 2, length), F32),
        ],
        compiler_params=params(28),
        cost_estimate=cost(15),
        name="attend",
    )(limit, mixed, mixed, mixed)


def gelu_both(values):
    root = math.sqrt(2.0 / math.pi)
    scaled = root * values
    inner = scaled * (1.0 + 0.044715 * (values * values))
    tanh = jnp.tanh(inner)
    half = 0.5 + 0.5 * tanh
    slope = half + (1.0 - tanh * tanh) * (1.5 * inner - scaled)
    return values * half, slope


def middle_kernel(
    groups, limit_ref, place_ref, x_ref, clock_ref, gain_ref, ctx_ref, og_ref, *refs
):
    weight_refs, refs = refs[:-17], refs[-17:]
    out_ref, cg_ref, mg_ref, gg_ref, up_send, down_send, up_keep, down_keep = refs[:8]
    wide, units, active_s, ug_s, n_turn, fg_turn, ag_turn, ctx_s, sems = refs[8:]
    step = pl.program_id(0)
    parts, _, hidden = active_s.shape
    blocks = pl.num_programs(0) - parts
    each = len(weight_refs) // parts

    def fetch(part, kind):
        target, wide_, own = (
            (wide, PAIR, slice(0, PAIR)),
            (units, 2 * hidden, slice(PAIR, PAIR + 2 * hidden)),
        )[kind]
        columns = slice(part * wide_, (part + 1) * wide_)
        copies = []
        for at, w_ref in enumerate(weight_refs[part * each : (part + 1) * each]):
            count = 1 if groups is None else groups // each
            rows = w_ref.shape[0] // count
            for group in range(count):
                index = at * count + group
                spot = pl.ds(0, rows)
                if groups is not None:
                    spot = pl.ds(pl.multiple_of(place_ref[index] * rows, rows), rows)
                copies.append(
                    pltpu.make_async_copy(
                        w_ref.at[pl.ds(group * rows, rows), own],
                        target.at[spot, columns],
                        sems.at[kind, part, index],
                    )
                )
        return copies

    @pl.when(step == 0)
    def _():
        gg_ref[...] = jnp.zeros_like(gg_ref)
        for part in range(parts):
            for copy in fetch(part, 0) + fetch(part, 1):
                copy.start()
        for part in range(parts):
            for copy in fetch(part, 0) + fetch(part, 1):
                copy.wait()

    dead = (step < blocks) & (step * ROWS >= limit_ref[0])

    @pl.when((step < blocks) & jnp.logical_not(dead))
    def _():
        spot = pl.ds(pl.multiple_of(step * ROWS, ROWS), ROWS)
        gain = gain_ref[...]
        live = step * ROWS + lax.broadcasted_iota(jnp.int32, (ROWS, 1), 0) < limit_ref[0]
        begin = join_tokens(x_ref) + clock_ref[...]
        middle = begin + mul(ctx_ref[...], wide[...], NT)
        unit, inverse = norm_parts(middle)
        normed = (unit * gain).astype(BF16)
        n_turn[:, spot] = normed.T
        res_grad = jnp.where(live, og_ref[0].astype(F32), 0.0)
        feed_grad = res_grad.astype(BF16)
        fg_turn[:, spot] = feed_grad.T
        feed = jnp.zeros_like(middle)
        two_grad = jnp.zeros_like(middle)
        for part in range(parts):
            up = slice(2 * part * hidden, (2 * part + 1) * hidden)
            down = slice((2 * part + 1) * hidden, (2 * part + 2) * hidden)
            upper = mul(normed, units[:, up])
            active, slope = gelu_both(upper)
            active = active.astype(BF16)
            active_s[part, spot] = active
            feed += mul(active, units[:, down], NT)
            upper_grad = (mul(feed_grad, units[:, down]) * slope).astype(BF16)
            ug_s[part, spot] = upper_grad
            two_grad += mul(upper_grad, units[:, up], NT)
        out_ref[0] = jnp.where(live, middle + feed, 0.0).astype(BF16)
        gg_ref[...] += jnp.sum(two_grad * unit, axis=0, keepdims=True)
        middle_grad = res_grad + norm_back(two_grad, gain, unit, inverse)
        mg_ref[...] = middle_grad
        att_grad = middle_grad.astype(BF16)
        ag_turn[:, spot] = att_grad.T
        cg_ref[...] = mul(att_grad, wide[...]).astype(BF16)
        for part in range(parts):
            ctx_s[part, spot] = ctx_ref[:, part * PAIR : (part + 1) * PAIR]

    @pl.when(dead)
    def _():
        spot = pl.ds(pl.multiple_of(step * ROWS, ROWS), ROWS)
        for ref in (out_ref, cg_ref, mg_ref):
            ref[...] = jnp.zeros_like(ref)
        for ref in (active_s, ug_s, ctx_s):
            ref[:, spot] = jnp.zeros((ref.shape[0], ROWS, ref.shape[2]), BF16)
        for ref in (n_turn, fg_turn, ag_turn):
            ref[:, spot] = jnp.zeros((ref.shape[0], ROWS), BF16)

    @pl.when(step >= blocks)
    def _():
        turn = step - blocks
        part = jnp.where(turn < 2, 3 - 2 * turn, 6 - 2 * turn)
        grads = (
            mul(ag_turn[...], ctx_s[part]).astype(BF16),
            mul(n_turn[...], ug_s[part]).astype(BF16),
            mul(fg_turn[...], active_s[part]).astype(BF16),
        )

        def into(up_ref, down_ref):
            up_ref[0, :, 0:PAIR], up_ref[0, :, PAIR:], down_ref[0] = grads

        pl.when(turn < 2)(lambda: into(up_send, down_send))
        pl.when(turn >= 2)(lambda: into(up_keep, down_keep))


def middle_block(limit, place, groups, x_blocks, clock, gain, ctx, w_parts, out_grad):
    senders, feature_parts, tall, width = x_blocks.shape
    tokens = tall - SPARE
    length = senders * tokens
    features = feature_parts * width
    parts = len(w_parts)
    weights = [in_hbm(w) for part in w_parts for w in part]
    columns = weights[0].shape[1]
    hidden = (columns - PAIR) // 2
    take = ROWS // tokens
    blocks = length // ROWS
    row = lambda i: jnp.minimum(i, blocks - 1)
    whole = lambda array: pl.BlockSpec(
        array.shape, lambda i, *s: (0,) * array.ndim, pipeline_mode=pl.Buffered(1)
    )
    rows = lambda n: pl.BlockSpec((ROWS, n), lambda i, *s: (row(i), 0))
    one = pl.BlockSpec((1, ROWS, features), lambda i, *s: (0, row(i), 0))
    grads = lambda first, n: pl.BlockSpec(
        (1, features, n), lambda i, *s: (jnp.clip(i - blocks - first, 0, 1), 0, 0)
    )
    up_shape = pltpu.HBM((2, features, PAIR + hidden), BF16)
    down_shape = pltpu.HBM((2, features, hidden), BF16)
    return pl.pallas_call(
        functools.partial(middle_kernel, groups),
        grid_spec=pltpu.PrefetchScalarGridSpec(
            num_scalar_prefetch=2,
            grid=(blocks + parts,),
            in_specs=[
                pl.BlockSpec(
                    (take, feature_parts, tall, width), lambda i, *s: (row(i), 0, 0, 0)
                ),
                whole(clock),
                whole(gain),
                rows(features),
                one,
            ]
            + [pl.BlockSpec(memory_space=pltpu.HBM)] * len(weights),
            out_specs=[
                one, rows(features), rows(features),
                pl.BlockSpec((1, features), lambda i, *s: (0, 0)),
                grads(0, PAIR + hidden), grads(0, hidden), grads(2, PAIR + hidden), grads(2, hidden),
            ],
            scratch_shapes=[
                pltpu.VMEM((features, parts * PAIR), BF16),
                pltpu.VMEM((features, parts * 2 * hidden), BF16),
                pltpu.VMEM((parts, length, hidden), BF16),
                pltpu.VMEM((parts, length, hidden), BF16),
                pltpu.VMEM((features, length), BF16),
                pltpu.VMEM((features, length), BF16),
                pltpu.VMEM((features, length), BF16),
                pltpu.VMEM((parts, length, PAIR), BF16),
                pltpu.SemaphoreType.DMA((2, parts, groups or 1)),
            ],
        ),
        out_shape=[
            jax.ShapeDtypeStruct((1, length, features), BF16),
            pltpu.HBM((length, features), BF16),
            pltpu.HBM((length, features), F32),
            jax.ShapeDtypeStruct((1, features), F32),
            up_shape, down_shape, up_shape, down_shape,
        ],
        compiler_params=params(48),
        cost_estimate=cost(25),
        name="middle",
    )(limit, place, x_blocks, clock, gain, in_hbm(ctx), in_hbm(out_grad), *weights)


def attend_back_kernel(
    limit_ref, q_ref, k_ref, v_ref, turn_ref, lse_ref, cg_ref, n_turn_ref,
    dm_ref, first_ref, second_ref, keys_s, q_s, qz_s, do_s, kt_s, delta_s,
):
    limit = limit_ref[0]
    length = q_ref.shape[0]
    kt_s[...] = k_ref[...].astype(F32).T.astype(BF16)
    along = cg_ref[...].astype(F32).T * turn_ref[...].astype(F32)
    for head in range(2):
        feats = slice(head * HEAD_DIM, (head + 1) * HEAD_DIM)
        delta_s[head : head + 1, :] = jnp.sum(along[feats, :], axis=0, keepdims=True)
        keys_s[head] = masked_keys(k_ref[...], head, limit)
        q_s[head] = masked_queries(q_ref[...], head)
        qz_s[head] = own_lanes(q_ref[...], head)
        do_s[head] = own_lanes(cg_ref[...], head)
    factor = SCORE_SCALE * LOG2E
    turned = [jnp.zeros((HEAD_DIM, length), F32)] * 2
    for at in range(0, length, BACK_KEYS):
        span = slice(at, at + BACK_KEYS)
        key_grad = jnp.zeros((BACK_KEYS, PAIR), F32)
        value_grad = jnp.zeros((BACK_KEYS, PAIR), F32)
        for head in range(2):
            feats = slice(head * HEAD_DIM, (head + 1) * HEAD_DIM)
            scores = mul(keys_s[head, span], q_s[head], NT)
            prob = jnp.exp2(scores * factor - lse_ref[0, head : head + 1, :])
            prob_grad = mul(v_ref[span, :], do_s[head], NT)
            score_grad = (prob * (prob_grad - delta_s[head : head + 1, :])).astype(BF16)
            value_grad += mul(prob.astype(BF16), do_s[head])
            key_grad += mul(score_grad, qz_s[head])
            turned[head] += mul(kt_s[feats, span], score_grad)
        dm_ref[span, PAIR : 2 * PAIR] = (key_grad * SCORE_SCALE).astype(BF16)
        dm_ref[span, 2 * PAIR : 3 * PAIR] = value_grad.astype(BF16)
    query_grad = jnp.concatenate(turned, axis=0) * SCORE_SCALE
    dm_ref[:, 0:PAIR] = query_grad.T.astype(BF16)
    grad = mul(n_turn_ref[...], dm_ref[...]).astype(BF16)

    @pl.when(pl.program_id(0) == 0)
    def _():
        first_ref[...] = grad

    @pl.when(pl.program_id(0) == 1)
    def _():
        second_ref[...] = grad


def attend_back(limit, mixed, ctx_turn, lse, context_grad, n_turn, first):
    length = mixed.shape[0]
    features = n_turn.shape[0]
    pair = lambda i: first - i
    column = lambda c: pl.BlockSpec((length, PAIR), lambda i, s: (0, pair(i) * 3 + c))
    return pl.pallas_call(
        attend_back_kernel,
        grid_spec=pltpu.PrefetchScalarGridSpec(
            num_scalar_prefetch=1,
            grid=(2,),
            in_specs=[
                column(0), column(1), column(2),
                pl.BlockSpec((PAIR, length), lambda i, s: (pair(i), 0)),
                pl.BlockSpec((1, 2, length), lambda i, s: (pair(i), 0, 0)),
                pl.BlockSpec((length, PAIR), lambda i, s: (0, pair(i))),
                pl.BlockSpec((features, length), lambda i, s: (0, 0)),
            ],
            out_specs=[
                pl.BlockSpec((length, 3 * PAIR), lambda i, s: (0, i)),
                pl.BlockSpec((features, 3 * PAIR), lambda i, s: (0, 0)),
                pl.BlockSpec((features, 3 * PAIR), lambda i, s: (0, 0)),
            ],
            scratch_shapes=[
                pltpu.VMEM((2, length, PAIR), BF16),
                pltpu.VMEM((2, length, PAIR), BF16),
                pltpu.VMEM((2, length, PAIR), BF16),
                pltpu.VMEM((2, length, PAIR), BF16),
                pltpu.VMEM((PAIR, length), BF16),
                pltpu.VMEM((8, length), F32),
            ],
        ),
        out_shape=[
            jax.ShapeDtypeStruct((length, 2 * 3 * PAIR), BF16),
            jax.ShapeDtypeStruct((features, 3 * PAIR), BF16),
            jax.ShapeDtypeStruct((features, 3 * PAIR), BF16),
        ],
        compiler_params=params(28),
        cost_estimate=cost(16),
        name="attend_back",
    )(limit, mixed, mixed, mixed, ctx_turn, lse, context_grad, n_turn)


def begin_kernel(
    limit_ref, x_ref, clock_ref, gain_ref, gg_two_ref, mg_ref, w_ref, high_ref, low_ref, bg_ref, gg_s
):
    step = pl.program_id(0)
    _, parts, tall, width = bg_ref.shape
    tokens = tall - SPARE
    blocks = ROWS // tokens
    spot = pl.ds(step * blocks, blocks)

    @pl.when(step == 0)
    def _():
        gg_s[...] = jnp.zeros_like(gg_s)

    @pl.when(step * ROWS < limit_ref[0])
    def _():
        begin = join_tokens(x_ref) + clock_ref[...]
        unit, inverse = norm_parts(begin)
        one_grad = jnp.zeros_like(begin)
        for part, (d_ref, at) in enumerate(((low_ref, 1), (low_ref, 0), (high_ref, 1), (high_ref, 0))):
            columns = slice(part * 3 * PAIR, (part + 1) * 3 * PAIR)
            own = slice(at * 3 * PAIR, (at + 1) * 3 * PAIR)
            one_grad += mul(d_ref[:, own], w_ref[:, columns], NT)
        gg_s[...] += jnp.sum(one_grad * unit, axis=0, keepdims=True)
        total = (mg_ref[...] + norm_back(one_grad, gain_ref[...], unit, inverse)).astype(BF16)
        for part in range(parts):
            piece = total[:, part * width : (part + 1) * width]
            bg_ref[spot, part, 0:tokens] = piece.reshape(blocks, tokens, width)

    @pl.when(step * ROWS >= limit_ref[0])
    def _():
        bg_ref[spot] = jnp.zeros((blocks,) + bg_ref.shape[1:], BF16)

    @pl.when(step == pl.num_programs(0) - 1)
    def _():
        rows = []
        for ref in (gg_s, gg_two_ref):
            for part in range(parts):
                rows.append(ref[:, part * width : (part + 1) * width])
        bg_ref[:, :, tokens:tall] = jnp.broadcast_to(
            jnp.concatenate(rows, axis=0).astype(BF16), bg_ref.shape[:2] + (SPARE, width)
        )


def begin_block(limit, x_blocks, clock, gain, two_grad, w_wide, middle_grad, high, low):
    senders, feature_parts, tall, width = x_blocks.shape
    tokens = tall - SPARE
    length = senders * tokens
    features = feature_parts * width
    take = ROWS // tokens
    whole = lambda array: pl.BlockSpec(array.shape, lambda i, s: (0,) * array.ndim)
    rows = lambda n: pl.BlockSpec((ROWS, n), lambda i, s: (i, 0))
    return pl.pallas_call(
        begin_kernel,
        grid_spec=pltpu.PrefetchScalarGridSpec(
            num_scalar_prefetch=1,
            grid=(length // ROWS,),
            in_specs=[
                pl.BlockSpec((take, feature_parts, tall, width), lambda i, s: (i, 0, 0, 0)),
                whole(clock), whole(gain), whole(two_grad), rows(features), whole(w_wide),
            ]
            + [rows(6 * PAIR)] * 2,
            out_specs=whole(x_blocks),
            scratch_shapes=[pltpu.VMEM((1, features), F32)],
        ),
        out_shape=jax.ShapeDtypeStruct(x_blocks.shape, BF16),
        compiler_params=params(20),
        cost_estimate=cost(7),
        name="begin_back",
    )(limit, x_blocks, clock, gain, two_grad, middle_grad, w_wide, high, low)


DIRECT = 8


def clock_rows(step_ids, features):
    half_width = features // 2
    ladder = jnp.arange(half_width, dtype=F32) / half_width
    rate_rows = jnp.exp(-math.log(10000.0) * ladder)
    angles = step_ids.astype(F32)[:, None] * rate_rows[None, :]
    return jnp.concatenate([jnp.sin(angles), jnp.cos(angles)], axis=-1)


def swap(value, apart):
    count = lax.axis_size("tensor")
    return lax.ppermute(value, "tensor", [(i, i ^ apart) for i in range(count)])


def along_dp(value, move):
    count = lax.axis_size("dp")
    return lax.ppermute(value, "dp", [(i, move(i)) for i in range(count)])


def across(value):
    return along_dp(value, lambda i: i ^ 1)


def ahead(value, step):
    count = lax.axis_size("dp") // 2
    return along_dp(value, lambda i: (i // 2 + step) % count * 2 + i % 2)


def places():
    count = lax.axis_size("dp") // 2
    own = lax.axis_index("dp")
    coarse = (own // 2 - jnp.arange(count, dtype=jnp.int32)) % count
    return jnp.concatenate([coarse * 2 + own % 2, coarse * 2 + 1 - own % 2])


def collect_coarse(shard):
    count = lax.axis_size("dp") // 2
    return jnp.concatenate([shard] + [ahead(shard, step) for step in range(1, count)], axis=0)


def collect_rows(shard):
    count = lax.axis_size("dp")
    rows = lax.all_to_all(
        jnp.broadcast_to(shard[None], (count,) + shard.shape), "dp", 0, 0, tiled=True
    )
    return rows.reshape(count * shard.shape[0], shard.shape[1])


def collect_columns(rows):
    far = swap(rows, 2)
    return rows, swap(rows, 1), far, swap(far, 1)


def add(*values):
    return add_wide(*values).astype(BF16)


def fold_pair(values):
    own = lax.axis_index("dp") % 2
    pick = lambda value, which: lax.dynamic_index_in_dim(value, which, value.ndim - 3, keepdims=False)
    sent = add(*[pick(value, 1 - own) for value in values])
    return sent, lambda: [pick(value, own) for value in values] + [across(sent)]


def fold_far(values):
    sent = add(*[value[0] for value in values])
    return sent, lambda: [value[1] for value in values] + [swap(sent, 2)]


def fold_coarse(values):
    count = lax.axis_size("dp") // 2
    own = lax.axis_index("dp") // 2
    pick = lambda value, which: lax.dynamic_index_in_dim(value, which % count, 0, keepdims=False)
    value = add(*values)
    came = [ahead(pick(value, own + step), step) for step in range(1, count)]
    return value, [pick(value, own)] + came


def add_wide(*values):
    total = values[0].astype(F32)
    for value in values[1:]:
        total += value.astype(F32)
    return total


def grouped(value):
    count = lax.axis_size("dp")
    two, rows, columns = value.shape
    return value.reshape(two, count // 2, 2, rows // count, columns)


def exchange_rows(value):
    count = lax.axis_size("dp")
    groups = value.reshape(count, value.shape[0] // count, value.shape[1])
    return jnp.sum(lax.all_to_all(groups, "dp", 0, 0, tiled=True).astype(F32), axis=0)


def three_terms(values):
    terms = []
    for _ in range(3):
        term = lax.reduce_precision(values, 8, 7)
        terms.append(term.astype(BF16))
        values = values - term
    return terms


def together(*values):
    return lax.optimization_barrier(values)


def after(value, *others):
    return lax.optimization_barrier((value,) + others)[0]


def on_device(
    states, timesteps, lengths, deal_order, w_qkv, w_out, w_up, w_down, gain_attn, gain_ffn, out_grad
):
    both = ("dp", "tensor")
    dp_count = lax.axis_size("dp")
    tensor_count = lax.axis_size("tensor")
    devices = dp_count * tensor_count
    total_seqs, tokens, width = states.shape
    assert tensor_count == 4 and total_seqs == devices
    features = width * tensor_count
    own = lax.axis_index("dp") * tensor_count + lax.axis_index("tensor")
    own_id = lax.dynamic_slice_in_dim(deal_order, own, 1)
    limit = lengths[own_id]
    clock = clock_rows(timesteps[own_id], features)
    per = gain_attn.shape[0]
    rows = w_qkv.shape[0]
    hidden = w_up.shape[1]

    rest = jnp.concatenate([w_out.T, w_up, w_down.T], axis=1)
    qkv = w_qkv.reshape(rows, -1)
    direct = dp_count <= DIRECT
    if direct:
        place, groups = places(), dp_count
        first = collect_coarse(jnp.concatenate([qkv, rest], axis=1))
        qkv_rows = first[:, : qkv.shape[1]]
        qkv_other = across(qkv_rows)
        qkv_parts = collect_columns(jnp.concatenate([qkv_rows, qkv_other], axis=0))
        mine = after(first[:, qkv.shape[1] :], qkv_other)
        other, far_mine = in_hbm(across(mine)), in_hbm(swap(after(mine, qkv_parts[2]), 2))
    else:
        place, groups = jnp.zeros((1,), jnp.int32), None
        first = collect_rows(qkv)
        qkv_parts = collect_columns(first)
        rest_parts = [(part,) for part in collect_columns(collect_rows(rest))]

    spare = jnp.stack(three_terms(gain_attn) + three_terms(gain_ffn)).reshape(1, 6 * per)
    spare = jnp.pad(spare, ((0, SPARE - 1), (0, width - 6 * per)))
    by_tensor = deal_order.reshape(dp_count, tensor_count).T.reshape(devices)
    arranged = jnp.concatenate(
        [states[by_tensor], jnp.broadcast_to(spare[None], (devices, SPARE, width))], axis=1
    )
    arranged = lax.all_to_all(arranged, "tensor", 0, 0, tiled=True)
    arranged = arranged.reshape(tensor_count, dp_count, tokens + SPARE, width).swapaxes(0, 1)
    x_blocks = lax.all_to_all(after(arranged, first), "dp", 0, 0, tiled=True)
    x_blocks = x_blocks.reshape(devices, tokens + SPARE, width)
    gains = jnp.sum(x_blocks[:, tokens, : 6 * per].reshape(devices, 2, 3, per).astype(F32), axis=2)
    gain_one = gains[:, 0].reshape(1, features)
    gain_two = gains[:, 1].reshape(1, features)
    x_blocks = x_blocks.reshape(dp_count, tensor_count, tokens + SPARE, width)

    mixed, n_one_turn, qkv_wide = project(
        limit, place, groups, x_blocks, clock, gain_one, qkv_parts
    )
    if direct:
        mixed, other = together(mixed, other)
        near_mine, near_other = in_hbm(swap(after(mine, mixed), 1)), in_hbm(swap(other, 1))
        far_other = in_hbm(swap(other, 2))
    ctx, ctx_turn, lse = attend(limit, mixed, tensor_count)
    if direct:
        ctx, near_mine, near_other, far_mine, far_other = together(
            ctx, near_mine, near_other, far_mine, far_other
        )
        last_mine, last_other = swap(far_mine, 1), swap(far_other, 1)
        rest_parts = (
            (mine, other), (near_mine, near_other), (far_mine, far_other), (last_mine, last_other)
        )
    output, context_grad, middle_grad, two_grad, up_send, down_send, up_keep, down_keep = middle_block(
        limit, place, groups, x_blocks, clock, gain_two, ctx, rest_parts, out_grad
    )
    up_came, down_came = swap(up_send, 1), swap(down_send, 1)

    back = functools.partial(attend_back, limit, mixed, ctx_turn, lse)
    if direct:
        down_sent, down_rest = fold_far([grouped(value) for value in (down_keep, down_came)])
        up_sent, up_rest = fold_pair([grouped(value) for value in (up_keep, up_came)])
        context_grad = after(context_grad, down_sent, up_sent)
    high, three, two = back(context_grad, n_one_turn, 3)
    if direct:
        *down_rest, down_came = down_rest()
        *up_rest, up_came = up_rest()
        high, three, two, down_came, up_came = together(high, three, two, down_came, up_came)
        down_value, down_pieces = fold_coarse([*down_rest, down_came])
        up_sent, up_rest = fold_far([add(*up_rest, up_came)])
        context_grad = after(context_grad, down_value, up_sent)
    far = add(two, swap(three, 1))
    came_far = swap(far, 2)
    low, one, own_part = back(after(context_grad, high, far), n_one_turn, 1)
    if direct:
        *up_rest, up_came = up_rest()
        low, one, own_part, up_came, came_far, *down_pieces = together(
            low, one, own_part, up_came, came_far, *down_pieces
        )
        up_value, up_pieces = fold_coarse([*up_rest, up_came])
        down_sent, down_rest = fold_pair([add_wide(*down_pieces)[..., None, :, :, :]])
        middle_grad = after(middle_grad, up_value, down_sent)
    came_one = swap(one, 1)
    begin_grad = begin_block(
        limit, x_blocks, clock, gain_one, two_grad, qkv_wide, middle_grad, high, low
    )
    if direct:
        begin_grad, came_one = together(begin_grad, came_one)
        near = [grouped(value[None])[0] for value in (own_part, came_one, came_far)]
        qkv_value, qkv_pieces = fold_coarse(fold_pair(near)[1]())
        *up_pieces, down_came, _ = together(*up_pieces, down_rest()[-1], qkv_value)
        up_total = add_wide(*up_pieces)
        down_total = add_wide(*down_rest()[:-1], down_came)[0]
        qkv_total = add_wide(*qkv_pieces)
    else:
        up_total = exchange_rows(add(*fold_far([up_keep, up_came])[1]()))
        down_total = exchange_rows(add(*fold_far([down_keep, down_came])[1]()))
        qkv_total = exchange_rows(add(own_part, came_one, came_far))
    returned = lax.all_to_all(
        begin_grad.reshape(devices, tokens + SPARE, width), both, 0, 0, tiled=True
    )
    inverse = (
        jnp.zeros((total_seqs,), jnp.int32)
        .at[deal_order]
        .set(jnp.arange(total_seqs, dtype=jnp.int32))
    )
    states_grad = returned[inverse][:, :tokens]
    gain_grads = jnp.sum(returned[:, tokens:].astype(F32), axis=0).reshape(2, devices, per)
    gain_grads = lax.dynamic_index_in_dim(gain_grads, own, 1, keepdims=False)
    return (
        output,
        states_grad,
        qkv_total.reshape(w_qkv.shape),
        up_total[:, :PAIR].T,
        up_total[:, PAIR:],
        down_total.T,
        gain_grads[0],
        gain_grads[1],
    )


def solution(mesh):
    in_specs = (
        P(None, "dp", "tensor"),
        P(),
        P(),
        P(),
        P("dp", None, "tensor"),
        P("tensor", "dp"),
        P("dp", "tensor"),
        P("tensor", "dp"),
        P(("dp", "tensor")),
        P(("dp", "tensor")),
        P(("dp", "tensor"), None, None),
    )
    out_specs = (
        P(("dp", "tensor"), None, None),
        P(None, "dp", "tensor"),
        P("dp", None, "tensor"),
        P("tensor", "dp"),
        P("dp", "tensor"),
        P("tensor", "dp"),
        P(("dp", "tensor")),
        P(("dp", "tensor")),
    )
    return jax.shard_map(
        on_device, mesh=mesh, in_specs=in_specs, out_specs=out_specs, check_vma=False
    )
```

```python
import functools
import math

import jax
import jax.numpy as jnp
from jax import lax
from jax.experimental import pallas as pl
from jax.experimental.pallas import tpu as pltpu
from jax.sharding import PartitionSpec as P

HEAD_DIM = 64
PAIR = 2 * HEAD_DIM
ROWS = 512
KEYS = 256
BACK_KEYS = 512
SPARE = 8
SCORE_SCALE = 1.0 / math.sqrt(HEAD_DIM)
LOG2E = math.log2(math.e)
F32 = jnp.float32
BF16 = jnp.bfloat16
NN = (((1,), (0,)), ((), ()))
NT = (((1,), (1,)), ((), ()))
MIB = 1024 * 1024


def mul(lhs, rhs, dims=NN):
    return lax.dot_general(lhs, rhs, dims, preferred_element_type=F32)


def join_tokens(ref):
    blocks, parts, tall, width = ref.shape
    tokens = tall - SPARE
    return jnp.concatenate(
        [ref[:, part, 0:tokens].reshape(blocks * tokens, width) for part in range(parts)], axis=-1
    ).astype(F32)


def place_rows(groups, place_ref, first, source, targets):
    if groups is None:
        for target, columns, own in targets:
            target[:, columns] = source[:, own]
        return
    rows = source.shape[0] // groups
    for group in range(groups):
        spot = pl.ds(pl.multiple_of(place_ref[first + group] * rows, rows), rows)
        for target, columns, own in targets:
            target[spot, columns] = source[group * rows : (group + 1) * rows, own]


def norm_parts(values):
    center = values - jnp.mean(values, axis=-1, keepdims=True)
    spread = jnp.mean(center * center, axis=-1, keepdims=True)
    inverse = lax.rsqrt(spread + 1e-05)
    return center * inverse, inverse


def norm_back(grad, gain, unit, inverse):
    scaled = grad * gain
    mean_scaled = jnp.mean(scaled, axis=-1, keepdims=True)
    mean_along = jnp.mean(scaled * unit, axis=-1, keepdims=True)
    return inverse * (scaled - mean_scaled - unit * mean_along)


def in_hbm(value):
    return pltpu.with_memory_space_constraint(value, pltpu.HBM)


def cost(microseconds):
    return pl.CostEstimate(
        flops=int(microseconds * 1.15e9), bytes_accessed=1 << 20, transcendentals=0
    )


def params(mebibytes):
    return pltpu.CompilerParams(vmem_limit_bytes=mebibytes * MIB)


def project_kernel(groups, limit_ref, place_ref, x_ref, clock_ref, gain_ref, *refs):
    w_refs, (mixed_ref, n_turn_ref, wide) = refs[:-3], refs[-3:]
    step = pl.program_id(0)

    @pl.when(step == 0)
    def _():
        for part, w_ref in enumerate(w_refs):
            width = w_ref.shape[1]
            columns = slice(part * width, (part + 1) * width)
            place_rows(groups, place_ref, 0, w_ref, [(wide, columns, slice(0, width))])

    @pl.when(step * ROWS < limit_ref[0])
    def _():
        begin = join_tokens(x_ref) + clock_ref[...]
        unit, _ = norm_parts(begin)
        normed = (unit * gain_ref[...]).astype(BF16)
        n_turn_ref[...] = normed.T
        mixed_ref[...] = mul(normed, wide[...]).astype(BF16)

    @pl.when(step * ROWS >= limit_ref[0])
    def _():
        n_turn_ref[...] = jnp.zeros_like(n_turn_ref)
        mixed_ref[...] = jnp.zeros_like(mixed_ref)


def project(limit, place, groups, x_blocks, clock, gain, w_parts):
    senders, feature_parts, tall, width = x_blocks.shape
    tokens = tall - SPARE
    length = senders * tokens
    features = feature_parts * width
    parts, columns = len(w_parts), w_parts[0].shape[1]
    take = ROWS // tokens
    return pl.pallas_call(
        functools.partial(project_kernel, groups),
        grid_spec=pltpu.PrefetchScalarGridSpec(
            num_scalar_prefetch=2,
            grid=(length // ROWS,),
            in_specs=[
                pl.BlockSpec((take, feature_parts, tall, width), lambda i, *s: (i, 0, 0, 0)),
                pl.BlockSpec((1, features), lambda i, *s: (0, 0)),
                pl.BlockSpec((1, features), lambda i, *s: (0, 0)),
            ]
            + [pl.BlockSpec((features, columns), lambda i, *s: (0, 0))] * parts,
            out_specs=[
                pl.BlockSpec((ROWS, parts * columns), lambda i, *s: (i, 0)),
                pl.BlockSpec((features, ROWS), lambda i, *s: (0, i)),
                pl.BlockSpec((features, parts * columns), lambda i, *s: (0, 0)),
            ],
        ),
        out_shape=[
            jax.ShapeDtypeStruct((length, parts * columns), BF16),
            pltpu.HBM((features, length), BF16),
            pltpu.HBM((features, parts * columns), BF16),
        ],
        compiler_params=params(20),
        cost_estimate=cost(5),
        name="project",
    )(limit, place, x_blocks, clock, gain, *w_parts)


def head_lanes(shape, head):
    lane = lax.broadcasted_iota(jnp.int32, shape, 1)
    return (lane >= head * HEAD_DIM) & (lane < (head + 1) * HEAD_DIM)


def spare_lane(shape, head):
    lane = lax.broadcasted_iota(jnp.int32, shape, 1)
    return lane == (1 - head) * HEAD_DIM


def masked_keys(keys, head, limit):
    row = lax.broadcasted_iota(jnp.int32, keys.shape, 0)
    spare = jnp.where(
        spare_lane(keys.shape, head) & (row >= limit), jnp.asarray(-1e30, F32), jnp.asarray(0.0, F32)
    )
    return jnp.where(head_lanes(keys.shape, head), keys.astype(F32), spare).astype(BF16)


def own_lanes(values, head):
    return jnp.where(head_lanes(values.shape, head), values.astype(F32), 0.0).astype(BF16)


def masked_queries(queries, head):
    spare = jnp.where(spare_lane(queries.shape, head), jnp.asarray(1.0, F32), jnp.asarray(0.0, F32))
    return jnp.where(head_lanes(queries.shape, head), queries.astype(F32), spare).astype(BF16)


def attend_kernel(limit_ref, q_ref, k_ref, v_ref, ctx_ref, turn_ref, lse_ref, keys_s, q_s, vt_s, sc_s):
    length = q_ref.shape[0]
    vt_s[...] = v_ref[...].astype(F32).T.astype(BF16)
    for head in range(2):
        keys_s[head] = masked_keys(k_ref[...], head, limit_ref[0])
        q_s[head] = masked_queries(q_ref[...], head)
    factor = SCORE_SCALE * LOG2E
    spans = [slice(at, at + KEYS) for at in range(0, length, KEYS)]
    outs = []
    for head in range(2):
        feats = slice(head * HEAD_DIM, (head + 1) * HEAD_DIM)
        peak = None
        for span in spans:
            scores = mul(keys_s[head, span], q_s[head], NT)
            sc_s[head, span] = scores
            high = jnp.max(scores, axis=0, keepdims=True)
            peak = high if peak is None else jnp.maximum(peak, high)
        peak = peak * factor
        total = jnp.zeros_like(peak)
        gathered = jnp.zeros((HEAD_DIM, length), F32)
        for span in spans:
            expo = jnp.exp2(sc_s[head, span] * factor - peak)
            total += jnp.sum(expo, axis=0, keepdims=True)
            gathered += mul(vt_s[feats, span], expo.astype(BF16))
        outs.append(gathered / total)
        lse_ref[0, head : head + 1, :] = peak + jnp.log2(total)
    both = jnp.concatenate(outs, axis=0)
    turn_ref[...] = both.astype(BF16)
    ctx_ref[...] = both.T.astype(BF16)


def attend(limit, mixed, pairs):
    length = mixed.shape[0]
    column = lambda c: pl.BlockSpec((length, PAIR), lambda i, s: (0, i * 3 + c))
    return pl.pallas_call(
        attend_kernel,
        grid_spec=pltpu.PrefetchScalarGridSpec(
            num_scalar_prefetch=1,
            grid=(pairs,),
            in_specs=[column(0), column(1), column(2)],
            out_specs=[
                pl.BlockSpec((length, PAIR), lambda i, s: (0, i)),
                pl.BlockSpec((PAIR, length), lambda i, s: (i, 0)),
                pl.BlockSpec((1, 2, length), lambda i, s: (i, 0, 0)),
            ],
            scratch_shapes=[
                pltpu.VMEM((2, length, PAIR), BF16),
                pltpu.VMEM((2, length, PAIR), BF16),
                pltpu.VMEM((PAIR, length), BF16),
                pltpu.VMEM((2, length, length), F32),
            ],
        ),
        out_shape=[
            pltpu.HBM((length, pairs * PAIR), BF16),
            pltpu.HBM((pairs * PAIR, length), BF16),
            jax.ShapeDtypeStruct((pairs, 2, length), F32),
        ],
        compiler_params=params(28),
        cost_estimate=cost(15),
        name="attend",
    )(limit, mixed, mixed, mixed)


def gelu_both(values):
    root = math.sqrt(2.0 / math.pi)
    scaled = root * values
    inner = scaled * (1.0 + 0.044715 * (values * values))
    tanh = jnp.tanh(inner)
    half = 0.5 + 0.5 * tanh
    slope = half + (1.0 - tanh * tanh) * (1.5 * inner - scaled)
    return values * half, slope


def middle_kernel(
    groups, limit_ref, place_ref, x_ref, clock_ref, gain_ref, ctx_ref, og_ref, *refs
):
    weight_refs, refs = refs[:-17], refs[-17:]
    out_ref, cg_ref, mg_ref, gg_ref, up_send, down_send, up_keep, down_keep = refs[:8]
    wide, units, active_s, ug_s, n_turn, fg_turn, ag_turn, ctx_s, sems = refs[8:]
    step = pl.program_id(0)
    parts, _, hidden = active_s.shape
    blocks = pl.num_programs(0) - parts
    each = len(weight_refs) // parts

    def fetch(part, kind):
        target, wide_, own = (
            (wide, PAIR, slice(0, PAIR)),
            (units, 2 * hidden, slice(PAIR, PAIR + 2 * hidden)),
        )[kind]
        columns = slice(part * wide_, (part + 1) * wide_)
        copies = []
        for at, w_ref in enumerate(weight_refs[part * each : (part + 1) * each]):
            count = 1 if groups is None else groups // each
            rows = w_ref.shape[0] // count
            for group in range(count):
                index = at * count + group
                spot = pl.ds(0, rows)
                if groups is not None:
                    spot = pl.ds(pl.multiple_of(place_ref[index] * rows, rows), rows)
                copies.append(
                    pltpu.make_async_copy(
                        w_ref.at[pl.ds(group * rows, rows), own],
                        target.at[spot, columns],
                        sems.at[kind, part, index],
                    )
                )
        return copies

    @pl.when(step == 0)
    def _():
        gg_ref[...] = jnp.zeros_like(gg_ref)
        for part in range(parts):
            for copy in fetch(part, 0) + fetch(part, 1):
                copy.start()
        for part in range(parts):
            for copy in fetch(part, 0) + fetch(part, 1):
                copy.wait()

    dead = (step < blocks) & (step * ROWS >= limit_ref[0])

    @pl.when((step < blocks) & jnp.logical_not(dead))
    def _():
        spot = pl.ds(pl.multiple_of(step * ROWS, ROWS), ROWS)
        gain = gain_ref[...]
        live = step * ROWS + lax.broadcasted_iota(jnp.int32, (ROWS, 1), 0) < limit_ref[0]
        begin = join_tokens(x_ref) + clock_ref[...]
        middle = begin + mul(ctx_ref[...], wide[...], NT)
        unit, inverse = norm_parts(middle)
        normed = (unit * gain).astype(BF16)
        n_turn[:, spot] = normed.T
        res_grad = jnp.where(live, og_ref[0].astype(F32), 0.0)
        feed_grad = res_grad.astype(BF16)
        fg_turn[:, spot] = feed_grad.T
        feed = jnp.zeros_like(middle)
        two_grad = jnp.zeros_like(middle)
        for part in range(parts):
            up = slice(2 * part * hidden, (2 * part + 1) * hidden)
            down = slice((2 * part + 1) * hidden, (2 * part + 2) * hidden)
            upper = mul(normed, units[:, up])
            active, slope = gelu_both(upper)
            active = active.astype(BF16)
            active_s[part, spot] = active
            feed += mul(active, units[:, down], NT)
            upper_grad = (mul(feed_grad, units[:, down]) * slope).astype(BF16)
            ug_s[part, spot] = upper_grad
            two_grad += mul(upper_grad, units[:, up], NT)
        out_ref[0] = jnp.where(live, middle + feed, 0.0).astype(BF16)
        gg_ref[...] += jnp.sum(two_grad * unit, axis=0, keepdims=True)
        middle_grad = res_grad + norm_back(two_grad, gain, unit, inverse)
        mg_ref[...] = middle_grad
        att_grad = middle_grad.astype(BF16)
        ag_turn[:, spot] = att_grad.T
        cg_ref[...] = mul(att_grad, wide[...]).astype(BF16)
        for part in range(parts):
            ctx_s[part, spot] = ctx_ref[:, part * PAIR : (part + 1) * PAIR]

    @pl.when(dead)
    def _():
        spot = pl.ds(pl.multiple_of(step * ROWS, ROWS), ROWS)
        for ref in (out_ref, cg_ref, mg_ref):
            ref[...] = jnp.zeros_like(ref)
        for ref in (active_s, ug_s, ctx_s):
            ref[:, spot] = jnp.zeros((ref.shape[0], ROWS, ref.shape[2]), BF16)
        for ref in (n_turn, fg_turn, ag_turn):
            ref[:, spot] = jnp.zeros((ref.shape[0], ROWS), BF16)

    @pl.when(step >= blocks)
    def _():
        turn = step - blocks
        part = jnp.where(turn < 2, 3 - 2 * turn, 6 - 2 * turn)
        grads = (
            mul(ag_turn[...], ctx_s[part]).astype(BF16),
            mul(n_turn[...], ug_s[part]).astype(BF16),
            mul(fg_turn[...], active_s[part]).astype(BF16),
        )

        def into(up_ref, down_ref):
            up_ref[0, :, 0:PAIR], up_ref[0, :, PAIR:], down_ref[0] = grads

        pl.when(turn < 2)(lambda: into(up_send, down_send))
        pl.when(turn >= 2)(lambda: into(up_keep, down_keep))


def middle_block(limit, place, groups, x_blocks, clock, gain, ctx, w_parts, out_grad):
    senders, feature_parts, tall, width = x_blocks.shape
    tokens = tall - SPARE
    length = senders * tokens
    features = feature_parts * width
    parts = len(w_parts)
    weights = [in_hbm(w) for part in w_parts for w in part]
    columns = weights[0].shape[1]
    hidden = (columns - PAIR) // 2
    take = ROWS // tokens
    blocks = length // ROWS
    row = lambda i: jnp.minimum(i, blocks - 1)
    whole = lambda array: pl.BlockSpec(
        array.shape, lambda i, *s: (0,) * array.ndim, pipeline_mode=pl.Buffered(1)
    )
    rows = lambda n: pl.BlockSpec((ROWS, n), lambda i, *s: (row(i), 0))
    one = pl.BlockSpec((1, ROWS, features), lambda i, *s: (0, row(i), 0))
    grads = lambda first, n: pl.BlockSpec(
        (1, features, n), lambda i, *s: (jnp.clip(i - blocks - first, 0, 1), 0, 0)
    )
    up_shape = pltpu.HBM((2, features, PAIR + hidden), BF16)
    down_shape = pltpu.HBM((2, features, hidden), BF16)
    return pl.pallas_call(
        functools.partial(middle_kernel, groups),
        grid_spec=pltpu.PrefetchScalarGridSpec(
            num_scalar_prefetch=2,
            grid=(blocks + parts,),
            in_specs=[
                pl.BlockSpec(
                    (take, feature_parts, tall, width), lambda i, *s: (row(i), 0, 0, 0)
                ),
                whole(clock),
                whole(gain),
                rows(features),
                one,
            ]
            + [pl.BlockSpec(memory_space=pltpu.HBM)] * len(weights),
            out_specs=[
                one, rows(features), rows(features),
                pl.BlockSpec((1, features), lambda i, *s: (0, 0)),
                grads(0, PAIR + hidden), grads(0, hidden), grads(2, PAIR + hidden), grads(2, hidden),
            ],
            scratch_shapes=[
                pltpu.VMEM((features, parts * PAIR), BF16),
                pltpu.VMEM((features, parts * 2 * hidden), BF16),
                pltpu.VMEM((parts, length, hidden), BF16),
                pltpu.VMEM((parts, length, hidden), BF16),
                pltpu.VMEM((features, length), BF16),
                pltpu.VMEM((features, length), BF16),
                pltpu.VMEM((features, length), BF16),
                pltpu.VMEM((parts, length, PAIR), BF16),
                pltpu.SemaphoreType.DMA((2, parts, groups or 1)),
            ],
        ),
        out_shape=[
            jax.ShapeDtypeStruct((1, length, features), BF16),
            pltpu.HBM((length, features), BF16),
            pltpu.HBM((length, features), F32),
            jax.ShapeDtypeStruct((1, features), F32),
            up_shape, down_shape, up_shape, down_shape,
        ],
        compiler_params=params(48),
        cost_estimate=cost(25),
        name="middle",
    )(limit, place, x_blocks, clock, gain, in_hbm(ctx), in_hbm(out_grad), *weights)


def attend_back_kernel(
    limit_ref, q_ref, k_ref, v_ref, turn_ref, lse_ref, cg_ref, n_turn_ref,
    dm_ref, first_ref, second_ref, keys_s, q_s, qz_s, do_s, kt_s, delta_s,
):
    limit = limit_ref[0]
    length = q_ref.shape[0]
    kt_s[...] = k_ref[...].astype(F32).T.astype(BF16)
    along = cg_ref[...].astype(F32).T * turn_ref[...].astype(F32)
    for head in range(2):
        feats = slice(head * HEAD_DIM, (head + 1) * HEAD_DIM)
        delta_s[head : head + 1, :] = jnp.sum(along[feats, :], axis=0, keepdims=True)
        keys_s[head] = masked_keys(k_ref[...], head, limit)
        q_s[head] = masked_queries(q_ref[...], head)
        qz_s[head] = own_lanes(q_ref[...], head)
        do_s[head] = own_lanes(cg_ref[...], head)
    factor = SCORE_SCALE * LOG2E
    turned = [jnp.zeros((HEAD_DIM, length), F32)] * 2
    for at in range(0, length, BACK_KEYS):
        span = slice(at, at + BACK_KEYS)
        key_grad = jnp.zeros((BACK_KEYS, PAIR), F32)
        value_grad = jnp.zeros((BACK_KEYS, PAIR), F32)
        for head in range(2):
            feats = slice(head * HEAD_DIM, (head + 1) * HEAD_DIM)
            scores = mul(keys_s[head, span], q_s[head], NT)
            prob = jnp.exp2(scores * factor - lse_ref[0, head : head + 1, :])
            prob_grad = mul(v_ref[span, :], do_s[head], NT)
            score_grad = (prob * (prob_grad - delta_s[head : head + 1, :])).astype(BF16)
            value_grad += mul(prob.astype(BF16), do_s[head])
            key_grad += mul(score_grad, qz_s[head])
            turned[head] += mul(kt_s[feats, span], score_grad)
        dm_ref[span, PAIR : 2 * PAIR] = (key_grad * SCORE_SCALE).astype(BF16)
        dm_ref[span, 2 * PAIR : 3 * PAIR] = value_grad.astype(BF16)
    query_grad = jnp.concatenate(turned, axis=0) * SCORE_SCALE
    dm_ref[:, 0:PAIR] = query_grad.T.astype(BF16)
    grad = mul(n_turn_ref[...], dm_ref[...]).astype(BF16)

    @pl.when(pl.program_id(0) == 0)
    def _():
        first_ref[...] = grad

    @pl.when(pl.program_id(0) == 1)
    def _():
        second_ref[...] = grad


def attend_back(limit, mixed, ctx_turn, lse, context_grad, n_turn, first):
    length = mixed.shape[0]
    features = n_turn.shape[0]
    pair = lambda i: first - i
    column = lambda c: pl.BlockSpec((length, PAIR), lambda i, s: (0, pair(i) * 3 + c))
    return pl.pallas_call(
        attend_back_kernel,
        grid_spec=pltpu.PrefetchScalarGridSpec(
            num_scalar_prefetch=1,
            grid=(2,),
            in_specs=[
                column(0), column(1), column(2),
                pl.BlockSpec((PAIR, length), lambda i, s: (pair(i), 0)),
                pl.BlockSpec((1, 2, length), lambda i, s: (pair(i), 0, 0)),
                pl.BlockSpec((length, PAIR), lambda i, s: (0, pair(i))),
                pl.BlockSpec((features, length), lambda i, s: (0, 0)),
            ],
            out_specs=[
                pl.BlockSpec((length, 3 * PAIR), lambda i, s: (0, i)),
                pl.BlockSpec((features, 3 * PAIR), lambda i, s: (0, 0)),
                pl.BlockSpec((features, 3 * PAIR), lambda i, s: (0, 0)),
            ],
            scratch_shapes=[
                pltpu.VMEM((2, length, PAIR), BF16),
                pltpu.VMEM((2, length, PAIR), BF16),
                pltpu.VMEM((2, length, PAIR), BF16),
                pltpu.VMEM((2, length, PAIR), BF16),
                pltpu.VMEM((PAIR, length), BF16),
                pltpu.VMEM((8, length), F32),
            ],
        ),
        out_shape=[
            jax.ShapeDtypeStruct((length, 2 * 3 * PAIR), BF16),
            jax.ShapeDtypeStruct((features, 3 * PAIR), BF16),
            jax.ShapeDtypeStruct((features, 3 * PAIR), BF16),
        ],
        compiler_params=params(28),
        cost_estimate=cost(16),
        name="attend_back",
    )(limit, mixed, mixed, mixed, ctx_turn, lse, context_grad, n_turn)


def begin_kernel(
    limit_ref, x_ref, clock_ref, gain_ref, gg_two_ref, mg_ref, w_ref, high_ref, low_ref, bg_ref, gg_s
):
    step = pl.program_id(0)
    _, parts, tall, width = bg_ref.shape
    tokens = tall - SPARE
    blocks = ROWS // tokens
    spot = pl.ds(step * blocks, blocks)

    @pl.when(step == 0)
    def _():
        gg_s[...] = jnp.zeros_like(gg_s)

    @pl.when(step * ROWS < limit_ref[0])
    def _():
        begin = join_tokens(x_ref) + clock_ref[...]
        unit, inverse = norm_parts(begin)
        one_grad = jnp.zeros_like(begin)
        for part, (d_ref, at) in enumerate(((low_ref, 1), (low_ref, 0), (high_ref, 1), (high_ref, 0))):
            columns = slice(part * 3 * PAIR, (part + 1) * 3 * PAIR)
            own = slice(at * 3 * PAIR, (at + 1) * 3 * PAIR)
            one_grad += mul(d_ref[:, own], w_ref[:, columns], NT)
        gg_s[...] += jnp.sum(one_grad * unit, axis=0, keepdims=True)
        total = (mg_ref[...] + norm_back(one_grad, gain_ref[...], unit, inverse)).astype(BF16)
        for part in range(parts):
            piece = total[:, part * width : (part + 1) * width]
            bg_ref[spot, part, 0:tokens] = piece.reshape(blocks, tokens, width)

    @pl.when(step * ROWS >= limit_ref[0])
    def _():
        bg_ref[spot] = jnp.zeros((blocks,) + bg_ref.shape[1:], BF16)

    @pl.when(step == pl.num_programs(0) - 1)
    def _():
        rows = []
        for ref in (gg_s, gg_two_ref):
            for part in range(parts):
                rows.append(ref[:, part * width : (part + 1) * width])
        bg_ref[:, :, tokens:tall] = jnp.broadcast_to(
            jnp.concatenate(rows, axis=0).astype(BF16), bg_ref.shape[:2] + (SPARE, width)
        )


def begin_block(limit, x_blocks, clock, gain, two_grad, w_wide, middle_grad, high, low):
    senders, feature_parts, tall, width = x_blocks.shape
    tokens = tall - SPARE
    length = senders * tokens
    features = feature_parts * width
    take = ROWS // tokens
    whole = lambda array: pl.BlockSpec(array.shape, lambda i, s: (0,) * array.ndim)
    rows = lambda n: pl.BlockSpec((ROWS, n), lambda i, s: (i, 0))
    return pl.pallas_call(
        begin_kernel,
        grid_spec=pltpu.PrefetchScalarGridSpec(
            num_scalar_prefetch=1,
            grid=(length // ROWS,),
            in_specs=[
                pl.BlockSpec((take, feature_parts, tall, width), lambda i, s: (i, 0, 0, 0)),
                whole(clock), whole(gain), whole(two_grad), rows(features), whole(w_wide),
            ]
            + [rows(6 * PAIR)] * 2,
            out_specs=whole(x_blocks),
            scratch_shapes=[pltpu.VMEM((1, features), F32)],
        ),
        out_shape=jax.ShapeDtypeStruct(x_blocks.shape, BF16),
        compiler_params=params(20),
        cost_estimate=cost(7),
        name="begin_back",
    )(limit, x_blocks, clock, gain, two_grad, middle_grad, w_wide, high, low)


DIRECT = 8


def clock_rows(step_ids, features):
    half_width = features // 2
    ladder = jnp.arange(half_width, dtype=F32) / half_width
    rate_rows = jnp.exp(-math.log(10000.0) * ladder)
    angles = step_ids.astype(F32)[:, None] * rate_rows[None, :]
    return jnp.concatenate([jnp.sin(angles), jnp.cos(angles)], axis=-1)


def swap(value, apart):
    count = lax.axis_size("tensor")
    return lax.ppermute(value, "tensor", [(i, i ^ apart) for i in range(count)])


def along_dp(value, move):
    count = lax.axis_size("dp")
    return lax.ppermute(value, "dp", [(i, move(i)) for i in range(count)])


def across(value):
    return ahead(value, 0, 1)


def ahead(value, step, flip=0):
    count = lax.axis_size("dp") // 2
    return along_dp(value, lambda i: (i // 2 + step) % count * 2 + (i + flip) % 2)


def places():
    count = lax.axis_size("dp") // 2
    own = lax.axis_index("dp")
    coarse = (own // 2 - jnp.arange(count, dtype=jnp.int32)) % count
    return jnp.concatenate([coarse * 2 + own % 2, coarse * 2 + 1 - own % 2])


def collect_coarse(shard, flips=(0,)):
    count = lax.axis_size("dp") // 2
    pieces = [ahead(shard, step, flip) for flip in flips for step in range(count)[1 - flip :]]
    return jnp.concatenate([shard] + pieces, axis=0)


def collect_rows(shard):
    count = lax.axis_size("dp")
    rows = lax.all_to_all(
        jnp.broadcast_to(shard[None], (count,) + shard.shape), "dp", 0, 0, tiled=True
    )
    return rows.reshape(count * shard.shape[0], shard.shape[1])


def collect_columns(rows):
    far = swap(rows, 2)
    return rows, swap(rows, 1), far, swap(far, 1)


def add(*values):
    return add_wide(*values).astype(BF16)


def fold_pair(values):
    own = lax.axis_index("dp") % 2
    pick = lambda value, which: lax.dynamic_index_in_dim(value, which, value.ndim - 3, keepdims=False)
    sent = add(*[pick(value, 1 - own) for value in values])
    return sent, lambda: [pick(value, own) for value in values] + [across(sent)]


def fold_far(values):
    sent = add(*[value[0] for value in values])
    return sent, lambda: [value[1] for value in values] + [swap(sent, 2)]


def fold_coarse(values):
    count = lax.axis_size("dp") // 2
    own = lax.axis_index("dp") // 2
    pick = lambda value, which: lax.dynamic_index_in_dim(value, which % count, 0, keepdims=False)
    value = add(*values)
    came = [ahead(pick(value, own + step), step) for step in range(1, count)]
    return value, [pick(value, own)] + came


def add_wide(*values):
    total = values[0].astype(F32)
    for value in values[1:]:
        total += value.astype(F32)
    return total


def grouped(value):
    count = lax.axis_size("dp")
    two, rows, columns = value.shape
    return value.reshape(two, count // 2, 2, rows // count, columns)


def exchange_rows(value):
    count = lax.axis_size("dp")
    groups = value.reshape(count, value.shape[0] // count, value.shape[1])
    return jnp.sum(lax.all_to_all(groups, "dp", 0, 0, tiled=True).astype(F32), axis=0)


def three_terms(values):
    terms = []
    for _ in range(3):
        term = lax.reduce_precision(values, 8, 7)
        terms.append(term.astype(BF16))
        values = values - term
    return terms


def together(*values):
    return lax.optimization_barrier(values)


def after(value, *others):
    return lax.optimization_barrier((value,) + others)[0]


def on_device(
    states, timesteps, lengths, deal_order, w_qkv, w_out, w_up, w_down, gain_attn, gain_ffn, out_grad
):
    both = ("dp", "tensor")
    dp_count = lax.axis_size("dp")
    tensor_count = lax.axis_size("tensor")
    devices = dp_count * tensor_count
    total_seqs, tokens, width = states.shape
    assert tensor_count == 4 and total_seqs == devices
    features = width * tensor_count
    own = lax.axis_index("dp") * tensor_count + lax.axis_index("tensor")
    own_id = lax.dynamic_slice_in_dim(deal_order, own, 1)
    limit = lengths[own_id]
    clock = clock_rows(timesteps[own_id], features)
    per = gain_attn.shape[0]
    rows = w_qkv.shape[0]
    hidden = w_up.shape[1]

    rest = jnp.concatenate([w_out.T, w_up, w_down.T], axis=1)
    qkv = w_qkv.reshape(rows, -1)
    direct = dp_count <= DIRECT
    if direct:
        place, groups = places(), dp_count
        qkv_rows = collect_coarse(qkv, (0, 1))
        mine = collect_coarse(rest)
        first = (qkv_rows, mine)
        far_rows, other, far_mine = together(
            swap(qkv_rows, 2), in_hbm(across(mine)), in_hbm(swap(mine, 2))
        )
        qkv_parts = (qkv_rows, swap(qkv_rows, 1), far_rows, swap(far_rows, 1))
    else:
        place, groups = jnp.zeros((1,), jnp.int32), None
        first = (collect_rows(qkv),)
        qkv_parts = collect_columns(first[0])
        rest_parts = [(part,) for part in collect_columns(collect_rows(rest))]

    spare = jnp.stack(three_terms(gain_attn) + three_terms(gain_ffn)).reshape(1, 6 * per)
    spare = jnp.pad(spare, ((0, SPARE - 1), (0, width - 6 * per)))
    by_tensor = deal_order.reshape(dp_count, tensor_count).T.reshape(devices)
    arranged = jnp.concatenate(
        [states[by_tensor], jnp.broadcast_to(spare[None], (devices, SPARE, width))], axis=1
    )
    arranged = lax.all_to_all(arranged, "tensor", 0, 0, tiled=True)
    arranged = arranged.reshape(tensor_count, dp_count, tokens + SPARE, width).swapaxes(0, 1)
    x_blocks = lax.all_to_all(after(arranged, *first), "dp", 0, 0, tiled=True)
    x_blocks = x_blocks.reshape(devices, tokens + SPARE, width)
    gains = jnp.sum(x_blocks[:, tokens, : 6 * per].reshape(devices, 2, 3, per).astype(F32), axis=2)
    gain_one = gains[:, 0].reshape(1, features)
    gain_two = gains[:, 1].reshape(1, features)
    x_blocks = x_blocks.reshape(dp_count, tensor_count, tokens + SPARE, width)

    mixed, n_one_turn, qkv_wide = project(
        limit, place, groups, x_blocks, clock, gain_one, qkv_parts
    )
    if direct:
        near_mine, near_other = in_hbm(swap(mine, 1)), in_hbm(swap(other, 1))
        last_mine, far_other = in_hbm(swap(far_mine, 1)), in_hbm(swap(other, 2))
    ctx, ctx_turn, lse = attend(limit, mixed, tensor_count)
    if direct:
        ctx, near_mine, near_other, last_mine, far_other = together(
            ctx, near_mine, near_other, last_mine, far_other
        )
        last_other = swap(far_other, 1)
        rest_parts = (
            (mine, other), (near_mine, near_other), (far_mine, far_other), (last_mine, last_other)
        )
    output, context_grad, middle_grad, two_grad, up_send, down_send, up_keep, down_keep = middle_block(
        limit, place, groups, x_blocks, clock, gain_two, ctx, rest_parts, out_grad
    )
    up_came, down_came = swap(up_send, 1), swap(down_send, 1)

    back = functools.partial(attend_back, limit, mixed, ctx_turn, lse)
    if direct:
        down_sent, down_rest = fold_far([grouped(value) for value in (down_keep, down_came)])
        up_sent, up_rest = fold_pair([grouped(value) for value in (up_keep, up_came)])
        context_grad = after(context_grad, down_sent, up_sent)
    high, three, two = back(context_grad, n_one_turn, 3)
    if direct:
        *down_rest, down_came = down_rest()
        *up_rest, up_came = up_rest()
        high, three, two, down_came, up_came = together(high, three, two, down_came, up_came)
        down_value, down_pieces = fold_coarse([*down_rest, down_came])
        up_sent, up_rest = fold_far([add(*up_rest, up_came)])
        context_grad = after(context_grad, down_value, up_sent)
    far = add(two, swap(three, 1))
    came_far = swap(far, 2)
    low, one, own_part = back(after(context_grad, high, far), n_one_turn, 1)
    if direct:
        *up_rest, up_came = up_rest()
        low, one, own_part, up_came, came_far, *down_pieces = together(
            low, one, own_part, up_came, came_far, *down_pieces
        )
        up_value, up_pieces = fold_coarse([*up_rest, up_came])
        down_sent, down_rest = fold_pair([add_wide(*down_pieces)[..., None, :, :, :]])
        middle_grad = after(middle_grad, up_value, down_sent)
    came_one = swap(one, 1)
    begin_grad = begin_block(
        limit, x_blocks, clock, gain_one, two_grad, qkv_wide, middle_grad, high, low
    )
    if direct:
        begin_grad, came_one = together(begin_grad, came_one)
        near = [grouped(value[None])[0] for value in (own_part, came_one, came_far)]
        qkv_value, qkv_pieces = fold_coarse(fold_pair(near)[1]())
        *up_pieces, down_came, _ = together(*up_pieces, down_rest()[-1], qkv_value)
        up_total = add_wide(*up_pieces)
        down_total = add_wide(*down_rest()[:-1], down_came)[0]
        qkv_total = add_wide(*qkv_pieces)
    else:
        up_total = exchange_rows(add(*fold_far([up_keep, up_came])[1]()))
        down_total = exchange_rows(add(*fold_far([down_keep, down_came])[1]()))
        qkv_total = exchange_rows(add(own_part, came_one, came_far))
    returned = lax.all_to_all(
        begin_grad.reshape(devices, tokens + SPARE, width), both, 0, 0, tiled=True
    )
    inverse = (
        jnp.zeros((total_seqs,), jnp.int32)
        .at[deal_order]
        .set(jnp.arange(total_seqs, dtype=jnp.int32))
    )
    states_grad = returned[inverse][:, :tokens]
    gain_grads = jnp.sum(returned[:, tokens:].astype(F32), axis=0).reshape(2, devices, per)
    gain_grads = lax.dynamic_index_in_dim(gain_grads, own, 1, keepdims=False)
    return (
        output,
        states_grad,
        qkv_total.reshape(w_qkv.shape),
        up_total[:, :PAIR].T,
        up_total[:, PAIR:],
        down_total.T,
        gain_grads[0],
        gain_grads[1],
    )


def solution(mesh):
    in_specs = (
        P(None, "dp", "tensor"),
        P(),
        P(),
        P(),
        P("dp", None, "tensor"),
        P("tensor", "dp"),
        P("dp", "tensor"),
        P("tensor", "dp"),
        P(("dp", "tensor")),
        P(("dp", "tensor")),
        P(("dp", "tensor"), None, None),
    )
    out_specs = (
        P(("dp", "tensor"), None, None),
        P(None, "dp", "tensor"),
        P("dp", None, "tensor"),
        P("tensor", "dp"),
        P("dp", "tensor"),
        P("tensor", "dp"),
        P(("dp", "tensor")),
        P(("dp", "tensor")),
    )
    return jax.shard_map(
        on_device, mesh=mesh, in_specs=in_specs, out_specs=out_specs, check_vma=False
    )
```

```python
import functools
import math

import jax
import jax.numpy as jnp
from jax import lax
from jax.experimental import pallas as pl
from jax.experimental.pallas import tpu as pltpu
from jax.sharding import PartitionSpec as P

HEAD_DIM = 64
PAIR = 2 * HEAD_DIM
ROWS = 512
KEYS = 256
BACK_KEYS = 512
SPARE = 8
SCORE_SCALE = 1.0 / math.sqrt(HEAD_DIM)
LOG2E = math.log2(math.e)
F32 = jnp.float32
BF16 = jnp.bfloat16
NN = (((1,), (0,)), ((), ()))
NT = (((1,), (1,)), ((), ()))
MIB = 1024 * 1024


def mul(lhs, rhs, dims=NN):
    return lax.dot_general(lhs, rhs, dims, preferred_element_type=F32)


def join_tokens(ref):
    blocks, parts, tall, width = ref.shape
    tokens = tall - SPARE
    return jnp.concatenate(
        [ref[:, part, 0:tokens].reshape(blocks * tokens, width) for part in range(parts)], axis=-1
    ).astype(F32)


def place_rows(groups, place_ref, first, source, targets):
    if groups is None:
        for target, columns, own in targets:
            target[:, columns] = source[:, own]
        return
    rows = source.shape[0] // groups
    for group in range(groups):
        spot = pl.ds(pl.multiple_of(place_ref[first + group] * rows, rows), rows)
        for target, columns, own in targets:
            target[spot, columns] = source[group * rows : (group + 1) * rows, own]


def norm_parts(values):
    center = values - jnp.mean(values, axis=-1, keepdims=True)
    spread = jnp.mean(center * center, axis=-1, keepdims=True)
    inverse = lax.rsqrt(spread + 1e-05)
    return center * inverse, inverse


def norm_back(grad, gain, unit, inverse):
    scaled = grad * gain
    mean_scaled = jnp.mean(scaled, axis=-1, keepdims=True)
    mean_along = jnp.mean(scaled * unit, axis=-1, keepdims=True)
    return inverse * (scaled - mean_scaled - unit * mean_along)


def in_hbm(value):
    return pltpu.with_memory_space_constraint(value, pltpu.HBM)


def cost(microseconds):
    return pl.CostEstimate(
        flops=int(microseconds * 1.15e9), bytes_accessed=1 << 20, transcendentals=0
    )


def params(mebibytes):
    return pltpu.CompilerParams(vmem_limit_bytes=mebibytes * MIB)


def project_kernel(groups, limit_ref, place_ref, x_ref, clock_ref, gain_ref, *refs):
    w_refs, (mixed_ref, n_turn_ref, wide) = refs[:-3], refs[-3:]
    step = pl.program_id(0)

    @pl.when(step == 0)
    def _():
        for part, w_ref in enumerate(w_refs):
            width = w_ref.shape[1]
            columns = slice(part * width, (part + 1) * width)
            place_rows(groups, place_ref, 0, w_ref, [(wide, columns, slice(0, width))])

    @pl.when(step * ROWS < limit_ref[0])
    def _():
        begin = join_tokens(x_ref) + clock_ref[...]
        unit, _ = norm_parts(begin)
        normed = (unit * gain_ref[...]).astype(BF16)
        n_turn_ref[...] = normed.T
        mixed_ref[...] = mul(normed, wide[...]).astype(BF16)

    @pl.when(step * ROWS >= limit_ref[0])
    def _():
        n_turn_ref[...] = jnp.zeros_like(n_turn_ref)
        mixed_ref[...] = jnp.zeros_like(mixed_ref)


def project(limit, place, groups, x_blocks, clock, gain, w_parts):
    senders, feature_parts, tall, width = x_blocks.shape
    tokens = tall - SPARE
    length = senders * tokens
    features = feature_parts * width
    parts, columns = len(w_parts), w_parts[0].shape[1]
    take = ROWS // tokens
    return pl.pallas_call(
        functools.partial(project_kernel, groups),
        grid_spec=pltpu.PrefetchScalarGridSpec(
            num_scalar_prefetch=2,
            grid=(length // ROWS,),
            in_specs=[
                pl.BlockSpec((take, feature_parts, tall, width), lambda i, *s: (i, 0, 0, 0)),
                pl.BlockSpec((1, features), lambda i, *s: (0, 0)),
                pl.BlockSpec((1, features), lambda i, *s: (0, 0)),
            ]
            + [pl.BlockSpec((features, columns), lambda i, *s: (0, 0))] * parts,
            out_specs=[
                pl.BlockSpec((ROWS, parts * columns), lambda i, *s: (i, 0)),
                pl.BlockSpec((features, ROWS), lambda i, *s: (0, i)),
                pl.BlockSpec((features, parts * columns), lambda i, *s: (0, 0)),
            ],
        ),
        out_shape=[
            jax.ShapeDtypeStruct((length, parts * columns), BF16),
            pltpu.HBM((features, length), BF16),
            pltpu.HBM((features, parts * columns), BF16),
        ],
        compiler_params=params(20),
        cost_estimate=cost(5),
        name="project",
    )(limit, place, x_blocks, clock, gain, *w_parts)


def head_lanes(shape, head):
    lane = lax.broadcasted_iota(jnp.int32, shape, 1)
    return (lane >= head * HEAD_DIM) & (lane < (head + 1) * HEAD_DIM)


def spare_lane(shape, head):
    lane = lax.broadcasted_iota(jnp.int32, shape, 1)
    return lane == (1 - head) * HEAD_DIM


def masked_keys(keys, head, limit):
    row = lax.broadcasted_iota(jnp.int32, keys.shape, 0)
    spare = jnp.where(
        spare_lane(keys.shape, head) & (row >= limit), jnp.asarray(-1e30, F32), jnp.asarray(0.0, F32)
    )
    return jnp.where(head_lanes(keys.shape, head), keys.astype(F32), spare).astype(BF16)


def own_lanes(values, head):
    return jnp.where(head_lanes(values.shape, head), values.astype(F32), 0.0).astype(BF16)


def masked_queries(queries, head):
    spare = jnp.where(spare_lane(queries.shape, head), jnp.asarray(1.0, F32), jnp.asarray(0.0, F32))
    return jnp.where(head_lanes(queries.shape, head), queries.astype(F32), spare).astype(BF16)


def attend_kernel(limit_ref, q_ref, k_ref, v_ref, ctx_ref, turn_ref, lse_ref, keys_s, q_s, vt_s, sc_s):
    length = q_ref.shape[0]
    vt_s[...] = v_ref[...].astype(F32).T.astype(BF16)
    for head in range(2):
        keys_s[head] = masked_keys(k_ref[...], head, limit_ref[0])
        q_s[head] = masked_queries(q_ref[...], head)
    factor = SCORE_SCALE * LOG2E
    spans = [slice(at, at + KEYS) for at in range(0, length, KEYS)]
    outs = []
    for head in range(2):
        feats = slice(head * HEAD_DIM, (head + 1) * HEAD_DIM)
        peak = None
        for span in spans:
            scores = mul(keys_s[head, span], q_s[head], NT)
            sc_s[head, span] = scores
            high = jnp.max(scores, axis=0, keepdims=True)
            peak = high if peak is None else jnp.maximum(peak, high)
        peak = peak * factor
        total = jnp.zeros_like(peak)
        gathered = jnp.zeros((HEAD_DIM, length), F32)
        for span in spans:
            expo = jnp.exp2(sc_s[head, span] * factor - peak)
            total += jnp.sum(expo, axis=0, keepdims=True)
            gathered += mul(vt_s[feats, span], expo.astype(BF16))
        outs.append(gathered / total)
        lse_ref[0, head : head + 1, :] = peak + jnp.log2(total)
    both = jnp.concatenate(outs, axis=0)
    turn_ref[...] = both.astype(BF16)
    ctx_ref[...] = both.T.astype(BF16)


def attend(limit, mixed, pairs):
    length = mixed.shape[0]
    column = lambda c: pl.BlockSpec((length, PAIR), lambda i, s: (0, i * 3 + c))
    return pl.pallas_call(
        attend_kernel,
        grid_spec=pltpu.PrefetchScalarGridSpec(
            num_scalar_prefetch=1,
            grid=(pairs,),
            in_specs=[column(0), column(1), column(2)],
            out_specs=[
                pl.BlockSpec((length, PAIR), lambda i, s: (0, i)),
                pl.BlockSpec((PAIR, length), lambda i, s: (i, 0)),
                pl.BlockSpec((1, 2, length), lambda i, s: (i, 0, 0)),
            ],
            scratch_shapes=[
                pltpu.VMEM((2, length, PAIR), BF16),
                pltpu.VMEM((2, length, PAIR), BF16),
                pltpu.VMEM((PAIR, length), BF16),
                pltpu.VMEM((2, length, length), F32),
            ],
        ),
        out_shape=[
            pltpu.HBM((length, pairs * PAIR), BF16),
            pltpu.HBM((pairs * PAIR, length), BF16),
            jax.ShapeDtypeStruct((pairs, 2, length), F32),
        ],
        compiler_params=params(28),
        cost_estimate=cost(15),
        name="attend",
    )(limit, mixed, mixed, mixed)


def gelu_both(values):
    root = math.sqrt(2.0 / math.pi)
    scaled = root * values
    inner = scaled * (1.0 + 0.044715 * (values * values))
    tanh = jnp.tanh(inner)
    half = 0.5 + 0.5 * tanh
    slope = half + (1.0 - tanh * tanh) * (1.5 * inner - scaled)
    return values * half, slope


def middle_kernel(
    groups, limit_ref, place_ref, x_ref, clock_ref, gain_ref, ctx_ref, og_ref, *refs
):
    weight_refs, refs = refs[:-17], refs[-17:]
    out_ref, cg_ref, mg_ref, gg_ref, up_send, down_send, up_keep, down_keep = refs[:8]
    wide, units, active_s, ug_s, n_turn, fg_turn, ag_turn, ctx_s, sems = refs[8:]
    step = pl.program_id(0)
    parts, _, hidden = active_s.shape
    blocks = pl.num_programs(0) - parts
    each = len(weight_refs) // parts

    def fetch(part, kind):
        target, wide_, own = (
            (wide, PAIR, slice(0, PAIR)),
            (units, 2 * hidden, slice(PAIR, PAIR + 2 * hidden)),
        )[kind]
        columns = slice(part * wide_, (part + 1) * wide_)
        copies = []
        for at, w_ref in enumerate(weight_refs[part * each : (part + 1) * each]):
            count = 1 if groups is None else groups // each
            rows = w_ref.shape[0] // count
            for group in range(count):
                index = at * count + group
                spot = pl.ds(0, rows)
                if groups is not None:
                    spot = pl.ds(pl.multiple_of(place_ref[index] * rows, rows), rows)
                copies.append(
                    pltpu.make_async_copy(
                        w_ref.at[pl.ds(group * rows, rows), own],
                        target.at[spot, columns],
                        sems.at[kind, part, index],
                    )
                )
        return copies

    @pl.when(step == 0)
    def _():
        gg_ref[...] = jnp.zeros_like(gg_ref)
        for part in range(parts):
            for copy in fetch(part, 0) + fetch(part, 1):
                copy.start()
        for part in range(parts):
            for copy in fetch(part, 0) + fetch(part, 1):
                copy.wait()

    dead = (step < blocks) & (step * ROWS >= limit_ref[0])

    @pl.when((step < blocks) & jnp.logical_not(dead))
    def _():
        spot = pl.ds(pl.multiple_of(step * ROWS, ROWS), ROWS)
        gain = gain_ref[...]
        live = step * ROWS + lax.broadcasted_iota(jnp.int32, (ROWS, 1), 0) < limit_ref[0]
        begin = join_tokens(x_ref) + clock_ref[...]
        middle = begin + mul(ctx_ref[...], wide[...], NT)
        unit, inverse = norm_parts(middle)
        normed = (unit * gain).astype(BF16)
        n_turn[:, spot] = normed.T
        res_grad = jnp.where(live, og_ref[0].astype(F32), 0.0)
        feed_grad = res_grad.astype(BF16)
        fg_turn[:, spot] = feed_grad.T
        feed = jnp.zeros_like(middle)
        two_grad = jnp.zeros_like(middle)
        for part in range(parts):
            up = slice(2 * part * hidden, (2 * part + 1) * hidden)
            down = slice((2 * part + 1) * hidden, (2 * part + 2) * hidden)
            upper = mul(normed, units[:, up])
            active, slope = gelu_both(upper)
            active = active.astype(BF16)
            active_s[part, spot] = active
            feed += mul(active, units[:, down], NT)
            upper_grad = (mul(feed_grad, units[:, down]) * slope).astype(BF16)
            ug_s[part, spot] = upper_grad
            two_grad += mul(upper_grad, units[:, up], NT)
        out_ref[0] = jnp.where(live, middle + feed, 0.0).astype(BF16)
        gg_ref[...] += jnp.sum(two_grad * unit, axis=0, keepdims=True)
        middle_grad = res_grad + norm_back(two_grad, gain, unit, inverse)
        mg_ref[...] = middle_grad
        att_grad = middle_grad.astype(BF16)
        ag_turn[:, spot] = att_grad.T
        cg_ref[...] = mul(att_grad, wide[...]).astype(BF16)
        for part in range(parts):
            ctx_s[part, spot] = ctx_ref[:, part * PAIR : (part + 1) * PAIR]

    @pl.when(dead)
    def _():
        spot = pl.ds(pl.multiple_of(step * ROWS, ROWS), ROWS)
        for ref in (out_ref, cg_ref, mg_ref):
            ref[...] = jnp.zeros_like(ref)
        for ref in (active_s, ug_s, ctx_s):
            ref[:, spot] = jnp.zeros((ref.shape[0], ROWS, ref.shape[2]), BF16)
        for ref in (n_turn, fg_turn, ag_turn):
            ref[:, spot] = jnp.zeros((ref.shape[0], ROWS), BF16)

    @pl.when(step >= blocks)
    def _():
        turn = step - blocks
        part = jnp.where(turn < 2, 3 - 2 * turn, 6 - 2 * turn)
        grads = (
            mul(ag_turn[...], ctx_s[part]).astype(BF16),
            mul(n_turn[...], ug_s[part]).astype(BF16),
            mul(fg_turn[...], active_s[part]).astype(BF16),
        )

        def into(up_ref, down_ref):
            up_ref[0, :, 0:PAIR], up_ref[0, :, PAIR:], down_ref[0] = grads

        pl.when(turn < 2)(lambda: into(up_send, down_send))
        pl.when(turn >= 2)(lambda: into(up_keep, down_keep))


def middle_block(limit, place, groups, x_blocks, clock, gain, ctx, w_parts, out_grad):
    senders, feature_parts, tall, width = x_blocks.shape
    tokens = tall - SPARE
    length = senders * tokens
    features = feature_parts * width
    parts = len(w_parts)
    weights = [in_hbm(w) for part in w_parts for w in part]
    columns = weights[0].shape[1]
    hidden = (columns - PAIR) // 2
    take = ROWS // tokens
    blocks = length // ROWS
    row = lambda i: jnp.minimum(i, blocks - 1)
    whole = lambda array: pl.BlockSpec(
        array.shape, lambda i, *s: (0,) * array.ndim, pipeline_mode=pl.Buffered(1)
    )
    rows = lambda n: pl.BlockSpec((ROWS, n), lambda i, *s: (row(i), 0))
    one = pl.BlockSpec((1, ROWS, features), lambda i, *s: (0, row(i), 0))
    grads = lambda first, n: pl.BlockSpec(
        (1, features, n), lambda i, *s: (jnp.clip(i - blocks - first, 0, 1), 0, 0)
    )
    up_shape = pltpu.HBM((2, features, PAIR + hidden), BF16)
    down_shape = pltpu.HBM((2, features, hidden), BF16)
    return pl.pallas_call(
        functools.partial(middle_kernel, groups),
        grid_spec=pltpu.PrefetchScalarGridSpec(
            num_scalar_prefetch=2,
            grid=(blocks + parts,),
            in_specs=[
                pl.BlockSpec(
                    (take, feature_parts, tall, width), lambda i, *s: (row(i), 0, 0, 0)
                ),
                whole(clock),
                whole(gain),
                rows(features),
                one,
            ]
            + [pl.BlockSpec(memory_space=pltpu.HBM)] * len(weights),
            out_specs=[
                one, rows(features), rows(features),
                pl.BlockSpec((1, features), lambda i, *s: (0, 0)),
                grads(0, PAIR + hidden), grads(0, hidden), grads(2, PAIR + hidden), grads(2, hidden),
            ],
            scratch_shapes=[
                pltpu.VMEM((features, parts * PAIR), BF16),
                pltpu.VMEM((features, parts * 2 * hidden), BF16),
                pltpu.VMEM((parts, length, hidden), BF16),
                pltpu.VMEM((parts, length, hidden), BF16),
                pltpu.VMEM((features, length), BF16),
                pltpu.VMEM((features, length), BF16),
                pltpu.VMEM((features, length), BF16),
                pltpu.VMEM((parts, length, PAIR), BF16),
                pltpu.SemaphoreType.DMA((2, parts, groups or 1)),
            ],
        ),
        out_shape=[
            jax.ShapeDtypeStruct((1, length, features), BF16),
            pltpu.HBM((length, features), BF16),
            pltpu.HBM((length, features), F32),
            jax.ShapeDtypeStruct((1, features), F32),
            up_shape, down_shape, up_shape, down_shape,
        ],
        compiler_params=params(48),
        cost_estimate=cost(25),
        name="middle",
    )(limit, place, x_blocks, clock, gain, in_hbm(ctx), in_hbm(out_grad), *weights)


def attend_back_kernel(
    limit_ref, q_ref, k_ref, v_ref, turn_ref, lse_ref, cg_ref, n_turn_ref,
    dm_ref, first_ref, second_ref, keys_s, q_s, qz_s, do_s, kt_s, delta_s,
):
    limit = limit_ref[0]
    length = q_ref.shape[0]
    kt_s[...] = k_ref[...].astype(F32).T.astype(BF16)
    along = cg_ref[...].astype(F32).T * turn_ref[...].astype(F32)
    for head in range(2):
        feats = slice(head * HEAD_DIM, (head + 1) * HEAD_DIM)
        delta_s[head : head + 1, :] = jnp.sum(along[feats, :], axis=0, keepdims=True)
        keys_s[head] = masked_keys(k_ref[...], head, limit)
        q_s[head] = masked_queries(q_ref[...], head)
        qz_s[head] = own_lanes(q_ref[...], head)
        do_s[head] = own_lanes(cg_ref[...], head)
    factor = SCORE_SCALE * LOG2E
    turned = [jnp.zeros((HEAD_DIM, length), F32)] * 2
    for at in range(0, length, BACK_KEYS):
        span = slice(at, at + BACK_KEYS)
        key_grad = jnp.zeros((BACK_KEYS, PAIR), F32)
        value_grad = jnp.zeros((BACK_KEYS, PAIR), F32)
        for head in range(2):
            feats = slice(head * HEAD_DIM, (head + 1) * HEAD_DIM)
            scores = mul(keys_s[head, span], q_s[head], NT)
            prob = jnp.exp2(scores * factor - lse_ref[0, head : head + 1, :])
            prob_grad = mul(v_ref[span, :], do_s[head], NT)
            score_grad = (prob * (prob_grad - delta_s[head : head + 1, :])).astype(BF16)
            value_grad += mul(prob.astype(BF16), do_s[head])
            key_grad += mul(score_grad, qz_s[head])
            turned[head] += mul(kt_s[feats, span], score_grad)
        dm_ref[span, PAIR : 2 * PAIR] = (key_grad * SCORE_SCALE).astype(BF16)
        dm_ref[span, 2 * PAIR : 3 * PAIR] = value_grad.astype(BF16)
    query_grad = jnp.concatenate(turned, axis=0) * SCORE_SCALE
    dm_ref[:, 0:PAIR] = query_grad.T.astype(BF16)
    grad = mul(n_turn_ref[...], dm_ref[...]).astype(BF16)

    @pl.when(pl.program_id(0) == 0)
    def _():
        first_ref[...] = grad

    @pl.when(pl.program_id(0) == 1)
    def _():
        second_ref[...] = grad


def attend_back(limit, mixed, ctx_turn, lse, context_grad, n_turn, first):
    length = mixed.shape[0]
    features = n_turn.shape[0]
    pair = lambda i: first - i
    column = lambda c: pl.BlockSpec((length, PAIR), lambda i, s: (0, pair(i) * 3 + c))
    return pl.pallas_call(
        attend_back_kernel,
        grid_spec=pltpu.PrefetchScalarGridSpec(
            num_scalar_prefetch=1,
            grid=(2,),
            in_specs=[
                column(0), column(1), column(2),
                pl.BlockSpec((PAIR, length), lambda i, s: (pair(i), 0)),
                pl.BlockSpec((1, 2, length), lambda i, s: (pair(i), 0, 0)),
                pl.BlockSpec((length, PAIR), lambda i, s: (0, pair(i))),
                pl.BlockSpec((features, length), lambda i, s: (0, 0)),
            ],
            out_specs=[
                pl.BlockSpec((length, 3 * PAIR), lambda i, s: (0, i)),
                pl.BlockSpec((features, 3 * PAIR), lambda i, s: (0, 0)),
                pl.BlockSpec((features, 3 * PAIR), lambda i, s: (0, 0)),
            ],
            scratch_shapes=[
                pltpu.VMEM((2, length, PAIR), BF16),
                pltpu.VMEM((2, length, PAIR), BF16),
                pltpu.VMEM((2, length, PAIR), BF16),
                pltpu.VMEM((2, length, PAIR), BF16),
                pltpu.VMEM((PAIR, length), BF16),
                pltpu.VMEM((8, length), F32),
            ],
        ),
        out_shape=[
            jax.ShapeDtypeStruct((length, 2 * 3 * PAIR), BF16),
            jax.ShapeDtypeStruct((features, 3 * PAIR), BF16),
            jax.ShapeDtypeStruct((features, 3 * PAIR), BF16),
        ],
        compiler_params=params(28),
        cost_estimate=cost(16),
        name="attend_back",
    )(limit, mixed, mixed, mixed, ctx_turn, lse, context_grad, n_turn)


def begin_kernel(
    limit_ref, x_ref, clock_ref, gain_ref, gg_two_ref, mg_ref, w_ref, high_ref, low_ref, bg_ref, gg_s
):
    step = pl.program_id(0)
    _, parts, tall, width = bg_ref.shape
    tokens = tall - SPARE
    blocks = ROWS // tokens
    spot = pl.ds(step * blocks, blocks)

    @pl.when(step == 0)
    def _():
        gg_s[...] = jnp.zeros_like(gg_s)

    @pl.when(step * ROWS < limit_ref[0])
    def _():
        begin = join_tokens(x_ref) + clock_ref[...]
        unit, inverse = norm_parts(begin)
        one_grad = jnp.zeros_like(begin)
        for part, (d_ref, at) in enumerate(((low_ref, 1), (low_ref, 0), (high_ref, 1), (high_ref, 0))):
            columns = slice(part * 3 * PAIR, (part + 1) * 3 * PAIR)
            own = slice(at * 3 * PAIR, (at + 1) * 3 * PAIR)
            one_grad += mul(d_ref[:, own], w_ref[:, columns], NT)
        gg_s[...] += jnp.sum(one_grad * unit, axis=0, keepdims=True)
        total = (mg_ref[...] + norm_back(one_grad, gain_ref[...], unit, inverse)).astype(BF16)
        for part in range(parts):
            piece = total[:, part * width : (part + 1) * width]
            bg_ref[spot, part, 0:tokens] = piece.reshape(blocks, tokens, width)

    @pl.when(step * ROWS >= limit_ref[0])
    def _():
        bg_ref[spot] = jnp.zeros((blocks,) + bg_ref.shape[1:], BF16)

    @pl.when(step == pl.num_programs(0) - 1)
    def _():
        rows = []
        for ref in (gg_s, gg_two_ref):
            for part in range(parts):
                rows.append(ref[:, part * width : (part + 1) * width])
        bg_ref[:, :, tokens:tall] = jnp.broadcast_to(
            jnp.concatenate(rows, axis=0).astype(BF16), bg_ref.shape[:2] + (SPARE, width)
        )


def begin_block(limit, x_blocks, clock, gain, two_grad, w_wide, middle_grad, high, low):
    senders, feature_parts, tall, width = x_blocks.shape
    tokens = tall - SPARE
    length = senders * tokens
    features = feature_parts * width
    take = ROWS // tokens
    whole = lambda array: pl.BlockSpec(array.shape, lambda i, s: (0,) * array.ndim)
    rows = lambda n: pl.BlockSpec((ROWS, n), lambda i, s: (i, 0))
    return pl.pallas_call(
        begin_kernel,
        grid_spec=pltpu.PrefetchScalarGridSpec(
            num_scalar_prefetch=1,
            grid=(length // ROWS,),
            in_specs=[
                pl.BlockSpec((take, feature_parts, tall, width), lambda i, s: (i, 0, 0, 0)),
                whole(clock), whole(gain), whole(two_grad), rows(features), whole(w_wide),
            ]
            + [rows(6 * PAIR)] * 2,
            out_specs=whole(x_blocks),
            scratch_shapes=[pltpu.VMEM((1, features), F32)],
        ),
        out_shape=jax.ShapeDtypeStruct(x_blocks.shape, BF16),
        compiler_params=params(20),
        cost_estimate=cost(7),
        name="begin_back",
    )(limit, x_blocks, clock, gain, two_grad, middle_grad, w_wide, high, low)


DIRECT = 8


def clock_rows(step_ids, features):
    half_width = features // 2
    ladder = jnp.arange(half_width, dtype=F32) / half_width
    rate_rows = jnp.exp(-math.log(10000.0) * ladder)
    angles = step_ids.astype(F32)[:, None] * rate_rows[None, :]
    return jnp.concatenate([jnp.sin(angles), jnp.cos(angles)], axis=-1)


def swap(value, apart):
    count = lax.axis_size("tensor")
    return lax.ppermute(value, "tensor", [(i, i ^ apart) for i in range(count)])


def along_dp(value, move):
    count = lax.axis_size("dp")
    return lax.ppermute(value, "dp", [(i, move(i)) for i in range(count)])


def across(value):
    return ahead(value, 0, 1)


def ahead(value, step, flip=0):
    count = lax.axis_size("dp") // 2
    return along_dp(value, lambda i: (i // 2 + step) % count * 2 + (i + flip) % 2)


def places():
    count = lax.axis_size("dp") // 2
    own = lax.axis_index("dp")
    coarse = (own // 2 - jnp.arange(count, dtype=jnp.int32)) % count
    return jnp.concatenate([coarse * 2 + own % 2, coarse * 2 + 1 - own % 2])


def collect_coarse(shard):
    count = lax.axis_size("dp") // 2
    return [shard] + [ahead(shard, step) for step in range(1, count)]


def collect_rows(shard):
    count = lax.axis_size("dp")
    rows = lax.all_to_all(
        jnp.broadcast_to(shard[None], (count,) + shard.shape), "dp", 0, 0, tiled=True
    )
    return rows.reshape(count * shard.shape[0], shard.shape[1])


def collect_columns(rows):
    far = swap(rows, 2)
    return rows, swap(rows, 1), far, swap(far, 1)


def add(*values):
    return add_wide(*values).astype(BF16)


def fold_pair(values):
    own = lax.axis_index("dp") % 2
    pick = lambda value, which: lax.dynamic_index_in_dim(value, which, value.ndim - 3, keepdims=False)
    sent = add(*[pick(value, 1 - own) for value in values])
    return sent, lambda: [pick(value, own) for value in values] + [across(sent)]


def fold_far(values):
    sent = add(*[value[0] for value in values])
    return sent, lambda: [value[1] for value in values] + [swap(sent, 2)]


def fold_coarse(values):
    count = lax.axis_size("dp") // 2
    own = lax.axis_index("dp") // 2
    pick = lambda value, which: lax.dynamic_index_in_dim(value, which % count, 0, keepdims=False)
    value = add(*values)
    came = [ahead(pick(value, own + step), step) for step in range(1, count)]
    return value, [pick(value, own)] + came


def add_wide(*values):
    total = values[0].astype(F32)
    for value in values[1:]:
        total += value.astype(F32)
    return total


def grouped(value):
    count = lax.axis_size("dp")
    two, rows, columns = value.shape
    return value.reshape(two, count // 2, 2, rows // count, columns)


def exchange_rows(value):
    count = lax.axis_size("dp")
    groups = value.reshape(count, value.shape[0] // count, value.shape[1])
    return jnp.sum(lax.all_to_all(groups, "dp", 0, 0, tiled=True).astype(F32), axis=0)


def three_terms(values):
    terms = []
    for _ in range(3):
        term = lax.reduce_precision(values, 8, 7)
        terms.append(term.astype(BF16))
        values = values - term
    return terms


def together(*values):
    return lax.optimization_barrier(values)


def after(value, *others):
    return lax.optimization_barrier((value,) + others)[0]


def on_device(
    states, timesteps, lengths, deal_order, w_qkv, w_out, w_up, w_down, gain_attn, gain_ffn, out_grad
):
    both = ("dp", "tensor")
    dp_count = lax.axis_size("dp")
    tensor_count = lax.axis_size("tensor")
    devices = dp_count * tensor_count
    total_seqs, tokens, width = states.shape
    assert tensor_count == 4 and total_seqs == devices
    features = width * tensor_count
    own = lax.axis_index("dp") * tensor_count + lax.axis_index("tensor")
    own_id = lax.dynamic_slice_in_dim(deal_order, own, 1)
    limit = lengths[own_id]
    clock = clock_rows(timesteps[own_id], features)
    per = gain_attn.shape[0]
    rows = w_qkv.shape[0]
    hidden = w_up.shape[1]

    rest = jnp.concatenate([w_out.T, w_up, w_down.T], axis=1)
    qkv = w_qkv.reshape(rows, -1)
    direct = dp_count <= DIRECT
    if direct:
        place, groups = places(), dp_count
        wide = qkv.shape[1]
        pieces = collect_coarse(jnp.concatenate([qkv, across(qkv)], axis=1))
        qkv_rows = jnp.concatenate(
            [piece[:, :wide] for piece in pieces] + [piece[:, wide:] for piece in pieces], axis=0
        )
        mine = jnp.concatenate(collect_coarse(rest), axis=0)
        first = (qkv_rows, mine)
        far_rows, other, far_mine = together(
            swap(qkv_rows, 2), in_hbm(across(mine)), in_hbm(swap(mine, 2))
        )
        qkv_parts = (qkv_rows, swap(qkv_rows, 1), far_rows, swap(far_rows, 1))
    else:
        place, groups = jnp.zeros((1,), jnp.int32), None
        first = (collect_rows(qkv),)
        qkv_parts = collect_columns(first[0])
        rest_parts = [(part,) for part in collect_columns(collect_rows(rest))]

    spare = jnp.stack(three_terms(gain_attn) + three_terms(gain_ffn)).reshape(1, 6 * per)
    spare = jnp.pad(spare, ((0, SPARE - 1), (0, width - 6 * per)))
    by_tensor = deal_order.reshape(dp_count, tensor_count).T.reshape(devices)
    arranged = jnp.concatenate(
        [states[by_tensor], jnp.broadcast_to(spare[None], (devices, SPARE, width))], axis=1
    )
    arranged = lax.all_to_all(arranged, "tensor", 0, 0, tiled=True)
    arranged = arranged.reshape(tensor_count, dp_count, tokens + SPARE, width).swapaxes(0, 1)
    x_blocks = lax.all_to_all(after(arranged, *first), "dp", 0, 0, tiled=True)
    x_blocks = x_blocks.reshape(devices, tokens + SPARE, width)
    gains = jnp.sum(x_blocks[:, tokens, : 6 * per].reshape(devices, 2, 3, per).astype(F32), axis=2)
    gain_one = gains[:, 0].reshape(1, features)
    gain_two = gains[:, 1].reshape(1, features)
    x_blocks = x_blocks.reshape(dp_count, tensor_count, tokens + SPARE, width)

    mixed, n_one_turn, qkv_wide = project(
        limit, place, groups, x_blocks, clock, gain_one, qkv_parts
    )
    if direct:
        near_mine, near_other = in_hbm(swap(mine, 1)), in_hbm(swap(other, 1))
        last_mine, far_other = in_hbm(swap(far_mine, 1)), in_hbm(swap(other, 2))
    ctx, ctx_turn, lse = attend(limit, mixed, tensor_count)
    if direct:
        ctx, near_mine, near_other, last_mine, far_other = together(
            ctx, near_mine, near_other, last_mine, far_other
        )
        last_other = swap(far_other, 1)
        rest_parts = (
            (mine, other), (near_mine, near_other), (far_mine, far_other), (last_mine, last_other)
        )
    output, context_grad, middle_grad, two_grad, up_send, down_send, up_keep, down_keep = middle_block(
        limit, place, groups, x_blocks, clock, gain_two, ctx, rest_parts, out_grad
    )
    up_came, down_came = swap(up_send, 1), swap(down_send, 1)

    back = functools.partial(attend_back, limit, mixed, ctx_turn, lse)
    if direct:
        down_sent, down_rest = fold_far([grouped(value) for value in (down_keep, down_came)])
        up_sent, up_rest = fold_pair([grouped(value) for value in (up_keep, up_came)])
        context_grad = after(context_grad, down_sent, up_sent)
    high, three, two = back(context_grad, n_one_turn, 3)
    if direct:
        *down_rest, down_came = down_rest()
        *up_rest, up_came = up_rest()
        high, three, two, down_came, up_came = together(high, three, two, down_came, up_came)
        down_value, down_pieces = fold_coarse([*down_rest, down_came])
        up_sent, up_rest = fold_far([add(*up_rest, up_came)])
        context_grad = after(context_grad, down_value, up_sent)
    far = add(two, swap(three, 1))
    came_far = swap(far, 2)
    low, one, own_part = back(after(context_grad, high, far), n_one_turn, 1)
    if direct:
        *up_rest, up_came = up_rest()
        low, one, own_part, up_came, came_far, *down_pieces = together(
            low, one, own_part, up_came, came_far, *down_pieces
        )
        up_value, up_pieces = fold_coarse([*up_rest, up_came])
        down_sent, down_rest = fold_pair([add_wide(*down_pieces)[..., None, :, :, :]])
        middle_grad = after(middle_grad, up_value, down_sent)
    came_one = swap(one, 1)
    begin_grad = begin_block(
        limit, x_blocks, clock, gain_one, two_grad, qkv_wide, middle_grad, high, low
    )
    if direct:
        begin_grad, came_one, up_pieces[2] = together(begin_grad, came_one, up_pieces[2])
        near = [grouped(value[None])[0] for value in (own_part, came_one, came_far)]
        qkv_value, qkv_pieces = fold_coarse(fold_pair(near)[1]())
        *up_pieces, down_came, _ = together(*up_pieces, down_rest()[-1], qkv_value)
        up_total = add_wide(*up_pieces)
        down_total = add_wide(*down_rest()[:-1], down_came)[0]
        qkv_total = add_wide(*qkv_pieces)
    else:
        up_total = exchange_rows(add(*fold_far([up_keep, up_came])[1]()))
        down_total = exchange_rows(add(*fold_far([down_keep, down_came])[1]()))
        qkv_total = exchange_rows(add(own_part, came_one, came_far))
    returned = lax.all_to_all(
        begin_grad.reshape(devices, tokens + SPARE, width), both, 0, 0, tiled=True
    )
    inverse = (
        jnp.zeros((total_seqs,), jnp.int32)
        .at[deal_order]
        .set(jnp.arange(total_seqs, dtype=jnp.int32))
    )
    states_grad = returned[inverse][:, :tokens]
    gain_grads = jnp.sum(returned[:, tokens:].astype(F32), axis=0).reshape(2, devices, per)
    gain_grads = lax.dynamic_index_in_dim(gain_grads, own, 1, keepdims=False)
    return (
        output,
        states_grad,
        qkv_total.reshape(w_qkv.shape),
        up_total[:, :PAIR].T,
        up_total[:, PAIR:],
        down_total.T,
        gain_grads[0],
        gain_grads[1],
    )


def solution(mesh):
    in_specs = (
        P(None, "dp", "tensor"),
        P(),
        P(),
        P(),
        P("dp", None, "tensor"),
        P("tensor", "dp"),
        P("dp", "tensor"),
        P("tensor", "dp"),
        P(("dp", "tensor")),
        P(("dp", "tensor")),
        P(("dp", "tensor"), None, None),
    )
    out_specs = (
        P(("dp", "tensor"), None, None),
        P(None, "dp", "tensor"),
        P("dp", None, "tensor"),
        P("tensor", "dp"),
        P("dp", "tensor"),
        P("tensor", "dp"),
        P(("dp", "tensor")),
        P(("dp", "tensor")),
    )
    return jax.shard_map(
        on_device, mesh=mesh, in_specs=in_specs, out_specs=out_specs, check_vma=False
    )
```

```python
import functools
import math

import jax
import jax.numpy as jnp
from jax import lax
from jax.experimental import pallas as pl
from jax.experimental.pallas import tpu as pltpu
from jax.sharding import PartitionSpec as P

HEAD_DIM = 64
PAIR = 2 * HEAD_DIM
ROWS = 512
KEYS = 256
BACK_KEYS = 512
SPARE = 8
SCORE_SCALE = 1.0 / math.sqrt(HEAD_DIM)
LOG2E = math.log2(math.e)
F32 = jnp.float32
BF16 = jnp.bfloat16
NN = (((1,), (0,)), ((), ()))
NT = (((1,), (1,)), ((), ()))
MIB = 1024 * 1024


def mul(lhs, rhs, dims=NN):
    return lax.dot_general(lhs, rhs, dims, preferred_element_type=F32)


def join_tokens(ref):
    blocks, parts, tall, width = ref.shape
    tokens = tall - SPARE
    return jnp.concatenate(
        [ref[:, part, 0:tokens].reshape(blocks * tokens, width) for part in range(parts)], axis=-1
    ).astype(F32)


def place_rows(groups, place_ref, first, source, targets):
    if groups is None:
        for target, columns, own in targets:
            target[:, columns] = source[:, own]
        return
    rows = source.shape[0] // groups
    for group in range(groups):
        spot = pl.ds(pl.multiple_of(place_ref[first + group] * rows, rows), rows)
        for target, columns, own in targets:
            target[spot, columns] = source[group * rows : (group + 1) * rows, own]


def norm_parts(values):
    center = values - jnp.mean(values, axis=-1, keepdims=True)
    spread = jnp.mean(center * center, axis=-1, keepdims=True)
    inverse = lax.rsqrt(spread + 1e-05)
    return center * inverse, inverse


def norm_back(grad, gain, unit, inverse):
    scaled = grad * gain
    mean_scaled = jnp.mean(scaled, axis=-1, keepdims=True)
    mean_along = jnp.mean(scaled * unit, axis=-1, keepdims=True)
    return inverse * (scaled - mean_scaled - unit * mean_along)


def in_hbm(value):
    return pltpu.with_memory_space_constraint(value, pltpu.HBM)


def cost(microseconds):
    return pl.CostEstimate(
        flops=int(microseconds * 1.15e9), bytes_accessed=1 << 20, transcendentals=0
    )


def params(mebibytes):
    return pltpu.CompilerParams(vmem_limit_bytes=mebibytes * MIB)


def project_kernel(groups, limit_ref, place_ref, x_ref, clock_ref, gain_ref, *refs):
    w_refs, (mixed_ref, n_turn_ref, wide) = refs[:-3], refs[-3:]
    step = pl.program_id(0)

    @pl.when(step == 0)
    def _():
        for part, w_ref in enumerate(w_refs):
            width = w_ref.shape[1]
            columns = slice(part * width, (part + 1) * width)
            place_rows(groups, place_ref, 0, w_ref, [(wide, columns, slice(0, width))])

    @pl.when(step * ROWS < limit_ref[0])
    def _():
        begin = join_tokens(x_ref) + clock_ref[...]
        unit, _ = norm_parts(begin)
        normed = (unit * gain_ref[...]).astype(BF16)
        n_turn_ref[...] = normed.T
        mixed_ref[...] = mul(normed, wide[...]).astype(BF16)

    @pl.when(step * ROWS >= limit_ref[0])
    def _():
        n_turn_ref[...] = jnp.zeros_like(n_turn_ref)
        mixed_ref[...] = jnp.zeros_like(mixed_ref)


def project(limit, place, groups, x_blocks, clock, gain, w_parts):
    senders, feature_parts, tall, width = x_blocks.shape
    tokens = tall - SPARE
    length = senders * tokens
    features = feature_parts * width
    parts, columns = len(w_parts), w_parts[0].shape[1]
    take = ROWS // tokens
    return pl.pallas_call(
        functools.partial(project_kernel, groups),
        grid_spec=pltpu.PrefetchScalarGridSpec(
            num_scalar_prefetch=2,
            grid=(length // ROWS,),
            in_specs=[
                pl.BlockSpec((take, feature_parts, tall, width), lambda i, *s: (i, 0, 0, 0)),
                pl.BlockSpec((1, features), lambda i, *s: (0, 0)),
                pl.BlockSpec((1, features), lambda i, *s: (0, 0)),
            ]
            + [pl.BlockSpec((features, columns), lambda i, *s: (0, 0))] * parts,
            out_specs=[
                pl.BlockSpec((ROWS, parts * columns), lambda i, *s: (i, 0)),
                pl.BlockSpec((features, ROWS), lambda i, *s: (0, i)),
                pl.BlockSpec((features, parts * columns), lambda i, *s: (0, 0)),
            ],
        ),
        out_shape=[
            jax.ShapeDtypeStruct((length, parts * columns), BF16),
            pltpu.HBM((features, length), BF16),
            pltpu.HBM((features, parts * columns), BF16),
        ],
        compiler_params=params(20),
        cost_estimate=cost(5),
        name="project",
    )(limit, place, x_blocks, clock, gain, *w_parts)


def head_lanes(shape, head):
    lane = lax.broadcasted_iota(jnp.int32, shape, 1)
    return (lane >= head * HEAD_DIM) & (lane < (head + 1) * HEAD_DIM)


def spare_lane(shape, head):
    lane = lax.broadcasted_iota(jnp.int32, shape, 1)
    return lane == (1 - head) * HEAD_DIM


def masked_keys(keys, head, limit):
    row = lax.broadcasted_iota(jnp.int32, keys.shape, 0)
    spare = jnp.where(
        spare_lane(keys.shape, head) & (row >= limit), jnp.asarray(-1e30, F32), jnp.asarray(0.0, F32)
    )
    return jnp.where(head_lanes(keys.shape, head), keys.astype(F32), spare).astype(BF16)


def own_lanes(values, head):
    return jnp.where(head_lanes(values.shape, head), values.astype(F32), 0.0).astype(BF16)


def masked_queries(queries, head):
    spare = jnp.where(spare_lane(queries.shape, head), jnp.asarray(1.0, F32), jnp.asarray(0.0, F32))
    return jnp.where(head_lanes(queries.shape, head), queries.astype(F32), spare).astype(BF16)


def attend_kernel(limit_ref, q_ref, k_ref, v_ref, ctx_ref, turn_ref, lse_ref, keys_s, q_s, vt_s, sc_s):
    length = q_ref.shape[0]
    vt_s[...] = v_ref[...].astype(F32).T.astype(BF16)
    for head in range(2):
        keys_s[head] = masked_keys(k_ref[...], head, limit_ref[0])
        q_s[head] = masked_queries(q_ref[...], head)
    factor = SCORE_SCALE * LOG2E
    spans = [slice(at, at + KEYS) for at in range(0, length, KEYS)]
    outs = []
    for head in range(2):
        feats = slice(head * HEAD_DIM, (head + 1) * HEAD_DIM)
        peak = None
        for span in spans:
            scores = mul(keys_s[head, span], q_s[head], NT)
            sc_s[head, span] = scores
            high = jnp.max(scores, axis=0, keepdims=True)
            peak = high if peak is None else jnp.maximum(peak, high)
        peak = peak * factor
        total = jnp.zeros_like(peak)
        gathered = jnp.zeros((HEAD_DIM, length), F32)
        for span in spans:
            expo = jnp.exp2(sc_s[head, span] * factor - peak)
            total += jnp.sum(expo, axis=0, keepdims=True)
            gathered += mul(vt_s[feats, span], expo.astype(BF16))
        outs.append(gathered / total)
        lse_ref[0, head : head + 1, :] = peak + jnp.log2(total)
    both = jnp.concatenate(outs, axis=0)
    turn_ref[...] = both.astype(BF16)
    ctx_ref[...] = both.T.astype(BF16)


def attend(limit, mixed, pairs):
    length = mixed.shape[0]
    column = lambda c: pl.BlockSpec((length, PAIR), lambda i, s: (0, i * 3 + c))
    return pl.pallas_call(
        attend_kernel,
        grid_spec=pltpu.PrefetchScalarGridSpec(
            num_scalar_prefetch=1,
            grid=(pairs,),
            in_specs=[column(0), column(1), column(2)],
            out_specs=[
                pl.BlockSpec((length, PAIR), lambda i, s: (0, i)),
                pl.BlockSpec((PAIR, length), lambda i, s: (i, 0)),
                pl.BlockSpec((1, 2, length), lambda i, s: (i, 0, 0)),
            ],
            scratch_shapes=[
                pltpu.VMEM((2, length, PAIR), BF16),
                pltpu.VMEM((2, length, PAIR), BF16),
                pltpu.VMEM((PAIR, length), BF16),
                pltpu.VMEM((2, length, length), F32),
            ],
        ),
        out_shape=[
            pltpu.HBM((length, pairs * PAIR), BF16),
            pltpu.HBM((pairs * PAIR, length), BF16),
            jax.ShapeDtypeStruct((pairs, 2, length), F32),
        ],
        compiler_params=params(28),
        cost_estimate=cost(15),
        name="attend",
    )(limit, mixed, mixed, mixed)


def gelu_both(values):
    root = math.sqrt(2.0 / math.pi)
    scaled = root * values
    inner = scaled * (1.0 + 0.044715 * (values * values))
    tanh = jnp.tanh(inner)
    half = 0.5 + 0.5 * tanh
    slope = half + (1.0 - tanh * tanh) * (1.5 * inner - scaled)
    return values * half, slope


def middle_kernel(
    groups, limit_ref, place_ref, x_ref, clock_ref, gain_ref, ctx_ref, og_ref, *refs
):
    weight_refs, refs = refs[:-17], refs[-17:]
    out_ref, cg_ref, mg_ref, gg_ref, up_send, down_send, up_keep, down_keep = refs[:8]
    wide, units, active_s, ug_s, n_turn, fg_turn, ag_turn, ctx_s, sems = refs[8:]
    step = pl.program_id(0)
    parts, _, hidden = active_s.shape
    blocks = pl.num_programs(0) - parts
    each = len(weight_refs) // parts

    def fetch(part, kind):
        target, wide_, own = (
            (wide, PAIR, slice(0, PAIR)),
            (units, 2 * hidden, slice(PAIR, PAIR + 2 * hidden)),
        )[kind]
        columns = slice(part * wide_, (part + 1) * wide_)
        copies = []
        for at, w_ref in enumerate(weight_refs[part * each : (part + 1) * each]):
            count = 1 if groups is None else groups // each
            rows = w_ref.shape[0] // count
            for group in range(count):
                index = at * count + group
                spot = pl.ds(0, rows)
                if groups is not None:
                    spot = pl.ds(pl.multiple_of(place_ref[index] * rows, rows), rows)
                copies.append(
                    pltpu.make_async_copy(
                        w_ref.at[pl.ds(group * rows, rows), own],
                        target.at[spot, columns],
                        sems.at[kind, part, index],
                    )
                )
        return copies

    @pl.when(step == 0)
    def _():
        gg_ref[...] = jnp.zeros_like(gg_ref)
        for part in range(parts):
            for copy in fetch(part, 0) + fetch(part, 1):
                copy.start()
        for part in range(parts):
            for copy in fetch(part, 0) + fetch(part, 1):
                copy.wait()

    dead = (step < blocks) & (step * ROWS >= limit_ref[0])

    @pl.when((step < blocks) & jnp.logical_not(dead))
    def _():
        spot = pl.ds(pl.multiple_of(step * ROWS, ROWS), ROWS)
        gain = gain_ref[...]
        live = step * ROWS + lax.broadcasted_iota(jnp.int32, (ROWS, 1), 0) < limit_ref[0]
        begin = join_tokens(x_ref) + clock_ref[...]
        middle = begin + mul(ctx_ref[...], wide[...], NT)
        unit, inverse = norm_parts(middle)
        normed = (unit * gain).astype(BF16)
        n_turn[:, spot] = normed.T
        res_grad = jnp.where(live, og_ref[0].astype(F32), 0.0)
        feed_grad = res_grad.astype(BF16)
        fg_turn[:, spot] = feed_grad.T
        feed = jnp.zeros_like(middle)
        two_grad = jnp.zeros_like(middle)
        for part in range(parts):
            up = slice(2 * part * hidden, (2 * part + 1) * hidden)
            down = slice((2 * part + 1) * hidden, (2 * part + 2) * hidden)
            upper = mul(normed, units[:, up])
            active, slope = gelu_both(upper)
            active = active.astype(BF16)
            active_s[part, spot] = active
            feed += mul(active, units[:, down], NT)
            upper_grad = (mul(feed_grad, units[:, down]) * slope).astype(BF16)
            ug_s[part, spot] = upper_grad
            two_grad += mul(upper_grad, units[:, up], NT)
        out_ref[0] = jnp.where(live, middle + feed, 0.0).astype(BF16)
        gg_ref[...] += jnp.sum(two_grad * unit, axis=0, keepdims=True)
        middle_grad = res_grad + norm_back(two_grad, gain, unit, inverse)
        mg_ref[...] = middle_grad
        att_grad = middle_grad.astype(BF16)
        ag_turn[:, spot] = att_grad.T
        cg_ref[...] = mul(att_grad, wide[...]).astype(BF16)
        for part in range(parts):
            ctx_s[part, spot] = ctx_ref[:, part * PAIR : (part + 1) * PAIR]

    @pl.when(dead)
    def _():
        spot = pl.ds(pl.multiple_of(step * ROWS, ROWS), ROWS)
        for ref in (out_ref, cg_ref, mg_ref):
            ref[...] = jnp.zeros_like(ref)
        for ref in (active_s, ug_s, ctx_s):
            ref[:, spot] = jnp.zeros((ref.shape[0], ROWS, ref.shape[2]), BF16)
        for ref in (n_turn, fg_turn, ag_turn):
            ref[:, spot] = jnp.zeros((ref.shape[0], ROWS), BF16)

    @pl.when(step >= blocks)
    def _():
        turn = step - blocks
        part = jnp.where(turn < 2, 3 - 2 * turn, 6 - 2 * turn)
        grads = (
            mul(ag_turn[...], ctx_s[part]).astype(BF16),
            mul(n_turn[...], ug_s[part]).astype(BF16),
            mul(fg_turn[...], active_s[part]).astype(BF16),
        )

        def into(up_ref, down_ref):
            up_ref[0, :, 0:PAIR], up_ref[0, :, PAIR:], down_ref[0] = grads

        pl.when(turn < 2)(lambda: into(up_send, down_send))
        pl.when(turn >= 2)(lambda: into(up_keep, down_keep))


def middle_block(limit, place, groups, x_blocks, clock, gain, ctx, w_parts, out_grad):
    senders, feature_parts, tall, width = x_blocks.shape
    tokens = tall - SPARE
    length = senders * tokens
    features = feature_parts * width
    parts = len(w_parts)
    weights = [in_hbm(w) for part in w_parts for w in part]
    columns = weights[0].shape[1]
    hidden = (columns - PAIR) // 2
    take = ROWS // tokens
    blocks = length // ROWS
    row = lambda i: jnp.minimum(i, blocks - 1)
    whole = lambda array: pl.BlockSpec(
        array.shape, lambda i, *s: (0,) * array.ndim, pipeline_mode=pl.Buffered(1)
    )
    rows = lambda n: pl.BlockSpec((ROWS, n), lambda i, *s: (row(i), 0))
    one = pl.BlockSpec((1, ROWS, features), lambda i, *s: (0, row(i), 0))
    grads = lambda first, n: pl.BlockSpec(
        (1, features, n), lambda i, *s: (jnp.clip(i - blocks - first, 0, 1), 0, 0)
    )
    up_shape = pltpu.HBM((2, features, PAIR + hidden), BF16)
    down_shape = pltpu.HBM((2, features, hidden), BF16)
    return pl.pallas_call(
        functools.partial(middle_kernel, groups),
        grid_spec=pltpu.PrefetchScalarGridSpec(
            num_scalar_prefetch=2,
            grid=(blocks + parts,),
            in_specs=[
                pl.BlockSpec(
                    (take, feature_parts, tall, width), lambda i, *s: (row(i), 0, 0, 0)
                ),
                whole(clock),
                whole(gain),
                rows(features),
                one,
            ]
            + [pl.BlockSpec(memory_space=pltpu.HBM)] * len(weights),
            out_specs=[
                one, rows(features), rows(features),
                pl.BlockSpec((1, features), lambda i, *s: (0, 0)),
                grads(0, PAIR + hidden), grads(0, hidden), grads(2, PAIR + hidden), grads(2, hidden),
            ],
            scratch_shapes=[
                pltpu.VMEM((features, parts * PAIR), BF16),
                pltpu.VMEM((features, parts * 2 * hidden), BF16),
                pltpu.VMEM((parts, length, hidden), BF16),
                pltpu.VMEM((parts, length, hidden), BF16),
                pltpu.VMEM((features, length), BF16),
                pltpu.VMEM((features, length), BF16),
                pltpu.VMEM((features, length), BF16),
                pltpu.VMEM((parts, length, PAIR), BF16),
                pltpu.SemaphoreType.DMA((2, parts, groups or 1)),
            ],
        ),
        out_shape=[
            jax.ShapeDtypeStruct((1, length, features), BF16),
            pltpu.HBM((length, features), BF16),
            pltpu.HBM((length, features), F32),
            jax.ShapeDtypeStruct((1, features), F32),
            up_shape, down_shape, up_shape, down_shape,
        ],
        compiler_params=params(48),
        cost_estimate=cost(25),
        name="middle",
    )(limit, place, x_blocks, clock, gain, in_hbm(ctx), in_hbm(out_grad), *weights)


def attend_back_kernel(
    limit_ref, q_ref, k_ref, v_ref, turn_ref, lse_ref, cg_ref, n_turn_ref,
    dm_ref, first_ref, second_ref, keys_s, q_s, qz_s, do_s, kt_s, delta_s,
):
    limit = limit_ref[0]
    length = q_ref.shape[0]
    kt_s[...] = k_ref[...].astype(F32).T.astype(BF16)
    along = cg_ref[...].astype(F32).T * turn_ref[...].astype(F32)
    for head in range(2):
        feats = slice(head * HEAD_DIM, (head + 1) * HEAD_DIM)
        delta_s[head : head + 1, :] = jnp.sum(along[feats, :], axis=0, keepdims=True)
        keys_s[head] = masked_keys(k_ref[...], head, limit)
        q_s[head] = masked_queries(q_ref[...], head)
        qz_s[head] = own_lanes(q_ref[...], head)
        do_s[head] = own_lanes(cg_ref[...], head)
    factor = SCORE_SCALE * LOG2E
    turned = [jnp.zeros((HEAD_DIM, length), F32)] * 2
    for at in range(0, length, BACK_KEYS):
        span = slice(at, at + BACK_KEYS)
        key_grad = jnp.zeros((BACK_KEYS, PAIR), F32)
        value_grad = jnp.zeros((BACK_KEYS, PAIR), F32)
        for head in range(2):
            feats = slice(head * HEAD_DIM, (head + 1) * HEAD_DIM)
            scores = mul(keys_s[head, span], q_s[head], NT)
            prob = jnp.exp2(scores * factor - lse_ref[0, head : head + 1, :])
            prob_grad = mul(v_ref[span, :], do_s[head], NT)
            score_grad = (prob * (prob_grad - delta_s[head : head + 1, :])).astype(BF16)
            value_grad += mul(prob.astype(BF16), do_s[head])
            key_grad += mul(score_grad, qz_s[head])
            turned[head] += mul(kt_s[feats, span], score_grad)
        dm_ref[span, PAIR : 2 * PAIR] = (key_grad * SCORE_SCALE).astype(BF16)
        dm_ref[span, 2 * PAIR : 3 * PAIR] = value_grad.astype(BF16)
    query_grad = jnp.concatenate(turned, axis=0) * SCORE_SCALE
    dm_ref[:, 0:PAIR] = query_grad.T.astype(BF16)
    grad = mul(n_turn_ref[...], dm_ref[...]).astype(BF16)

    @pl.when(pl.program_id(0) == 0)
    def _():
        first_ref[...] = grad

    @pl.when(pl.program_id(0) == 1)
    def _():
        second_ref[...] = grad


def attend_back(limit, mixed, ctx_turn, lse, context_grad, n_turn, first):
    length = mixed.shape[0]
    features = n_turn.shape[0]
    pair = lambda i: first - i
    column = lambda c: pl.BlockSpec((length, PAIR), lambda i, s: (0, pair(i) * 3 + c))
    return pl.pallas_call(
        attend_back_kernel,
        grid_spec=pltpu.PrefetchScalarGridSpec(
            num_scalar_prefetch=1,
            grid=(2,),
            in_specs=[
                column(0), column(1), column(2),
                pl.BlockSpec((PAIR, length), lambda i, s: (pair(i), 0)),
                pl.BlockSpec((1, 2, length), lambda i, s: (pair(i), 0, 0)),
                pl.BlockSpec((length, PAIR), lambda i, s: (0, pair(i))),
                pl.BlockSpec((features, length), lambda i, s: (0, 0)),
            ],
            out_specs=[
                pl.BlockSpec((length, 3 * PAIR), lambda i, s: (0, i)),
                pl.BlockSpec((features, 3 * PAIR), lambda i, s: (0, 0)),
                pl.BlockSpec((features, 3 * PAIR), lambda i, s: (0, 0)),
            ],
            scratch_shapes=[
                pltpu.VMEM((2, length, PAIR), BF16),
                pltpu.VMEM((2, length, PAIR), BF16),
                pltpu.VMEM((2, length, PAIR), BF16),
                pltpu.VMEM((2, length, PAIR), BF16),
                pltpu.VMEM((PAIR, length), BF16),
                pltpu.VMEM((8, length), F32),
            ],
        ),
        out_shape=[
            jax.ShapeDtypeStruct((length, 2 * 3 * PAIR), BF16),
            jax.ShapeDtypeStruct((features, 3 * PAIR), BF16),
            jax.ShapeDtypeStruct((features, 3 * PAIR), BF16),
        ],
        compiler_params=params(28),
        cost_estimate=cost(16),
        name="attend_back",
    )(limit, mixed, mixed, mixed, ctx_turn, lse, context_grad, n_turn)


def begin_kernel(
    limit_ref, x_ref, clock_ref, gain_ref, gg_two_ref, mg_ref, w_ref, high_ref, low_ref, bg_ref, gg_s
):
    step = pl.program_id(0)
    _, parts, tall, width = bg_ref.shape
    tokens = tall - SPARE
    blocks = ROWS // tokens
    spot = pl.ds(step * blocks, blocks)

    @pl.when(step == 0)
    def _():
        gg_s[...] = jnp.zeros_like(gg_s)

    @pl.when(step * ROWS < limit_ref[0])
    def _():
        begin = join_tokens(x_ref) + clock_ref[...]
        unit, inverse = norm_parts(begin)
        one_grad = jnp.zeros_like(begin)
        for part, (d_ref, at) in enumerate(((low_ref, 1), (low_ref, 0), (high_ref, 1), (high_ref, 0))):
            columns = slice(part * 3 * PAIR, (part + 1) * 3 * PAIR)
            own = slice(at * 3 * PAIR, (at + 1) * 3 * PAIR)
            one_grad += mul(d_ref[:, own], w_ref[:, columns], NT)
        gg_s[...] += jnp.sum(one_grad * unit, axis=0, keepdims=True)
        total = (mg_ref[...] + norm_back(one_grad, gain_ref[...], unit, inverse)).astype(BF16)
        for part in range(parts):
            piece = total[:, part * width : (part + 1) * width]
            bg_ref[spot, part, 0:tokens] = piece.reshape(blocks, tokens, width)

    @pl.when(step * ROWS >= limit_ref[0])
    def _():
        bg_ref[spot] = jnp.zeros((blocks,) + bg_ref.shape[1:], BF16)

    @pl.when(step == pl.num_programs(0) - 1)
    def _():
        rows = []
        for ref in (gg_s, gg_two_ref):
            for part in range(parts):
                rows.append(ref[:, part * width : (part + 1) * width])
        bg_ref[:, :, tokens:tall] = jnp.broadcast_to(
            jnp.concatenate(rows, axis=0).astype(BF16), bg_ref.shape[:2] + (SPARE, width)
        )


def begin_block(limit, x_blocks, clock, gain, two_grad, w_wide, middle_grad, high, low):
    senders, feature_parts, tall, width = x_blocks.shape
    tokens = tall - SPARE
    length = senders * tokens
    features = feature_parts * width
    take = ROWS // tokens
    whole = lambda array: pl.BlockSpec(array.shape, lambda i, s: (0,) * array.ndim)
    rows = lambda n: pl.BlockSpec((ROWS, n), lambda i, s: (i, 0))
    return pl.pallas_call(
        begin_kernel,
        grid_spec=pltpu.PrefetchScalarGridSpec(
            num_scalar_prefetch=1,
            grid=(length // ROWS,),
            in_specs=[
                pl.BlockSpec((take, feature_parts, tall, width), lambda i, s: (i, 0, 0, 0)),
                whole(clock), whole(gain), whole(two_grad), rows(features), whole(w_wide),
            ]
            + [rows(6 * PAIR)] * 2,
            out_specs=whole(x_blocks),
            scratch_shapes=[pltpu.VMEM((1, features), F32)],
        ),
        out_shape=jax.ShapeDtypeStruct(x_blocks.shape, BF16),
        compiler_params=params(20),
        cost_estimate=cost(7),
        name="begin_back",
    )(limit, x_blocks, clock, gain, two_grad, middle_grad, w_wide, high, low)


DIRECT = 8


def clock_rows(step_ids, features):
    half_width = features // 2
    ladder = jnp.arange(half_width, dtype=F32) / half_width
    rate_rows = jnp.exp(-math.log(10000.0) * ladder)
    angles = step_ids.astype(F32)[:, None] * rate_rows[None, :]
    return jnp.concatenate([jnp.sin(angles), jnp.cos(angles)], axis=-1)


def swap(value, apart):
    count = lax.axis_size("tensor")
    return lax.ppermute(value, "tensor", [(i, i ^ apart) for i in range(count)])


def along_dp(value, move):
    count = lax.axis_size("dp")
    return lax.ppermute(value, "dp", [(i, move(i)) for i in range(count)])


def across(value):
    return ahead(value, 0, 1)


def ahead(value, step, flip=0):
    count = lax.axis_size("dp") // 2
    return along_dp(value, lambda i: (i // 2 + step) % count * 2 + (i + flip) % 2)


def places():
    count = lax.axis_size("dp") // 2
    own = lax.axis_index("dp")
    coarse = (own // 2 - jnp.arange(count, dtype=jnp.int32)) % count
    return jnp.concatenate([coarse * 2 + own % 2, coarse * 2 + 1 - own % 2])


def collect_coarse(shard):
    count = lax.axis_size("dp") // 2
    return [shard] + [ahead(shard, step) for step in range(1, count)]


def collect_rows(shard):
    count = lax.axis_size("dp")
    rows = lax.all_to_all(
        jnp.broadcast_to(shard[None], (count,) + shard.shape), "dp", 0, 0, tiled=True
    )
    return rows.reshape(count * shard.shape[0], shard.shape[1])


def collect_columns(rows):
    far = swap(rows, 2)
    return rows, swap(rows, 1), far, swap(far, 1)


def add(*values):
    return add_wide(*values).astype(BF16)


def fold_pair(values):
    own = lax.axis_index("dp") % 2
    pick = lambda value, which: lax.dynamic_index_in_dim(value, which, value.ndim - 3, keepdims=False)
    sent = add(*[pick(value, 1 - own) for value in values])
    return sent, lambda: [pick(value, own) for value in values] + [across(sent)]


def fold_far(values):
    sent = add(*[value[0] for value in values])
    return sent, lambda: [value[1] for value in values] + [swap(sent, 2)]


def fold_coarse(values):
    count = lax.axis_size("dp") // 2
    own = lax.axis_index("dp") // 2
    pick = lambda value, which: lax.dynamic_index_in_dim(value, which % count, 0, keepdims=False)
    value = add(*values)
    came = [ahead(pick(value, own + step), step) for step in range(1, count)]
    return value, [pick(value, own)] + came


def add_wide(*values):
    total = values[0].astype(F32)
    for value in values[1:]:
        total += value.astype(F32)
    return total


def grouped(value):
    count = lax.axis_size("dp")
    two, rows, columns = value.shape
    return value.reshape(two, count // 2, 2, rows // count, columns)


def exchange_rows(value):
    count = lax.axis_size("dp")
    groups = value.reshape(count, value.shape[0] // count, value.shape[1])
    return jnp.sum(lax.all_to_all(groups, "dp", 0, 0, tiled=True).astype(F32), axis=0)


def three_terms(values):
    terms = []
    for _ in range(3):
        term = lax.reduce_precision(values, 8, 7)
        terms.append(term.astype(BF16))
        values = values - term
    return terms


def together(*values):
    return lax.optimization_barrier(values)


def after(value, *others):
    return lax.optimization_barrier((value,) + others)[0]


def on_device(
    states, timesteps, lengths, deal_order, w_qkv, w_out, w_up, w_down, gain_attn, gain_ffn, out_grad
):
    both = ("dp", "tensor")
    dp_count = lax.axis_size("dp")
    tensor_count = lax.axis_size("tensor")
    devices = dp_count * tensor_count
    total_seqs, tokens, width = states.shape
    assert tensor_count == 4 and total_seqs == devices
    features = width * tensor_count
    own = lax.axis_index("dp") * tensor_count + lax.axis_index("tensor")
    own_id = lax.dynamic_slice_in_dim(deal_order, own, 1)
    limit = lengths[own_id]
    clock = clock_rows(timesteps[own_id], features)
    per = gain_attn.shape[0]
    rows = w_qkv.shape[0]
    hidden = w_up.shape[1]

    rest = jnp.concatenate([w_out.T, w_up, w_down.T], axis=1)
    qkv = w_qkv.reshape(rows, -1)
    direct = dp_count <= DIRECT
    if direct:
        place, groups = places(), dp_count
        wide = qkv.shape[1]
        pieces = collect_coarse(jnp.concatenate([qkv, across(qkv)], axis=1))
        qkv_rows = jnp.concatenate(
            [piece[:, :wide] for piece in pieces] + [piece[:, wide:] for piece in pieces], axis=0
        )
        mine = jnp.concatenate(collect_coarse(rest), axis=0)
        far_rows, other, far_mine = together(
            swap(qkv_rows, 2), in_hbm(across(mine)), in_hbm(swap(mine, 2))
        )
        qkv_parts = (qkv_rows, swap(qkv_rows, 1), far_rows, swap(far_rows, 1))
    else:
        place, groups = jnp.zeros((1,), jnp.int32), None
        qkv_parts = collect_columns(collect_rows(qkv))
        rest_parts = [(part,) for part in collect_columns(collect_rows(rest))]

    spare = jnp.stack(three_terms(gain_attn) + three_terms(gain_ffn)).reshape(1, 6 * per)
    spare = jnp.pad(spare, ((0, SPARE - 1), (0, width - 6 * per)))
    arranged = jnp.concatenate(
        [states[deal_order], jnp.broadcast_to(spare[None], (devices, SPARE, width))], axis=1
    )
    x_blocks = lax.all_to_all(arranged, both, 0, 0, tiled=True)
    gains = jnp.sum(x_blocks[:, tokens, : 6 * per].reshape(devices, 2, 3, per).astype(F32), axis=2)
    gain_one = gains[:, 0].reshape(1, features)
    gain_two = gains[:, 1].reshape(1, features)
    x_blocks = x_blocks.reshape(dp_count, tensor_count, tokens + SPARE, width)

    mixed, n_one_turn, qkv_wide = project(
        limit, place, groups, x_blocks, clock, gain_one, qkv_parts
    )
    if direct:
        near_mine, near_other = in_hbm(swap(mine, 1)), in_hbm(swap(other, 1))
        last_mine, far_other = in_hbm(swap(far_mine, 1)), in_hbm(swap(other, 2))
    ctx, ctx_turn, lse = attend(limit, mixed, tensor_count)
    if direct:
        ctx, near_mine, near_other, last_mine, far_other = together(
            ctx, near_mine, near_other, last_mine, far_other
        )
        last_other = swap(far_other, 1)
        rest_parts = (
            (mine, other), (near_mine, near_other), (far_mine, far_other), (last_mine, last_other)
        )
    output, context_grad, middle_grad, two_grad, up_send, down_send, up_keep, down_keep = middle_block(
        limit, place, groups, x_blocks, clock, gain_two, ctx, rest_parts, out_grad
    )
    up_came, down_came = swap(up_send, 1), swap(down_send, 1)

    back = functools.partial(attend_back, limit, mixed, ctx_turn, lse)
    if direct:
        down_sent, down_rest = fold_far([grouped(value) for value in (down_keep, down_came)])
        up_sent, up_rest = fold_pair([grouped(value) for value in (up_keep, up_came)])
        context_grad = after(context_grad, down_sent, up_sent)
    high, three, two = back(context_grad, n_one_turn, 3)
    if direct:
        *down_rest, down_came = down_rest()
        *up_rest, up_came = up_rest()
        high, three, two, down_came, up_came = together(high, three, two, down_came, up_came)
        down_value, down_pieces = fold_coarse([*down_rest, down_came])
        up_sent, up_rest = fold_far([add(*up_rest, up_came)])
        context_grad = after(context_grad, down_value, up_sent)
    far = add(two, swap(three, 1))
    came_far = swap(far, 2)
    low, one, own_part = back(after(context_grad, high, far), n_one_turn, 1)
    if direct:
        *up_rest, up_came = up_rest()
        low, one, own_part, up_came, came_far, *down_pieces = together(
            low, one, own_part, up_came, came_far, *down_pieces
        )
        up_value, up_pieces = fold_coarse([*up_rest, up_came])
        down_sent, down_rest = fold_pair([add_wide(*down_pieces)[..., None, :, :, :]])
        middle_grad = after(middle_grad, up_value, down_sent)
    came_one = swap(one, 1)
    begin_grad = begin_block(
        limit, x_blocks, clock, gain_one, two_grad, qkv_wide, middle_grad, high, low
    )
    if direct:
        begin_grad, came_one, up_pieces[2] = together(begin_grad, came_one, up_pieces[2])
        near = [grouped(value[None])[0] for value in (own_part, came_one, came_far)]
        qkv_value, qkv_pieces = fold_coarse(fold_pair(near)[1]())
        *up_pieces, down_came, _ = together(*up_pieces, down_rest()[-1], qkv_value)
        up_total = add_wide(*up_pieces)
        down_total = add_wide(*down_rest()[:-1], down_came)[0]
        qkv_total = add_wide(*qkv_pieces)
    else:
        up_total = exchange_rows(add(*fold_far([up_keep, up_came])[1]()))
        down_total = exchange_rows(add(*fold_far([down_keep, down_came])[1]()))
        qkv_total = exchange_rows(add(own_part, came_one, came_far))
    returned = lax.all_to_all(
        begin_grad.reshape(devices, tokens + SPARE, width), both, 0, 0, tiled=True
    )
    inverse = (
        jnp.zeros((total_seqs,), jnp.int32)
        .at[deal_order]
        .set(jnp.arange(total_seqs, dtype=jnp.int32))
    )
    states_grad = returned[inverse][:, :tokens]
    gain_grads = jnp.sum(returned[:, tokens:].astype(F32), axis=0).reshape(2, devices, per)
    gain_grads = lax.dynamic_index_in_dim(gain_grads, own, 1, keepdims=False)
    return (
        output,
        states_grad,
        qkv_total.reshape(w_qkv.shape),
        up_total[:, :PAIR].T,
        up_total[:, PAIR:],
        down_total.T,
        gain_grads[0],
        gain_grads[1],
    )


def solution(mesh):
    in_specs = (
        P(None, "dp", "tensor"),
        P(),
        P(),
        P(),
        P("dp", None, "tensor"),
        P("tensor", "dp"),
        P("dp", "tensor"),
        P("tensor", "dp"),
        P(("dp", "tensor")),
        P(("dp", "tensor")),
        P(("dp", "tensor"), None, None),
    )
    out_specs = (
        P(("dp", "tensor"), None, None),
        P(None, "dp", "tensor"),
        P("dp", None, "tensor"),
        P("tensor", "dp"),
        P("dp", "tensor"),
        P("tensor", "dp"),
        P(("dp", "tensor")),
        P(("dp", "tensor")),
    )
    return jax.shard_map(
        on_device, mesh=mesh, in_specs=in_specs, out_specs=out_specs, check_vma=False
    )
```

```python
import functools
import math

import jax
import jax.numpy as jnp
from jax import lax
from jax.experimental import pallas as pl
from jax.experimental.pallas import tpu as pltpu
from jax.sharding import PartitionSpec as P

HEAD_DIM = 64
PAIR = 2 * HEAD_DIM
ROWS = 512
KEYS = 256
BACK_KEYS = 512
SPARE = 8
SCORE_SCALE = 1.0 / math.sqrt(HEAD_DIM)
LOG2E = math.log2(math.e)
F32 = jnp.float32
BF16 = jnp.bfloat16
NN = (((1,), (0,)), ((), ()))
NT = (((1,), (1,)), ((), ()))
MIB = 1024 * 1024


def mul(lhs, rhs, dims=NN):
    return lax.dot_general(lhs, rhs, dims, preferred_element_type=F32)


def join_tokens(ref):
    blocks, parts, tall, width = ref.shape
    tokens = tall - SPARE
    return jnp.concatenate(
        [ref[:, part, 0:tokens].reshape(blocks * tokens, width) for part in range(parts)], axis=-1
    ).astype(F32)


def place_rows(groups, place_ref, first, source, targets):
    if groups is None:
        for target, columns, own in targets:
            target[:, columns] = source[:, own]
        return
    rows = source.shape[0] // groups
    for group in range(groups):
        spot = pl.ds(pl.multiple_of(place_ref[first + group] * rows, rows), rows)
        for target, columns, own in targets:
            target[spot, columns] = source[group * rows : (group + 1) * rows, own]


def norm_parts(values):
    center = values - jnp.mean(values, axis=-1, keepdims=True)
    spread = jnp.mean(center * center, axis=-1, keepdims=True)
    inverse = lax.rsqrt(spread + 1e-05)
    return center * inverse, inverse


def norm_back(grad, gain, unit, inverse):
    scaled = grad * gain
    mean_scaled = jnp.mean(scaled, axis=-1, keepdims=True)
    mean_along = jnp.mean(scaled * unit, axis=-1, keepdims=True)
    return inverse * (scaled - mean_scaled - unit * mean_along)


def in_hbm(value):
    return pltpu.with_memory_space_constraint(value, pltpu.HBM)


def cost(microseconds):
    return pl.CostEstimate(
        flops=int(microseconds * 1.15e9), bytes_accessed=1 << 20, transcendentals=0
    )


def params(mebibytes):
    return pltpu.CompilerParams(vmem_limit_bytes=mebibytes * MIB)


def project_kernel(groups, limit_ref, place_ref, x_ref, clock_ref, gain_ref, *refs):
    w_refs, (mixed_ref, n_turn_ref, wide) = refs[:-3], refs[-3:]
    step = pl.program_id(0)

    @pl.when(step == 0)
    def _():
        for part, w_ref in enumerate(w_refs):
            width = w_ref.shape[1]
            columns = slice(part * width, (part + 1) * width)
            place_rows(groups, place_ref, 0, w_ref, [(wide, columns, slice(0, width))])

    @pl.when(step * ROWS < limit_ref[0])
    def _():
        begin = join_tokens(x_ref) + clock_ref[...]
        unit, _ = norm_parts(begin)
        normed = (unit * gain_ref[...]).astype(BF16)
        n_turn_ref[...] = normed.T
        mixed_ref[...] = mul(normed, wide[...]).astype(BF16)

    @pl.when(step * ROWS >= limit_ref[0])
    def _():
        n_turn_ref[...] = jnp.zeros_like(n_turn_ref)
        mixed_ref[...] = jnp.zeros_like(mixed_ref)


def project(limit, place, groups, x_blocks, clock, gain, w_parts):
    senders, feature_parts, tall, width = x_blocks.shape
    tokens = tall - SPARE
    length = senders * tokens
    features = feature_parts * width
    parts, columns = len(w_parts), w_parts[0].shape[1]
    take = ROWS // tokens
    return pl.pallas_call(
        functools.partial(project_kernel, groups),
        grid_spec=pltpu.PrefetchScalarGridSpec(
            num_scalar_prefetch=2,
            grid=(length // ROWS,),
            in_specs=[
                pl.BlockSpec((take, feature_parts, tall, width), lambda i, *s: (i, 0, 0, 0)),
                pl.BlockSpec((1, features), lambda i, *s: (0, 0)),
                pl.BlockSpec((1, features), lambda i, *s: (0, 0)),
            ]
            + [pl.BlockSpec((features, columns), lambda i, *s: (0, 0))] * parts,
            out_specs=[
                pl.BlockSpec((ROWS, parts * columns), lambda i, *s: (i, 0)),
                pl.BlockSpec((features, ROWS), lambda i, *s: (0, i)),
                pl.BlockSpec((features, parts * columns), lambda i, *s: (0, 0)),
            ],
        ),
        out_shape=[
            jax.ShapeDtypeStruct((length, parts * columns), BF16),
            pltpu.HBM((features, length), BF16),
            pltpu.HBM((features, parts * columns), BF16),
        ],
        compiler_params=params(20),
        cost_estimate=cost(5),
        name="project",
    )(limit, place, x_blocks, clock, gain, *w_parts)


def head_lanes(shape, head):
    lane = lax.broadcasted_iota(jnp.int32, shape, 1)
    return (lane >= head * HEAD_DIM) & (lane < (head + 1) * HEAD_DIM)


def spare_lane(shape, head):
    lane = lax.broadcasted_iota(jnp.int32, shape, 1)
    return lane == (1 - head) * HEAD_DIM


def masked_keys(keys, head, limit):
    row = lax.broadcasted_iota(jnp.int32, keys.shape, 0)
    spare = jnp.where(
        spare_lane(keys.shape, head) & (row >= limit), jnp.asarray(-1e30, F32), jnp.asarray(0.0, F32)
    )
    return jnp.where(head_lanes(keys.shape, head), keys.astype(F32), spare).astype(BF16)


def own_lanes(values, head):
    return jnp.where(head_lanes(values.shape, head), values.astype(F32), 0.0).astype(BF16)


def masked_queries(queries, head):
    spare = jnp.where(spare_lane(queries.shape, head), jnp.asarray(1.0, F32), jnp.asarray(0.0, F32))
    return jnp.where(head_lanes(queries.shape, head), queries.astype(F32), spare).astype(BF16)


def attend_kernel(limit_ref, q_ref, k_ref, v_ref, ctx_ref, turn_ref, lse_ref, keys_s, q_s, vt_s, sc_s):
    length = q_ref.shape[0]
    vt_s[...] = v_ref[...].astype(F32).T.astype(BF16)
    for head in range(2):
        keys_s[head] = masked_keys(k_ref[...], head, limit_ref[0])
        q_s[head] = masked_queries(q_ref[...], head)
    factor = SCORE_SCALE * LOG2E
    spans = [slice(at, at + KEYS) for at in range(0, length, KEYS)]
    outs = []
    for head in range(2):
        feats = slice(head * HEAD_DIM, (head + 1) * HEAD_DIM)
        peak = None
        for span in spans:
            scores = mul(keys_s[head, span], q_s[head], NT)
            sc_s[head, span] = scores
            high = jnp.max(scores, axis=0, keepdims=True)
            peak = high if peak is None else jnp.maximum(peak, high)
        peak = peak * factor
        total = jnp.zeros_like(peak)
        gathered = jnp.zeros((HEAD_DIM, length), F32)
        for span in spans:
            expo = jnp.exp2(sc_s[head, span] * factor - peak)
            total += jnp.sum(expo, axis=0, keepdims=True)
            gathered += mul(vt_s[feats, span], expo.astype(BF16))
        outs.append(gathered / total)
        lse_ref[0, head : head + 1, :] = peak + jnp.log2(total)
    both = jnp.concatenate(outs, axis=0)
    turn_ref[...] = both.astype(BF16)
    ctx_ref[...] = both.T.astype(BF16)


def attend(limit, mixed, pairs):
    length = mixed.shape[0]
    column = lambda c: pl.BlockSpec((length, PAIR), lambda i, s: (0, i * 3 + c))
    return pl.pallas_call(
        attend_kernel,
        grid_spec=pltpu.PrefetchScalarGridSpec(
            num_scalar_prefetch=1,
            grid=(pairs,),
            in_specs=[column(0), column(1), column(2)],
            out_specs=[
                pl.BlockSpec((length, PAIR), lambda i, s: (0, i)),
                pl.BlockSpec((PAIR, length), lambda i, s: (i, 0)),
                pl.BlockSpec((1, 2, length), lambda i, s: (i, 0, 0)),
            ],
            scratch_shapes=[
                pltpu.VMEM((2, length, PAIR), BF16),
                pltpu.VMEM((2, length, PAIR), BF16),
                pltpu.VMEM((PAIR, length), BF16),
                pltpu.VMEM((2, length, length), F32),
            ],
        ),
        out_shape=[
            pltpu.HBM((length, pairs * PAIR), BF16),
            pltpu.HBM((pairs * PAIR, length), BF16),
            jax.ShapeDtypeStruct((pairs, 2, length), F32),
        ],
        compiler_params=params(28),
        cost_estimate=cost(15),
        name="attend",
    )(limit, mixed, mixed, mixed)


def gelu_both(values):
    root = math.sqrt(2.0 / math.pi)
    scaled = root * values
    inner = scaled * (1.0 + 0.044715 * (values * values))
    tanh = jnp.tanh(inner)
    half = 0.5 + 0.5 * tanh
    slope = half + (1.0 - tanh * tanh) * (1.5 * inner - scaled)
    return values * half, slope


def middle_kernel(
    groups, limit_ref, place_ref, x_ref, clock_ref, gain_ref, ctx_ref, og_ref, *refs
):
    weight_refs, refs = refs[:-17], refs[-17:]
    out_ref, cg_ref, mg_ref, gg_ref, up_send, down_send, up_keep, down_keep = refs[:8]
    wide, units, active_s, ug_s, n_turn, fg_turn, ag_turn, ctx_s, sems = refs[8:]
    step = pl.program_id(0)
    parts, _, hidden = active_s.shape
    blocks = pl.num_programs(0) - parts
    each = len(weight_refs) // parts

    def fetch(part, kind):
        target, wide_, own = (
            (wide, PAIR, slice(0, PAIR)),
            (units, 2 * hidden, slice(PAIR, PAIR + 2 * hidden)),
        )[kind]
        columns = slice(part * wide_, (part + 1) * wide_)
        copies = []
        for at, w_ref in enumerate(weight_refs[part * each : (part + 1) * each]):
            count = 1 if groups is None else groups // each
            rows = w_ref.shape[0] // count
            for group in range(count):
                index = at * count + group
                spot = pl.ds(0, rows)
                if groups is not None:
                    spot = pl.ds(pl.multiple_of(place_ref[index] * rows, rows), rows)
                copies.append(
                    pltpu.make_async_copy(
                        w_ref.at[pl.ds(group * rows, rows), own],
                        target.at[spot, columns],
                        sems.at[kind, part, index],
                    )
                )
        return copies

    @pl.when(step == 0)
    def _():
        gg_ref[...] = jnp.zeros_like(gg_ref)
        for part in range(parts):
            for copy in fetch(part, 0) + fetch(part, 1):
                copy.start()
        for part in range(parts):
            for copy in fetch(part, 0) + fetch(part, 1):
                copy.wait()

    dead = (step < blocks) & (step * ROWS >= limit_ref[0])

    @pl.when((step < blocks) & jnp.logical_not(dead))
    def _():
        spot = pl.ds(pl.multiple_of(step * ROWS, ROWS), ROWS)
        gain = gain_ref[...]
        live = step * ROWS + lax.broadcasted_iota(jnp.int32, (ROWS, 1), 0) < limit_ref[0]
        begin = join_tokens(x_ref) + clock_ref[...]
        middle = begin + mul(ctx_ref[...], wide[...], NT)
        unit, inverse = norm_parts(middle)
        normed = (unit * gain).astype(BF16)
        n_turn[:, spot] = normed.T
        res_grad = jnp.where(live, og_ref[0].astype(F32), 0.0)
        feed_grad = res_grad.astype(BF16)
        fg_turn[:, spot] = feed_grad.T
        feed = jnp.zeros_like(middle)
        two_grad = jnp.zeros_like(middle)
        for part in range(parts):
            up = slice(2 * part * hidden, (2 * part + 1) * hidden)
            down = slice((2 * part + 1) * hidden, (2 * part + 2) * hidden)
            upper = mul(normed, units[:, up])
            active, slope = gelu_both(upper)
            active = active.astype(BF16)
            active_s[part, spot] = active
            feed += mul(active, units[:, down], NT)
            upper_grad = (mul(feed_grad, units[:, down]) * slope).astype(BF16)
            ug_s[part, spot] = upper_grad
            two_grad += mul(upper_grad, units[:, up], NT)
        out_ref[0] = jnp.where(live, middle + feed, 0.0).astype(BF16)
        gg_ref[...] += jnp.sum(two_grad * unit, axis=0, keepdims=True)
        middle_grad = res_grad + norm_back(two_grad, gain, unit, inverse)
        mg_ref[...] = middle_grad
        att_grad = middle_grad.astype(BF16)
        ag_turn[:, spot] = att_grad.T
        cg_ref[...] = mul(att_grad, wide[...]).astype(BF16)
        for part in range(parts):
            ctx_s[part, spot] = ctx_ref[:, part * PAIR : (part + 1) * PAIR]

    @pl.when(dead)
    def _():
        spot = pl.ds(pl.multiple_of(step * ROWS, ROWS), ROWS)
        for ref in (out_ref, cg_ref, mg_ref):
            ref[...] = jnp.zeros_like(ref)
        for ref in (active_s, ug_s, ctx_s):
            ref[:, spot] = jnp.zeros((ref.shape[0], ROWS, ref.shape[2]), BF16)
        for ref in (n_turn, fg_turn, ag_turn):
            ref[:, spot] = jnp.zeros((ref.shape[0], ROWS), BF16)

    @pl.when(step >= blocks)
    def _():
        turn = step - blocks
        part = jnp.where(turn < 2, 3 - 2 * turn, 6 - 2 * turn)
        grads = (
            mul(ag_turn[...], ctx_s[part]).astype(BF16),
            mul(n_turn[...], ug_s[part]).astype(BF16),
            mul(fg_turn[...], active_s[part]).astype(BF16),
        )

        def into(up_ref, down_ref):
            up_ref[0, :, 0:PAIR], up_ref[0, :, PAIR:], down_ref[0] = grads

        pl.when(turn < 2)(lambda: into(up_send, down_send))
        pl.when(turn >= 2)(lambda: into(up_keep, down_keep))


def middle_block(limit, place, groups, x_blocks, clock, gain, ctx, w_parts, out_grad):
    senders, feature_parts, tall, width = x_blocks.shape
    tokens = tall - SPARE
    length = senders * tokens
    features = feature_parts * width
    parts = len(w_parts)
    weights = [in_hbm(w) for part in w_parts for w in part]
    columns = weights[0].shape[1]
    hidden = (columns - PAIR) // 2
    take = ROWS // tokens
    blocks = length // ROWS
    row = lambda i: jnp.minimum(i, blocks - 1)
    whole = lambda array: pl.BlockSpec(
        array.shape, lambda i, *s: (0,) * array.ndim, pipeline_mode=pl.Buffered(1)
    )
    rows = lambda n: pl.BlockSpec((ROWS, n), lambda i, *s: (row(i), 0))
    one = pl.BlockSpec((1, ROWS, features), lambda i, *s: (0, row(i), 0))
    grads = lambda first, n: pl.BlockSpec(
        (1, features, n), lambda i, *s: (jnp.clip(i - blocks - first, 0, 1), 0, 0)
    )
    up_shape = pltpu.HBM((2, features, PAIR + hidden), BF16)
    down_shape = pltpu.HBM((2, features, hidden), BF16)
    return pl.pallas_call(
        functools.partial(middle_kernel, groups),
        grid_spec=pltpu.PrefetchScalarGridSpec(
            num_scalar_prefetch=2,
            grid=(blocks + parts,),
            in_specs=[
                pl.BlockSpec(
                    (take, feature_parts, tall, width), lambda i, *s: (row(i), 0, 0, 0)
                ),
                whole(clock),
                whole(gain),
                rows(features),
                one,
            ]
            + [pl.BlockSpec(memory_space=pltpu.HBM)] * len(weights),
            out_specs=[
                one, rows(features), rows(features),
                pl.BlockSpec((1, features), lambda i, *s: (0, 0)),
                grads(0, PAIR + hidden), grads(0, hidden), grads(2, PAIR + hidden), grads(2, hidden),
            ],
            scratch_shapes=[
                pltpu.VMEM((features, parts * PAIR), BF16),
                pltpu.VMEM((features, parts * 2 * hidden), BF16),
                pltpu.VMEM((parts, length, hidden), BF16),
                pltpu.VMEM((parts, length, hidden), BF16),
                pltpu.VMEM((features, length), BF16),
                pltpu.VMEM((features, length), BF16),
                pltpu.VMEM((features, length), BF16),
                pltpu.VMEM((parts, length, PAIR), BF16),
                pltpu.SemaphoreType.DMA((2, parts, groups or 1)),
            ],
        ),
        out_shape=[
            jax.ShapeDtypeStruct((1, length, features), BF16),
            pltpu.HBM((length, features), BF16),
            pltpu.HBM((length, features), F32),
            jax.ShapeDtypeStruct((1, features), F32),
            up_shape, down_shape, up_shape, down_shape,
        ],
        compiler_params=params(48),
        cost_estimate=cost(25),
        name="middle",
    )(limit, place, x_blocks, clock, gain, in_hbm(ctx), in_hbm(out_grad), *weights)


def attend_back_kernel(
    limit_ref, q_ref, k_ref, v_ref, turn_ref, lse_ref, cg_ref, n_turn_ref,
    dm_ref, first_ref, second_ref, keys_s, q_s, qz_s, do_s, kt_s, delta_s,
):
    limit = limit_ref[0]
    length = q_ref.shape[0]
    kt_s[...] = k_ref[...].astype(F32).T.astype(BF16)
    along = cg_ref[...].astype(F32).T * turn_ref[...].astype(F32)
    for head in range(2):
        feats = slice(head * HEAD_DIM, (head + 1) * HEAD_DIM)
        delta_s[head : head + 1, :] = jnp.sum(along[feats, :], axis=0, keepdims=True)
        keys_s[head] = masked_keys(k_ref[...], head, limit)
        q_s[head] = masked_queries(q_ref[...], head)
        qz_s[head] = own_lanes(q_ref[...], head)
        do_s[head] = own_lanes(cg_ref[...], head)
    factor = SCORE_SCALE * LOG2E
    turned = [jnp.zeros((HEAD_DIM, length), F32)] * 2
    for at in range(0, length, BACK_KEYS):
        span = slice(at, at + BACK_KEYS)
        key_grad = jnp.zeros((BACK_KEYS, PAIR), F32)
        value_grad = jnp.zeros((BACK_KEYS, PAIR), F32)
        for head in range(2):
            feats = slice(head * HEAD_DIM, (head + 1) * HEAD_DIM)
            scores = mul(keys_s[head, span], q_s[head], NT)
            prob = jnp.exp2(scores * factor - lse_ref[0, head : head + 1, :])
            prob_grad = mul(v_ref[span, :], do_s[head], NT)
            score_grad = (prob * (prob_grad - delta_s[head : head + 1, :])).astype(BF16)
            value_grad += mul(prob.astype(BF16), do_s[head])
            key_grad += mul(score_grad, qz_s[head])
            turned[head] += mul(kt_s[feats, span], score_grad)
        dm_ref[span, PAIR : 2 * PAIR] = (key_grad * SCORE_SCALE).astype(BF16)
        dm_ref[span, 2 * PAIR : 3 * PAIR] = value_grad.astype(BF16)
    query_grad = jnp.concatenate(turned, axis=0) * SCORE_SCALE
    dm_ref[:, 0:PAIR] = query_grad.T.astype(BF16)
    grad = mul(n_turn_ref[...], dm_ref[...]).astype(BF16)

    @pl.when(pl.program_id(0) == 0)
    def _():
        first_ref[...] = grad

    @pl.when(pl.program_id(0) == 1)
    def _():
        second_ref[...] = grad


def attend_back(limit, mixed, ctx_turn, lse, context_grad, n_turn, first):
    length = mixed.shape[0]
    features = n_turn.shape[0]
    pair = lambda i: first - i
    column = lambda c: pl.BlockSpec((length, PAIR), lambda i, s: (0, pair(i) * 3 + c))
    return pl.pallas_call(
        attend_back_kernel,
        grid_spec=pltpu.PrefetchScalarGridSpec(
            num_scalar_prefetch=1,
            grid=(2,),
            in_specs=[
                column(0), column(1), column(2),
                pl.BlockSpec((PAIR, length), lambda i, s: (pair(i), 0)),
                pl.BlockSpec((1, 2, length), lambda i, s: (pair(i), 0, 0)),
                pl.BlockSpec((length, PAIR), lambda i, s: (0, pair(i))),
                pl.BlockSpec((features, length), lambda i, s: (0, 0)),
            ],
            out_specs=[
                pl.BlockSpec((length, 3 * PAIR), lambda i, s: (0, i)),
                pl.BlockSpec((features, 3 * PAIR), lambda i, s: (0, 0)),
                pl.BlockSpec((features, 3 * PAIR), lambda i, s: (0, 0)),
            ],
            scratch_shapes=[
                pltpu.VMEM((2, length, PAIR), BF16),
                pltpu.VMEM((2, length, PAIR), BF16),
                pltpu.VMEM((2, length, PAIR), BF16),
                pltpu.VMEM((2, length, PAIR), BF16),
                pltpu.VMEM((PAIR, length), BF16),
                pltpu.VMEM((8, length), F32),
            ],
        ),
        out_shape=[
            jax.ShapeDtypeStruct((length, 2 * 3 * PAIR), BF16),
            jax.ShapeDtypeStruct((features, 3 * PAIR), BF16),
            jax.ShapeDtypeStruct((features, 3 * PAIR), BF16),
        ],
        compiler_params=params(28),
        cost_estimate=cost(16),
        name="attend_back",
    )(limit, mixed, mixed, mixed, ctx_turn, lse, context_grad, n_turn)


def begin_kernel(
    limit_ref, x_ref, clock_ref, gain_ref, gg_two_ref, mg_ref, w_ref, high_ref, low_ref, bg_ref, gg_s
):
    step = pl.program_id(0)
    _, parts, tall, width = bg_ref.shape
    tokens = tall - SPARE
    blocks = ROWS // tokens
    spot = pl.ds(step * blocks, blocks)

    @pl.when(step == 0)
    def _():
        gg_s[...] = jnp.zeros_like(gg_s)

    @pl.when(step * ROWS < limit_ref[0])
    def _():
        begin = join_tokens(x_ref) + clock_ref[...]
        unit, inverse = norm_parts(begin)
        one_grad = jnp.zeros_like(begin)
        for part, (d_ref, at) in enumerate(((low_ref, 1), (low_ref, 0), (high_ref, 1), (high_ref, 0))):
            columns = slice(part * 3 * PAIR, (part + 1) * 3 * PAIR)
            own = slice(at * 3 * PAIR, (at + 1) * 3 * PAIR)
            one_grad += mul(d_ref[:, own], w_ref[:, columns], NT)
        gg_s[...] += jnp.sum(one_grad * unit, axis=0, keepdims=True)
        total = (mg_ref[...] + norm_back(one_grad, gain_ref[...], unit, inverse)).astype(BF16)
        for part in range(parts):
            piece = total[:, part * width : (part + 1) * width]
            bg_ref[spot, part, 0:tokens] = piece.reshape(blocks, tokens, width)

    @pl.when(step * ROWS >= limit_ref[0])
    def _():
        bg_ref[spot] = jnp.zeros((blocks,) + bg_ref.shape[1:], BF16)

    @pl.when(step == pl.num_programs(0) - 1)
    def _():
        rows = []
        for ref in (gg_s, gg_two_ref):
            for part in range(parts):
                rows.append(ref[:, part * width : (part + 1) * width])
        bg_ref[:, :, tokens:tall] = jnp.broadcast_to(
            jnp.concatenate(rows, axis=0).astype(BF16), bg_ref.shape[:2] + (SPARE, width)
        )


def begin_block(limit, x_blocks, clock, gain, two_grad, w_wide, middle_grad, high, low):
    senders, feature_parts, tall, width = x_blocks.shape
    tokens = tall - SPARE
    length = senders * tokens
    features = feature_parts * width
    take = ROWS // tokens
    whole = lambda array: pl.BlockSpec(array.shape, lambda i, s: (0,) * array.ndim)
    rows = lambda n: pl.BlockSpec((ROWS, n), lambda i, s: (i, 0))
    return pl.pallas_call(
        begin_kernel,
        grid_spec=pltpu.PrefetchScalarGridSpec(
            num_scalar_prefetch=1,
            grid=(length // ROWS,),
            in_specs=[
                pl.BlockSpec((take, feature_parts, tall, width), lambda i, s: (i, 0, 0, 0)),
                whole(clock), whole(gain), whole(two_grad), rows(features), whole(w_wide),
            ]
            + [rows(6 * PAIR)] * 2,
            out_specs=whole(x_blocks),
            scratch_shapes=[pltpu.VMEM((1, features), F32)],
        ),
        out_shape=jax.ShapeDtypeStruct(x_blocks.shape, BF16),
        compiler_params=params(20),
        cost_estimate=cost(7),
        name="begin_back",
    )(limit, x_blocks, clock, gain, two_grad, middle_grad, w_wide, high, low)


DIRECT = 8


def clock_rows(step_ids, features):
    half_width = features // 2
    ladder = jnp.arange(half_width, dtype=F32) / half_width
    rate_rows = jnp.exp(-math.log(10000.0) * ladder)
    angles = step_ids.astype(F32)[:, None] * rate_rows[None, :]
    return jnp.concatenate([jnp.sin(angles), jnp.cos(angles)], axis=-1)


def swap(value, apart):
    count = lax.axis_size("tensor")
    return lax.ppermute(value, "tensor", [(i, i ^ apart) for i in range(count)])


def along_dp(value, move):
    count = lax.axis_size("dp")
    return lax.ppermute(value, "dp", [(i, move(i)) for i in range(count)])


def across(value):
    return ahead(value, 0, 1)


def ahead(value, step, flip=0):
    count = lax.axis_size("dp") // 2
    return along_dp(value, lambda i: (i // 2 + step) % count * 2 + (i + flip) % 2)


def places():
    count = lax.axis_size("dp") // 2
    own = lax.axis_index("dp")
    coarse = (own // 2 - jnp.arange(count, dtype=jnp.int32)) % count
    return jnp.concatenate([coarse * 2 + own % 2, coarse * 2 + 1 - own % 2])


def collect_coarse(shard):
    count = lax.axis_size("dp") // 2
    return [shard] + [ahead(shard, step) for step in range(1, count)]


def collect_rows(shard):
    count = lax.axis_size("dp")
    rows = lax.all_to_all(
        jnp.broadcast_to(shard[None], (count,) + shard.shape), "dp", 0, 0, tiled=True
    )
    return rows.reshape(count * shard.shape[0], shard.shape[1])


def collect_columns(rows):
    far = swap(rows, 2)
    return rows, swap(rows, 1), far, swap(far, 1)


def add(*values):
    return add_wide(*values).astype(BF16)


def fold_pair(values):
    own = lax.axis_index("dp") % 2
    pick = lambda value, which: lax.dynamic_index_in_dim(value, which, value.ndim - 3, keepdims=False)
    sent = add(*[pick(value, 1 - own) for value in values])
    return sent, lambda: [pick(value, own) for value in values] + [across(sent)]


def fold_far(values):
    sent = add(*[value[0] for value in values])
    return sent, lambda: [value[1] for value in values] + [swap(sent, 2)]


def fold_coarse(values):
    count = lax.axis_size("dp") // 2
    own = lax.axis_index("dp") // 2
    pick = lambda value, which: lax.dynamic_index_in_dim(value, which % count, 0, keepdims=False)
    value = add(*values)
    came = [ahead(pick(value, own + step), step) for step in range(1, count)]
    return value, [pick(value, own)] + came


def add_wide(*values):
    total = values[0].astype(F32)
    for value in values[1:]:
        total += value.astype(F32)
    return total


def grouped(value):
    count = lax.axis_size("dp")
    two, rows, columns = value.shape
    return value.reshape(two, count // 2, 2, rows // count, columns)


def exchange_rows(value):
    count = lax.axis_size("dp")
    groups = value.reshape(count, value.shape[0] // count, value.shape[1])
    return jnp.sum(lax.all_to_all(groups, "dp", 0, 0, tiled=True).astype(F32), axis=0)


def three_terms(values):
    terms = []
    for _ in range(3):
        term = lax.reduce_precision(values, 8, 7)
        terms.append(term.astype(BF16))
        values = values - term
    return terms


def together(*values):
    return lax.optimization_barrier(values)


def after(value, *others):
    return lax.optimization_barrier((value,) + others)[0]


def on_device(
    states, timesteps, lengths, deal_order, w_qkv, w_out, w_up, w_down, gain_attn, gain_ffn, out_grad
):
    both = ("dp", "tensor")
    dp_count = lax.axis_size("dp")
    tensor_count = lax.axis_size("tensor")
    devices = dp_count * tensor_count
    total_seqs, tokens, width = states.shape
    assert tensor_count == 4 and total_seqs == devices
    features = width * tensor_count
    own = lax.axis_index("dp") * tensor_count + lax.axis_index("tensor")
    own_id = lax.dynamic_slice_in_dim(deal_order, own, 1)
    limit = lengths[own_id]
    clock = clock_rows(timesteps[own_id], features)
    per = gain_attn.shape[0]
    rows = w_qkv.shape[0]
    hidden = w_up.shape[1]

    rest = jnp.concatenate([w_out.T, w_up, w_down.T], axis=1)
    qkv = w_qkv.reshape(rows, -1)
    direct = dp_count <= DIRECT
    if direct:
        place, groups = places(), dp_count
        wide = qkv.shape[1]
        pieces = collect_coarse(jnp.concatenate([qkv, rest], axis=1))
        first = jnp.concatenate(pieces, axis=0)
        qkv_rows, mine = first[:, :wide], first[:, wide:]
        qkv_other = across(qkv_rows)
        qkv_rows = jnp.concatenate([qkv_rows, qkv_other], axis=0)
        far_rows, other, far_mine = together(
            swap(qkv_rows, 2), in_hbm(across(after(mine, qkv_other))), in_hbm(swap(mine, 2))
        )
        qkv_parts = (qkv_rows, swap(qkv_rows, 1), far_rows, swap(far_rows, 1))
    else:
        place, groups = jnp.zeros((1,), jnp.int32), None
        qkv_parts = collect_columns(collect_rows(qkv))
        rest_parts = [(part,) for part in collect_columns(collect_rows(rest))]

    spare = jnp.stack(three_terms(gain_attn) + three_terms(gain_ffn)).reshape(1, 6 * per)
    spare = jnp.pad(spare, ((0, SPARE - 1), (0, width - 6 * per)))
    arranged = jnp.concatenate(
        [states[deal_order], jnp.broadcast_to(spare[None], (devices, SPARE, width))], axis=1
    )
    if direct:
        arranged = after(arranged, *pieces[1:])
    x_blocks = lax.all_to_all(arranged, both, 0, 0, tiled=True)
    gains = jnp.sum(x_blocks[:, tokens, : 6 * per].reshape(devices, 2, 3, per).astype(F32), axis=2)
    gain_one = gains[:, 0].reshape(1, features)
    gain_two = gains[:, 1].reshape(1, features)
    x_blocks = x_blocks.reshape(dp_count, tensor_count, tokens + SPARE, width)

    mixed, n_one_turn, qkv_wide = project(
        limit, place, groups, x_blocks, clock, gain_one, qkv_parts
    )
    if direct:
        near_mine, near_other = in_hbm(swap(mine, 1)), in_hbm(swap(other, 1))
        last_mine, far_other = in_hbm(swap(far_mine, 1)), in_hbm(swap(other, 2))
    ctx, ctx_turn, lse = attend(limit, mixed, tensor_count)
    if direct:
        ctx, near_mine, near_other, last_mine, far_other = together(
            ctx, near_mine, near_other, last_mine, far_other
        )
        last_other = swap(far_other, 1)
        rest_parts = (
            (mine, other), (near_mine, near_other), (far_mine, far_other), (last_mine, last_other)
        )
    output, context_grad, middle_grad, two_grad, up_send, down_send, up_keep, down_keep = middle_block(
        limit, place, groups, x_blocks, clock, gain_two, ctx, rest_parts, out_grad
    )
    up_came, down_came = swap(up_send, 1), swap(down_send, 1)

    back = functools.partial(attend_back, limit, mixed, ctx_turn, lse)
    if direct:
        down_sent, down_rest = fold_far([grouped(value) for value in (down_keep, down_came)])
        up_sent, up_rest = fold_pair([grouped(value) for value in (up_keep, up_came)])
        context_grad = after(context_grad, down_sent, up_sent)
    high, three, two = back(context_grad, n_one_turn, 3)
    if direct:
        *down_rest, down_came = down_rest()
        *up_rest, up_came = up_rest()
        high, three, two, down_came, up_came = together(high, three, two, down_came, up_came)
        down_value, down_pieces = fold_coarse([*down_rest, down_came])
        up_sent, up_rest = fold_far([add(*up_rest, up_came)])
        context_grad = after(context_grad, down_value, up_sent)
    far = add(two, swap(three, 1))
    came_far = swap(far, 2)
    low, one, own_part = back(after(context_grad, high, far), n_one_turn, 1)
    if direct:
        *up_rest, up_came = up_rest()
        low, one, own_part, up_came, came_far, *down_pieces = together(
            low, one, own_part, up_came, came_far, *down_pieces
        )
        up_value, up_pieces = fold_coarse([*up_rest, up_came])
        down_sent, down_rest = fold_pair([add_wide(*down_pieces)[..., None, :, :, :]])
        middle_grad = after(middle_grad, up_value, down_sent)
    came_one = swap(one, 1)
    begin_grad = begin_block(
        limit, x_blocks, clock, gain_one, two_grad, qkv_wide, middle_grad, high, low
    )
    if direct:
        begin_grad, came_one, up_pieces[2] = together(begin_grad, came_one, up_pieces[2])
        near = [grouped(value[None])[0] for value in (own_part, came_one, came_far)]
        qkv_value, qkv_pieces = fold_coarse(fold_pair(near)[1]())
        *up_pieces, down_came, _ = together(*up_pieces, down_rest()[-1], qkv_value)
        up_total = add_wide(*up_pieces)
        down_total = add_wide(*down_rest()[:-1], down_came)[0]
        qkv_total = add_wide(*qkv_pieces)
    else:
        up_total = exchange_rows(add(*fold_far([up_keep, up_came])[1]()))
        down_total = exchange_rows(add(*fold_far([down_keep, down_came])[1]()))
        qkv_total = exchange_rows(add(own_part, came_one, came_far))
    returned = lax.all_to_all(
        begin_grad.reshape(devices, tokens + SPARE, width), both, 0, 0, tiled=True
    )
    inverse = (
        jnp.zeros((total_seqs,), jnp.int32)
        .at[deal_order]
        .set(jnp.arange(total_seqs, dtype=jnp.int32))
    )
    states_grad = returned[inverse][:, :tokens]
    gain_grads = jnp.sum(returned[:, tokens:].astype(F32), axis=0).reshape(2, devices, per)
    gain_grads = lax.dynamic_index_in_dim(gain_grads, own, 1, keepdims=False)
    return (
        output,
        states_grad,
        qkv_total.reshape(w_qkv.shape),
        up_total[:, :PAIR].T,
        up_total[:, PAIR:],
        down_total.T,
        gain_grads[0],
        gain_grads[1],
    )


def solution(mesh):
    in_specs = (
        P(None, "dp", "tensor"),
        P(),
        P(),
        P(),
        P("dp", None, "tensor"),
        P("tensor", "dp"),
        P("dp", "tensor"),
        P("tensor", "dp"),
        P(("dp", "tensor")),
        P(("dp", "tensor")),
        P(("dp", "tensor"), None, None),
    )
    out_specs = (
        P(("dp", "tensor"), None, None),
        P(None, "dp", "tensor"),
        P("dp", None, "tensor"),
        P("tensor", "dp"),
        P("dp", "tensor"),
        P("tensor", "dp"),
        P(("dp", "tensor")),
        P(("dp", "tensor")),
    )
    return jax.shard_map(
        on_device, mesh=mesh, in_specs=in_specs, out_specs=out_specs, check_vma=False
    )
```

```python
import functools
import math

import jax
import jax.numpy as jnp
from jax import lax
from jax.experimental import pallas as pl
from jax.experimental.pallas import tpu as pltpu
from jax.sharding import PartitionSpec as P

HEAD_DIM = 64
PAIR = 2 * HEAD_DIM
ROWS = 512
KEYS = 256
BACK_KEYS = 512
SPARE = 8
SCORE_SCALE = 1.0 / math.sqrt(HEAD_DIM)
LOG2E = math.log2(math.e)
F32 = jnp.float32
BF16 = jnp.bfloat16
NN = (((1,), (0,)), ((), ()))
NT = (((1,), (1,)), ((), ()))
MIB = 1024 * 1024


def mul(lhs, rhs, dims=NN):
    return lax.dot_general(lhs, rhs, dims, preferred_element_type=F32)


def join_tokens(ref):
    blocks, parts, tall, width = ref.shape
    tokens = tall - SPARE
    return jnp.concatenate(
        [ref[:, part, 0:tokens].reshape(blocks * tokens, width) for part in range(parts)], axis=-1
    ).astype(F32)


def place_rows(groups, place_ref, first, source, targets):
    if groups is None:
        for target, columns, own in targets:
            target[:, columns] = source[:, own]
        return
    rows = source.shape[0] // groups
    for group in range(groups):
        spot = pl.ds(pl.multiple_of(place_ref[first + group] * rows, rows), rows)
        for target, columns, own in targets:
            target[spot, columns] = source[group * rows : (group + 1) * rows, own]


def norm_parts(values):
    center = values - jnp.mean(values, axis=-1, keepdims=True)
    spread = jnp.mean(center * center, axis=-1, keepdims=True)
    inverse = lax.rsqrt(spread + 1e-05)
    return center * inverse, inverse


def norm_back(grad, gain, unit, inverse):
    scaled = grad * gain
    mean_scaled = jnp.mean(scaled, axis=-1, keepdims=True)
    mean_along = jnp.mean(scaled * unit, axis=-1, keepdims=True)
    return inverse * (scaled - mean_scaled - unit * mean_along)


def in_hbm(value):
    return pltpu.with_memory_space_constraint(value, pltpu.HBM)


def cost(microseconds):
    return pl.CostEstimate(
        flops=int(microseconds * 1.15e9), bytes_accessed=1 << 20, transcendentals=0
    )


def params(mebibytes):
    return pltpu.CompilerParams(vmem_limit_bytes=mebibytes * MIB)


def project_kernel(groups, limit_ref, place_ref, x_ref, clock_ref, gain_ref, *refs):
    w_refs, (mixed_ref, n_turn_ref, wide) = refs[:-3], refs[-3:]
    step = pl.program_id(0)

    @pl.when(step == 0)
    def _():
        for part, w_ref in enumerate(w_refs):
            width = w_ref.shape[1]
            columns = slice(part * width, (part + 1) * width)
            place_rows(groups, place_ref, 0, w_ref, [(wide, columns, slice(0, width))])

    @pl.when(step * ROWS < limit_ref[0])
    def _():
        begin = join_tokens(x_ref) + clock_ref[...]
        unit, _ = norm_parts(begin)
        normed = (unit * gain_ref[...]).astype(BF16)
        n_turn_ref[...] = normed.T
        mixed_ref[...] = mul(normed, wide[...]).astype(BF16)

    @pl.when(step * ROWS >= limit_ref[0])
    def _():
        n_turn_ref[...] = jnp.zeros_like(n_turn_ref)
        mixed_ref[...] = jnp.zeros_like(mixed_ref)


def project(limit, place, groups, x_blocks, clock, gain, w_parts):
    senders, feature_parts, tall, width = x_blocks.shape
    tokens = tall - SPARE
    length = senders * tokens
    features = feature_parts * width
    parts, columns = len(w_parts), w_parts[0].shape[1]
    take = ROWS // tokens
    return pl.pallas_call(
        functools.partial(project_kernel, groups),
        grid_spec=pltpu.PrefetchScalarGridSpec(
            num_scalar_prefetch=2,
            grid=(length // ROWS,),
            in_specs=[
                pl.BlockSpec((take, feature_parts, tall, width), lambda i, *s: (i, 0, 0, 0)),
                pl.BlockSpec((1, features), lambda i, *s: (0, 0)),
                pl.BlockSpec((1, features), lambda i, *s: (0, 0)),
            ]
            + [pl.BlockSpec((features, columns), lambda i, *s: (0, 0))] * parts,
            out_specs=[
                pl.BlockSpec((ROWS, parts * columns), lambda i, *s: (i, 0)),
                pl.BlockSpec((features, ROWS), lambda i, *s: (0, i)),
                pl.BlockSpec((features, parts * columns), lambda i, *s: (0, 0)),
            ],
        ),
        out_shape=[
            jax.ShapeDtypeStruct((length, parts * columns), BF16),
            pltpu.HBM((features, length), BF16),
            pltpu.HBM((features, parts * columns), BF16),
        ],
        compiler_params=params(20),
        cost_estimate=cost(5),
        name="project",
    )(limit, place, x_blocks, clock, gain, *w_parts)


def head_lanes(shape, head):
    lane = lax.broadcasted_iota(jnp.int32, shape, 1)
    return (lane >= head * HEAD_DIM) & (lane < (head + 1) * HEAD_DIM)


def spare_lane(shape, head):
    lane = lax.broadcasted_iota(jnp.int32, shape, 1)
    return lane == (1 - head) * HEAD_DIM


def masked_keys(keys, head, limit):
    row = lax.broadcasted_iota(jnp.int32, keys.shape, 0)
    spare = jnp.where(
        spare_lane(keys.shape, head) & (row >= limit), jnp.asarray(-1e30, F32), jnp.asarray(0.0, F32)
    )
    return jnp.where(head_lanes(keys.shape, head), keys.astype(F32), spare).astype(BF16)


def own_lanes(values, head):
    return jnp.where(head_lanes(values.shape, head), values.astype(F32), 0.0).astype(BF16)


def masked_queries(queries, head):
    spare = jnp.where(spare_lane(queries.shape, head), jnp.asarray(1.0, F32), jnp.asarray(0.0, F32))
    return jnp.where(head_lanes(queries.shape, head), queries.astype(F32), spare).astype(BF16)


def attend_kernel(limit_ref, q_ref, k_ref, v_ref, ctx_ref, turn_ref, lse_ref, keys_s, q_s, vt_s, sc_s):
    length = q_ref.shape[0]
    vt_s[...] = v_ref[...].astype(F32).T.astype(BF16)
    for head in range(2):
        keys_s[head] = masked_keys(k_ref[...], head, limit_ref[0])
        q_s[head] = masked_queries(q_ref[...], head)
    factor = SCORE_SCALE * LOG2E
    spans = [slice(at, at + KEYS) for at in range(0, length, KEYS)]
    outs = []
    for head in range(2):
        feats = slice(head * HEAD_DIM, (head + 1) * HEAD_DIM)
        peak = None
        for span in spans:
            scores = mul(keys_s[head, span], q_s[head], NT)
            sc_s[head, span] = scores
            high = jnp.max(scores, axis=0, keepdims=True)
            peak = high if peak is None else jnp.maximum(peak, high)
        peak = peak * factor
        total = jnp.zeros_like(peak)
        gathered = jnp.zeros((HEAD_DIM, length), F32)
        for span in spans:
            expo = jnp.exp2(sc_s[head, span] * factor - peak)
            total += jnp.sum(expo, axis=0, keepdims=True)
            gathered += mul(vt_s[feats, span], expo.astype(BF16))
        outs.append(gathered / total)
        lse_ref[0, head : head + 1, :] = peak + jnp.log2(total)
    both = jnp.concatenate(outs, axis=0)
    turn_ref[...] = both.astype(BF16)
    ctx_ref[...] = both.T.astype(BF16)


def attend(limit, mixed, pairs):
    length = mixed.shape[0]
    column = lambda c: pl.BlockSpec((length, PAIR), lambda i, s: (0, i * 3 + c))
    return pl.pallas_call(
        attend_kernel,
        grid_spec=pltpu.PrefetchScalarGridSpec(
            num_scalar_prefetch=1,
            grid=(pairs,),
            in_specs=[column(0), column(1), column(2)],
            out_specs=[
                pl.BlockSpec((length, PAIR), lambda i, s: (0, i)),
                pl.BlockSpec((PAIR, length), lambda i, s: (i, 0)),
                pl.BlockSpec((1, 2, length), lambda i, s: (i, 0, 0)),
            ],
            scratch_shapes=[
                pltpu.VMEM((2, length, PAIR), BF16),
                pltpu.VMEM((2, length, PAIR), BF16),
                pltpu.VMEM((PAIR, length), BF16),
                pltpu.VMEM((2, length, length), F32),
            ],
        ),
        out_shape=[
            pltpu.HBM((length, pairs * PAIR), BF16),
            pltpu.HBM((pairs * PAIR, length), BF16),
            jax.ShapeDtypeStruct((pairs, 2, length), F32),
        ],
        compiler_params=params(28),
        cost_estimate=cost(15),
        name="attend",
    )(limit, mixed, mixed, mixed)


def gelu_both(values):
    root = math.sqrt(2.0 / math.pi)
    scaled = root * values
    inner = scaled * (1.0 + 0.044715 * (values * values))
    tanh = jnp.tanh(inner)
    half = 0.5 + 0.5 * tanh
    slope = half + (1.0 - tanh * tanh) * (1.5 * inner - scaled)
    return values * half, slope


def middle_kernel(
    groups, limit_ref, place_ref, x_ref, clock_ref, gain_ref, ctx_ref, og_ref, *refs
):
    weight_refs, refs = refs[:-17], refs[-17:]
    out_ref, cg_ref, mg_ref, gg_ref, up_send, down_send, up_keep, down_keep = refs[:8]
    wide, units, active_s, ug_s, n_turn, fg_turn, ag_turn, ctx_s, sems = refs[8:]
    step = pl.program_id(0)
    parts, _, hidden = active_s.shape
    blocks = pl.num_programs(0) - parts
    each = len(weight_refs) // parts

    def fetch(part, kind):
        target, wide_, own = (
            (wide, PAIR, slice(0, PAIR)),
            (units, 2 * hidden, slice(PAIR, PAIR + 2 * hidden)),
        )[kind]
        columns = slice(part * wide_, (part + 1) * wide_)
        copies = []
        for at, w_ref in enumerate(weight_refs[part * each : (part + 1) * each]):
            count = 1 if groups is None else groups // each
            rows = w_ref.shape[0] // count
            for group in range(count):
                index = at * count + group
                spot = pl.ds(0, rows)
                if groups is not None:
                    spot = pl.ds(pl.multiple_of(place_ref[index] * rows, rows), rows)
                copies.append(
                    pltpu.make_async_copy(
                        w_ref.at[pl.ds(group * rows, rows), own],
                        target.at[spot, columns],
                        sems.at[kind, part, index],
                    )
                )
        return copies

    @pl.when(step == 0)
    def _():
        gg_ref[...] = jnp.zeros_like(gg_ref)
        for part in range(parts):
            for copy in fetch(part, 0) + fetch(part, 1):
                copy.start()
        for part in range(parts):
            for copy in fetch(part, 0) + fetch(part, 1):
                copy.wait()

    dead = (step < blocks) & (step * ROWS >= limit_ref[0])

    @pl.when((step < blocks) & jnp.logical_not(dead))
    def _():
        spot = pl.ds(pl.multiple_of(step * ROWS, ROWS), ROWS)
        gain = gain_ref[...]
        live = step * ROWS + lax.broadcasted_iota(jnp.int32, (ROWS, 1), 0) < limit_ref[0]
        begin = join_tokens(x_ref) + clock_ref[...]
        middle = begin + mul(ctx_ref[...], wide[...], NT)
        unit, inverse = norm_parts(middle)
        normed = (unit * gain).astype(BF16)
        n_turn[:, spot] = normed.T
        res_grad = jnp.where(live, og_ref[0].astype(F32), 0.0)
        feed_grad = res_grad.astype(BF16)
        fg_turn[:, spot] = feed_grad.T
        feed = jnp.zeros_like(middle)
        two_grad = jnp.zeros_like(middle)
        for part in range(parts):
            up = slice(2 * part * hidden, (2 * part + 1) * hidden)
            down = slice((2 * part + 1) * hidden, (2 * part + 2) * hidden)
            upper = mul(normed, units[:, up])
            active, slope = gelu_both(upper)
            active = active.astype(BF16)
            active_s[part, spot] = active
            feed += mul(active, units[:, down], NT)
            upper_grad = (mul(feed_grad, units[:, down]) * slope).astype(BF16)
            ug_s[part, spot] = upper_grad
            two_grad += mul(upper_grad, units[:, up], NT)
        out_ref[0] = jnp.where(live, middle + feed, 0.0).astype(BF16)
        gg_ref[...] += jnp.sum(two_grad * unit, axis=0, keepdims=True)
        middle_grad = res_grad + norm_back(two_grad, gain, unit, inverse)
        mg_ref[...] = middle_grad
        att_grad = middle_grad.astype(BF16)
        ag_turn[:, spot] = att_grad.T
        cg_ref[...] = mul(att_grad, wide[...]).astype(BF16)
        for part in range(parts):
            ctx_s[part, spot] = ctx_ref[:, part * PAIR : (part + 1) * PAIR]

    @pl.when(dead)
    def _():
        spot = pl.ds(pl.multiple_of(step * ROWS, ROWS), ROWS)
        for ref in (out_ref, cg_ref, mg_ref):
            ref[...] = jnp.zeros_like(ref)
        for ref in (active_s, ug_s, ctx_s):
            ref[:, spot] = jnp.zeros((ref.shape[0], ROWS, ref.shape[2]), BF16)
        for ref in (n_turn, fg_turn, ag_turn):
            ref[:, spot] = jnp.zeros((ref.shape[0], ROWS), BF16)

    @pl.when(step >= blocks)
    def _():
        turn = step - blocks
        part = jnp.where(turn < 2, 3 - 2 * turn, 6 - 2 * turn)
        grads = (
            mul(ag_turn[...], ctx_s[part]).astype(BF16),
            mul(n_turn[...], ug_s[part]).astype(BF16),
            mul(fg_turn[...], active_s[part]).astype(BF16),
        )

        def into(up_ref, down_ref):
            up_ref[0, :, 0:PAIR], up_ref[0, :, PAIR:], down_ref[0] = grads

        pl.when(turn < 2)(lambda: into(up_send, down_send))
        pl.when(turn >= 2)(lambda: into(up_keep, down_keep))


def middle_block(limit, place, groups, x_blocks, clock, gain, ctx, w_parts, out_grad):
    senders, feature_parts, tall, width = x_blocks.shape
    tokens = tall - SPARE
    length = senders * tokens
    features = feature_parts * width
    parts = len(w_parts)
    weights = [in_hbm(w) for part in w_parts for w in part]
    columns = weights[0].shape[1]
    hidden = (columns - PAIR) // 2
    take = ROWS // tokens
    blocks = length // ROWS
    row = lambda i: jnp.minimum(i, blocks - 1)
    whole = lambda array: pl.BlockSpec(
        array.shape, lambda i, *s: (0,) * array.ndim, pipeline_mode=pl.Buffered(1)
    )
    rows = lambda n: pl.BlockSpec((ROWS, n), lambda i, *s: (row(i), 0))
    one = pl.BlockSpec((1, ROWS, features), lambda i, *s: (0, row(i), 0))
    grads = lambda first, n: pl.BlockSpec(
        (1, features, n), lambda i, *s: (jnp.clip(i - blocks - first, 0, 1), 0, 0)
    )
    up_shape = pltpu.HBM((2, features, PAIR + hidden), BF16)
    down_shape = pltpu.HBM((2, features, hidden), BF16)
    return pl.pallas_call(
        functools.partial(middle_kernel, groups),
        grid_spec=pltpu.PrefetchScalarGridSpec(
            num_scalar_prefetch=2,
            grid=(blocks + parts,),
            in_specs=[
                pl.BlockSpec(
                    (take, feature_parts, tall, width), lambda i, *s: (row(i), 0, 0, 0)
                ),
                whole(clock),
                whole(gain),
                rows(features),
                one,
            ]
            + [pl.BlockSpec(memory_space=pltpu.HBM)] * len(weights),
            out_specs=[
                one, rows(features), rows(features),
                pl.BlockSpec((1, features), lambda i, *s: (0, 0)),
                grads(0, PAIR + hidden), grads(0, hidden), grads(2, PAIR + hidden), grads(2, hidden),
            ],
            scratch_shapes=[
                pltpu.VMEM((features, parts * PAIR), BF16),
                pltpu.VMEM((features, parts * 2 * hidden), BF16),
                pltpu.VMEM((parts, length, hidden), BF16),
                pltpu.VMEM((parts, length, hidden), BF16),
                pltpu.VMEM((features, length), BF16),
                pltpu.VMEM((features, length), BF16),
                pltpu.VMEM((features, length), BF16),
                pltpu.VMEM((parts, length, PAIR), BF16),
                pltpu.SemaphoreType.DMA((2, parts, groups or 1)),
            ],
        ),
        out_shape=[
            jax.ShapeDtypeStruct((1, length, features), BF16),
            pltpu.HBM((length, features), BF16),
            pltpu.HBM((length, features), F32),
            jax.ShapeDtypeStruct((1, features), F32),
            up_shape, down_shape, up_shape, down_shape,
        ],
        compiler_params=params(48),
        cost_estimate=cost(25),
        name="middle",
    )(limit, place, x_blocks, clock, gain, in_hbm(ctx), in_hbm(out_grad), *weights)


def attend_back_kernel(
    limit_ref, q_ref, k_ref, v_ref, turn_ref, lse_ref, cg_ref, n_turn_ref,
    dm_ref, first_ref, second_ref, keys_s, q_s, qz_s, do_s, kt_s, delta_s,
):
    limit = limit_ref[0]
    length = q_ref.shape[0]
    kt_s[...] = k_ref[...].astype(F32).T.astype(BF16)
    along = cg_ref[...].astype(F32).T * turn_ref[...].astype(F32)
    for head in range(2):
        feats = slice(head * HEAD_DIM, (head + 1) * HEAD_DIM)
        delta_s[head : head + 1, :] = jnp.sum(along[feats, :], axis=0, keepdims=True)
        keys_s[head] = masked_keys(k_ref[...], head, limit)
        q_s[head] = masked_queries(q_ref[...], head)
        qz_s[head] = own_lanes(q_ref[...], head)
        do_s[head] = own_lanes(cg_ref[...], head)
    factor = SCORE_SCALE * LOG2E
    turned = [jnp.zeros((HEAD_DIM, length), F32)] * 2
    for at in range(0, length, BACK_KEYS):
        span = slice(at, at + BACK_KEYS)
        key_grad = jnp.zeros((BACK_KEYS, PAIR), F32)
        value_grad = jnp.zeros((BACK_KEYS, PAIR), F32)
        for head in range(2):
            feats = slice(head * HEAD_DIM, (head + 1) * HEAD_DIM)
            scores = mul(keys_s[head, span], q_s[head], NT)
            prob = jnp.exp2(scores * factor - lse_ref[0, head : head + 1, :])
            prob_grad = mul(v_ref[span, :], do_s[head], NT)
            score_grad = (prob * (prob_grad - delta_s[head : head + 1, :])).astype(BF16)
            value_grad += mul(prob.astype(BF16), do_s[head])
            key_grad += mul(score_grad, qz_s[head])
            turned[head] += mul(kt_s[feats, span], score_grad)
        dm_ref[span, PAIR : 2 * PAIR] = (key_grad * SCORE_SCALE).astype(BF16)
        dm_ref[span, 2 * PAIR : 3 * PAIR] = value_grad.astype(BF16)
    query_grad = jnp.concatenate(turned, axis=0) * SCORE_SCALE
    dm_ref[:, 0:PAIR] = query_grad.T.astype(BF16)
    grad = mul(n_turn_ref[...], dm_ref[...]).astype(BF16)

    @pl.when(pl.program_id(0) == 0)
    def _():
        first_ref[...] = grad

    @pl.when(pl.program_id(0) == 1)
    def _():
        second_ref[...] = grad


def attend_back(limit, mixed, ctx_turn, lse, context_grad, n_turn, first):
    length = mixed.shape[0]
    features = n_turn.shape[0]
    pair = lambda i: first - i
    column = lambda c: pl.BlockSpec((length, PAIR), lambda i, s: (0, pair(i) * 3 + c))
    return pl.pallas_call(
        attend_back_kernel,
        grid_spec=pltpu.PrefetchScalarGridSpec(
            num_scalar_prefetch=1,
            grid=(2,),
            in_specs=[
                column(0), column(1), column(2),
                pl.BlockSpec((PAIR, length), lambda i, s: (pair(i), 0)),
                pl.BlockSpec((1, 2, length), lambda i, s: (pair(i), 0, 0)),
                pl.BlockSpec((length, PAIR), lambda i, s: (0, pair(i))),
                pl.BlockSpec((features, length), lambda i, s: (0, 0)),
            ],
            out_specs=[
                pl.BlockSpec((length, 3 * PAIR), lambda i, s: (0, i)),
                pl.BlockSpec((features, 3 * PAIR), lambda i, s: (0, 0)),
                pl.BlockSpec((features, 3 * PAIR), lambda i, s: (0, 0)),
            ],
            scratch_shapes=[
                pltpu.VMEM((2, length, PAIR), BF16),
                pltpu.VMEM((2, length, PAIR), BF16),
                pltpu.VMEM((2, length, PAIR), BF16),
                pltpu.VMEM((2, length, PAIR), BF16),
                pltpu.VMEM((PAIR, length), BF16),
                pltpu.VMEM((8, length), F32),
            ],
        ),
        out_shape=[
            jax.ShapeDtypeStruct((length, 2 * 3 * PAIR), BF16),
            jax.ShapeDtypeStruct((features, 3 * PAIR), BF16),
            jax.ShapeDtypeStruct((features, 3 * PAIR), BF16),
        ],
        compiler_params=params(28),
        cost_estimate=cost(16),
        name="attend_back",
    )(limit, mixed, mixed, mixed, ctx_turn, lse, context_grad, n_turn)


def begin_kernel(
    limit_ref, x_ref, clock_ref, gain_ref, gg_two_ref, mg_ref, w_ref, high_ref, low_ref, bg_ref, gg_s
):
    step = pl.program_id(0)
    _, parts, tall, width = bg_ref.shape
    tokens = tall - SPARE
    blocks = ROWS // tokens
    spot = pl.ds(step * blocks, blocks)

    @pl.when(step == 0)
    def _():
        gg_s[...] = jnp.zeros_like(gg_s)

    @pl.when(step * ROWS < limit_ref[0])
    def _():
        begin = join_tokens(x_ref) + clock_ref[...]
        unit, inverse = norm_parts(begin)
        one_grad = jnp.zeros_like(begin)
        for part, (d_ref, at) in enumerate(((low_ref, 1), (low_ref, 0), (high_ref, 1), (high_ref, 0))):
            columns = slice(part * 3 * PAIR, (part + 1) * 3 * PAIR)
            own = slice(at * 3 * PAIR, (at + 1) * 3 * PAIR)
            one_grad += mul(d_ref[:, own], w_ref[:, columns], NT)
        gg_s[...] += jnp.sum(one_grad * unit, axis=0, keepdims=True)
        total = (mg_ref[...] + norm_back(one_grad, gain_ref[...], unit, inverse)).astype(BF16)
        for part in range(parts):
            piece = total[:, part * width : (part + 1) * width]
            bg_ref[spot, part, 0:tokens] = piece.reshape(blocks, tokens, width)

    @pl.when(step * ROWS >= limit_ref[0])
    def _():
        bg_ref[spot] = jnp.zeros((blocks,) + bg_ref.shape[1:], BF16)

    @pl.when(step == pl.num_programs(0) - 1)
    def _():
        rows = []
        for ref in (gg_s, gg_two_ref):
            for part in range(parts):
                rows.append(ref[:, part * width : (part + 1) * width])
        bg_ref[:, :, tokens:tall] = jnp.broadcast_to(
            jnp.concatenate(rows, axis=0).astype(BF16), bg_ref.shape[:2] + (SPARE, width)
        )


def begin_block(limit, x_blocks, clock, gain, two_grad, w_wide, middle_grad, high, low):
    senders, feature_parts, tall, width = x_blocks.shape
    tokens = tall - SPARE
    length = senders * tokens
    features = feature_parts * width
    take = ROWS // tokens
    whole = lambda array: pl.BlockSpec(array.shape, lambda i, s: (0,) * array.ndim)
    rows = lambda n: pl.BlockSpec((ROWS, n), lambda i, s: (i, 0))
    return pl.pallas_call(
        begin_kernel,
        grid_spec=pltpu.PrefetchScalarGridSpec(
            num_scalar_prefetch=1,
            grid=(length // ROWS,),
            in_specs=[
                pl.BlockSpec((take, feature_parts, tall, width), lambda i, s: (i, 0, 0, 0)),
                whole(clock), whole(gain), whole(two_grad), rows(features), whole(w_wide),
            ]
            + [rows(6 * PAIR)] * 2,
            out_specs=whole(x_blocks),
            scratch_shapes=[pltpu.VMEM((1, features), F32)],
        ),
        out_shape=jax.ShapeDtypeStruct(x_blocks.shape, BF16),
        compiler_params=params(20),
        cost_estimate=cost(7),
        name="begin_back",
    )(limit, x_blocks, clock, gain, two_grad, middle_grad, w_wide, high, low)


DIRECT = 8


def clock_rows(step_ids, features):
    half_width = features // 2
    ladder = jnp.arange(half_width, dtype=F32) / half_width
    rate_rows = jnp.exp(-math.log(10000.0) * ladder)
    angles = step_ids.astype(F32)[:, None] * rate_rows[None, :]
    return jnp.concatenate([jnp.sin(angles), jnp.cos(angles)], axis=-1)


def swap(value, apart):
    count = lax.axis_size("tensor")
    return lax.ppermute(value, "tensor", [(i, i ^ apart) for i in range(count)])


def along_dp(value, move):
    count = lax.axis_size("dp")
    return lax.ppermute(value, "dp", [(i, move(i)) for i in range(count)])


def across(value):
    return ahead(value, 0, 1)


def ahead(value, step, flip=0):
    count = lax.axis_size("dp") // 2
    return along_dp(value, lambda i: (i // 2 + step) % count * 2 + (i + flip) % 2)


def places():
    count = lax.axis_size("dp") // 2
    own = lax.axis_index("dp")
    coarse = (own // 2 - jnp.arange(count, dtype=jnp.int32)) % count
    return jnp.concatenate([coarse * 2 + own % 2, coarse * 2 + 1 - own % 2])


def collect_coarse(shard):
    count = lax.axis_size("dp") // 2
    return [shard] + [ahead(shard, step) for step in range(1, count)]


def collect_rows(shard):
    count = lax.axis_size("dp")
    rows = lax.all_to_all(
        jnp.broadcast_to(shard[None], (count,) + shard.shape), "dp", 0, 0, tiled=True
    )
    return rows.reshape(count * shard.shape[0], shard.shape[1])


def collect_columns(rows):
    far = swap(rows, 2)
    return rows, swap(rows, 1), far, swap(far, 1)


def add(*values):
    return add_wide(*values).astype(BF16)


def fold_pair(values):
    own = lax.axis_index("dp") % 2
    pick = lambda value, which: lax.dynamic_index_in_dim(value, which, value.ndim - 3, keepdims=False)
    sent = add(*[pick(value, 1 - own) for value in values])
    return sent, lambda: [pick(value, own) for value in values] + [across(sent)]


def fold_far(values):
    sent = add(*[value[0] for value in values])
    return sent, lambda: [value[1] for value in values] + [swap(sent, 2)]


def fold_coarse(values):
    count = lax.axis_size("dp") // 2
    own = lax.axis_index("dp") // 2
    pick = lambda value, which: lax.dynamic_index_in_dim(value, which % count, 0, keepdims=False)
    value = add(*values)
    came = [ahead(pick(value, own + step), step) for step in range(1, count)]
    return value, [pick(value, own)] + came


def add_wide(*values):
    total = values[0].astype(F32)
    for value in values[1:]:
        total += value.astype(F32)
    return total


def grouped(value):
    count = lax.axis_size("dp")
    two, rows, columns = value.shape
    return value.reshape(two, count // 2, 2, rows // count, columns)


def exchange_rows(value):
    count = lax.axis_size("dp")
    groups = value.reshape(count, value.shape[0] // count, value.shape[1])
    return jnp.sum(lax.all_to_all(groups, "dp", 0, 0, tiled=True).astype(F32), axis=0)


def three_terms(values):
    terms = []
    for _ in range(3):
        term = lax.reduce_precision(values, 8, 7)
        terms.append(term.astype(BF16))
        values = values - term
    return terms


def together(*values):
    return lax.optimization_barrier(values)


def after(value, *others):
    return lax.optimization_barrier((value,) + others)[0]


def on_device(
    states, timesteps, lengths, deal_order, w_qkv, w_out, w_up, w_down, gain_attn, gain_ffn, out_grad
):
    both = ("dp", "tensor")
    dp_count = lax.axis_size("dp")
    tensor_count = lax.axis_size("tensor")
    devices = dp_count * tensor_count
    total_seqs, tokens, width = states.shape
    assert tensor_count == 4 and total_seqs == devices
    features = width * tensor_count
    own = lax.axis_index("dp") * tensor_count + lax.axis_index("tensor")
    own_id = lax.dynamic_slice_in_dim(deal_order, own, 1)
    limit = lengths[own_id]
    clock = clock_rows(timesteps[own_id], features)
    per = gain_attn.shape[0]
    rows = w_qkv.shape[0]
    hidden = w_up.shape[1]

    rest = jnp.concatenate([w_out.T, w_up, w_down.T], axis=1)
    qkv = w_qkv.reshape(rows, -1)
    direct = dp_count <= DIRECT
    if direct:
        place, groups = places(), dp_count
        wide = qkv.shape[1]
        pieces = collect_coarse(jnp.concatenate([qkv, across(qkv)], axis=1))
        qkv_rows = jnp.concatenate(
            [piece[:, :wide] for piece in pieces] + [piece[:, wide:] for piece in pieces], axis=0
        )
        mine = jnp.concatenate(collect_coarse(rest), axis=0)
        far_rows, other, far_mine = together(
            swap(qkv_rows, 2), in_hbm(across(mine)), in_hbm(swap(mine, 2))
        )
        qkv_parts = (qkv_rows, swap(qkv_rows, 1), far_rows, swap(far_rows, 1))
    else:
        place, groups = jnp.zeros((1,), jnp.int32), None
        qkv_parts = collect_columns(collect_rows(qkv))
        rest_parts = [(part,) for part in collect_columns(collect_rows(rest))]

    spare = jnp.stack(three_terms(gain_attn) + three_terms(gain_ffn)).reshape(1, 6 * per)
    spare = jnp.pad(spare, ((0, SPARE - 1), (0, width - 6 * per)))
    arranged = jnp.concatenate(
        [states[deal_order], jnp.broadcast_to(spare[None], (devices, SPARE, width))], axis=1
    )
    x_blocks = lax.all_to_all(arranged, both, 0, 0, tiled=True)
    gains = jnp.sum(x_blocks[:, tokens, : 6 * per].reshape(devices, 2, 3, per).astype(F32), axis=2)
    gain_one = gains[:, 0].reshape(1, features)
    gain_two = gains[:, 1].reshape(1, features)
    x_blocks = x_blocks.reshape(dp_count, tensor_count, tokens + SPARE, width)

    mixed, n_one_turn, qkv_wide = project(
        limit, place, groups, x_blocks, clock, gain_one, qkv_parts
    )
    if direct:
        near_mine, near_other = in_hbm(swap(mine, 1)), in_hbm(swap(other, 1))
        last_mine, far_other = in_hbm(swap(far_mine, 1)), in_hbm(swap(other, 2))
    ctx, ctx_turn, lse = attend(limit, mixed, tensor_count)
    if direct:
        ctx, near_mine, near_other, last_mine, far_other = together(
            ctx, near_mine, near_other, last_mine, far_other
        )
        last_other = swap(far_other, 1)
        rest_parts = (
            (mine, other), (near_mine, near_other), (far_mine, far_other), (last_mine, last_other)
        )
    output, context_grad, middle_grad, two_grad, up_send, down_send, up_keep, down_keep = middle_block(
        limit, place, groups, x_blocks, clock, gain_two, ctx, rest_parts, out_grad
    )
    up_came, down_came = swap(up_send, 1), swap(down_send, 1)

    back = functools.partial(attend_back, limit, mixed, ctx_turn, lse)
    if direct:
        down_sent, down_rest = fold_far([grouped(value) for value in (down_keep, down_came)])
        up_sent, up_rest = fold_pair([grouped(value) for value in (up_keep, up_came)])
        context_grad = after(context_grad, down_sent, up_sent)
    high, three, two = back(in_hbm(context_grad), n_one_turn, 3)
    if direct:
        *down_rest, down_came = down_rest()
        *up_rest, up_came = up_rest()
        high, three, two, down_came, up_came = together(high, three, two, down_came, up_came)
        down_value, down_pieces = fold_coarse([*down_rest, down_came])
        up_sent, up_rest = fold_far([add(*up_rest, up_came)])
        context_grad = after(context_grad, down_value, up_sent)
    far = add(two, swap(three, 1))
    came_far = swap(far, 2)
    low, one, own_part = back(after(context_grad, high, far), n_one_turn, 1)
    if direct:
        *up_rest, up_came = up_rest()
        low, one, own_part, up_came, came_far, *down_pieces = together(
            low, one, own_part, up_came, came_far, *down_pieces
        )
        up_value, up_pieces = fold_coarse([*up_rest, up_came])
        down_sent, down_rest = fold_pair([add_wide(*down_pieces)[..., None, :, :, :]])
        middle_grad = after(middle_grad, up_value, down_sent)
    came_one = swap(one, 1)
    begin_grad = begin_block(
        limit, x_blocks, clock, gain_one, two_grad, qkv_wide, middle_grad, high, low
    )
    if direct:
        begin_grad, came_one, up_pieces[2] = together(begin_grad, came_one, up_pieces[2])
        near = [grouped(value[None])[0] for value in (own_part, came_one, came_far)]
        qkv_value, qkv_pieces = fold_coarse(fold_pair(near)[1]())
        down_total = add_wide(*down_rest())[0]
        pieces = together(*up_pieces, *qkv_pieces)
        up_total = add_wide(*pieces[: len(up_pieces)])
        qkv_total = add_wide(*pieces[len(up_pieces) :])
    else:
        up_total = exchange_rows(add(*fold_far([up_keep, up_came])[1]()))
        down_total = exchange_rows(add(*fold_far([down_keep, down_came])[1]()))
        qkv_total = exchange_rows(add(own_part, came_one, came_far))
    returned = lax.all_to_all(
        begin_grad.reshape(devices, tokens + SPARE, width), both, 0, 0, tiled=True
    )
    inverse = (
        jnp.zeros((total_seqs,), jnp.int32)
        .at[deal_order]
        .set(jnp.arange(total_seqs, dtype=jnp.int32))
    )
    states_grad = returned[inverse][:, :tokens]
    gain_grads = jnp.sum(returned[:, tokens:].astype(F32), axis=0).reshape(2, devices, per)
    gain_grads = lax.dynamic_index_in_dim(gain_grads, own, 1, keepdims=False)
    return (
        output,
        states_grad,
        qkv_total.reshape(w_qkv.shape),
        up_total[:, :PAIR].T,
        up_total[:, PAIR:],
        down_total.T,
        gain_grads[0],
        gain_grads[1],
    )


def solution(mesh):
    in_specs = (
        P(None, "dp", "tensor"),
        P(),
        P(),
        P(),
        P("dp", None, "tensor"),
        P("tensor", "dp"),
        P("dp", "tensor"),
        P("tensor", "dp"),
        P(("dp", "tensor")),
        P(("dp", "tensor")),
        P(("dp", "tensor"), None, None),
    )
    out_specs = (
        P(("dp", "tensor"), None, None),
        P(None, "dp", "tensor"),
        P("dp", None, "tensor"),
        P("tensor", "dp"),
        P("dp", "tensor"),
        P("tensor", "dp"),
        P(("dp", "tensor")),
        P(("dp", "tensor")),
    )
    return jax.shard_map(
        on_device, mesh=mesh, in_specs=in_specs, out_specs=out_specs, check_vma=False
    )
```

```python
import functools
import math

import jax
import jax.numpy as jnp
from jax import lax
from jax.experimental import pallas as pl
from jax.experimental.pallas import tpu as pltpu
from jax.sharding import PartitionSpec as P

HEAD_DIM = 64
PAIR = 2 * HEAD_DIM
ROWS = 512
KEYS = 256
BACK_KEYS = 512
SPARE = 8
SCORE_SCALE = 1.0 / math.sqrt(HEAD_DIM)
LOG2E = math.log2(math.e)
F32 = jnp.float32
BF16 = jnp.bfloat16
NN = (((1,), (0,)), ((), ()))
NT = (((1,), (1,)), ((), ()))
MIB = 1024 * 1024


def mul(lhs, rhs, dims=NN):
    return lax.dot_general(lhs, rhs, dims, preferred_element_type=F32)


def join_tokens(ref):
    blocks, parts, tall, width = ref.shape
    tokens = tall - SPARE
    return jnp.concatenate(
        [ref[:, part, 0:tokens].reshape(blocks * tokens, width) for part in range(parts)], axis=-1
    ).astype(F32)


def place_rows(groups, place_ref, first, source, targets):
    if groups is None:
        for target, columns, own in targets:
            target[:, columns] = source[:, own]
        return
    rows = source.shape[0] // groups
    for group in range(groups):
        spot = pl.ds(pl.multiple_of(place_ref[first + group] * rows, rows), rows)
        for target, columns, own in targets:
            target[spot, columns] = source[group * rows : (group + 1) * rows, own]


def norm_parts(values):
    center = values - jnp.mean(values, axis=-1, keepdims=True)
    spread = jnp.mean(center * center, axis=-1, keepdims=True)
    inverse = lax.rsqrt(spread + 1e-05)
    return center * inverse, inverse


def norm_back(grad, gain, unit, inverse):
    scaled = grad * gain
    mean_scaled = jnp.mean(scaled, axis=-1, keepdims=True)
    mean_along = jnp.mean(scaled * unit, axis=-1, keepdims=True)
    return inverse * (scaled - mean_scaled - unit * mean_along)


def in_hbm(value):
    return pltpu.with_memory_space_constraint(value, pltpu.HBM)


def cost(microseconds):
    return pl.CostEstimate(
        flops=int(microseconds * 1.15e9), bytes_accessed=1 << 20, transcendentals=0
    )


def params(mebibytes):
    return pltpu.CompilerParams(vmem_limit_bytes=mebibytes * MIB)


def project_kernel(groups, limit_ref, place_ref, x_ref, clock_ref, gain_ref, *refs):
    w_refs, (mixed_ref, n_turn_ref, wide) = refs[:-3], refs[-3:]
    step = pl.program_id(0)

    @pl.when(step == 0)
    def _():
        for part, w_ref in enumerate(w_refs):
            width = w_ref.shape[1]
            columns = slice(part * width, (part + 1) * width)
            place_rows(groups, place_ref, 0, w_ref, [(wide, columns, slice(0, width))])

    @pl.when(step * ROWS < limit_ref[0])
    def _():
        begin = join_tokens(x_ref) + clock_ref[...]
        unit, _ = norm_parts(begin)
        normed = (unit * gain_ref[...]).astype(BF16)
        n_turn_ref[...] = normed.T
        mixed_ref[...] = mul(normed, wide[...]).astype(BF16)

    @pl.when(step * ROWS >= limit_ref[0])
    def _():
        n_turn_ref[...] = jnp.zeros_like(n_turn_ref)
        mixed_ref[...] = jnp.zeros_like(mixed_ref)


def project(limit, place, groups, x_blocks, clock, gain, w_parts):
    senders, feature_parts, tall, width = x_blocks.shape
    tokens = tall - SPARE
    length = senders * tokens
    features = feature_parts * width
    parts, columns = len(w_parts), w_parts[0].shape[1]
    take = ROWS // tokens
    return pl.pallas_call(
        functools.partial(project_kernel, groups),
        grid_spec=pltpu.PrefetchScalarGridSpec(
            num_scalar_prefetch=2,
            grid=(length // ROWS,),
            in_specs=[
                pl.BlockSpec((take, feature_parts, tall, width), lambda i, *s: (i, 0, 0, 0)),
                pl.BlockSpec((1, features), lambda i, *s: (0, 0)),
                pl.BlockSpec((1, features), lambda i, *s: (0, 0)),
            ]
            + [pl.BlockSpec((features, columns), lambda i, *s: (0, 0))] * parts,
            out_specs=[
                pl.BlockSpec((ROWS, parts * columns), lambda i, *s: (i, 0)),
                pl.BlockSpec((features, ROWS), lambda i, *s: (0, i)),
                pl.BlockSpec((features, parts * columns), lambda i, *s: (0, 0)),
            ],
        ),
        out_shape=[
            jax.ShapeDtypeStruct((length, parts * columns), BF16),
            pltpu.HBM((features, length), BF16),
            pltpu.HBM((features, parts * columns), BF16),
        ],
        compiler_params=params(20),
        cost_estimate=cost(5),
        name="project",
    )(limit, place, x_blocks, clock, gain, *w_parts)


def head_lanes(shape, head):
    lane = lax.broadcasted_iota(jnp.int32, shape, 1)
    return (lane >= head * HEAD_DIM) & (lane < (head + 1) * HEAD_DIM)


def spare_lane(shape, head):
    lane = lax.broadcasted_iota(jnp.int32, shape, 1)
    return lane == (1 - head) * HEAD_DIM


def masked_keys(keys, head, limit):
    row = lax.broadcasted_iota(jnp.int32, keys.shape, 0)
    spare = jnp.where(
        spare_lane(keys.shape, head) & (row >= limit), jnp.asarray(-1e30, F32), jnp.asarray(0.0, F32)
    )
    return jnp.where(head_lanes(keys.shape, head), keys.astype(F32), spare).astype(BF16)


def own_lanes(values, head):
    return jnp.where(head_lanes(values.shape, head), values.astype(F32), 0.0).astype(BF16)


def masked_queries(queries, head):
    spare = jnp.where(spare_lane(queries.shape, head), jnp.asarray(1.0, F32), jnp.asarray(0.0, F32))
    return jnp.where(head_lanes(queries.shape, head), queries.astype(F32), spare).astype(BF16)


def attend_kernel(limit_ref, q_ref, k_ref, v_ref, ctx_ref, turn_ref, lse_ref, keys_s, q_s, vt_s, sc_s):
    length = q_ref.shape[0]
    vt_s[...] = v_ref[...].astype(F32).T.astype(BF16)
    for head in range(2):
        keys_s[head] = masked_keys(k_ref[...], head, limit_ref[0])
        q_s[head] = masked_queries(q_ref[...], head)
    factor = SCORE_SCALE * LOG2E
    spans = [slice(at, at + KEYS) for at in range(0, length, KEYS)]
    outs = []
    for head in range(2):
        feats = slice(head * HEAD_DIM, (head + 1) * HEAD_DIM)
        peak = None
        for span in spans:
            scores = mul(keys_s[head, span], q_s[head], NT)
            sc_s[head, span] = scores
            high = jnp.max(scores, axis=0, keepdims=True)
            peak = high if peak is None else jnp.maximum(peak, high)
        peak = peak * factor
        total = jnp.zeros_like(peak)
        gathered = jnp.zeros((HEAD_DIM, length), F32)
        for span in spans:
            expo = jnp.exp2(sc_s[head, span] * factor - peak)
            total += jnp.sum(expo, axis=0, keepdims=True)
            gathered += mul(vt_s[feats, span], expo.astype(BF16))
        outs.append(gathered / total)
        lse_ref[0, head : head + 1, :] = peak + jnp.log2(total)
    both = jnp.concatenate(outs, axis=0)
    turn_ref[...] = both.astype(BF16)
    ctx_ref[...] = both.T.astype(BF16)


def attend(limit, mixed, pairs):
    length = mixed.shape[0]
    column = lambda c: pl.BlockSpec((length, PAIR), lambda i, s: (0, i * 3 + c))
    return pl.pallas_call(
        attend_kernel,
        grid_spec=pltpu.PrefetchScalarGridSpec(
            num_scalar_prefetch=1,
            grid=(pairs,),
            in_specs=[column(0), column(1), column(2)],
            out_specs=[
                pl.BlockSpec((length, PAIR), lambda i, s: (0, i)),
                pl.BlockSpec((PAIR, length), lambda i, s: (i, 0)),
                pl.BlockSpec((1, 2, length), lambda i, s: (i, 0, 0)),
            ],
            scratch_shapes=[
                pltpu.VMEM((2, length, PAIR), BF16),
                pltpu.VMEM((2, length, PAIR), BF16),
                pltpu.VMEM((PAIR, length), BF16),
                pltpu.VMEM((2, length, length), F32),
            ],
        ),
        out_shape=[
            pltpu.HBM((length, pairs * PAIR), BF16),
            pltpu.HBM((pairs * PAIR, length), BF16),
            jax.ShapeDtypeStruct((pairs, 2, length), F32),
        ],
        compiler_params=params(28),
        cost_estimate=cost(15),
        name="attend",
    )(limit, mixed, mixed, mixed)


def gelu_both(values):
    root = math.sqrt(2.0 / math.pi)
    scaled = root * values
    inner = scaled * (1.0 + 0.044715 * (values * values))
    tanh = jnp.tanh(inner)
    half = 0.5 + 0.5 * tanh
    slope = half + (1.0 - tanh * tanh) * (1.5 * inner - scaled)
    return values * half, slope


def middle_kernel(
    groups, limit_ref, place_ref, x_ref, clock_ref, gain_ref, ctx_ref, og_ref, *refs
):
    weight_refs, refs = refs[:-17], refs[-17:]
    out_ref, cg_ref, mg_ref, gg_ref, up_send, down_send, up_keep, down_keep = refs[:8]
    wide, units, active_s, ug_s, n_turn, fg_turn, ag_turn, ctx_s, sems = refs[8:]
    step = pl.program_id(0)
    parts, _, hidden = active_s.shape
    blocks = pl.num_programs(0) - parts
    each = len(weight_refs) // parts

    def fetch(part, kind):
        target, wide_, own = (
            (wide, PAIR, slice(0, PAIR)),
            (units, 2 * hidden, slice(PAIR, PAIR + 2 * hidden)),
        )[kind]
        columns = slice(part * wide_, (part + 1) * wide_)
        copies = []
        for at, w_ref in enumerate(weight_refs[part * each : (part + 1) * each]):
            count = 1 if groups is None else groups // each
            rows = w_ref.shape[0] // count
            for group in range(count):
                index = at * count + group
                spot = pl.ds(0, rows)
                if groups is not None:
                    spot = pl.ds(pl.multiple_of(place_ref[index] * rows, rows), rows)
                copies.append(
                    pltpu.make_async_copy(
                        w_ref.at[pl.ds(group * rows, rows), own],
                        target.at[spot, columns],
                        sems.at[kind, part, index],
                    )
                )
        return copies

    @pl.when(step == 0)
    def _():
        gg_ref[...] = jnp.zeros_like(gg_ref)
        for part in range(parts):
            for copy in fetch(part, 0) + fetch(part, 1):
                copy.start()
        for part in range(parts):
            for copy in fetch(part, 0) + fetch(part, 1):
                copy.wait()

    dead = (step < blocks) & (step * ROWS >= limit_ref[0])

    @pl.when((step < blocks) & jnp.logical_not(dead))
    def _():
        spot = pl.ds(pl.multiple_of(step * ROWS, ROWS), ROWS)
        gain = gain_ref[...]
        live = step * ROWS + lax.broadcasted_iota(jnp.int32, (ROWS, 1), 0) < limit_ref[0]
        begin = join_tokens(x_ref) + clock_ref[...]
        middle = begin + mul(ctx_ref[...], wide[...], NT)
        unit, inverse = norm_parts(middle)
        normed = (unit * gain).astype(BF16)
        n_turn[:, spot] = normed.T
        res_grad = jnp.where(live, og_ref[0].astype(F32), 0.0)
        feed_grad = res_grad.astype(BF16)
        fg_turn[:, spot] = feed_grad.T
        feed = jnp.zeros_like(middle)
        two_grad = jnp.zeros_like(middle)
        for part in range(parts):
            up = slice(2 * part * hidden, (2 * part + 1) * hidden)
            down = slice((2 * part + 1) * hidden, (2 * part + 2) * hidden)
            upper = mul(normed, units[:, up])
            active, slope = gelu_both(upper)
            active = active.astype(BF16)
            active_s[part, spot] = active
            feed += mul(active, units[:, down], NT)
            upper_grad = (mul(feed_grad, units[:, down]) * slope).astype(BF16)
            ug_s[part, spot] = upper_grad
            two_grad += mul(upper_grad, units[:, up], NT)
        out_ref[0] = jnp.where(live, middle + feed, 0.0).astype(BF16)
        gg_ref[...] += jnp.sum(two_grad * unit, axis=0, keepdims=True)
        middle_grad = res_grad + norm_back(two_grad, gain, unit, inverse)
        mg_ref[...] = middle_grad
        att_grad = middle_grad.astype(BF16)
        ag_turn[:, spot] = att_grad.T
        cg_ref[...] = mul(att_grad, wide[...]).astype(BF16)
        for part in range(parts):
            ctx_s[part, spot] = ctx_ref[:, part * PAIR : (part + 1) * PAIR]

    @pl.when(dead)
    def _():
        spot = pl.ds(pl.multiple_of(step * ROWS, ROWS), ROWS)
        for ref in (out_ref, cg_ref, mg_ref):
            ref[...] = jnp.zeros_like(ref)
        for ref in (active_s, ug_s, ctx_s):
            ref[:, spot] = jnp.zeros((ref.shape[0], ROWS, ref.shape[2]), BF16)
        for ref in (n_turn, fg_turn, ag_turn):
            ref[:, spot] = jnp.zeros((ref.shape[0], ROWS), BF16)

    @pl.when(step >= blocks)
    def _():
        turn = step - blocks
        part = jnp.where(turn < 2, 3 - 2 * turn, 6 - 2 * turn)
        grads = (
            mul(ag_turn[...], ctx_s[part]).astype(BF16),
            mul(n_turn[...], ug_s[part]).astype(BF16),
            mul(fg_turn[...], active_s[part]).astype(BF16),
        )

        def into(up_ref, down_ref):
            up_ref[0, :, 0:PAIR], up_ref[0, :, PAIR:], down_ref[0] = grads

        pl.when(turn < 2)(lambda: into(up_send, down_send))
        pl.when(turn >= 2)(lambda: into(up_keep, down_keep))


def middle_block(limit, place, groups, x_blocks, clock, gain, ctx, w_parts, out_grad):
    senders, feature_parts, tall, width = x_blocks.shape
    tokens = tall - SPARE
    length = senders * tokens
    features = feature_parts * width
    parts = len(w_parts)
    weights = [in_hbm(w) for part in w_parts for w in part]
    columns = weights[0].shape[1]
    hidden = (columns - PAIR) // 2
    take = ROWS // tokens
    blocks = length // ROWS
    row = lambda i: jnp.minimum(i, blocks - 1)
    whole = lambda array: pl.BlockSpec(
        array.shape, lambda i, *s: (0,) * array.ndim, pipeline_mode=pl.Buffered(1)
    )
    rows = lambda n: pl.BlockSpec((ROWS, n), lambda i, *s: (row(i), 0))
    one = pl.BlockSpec((1, ROWS, features), lambda i, *s: (0, row(i), 0))
    grads = lambda first, n: pl.BlockSpec(
        (1, features, n), lambda i, *s: (jnp.clip(i - blocks - first, 0, 1), 0, 0)
    )
    up_shape = pltpu.HBM((2, features, PAIR + hidden), BF16)
    down_shape = pltpu.HBM((2, features, hidden), BF16)
    return pl.pallas_call(
        functools.partial(middle_kernel, groups),
        grid_spec=pltpu.PrefetchScalarGridSpec(
            num_scalar_prefetch=2,
            grid=(blocks + parts,),
            in_specs=[
                pl.BlockSpec(
                    (take, feature_parts, tall, width), lambda i, *s: (row(i), 0, 0, 0)
                ),
                whole(clock),
                whole(gain),
                rows(features),
                one,
            ]
            + [pl.BlockSpec(memory_space=pltpu.HBM)] * len(weights),
            out_specs=[
                one, rows(features), rows(features),
                pl.BlockSpec((1, features), lambda i, *s: (0, 0)),
                grads(0, PAIR + hidden), grads(0, hidden), grads(2, PAIR + hidden), grads(2, hidden),
            ],
            scratch_shapes=[
                pltpu.VMEM((features, parts * PAIR), BF16),
                pltpu.VMEM((features, parts * 2 * hidden), BF16),
                pltpu.VMEM((parts, length, hidden), BF16),
                pltpu.VMEM((parts, length, hidden), BF16),
                pltpu.VMEM((features, length), BF16),
                pltpu.VMEM((features, length), BF16),
                pltpu.VMEM((features, length), BF16),
                pltpu.VMEM((parts, length, PAIR), BF16),
                pltpu.SemaphoreType.DMA((2, parts, groups or 1)),
            ],
        ),
        out_shape=[
            jax.ShapeDtypeStruct((1, length, features), BF16),
            pltpu.HBM((length, features), BF16),
            pltpu.HBM((length, features), F32),
            jax.ShapeDtypeStruct((1, features), F32),
            up_shape, down_shape, up_shape, down_shape,
        ],
        compiler_params=params(48),
        cost_estimate=cost(25),
        name="middle",
    )(limit, place, x_blocks, clock, gain, in_hbm(ctx), in_hbm(out_grad), *weights)


def attend_back_kernel(
    limit_ref, q_ref, k_ref, v_ref, turn_ref, lse_ref, cg_ref, n_turn_ref,
    dm_ref, first_ref, second_ref, keys_s, q_s, qz_s, do_s, kt_s, delta_s,
):
    limit = limit_ref[0]
    length = q_ref.shape[0]
    kt_s[...] = k_ref[...].astype(F32).T.astype(BF16)
    along = cg_ref[...].astype(F32).T * turn_ref[...].astype(F32)
    for head in range(2):
        feats = slice(head * HEAD_DIM, (head + 1) * HEAD_DIM)
        delta_s[head : head + 1, :] = jnp.sum(along[feats, :], axis=0, keepdims=True)
        keys_s[head] = masked_keys(k_ref[...], head, limit)
        q_s[head] = masked_queries(q_ref[...], head)
        qz_s[head] = own_lanes(q_ref[...], head)
        do_s[head] = own_lanes(cg_ref[...], head)
    factor = SCORE_SCALE * LOG2E
    turned = [jnp.zeros((HEAD_DIM, length), F32)] * 2
    for at in range(0, length, BACK_KEYS):
        span = slice(at, at + BACK_KEYS)
        key_grad = jnp.zeros((BACK_KEYS, PAIR), F32)
        value_grad = jnp.zeros((BACK_KEYS, PAIR), F32)
        for head in range(2):
            feats = slice(head * HEAD_DIM, (head + 1) * HEAD_DIM)
            scores = mul(keys_s[head, span], q_s[head], NT)
            prob = jnp.exp2(scores * factor - lse_ref[0, head : head + 1, :])
            prob_grad = mul(v_ref[span, :], do_s[head], NT)
            score_grad = (prob * (prob_grad - delta_s[head : head + 1, :])).astype(BF16)
            value_grad += mul(prob.astype(BF16), do_s[head])
            key_grad += mul(score_grad, qz_s[head])
            turned[head] += mul(kt_s[feats, span], score_grad)
        dm_ref[span, PAIR : 2 * PAIR] = (key_grad * SCORE_SCALE).astype(BF16)
        dm_ref[span, 2 * PAIR : 3 * PAIR] = value_grad.astype(BF16)
    query_grad = jnp.concatenate(turned, axis=0) * SCORE_SCALE
    dm_ref[:, 0:PAIR] = query_grad.T.astype(BF16)
    grad = mul(n_turn_ref[...], dm_ref[...]).astype(BF16)

    @pl.when(pl.program_id(0) == 0)
    def _():
        first_ref[...] = grad

    @pl.when(pl.program_id(0) == 1)
    def _():
        second_ref[...] = grad


def attend_back(limit, mixed, ctx_turn, lse, context_grad, n_turn, first):
    length = mixed.shape[0]
    features = n_turn.shape[0]
    pair = lambda i: first - i
    column = lambda c: pl.BlockSpec((length, PAIR), lambda i, s: (0, pair(i) * 3 + c))
    return pl.pallas_call(
        attend_back_kernel,
        grid_spec=pltpu.PrefetchScalarGridSpec(
            num_scalar_prefetch=1,
            grid=(2,),
            in_specs=[
                column(0), column(1), column(2),
                pl.BlockSpec((PAIR, length), lambda i, s: (pair(i), 0)),
                pl.BlockSpec((1, 2, length), lambda i, s: (pair(i), 0, 0)),
                pl.BlockSpec((length, PAIR), lambda i, s: (0, pair(i))),
                pl.BlockSpec((features, length), lambda i, s: (0, 0)),
            ],
            out_specs=[
                pl.BlockSpec((length, 3 * PAIR), lambda i, s: (0, i)),
                pl.BlockSpec((features, 3 * PAIR), lambda i, s: (0, 0)),
                pl.BlockSpec((features, 3 * PAIR), lambda i, s: (0, 0)),
            ],
            scratch_shapes=[
                pltpu.VMEM((2, length, PAIR), BF16),
                pltpu.VMEM((2, length, PAIR), BF16),
                pltpu.VMEM((2, length, PAIR), BF16),
                pltpu.VMEM((2, length, PAIR), BF16),
                pltpu.VMEM((PAIR, length), BF16),
                pltpu.VMEM((8, length), F32),
            ],
        ),
        out_shape=[
            jax.ShapeDtypeStruct((length, 2 * 3 * PAIR), BF16),
            jax.ShapeDtypeStruct((features, 3 * PAIR), BF16),
            jax.ShapeDtypeStruct((features, 3 * PAIR), BF16),
        ],
        compiler_params=params(28),
        cost_estimate=cost(16),
        name="attend_back",
    )(limit, mixed, mixed, mixed, ctx_turn, lse, context_grad, n_turn)


def begin_kernel(
    limit_ref, x_ref, clock_ref, gain_ref, gg_two_ref, mg_ref, w_ref, high_ref, low_ref, bg_ref, gg_s
):
    step = pl.program_id(0)
    _, parts, tall, width = bg_ref.shape
    tokens = tall - SPARE
    blocks = ROWS // tokens
    spot = pl.ds(step * blocks, blocks)

    @pl.when(step == 0)
    def _():
        gg_s[...] = jnp.zeros_like(gg_s)

    @pl.when(step * ROWS < limit_ref[0])
    def _():
        begin = join_tokens(x_ref) + clock_ref[...]
        unit, inverse = norm_parts(begin)
        one_grad = jnp.zeros_like(begin)
        for part, (d_ref, at) in enumerate(((low_ref, 1), (low_ref, 0), (high_ref, 1), (high_ref, 0))):
            columns = slice(part * 3 * PAIR, (part + 1) * 3 * PAIR)
            own = slice(at * 3 * PAIR, (at + 1) * 3 * PAIR)
            one_grad += mul(d_ref[:, own], w_ref[:, columns], NT)
        gg_s[...] += jnp.sum(one_grad * unit, axis=0, keepdims=True)
        total = (mg_ref[...] + norm_back(one_grad, gain_ref[...], unit, inverse)).astype(BF16)
        for part in range(parts):
            piece = total[:, part * width : (part + 1) * width]
            bg_ref[spot, part, 0:tokens] = piece.reshape(blocks, tokens, width)

    @pl.when(step * ROWS >= limit_ref[0])
    def _():
        bg_ref[spot] = jnp.zeros((blocks,) + bg_ref.shape[1:], BF16)

    @pl.when(step == pl.num_programs(0) - 1)
    def _():
        rows = []
        for ref in (gg_s, gg_two_ref):
            for part in range(parts):
                rows.append(ref[:, part * width : (part + 1) * width])
        bg_ref[:, :, tokens:tall] = jnp.broadcast_to(
            jnp.concatenate(rows, axis=0).astype(BF16), bg_ref.shape[:2] + (SPARE, width)
        )


def begin_block(limit, x_blocks, clock, gain, two_grad, w_wide, middle_grad, high, low):
    senders, feature_parts, tall, width = x_blocks.shape
    tokens = tall - SPARE
    length = senders * tokens
    features = feature_parts * width
    take = ROWS // tokens
    whole = lambda array: pl.BlockSpec(array.shape, lambda i, s: (0,) * array.ndim)
    rows = lambda n: pl.BlockSpec((ROWS, n), lambda i, s: (i, 0))
    return pl.pallas_call(
        begin_kernel,
        grid_spec=pltpu.PrefetchScalarGridSpec(
            num_scalar_prefetch=1,
            grid=(length // ROWS,),
            in_specs=[
                pl.BlockSpec((take, feature_parts, tall, width), lambda i, s: (i, 0, 0, 0)),
                whole(clock), whole(gain), whole(two_grad), rows(features), whole(w_wide),
            ]
            + [rows(6 * PAIR)] * 2,
            out_specs=whole(x_blocks),
            scratch_shapes=[pltpu.VMEM((1, features), F32)],
        ),
        out_shape=jax.ShapeDtypeStruct(x_blocks.shape, BF16),
        compiler_params=params(20),
        cost_estimate=cost(7),
        name="begin_back",
    )(limit, x_blocks, clock, gain, two_grad, middle_grad, w_wide, high, low)


DIRECT = 8


def clock_rows(step_ids, features):
    half_width = features // 2
    ladder = jnp.arange(half_width, dtype=F32) / half_width
    rate_rows = jnp.exp(-math.log(10000.0) * ladder)
    angles = step_ids.astype(F32)[:, None] * rate_rows[None, :]
    return jnp.concatenate([jnp.sin(angles), jnp.cos(angles)], axis=-1)


def swap(value, apart):
    count = lax.axis_size("tensor")
    return lax.ppermute(value, "tensor", [(i, i ^ apart) for i in range(count)])


def along_dp(value, move):
    count = lax.axis_size("dp")
    return lax.ppermute(value, "dp", [(i, move(i)) for i in range(count)])


def across(value):
    return ahead(value, 0, 1)


def ahead(value, step, flip=0):
    count = lax.axis_size("dp") // 2
    return along_dp(value, lambda i: (i // 2 + step) % count * 2 + (i + flip) % 2)


def places():
    count = lax.axis_size("dp") // 2
    own = lax.axis_index("dp")
    coarse = (own // 2 - jnp.arange(count, dtype=jnp.int32)) % count
    return jnp.concatenate([coarse * 2 + own % 2, coarse * 2 + 1 - own % 2])


def collect_coarse(shard):
    count = lax.axis_size("dp") // 2
    return [shard] + [ahead(shard, step) for step in range(1, count)]


def collect_rows(shard):
    count = lax.axis_size("dp")
    rows = lax.all_to_all(
        jnp.broadcast_to(shard[None], (count,) + shard.shape), "dp", 0, 0, tiled=True
    )
    return rows.reshape(count * shard.shape[0], shard.shape[1])


def collect_columns(rows):
    far = swap(rows, 2)
    return rows, swap(rows, 1), far, swap(far, 1)


def add(*values):
    return add_wide(*values).astype(BF16)


def fold_pair(values):
    own = lax.axis_index("dp") % 2
    pick = lambda value, which: lax.dynamic_index_in_dim(value, which, value.ndim - 3, keepdims=False)
    sent = add(*[pick(value, 1 - own) for value in values])
    return sent, lambda: [pick(value, own) for value in values] + [across(sent)]


def fold_far(values):
    sent = add(*[value[0] for value in values])
    return sent, lambda: [value[1] for value in values] + [swap(sent, 2)]


def fold_coarse(values):
    count = lax.axis_size("dp") // 2
    own = lax.axis_index("dp") // 2
    pick = lambda value, which: lax.dynamic_index_in_dim(value, which % count, 0, keepdims=False)
    value = add(*values)
    came = [ahead(pick(value, own + step), step) for step in range(1, count)]
    return value, [pick(value, own)] + came


def add_wide(*values):
    total = values[0].astype(F32)
    for value in values[1:]:
        total += value.astype(F32)
    return total


def grouped(value):
    count = lax.axis_size("dp")
    two, rows, columns = value.shape
    return value.reshape(two, count // 2, 2, rows // count, columns)


def exchange_rows(value):
    count = lax.axis_size("dp")
    groups = value.reshape(count, value.shape[0] // count, value.shape[1])
    return jnp.sum(lax.all_to_all(groups, "dp", 0, 0, tiled=True).astype(F32), axis=0)


def three_terms(values):
    terms = []
    for _ in range(3):
        term = lax.reduce_precision(values, 8, 7)
        terms.append(term.astype(BF16))
        values = values - term
    return terms


def together(*values):
    return lax.optimization_barrier(values)


def after(value, *others):
    return lax.optimization_barrier((value,) + others)[0]


def on_device(
    states, timesteps, lengths, deal_order, w_qkv, w_out, w_up, w_down, gain_attn, gain_ffn, out_grad
):
    both = ("dp", "tensor")
    dp_count = lax.axis_size("dp")
    tensor_count = lax.axis_size("tensor")
    devices = dp_count * tensor_count
    total_seqs, tokens, width = states.shape
    assert tensor_count == 4 and total_seqs == devices
    features = width * tensor_count
    own = lax.axis_index("dp") * tensor_count + lax.axis_index("tensor")
    own_id = lax.dynamic_slice_in_dim(deal_order, own, 1)
    limit = lengths[own_id]
    clock = clock_rows(timesteps[own_id], features)
    per = gain_attn.shape[0]
    rows = w_qkv.shape[0]
    hidden = w_up.shape[1]

    rest = jnp.concatenate([w_out.T, w_up, w_down.T], axis=1)
    qkv = w_qkv.reshape(rows, -1)
    direct = dp_count <= DIRECT
    if direct:
        place, groups = places(), dp_count
        wide = qkv.shape[1]
        pair = jnp.concatenate([qkv, across(qkv)], axis=1)
        pieces = collect_coarse(pair)
        qkv_rows = jnp.concatenate(
            [piece[:, :wide] for piece in pieces] + [piece[:, wide:] for piece in pieces], axis=0
        )
        mine = jnp.concatenate(collect_coarse(rest), axis=0)
        far_rows, other, far_mine = together(
            swap(qkv_rows, 2), in_hbm(across(mine)), in_hbm(swap(mine, 2))
        )
        qkv_parts = (qkv_rows, swap(qkv_rows, 1), far_rows, swap(far_rows, 1))
    else:
        place, groups = jnp.zeros((1,), jnp.int32), None
        qkv_parts = collect_columns(collect_rows(qkv))
        rest_parts = [(part,) for part in collect_columns(collect_rows(rest))]

    spare = jnp.stack(three_terms(gain_attn) + three_terms(gain_ffn)).reshape(1, 6 * per)
    spare = jnp.pad(spare, ((0, SPARE - 1), (0, width - 6 * per)))
    arranged = jnp.concatenate(
        [states[deal_order], jnp.broadcast_to(spare[None], (devices, SPARE, width))], axis=1
    )
    if direct:
        arranged = after(arranged, pair)
    x_blocks = lax.all_to_all(arranged, both, 0, 0, tiled=True)
    gains = jnp.sum(x_blocks[:, tokens, : 6 * per].reshape(devices, 2, 3, per).astype(F32), axis=2)
    gain_one = gains[:, 0].reshape(1, features)
    gain_two = gains[:, 1].reshape(1, features)
    x_blocks = x_blocks.reshape(dp_count, tensor_count, tokens + SPARE, width)

    mixed, n_one_turn, qkv_wide = project(
        limit, place, groups, x_blocks, clock, gain_one, qkv_parts
    )
    if direct:
        near_mine, near_other = in_hbm(swap(mine, 1)), in_hbm(swap(other, 1))
        last_mine, far_other = in_hbm(swap(far_mine, 1)), in_hbm(swap(other, 2))
    ctx, ctx_turn, lse = attend(limit, mixed, tensor_count)
    if direct:
        ctx, near_mine, near_other, last_mine, far_other = together(
            ctx, near_mine, near_other, last_mine, far_other
        )
        last_other = swap(far_other, 1)
        rest_parts = (
            (mine, other), (near_mine, near_other), (far_mine, far_other), (last_mine, last_other)
        )
    output, context_grad, middle_grad, two_grad, up_send, down_send, up_keep, down_keep = middle_block(
        limit, place, groups, x_blocks, clock, gain_two, ctx, rest_parts, out_grad
    )
    up_came, down_came = swap(up_send, 1), swap(down_send, 1)

    back = functools.partial(attend_back, limit, mixed, ctx_turn, lse)
    if direct:
        down_sent, down_rest = fold_far([grouped(value) for value in (down_keep, down_came)])
        up_sent, up_rest = fold_pair([grouped(value) for value in (up_keep, up_came)])
        context_grad = after(context_grad, down_sent, up_sent)
    high, three, two = back(in_hbm(context_grad), n_one_turn, 3)
    if direct:
        *down_rest, down_came = down_rest()
        *up_rest, up_came = up_rest()
        high, three, two, down_came, up_came = together(high, three, two, down_came, up_came)
        down_value, down_pieces = fold_coarse([*down_rest, down_came])
        up_sent, up_rest = fold_far([add(*up_rest, up_came)])
        context_grad = after(context_grad, down_value, up_sent)
    far = add(two, swap(three, 1))
    came_far = swap(far, 2)
    low, one, own_part = back(after(context_grad, high, far), n_one_turn, 1)
    if direct:
        *up_rest, up_came = up_rest()
        low, one, own_part, up_came, came_far, *down_pieces = together(
            low, one, own_part, up_came, came_far, *down_pieces
        )
        up_value, up_pieces = fold_coarse([*up_rest, up_came])
        down_sent, down_rest = fold_pair([add_wide(*down_pieces)[..., None, :, :, :]])
        middle_grad = after(middle_grad, up_value, down_sent)
    came_one = swap(one, 1)
    begin_grad = begin_block(
        limit, x_blocks, clock, gain_one, two_grad, qkv_wide, middle_grad, high, low
    )
    if direct:
        begin_grad, came_one, up_pieces[2] = together(begin_grad, came_one, up_pieces[2])
        near = [grouped(value[None])[0] for value in (own_part, came_one, came_far)]
        qkv_value, qkv_pieces = fold_coarse(fold_pair(near)[1]())
        down_total = add_wide(*down_rest())[0]
        pieces = together(*up_pieces, *qkv_pieces)
        up_total = add_wide(*pieces[: len(up_pieces)])
        qkv_total = add_wide(*pieces[len(up_pieces) :])
    else:
        up_total = exchange_rows(add(*fold_far([up_keep, up_came])[1]()))
        down_total = exchange_rows(add(*fold_far([down_keep, down_came])[1]()))
        qkv_total = exchange_rows(add(own_part, came_one, came_far))
    returned = lax.all_to_all(
        begin_grad.reshape(devices, tokens + SPARE, width), both, 0, 0, tiled=True
    )
    inverse = (
        jnp.zeros((total_seqs,), jnp.int32)
        .at[deal_order]
        .set(jnp.arange(total_seqs, dtype=jnp.int32))
    )
    states_grad = returned[inverse][:, :tokens]
    gain_grads = jnp.sum(returned[:, tokens:].astype(F32), axis=0).reshape(2, devices, per)
    gain_grads = lax.dynamic_index_in_dim(gain_grads, own, 1, keepdims=False)
    return (
        output,
        states_grad,
        qkv_total.reshape(w_qkv.shape),
        up_total[:, :PAIR].T,
        up_total[:, PAIR:],
        down_total.T,
        gain_grads[0],
        gain_grads[1],
    )


def solution(mesh):
    in_specs = (
        P(None, "dp", "tensor"),
        P(),
        P(),
        P(),
        P("dp", None, "tensor"),
        P("tensor", "dp"),
        P("dp", "tensor"),
        P("tensor", "dp"),
        P(("dp", "tensor")),
        P(("dp", "tensor")),
        P(("dp", "tensor"), None, None),
    )
    out_specs = (
        P(("dp", "tensor"), None, None),
        P(None, "dp", "tensor"),
        P("dp", None, "tensor"),
        P("tensor", "dp"),
        P("dp", "tensor"),
        P("tensor", "dp"),
        P(("dp", "tensor")),
        P(("dp", "tensor")),
    )
    return jax.shard_map(
        on_device, mesh=mesh, in_specs=in_specs, out_specs=out_specs, check_vma=False
    )
```

```python
import functools
import math

import jax
import jax.numpy as jnp
from jax import lax
from jax.experimental import pallas as pl
from jax.experimental.pallas import tpu as pltpu
from jax.sharding import PartitionSpec as P

HEAD_DIM = 64
PAIR = 2 * HEAD_DIM
ROWS = 512
KEYS = 256
BACK_KEYS = 512
SPARE = 8
SCORE_SCALE = 1.0 / math.sqrt(HEAD_DIM)
LOG2E = math.log2(math.e)
F32 = jnp.float32
BF16 = jnp.bfloat16
NN = (((1,), (0,)), ((), ()))
NT = (((1,), (1,)), ((), ()))
MIB = 1024 * 1024


def mul(lhs, rhs, dims=NN):
    return lax.dot_general(lhs, rhs, dims, preferred_element_type=F32)


def join_tokens(ref):
    blocks, parts, tall, width = ref.shape
    tokens = tall - SPARE
    return jnp.concatenate(
        [ref[:, part, 0:tokens].reshape(blocks * tokens, width) for part in range(parts)], axis=-1
    ).astype(F32)


def place_rows(groups, place_ref, first, source, targets):
    if groups is None:
        for target, columns, own in targets:
            target[:, columns] = source[:, own]
        return
    rows = source.shape[0] // groups
    for group in range(groups):
        spot = pl.ds(pl.multiple_of(place_ref[first + group] * rows, rows), rows)
        for target, columns, own in targets:
            target[spot, columns] = source[group * rows : (group + 1) * rows, own]


def norm_parts(values):
    center = values - jnp.mean(values, axis=-1, keepdims=True)
    spread = jnp.mean(center * center, axis=-1, keepdims=True)
    inverse = lax.rsqrt(spread + 1e-05)
    return center * inverse, inverse


def norm_back(grad, gain, unit, inverse):
    scaled = grad * gain
    mean_scaled = jnp.mean(scaled, axis=-1, keepdims=True)
    mean_along = jnp.mean(scaled * unit, axis=-1, keepdims=True)
    return inverse * (scaled - mean_scaled - unit * mean_along)


def in_hbm(value):
    return pltpu.with_memory_space_constraint(value, pltpu.HBM)


def cost(microseconds):
    return pl.CostEstimate(
        flops=int(microseconds * 1.15e9), bytes_accessed=1 << 20, transcendentals=0
    )


def params(mebibytes):
    return pltpu.CompilerParams(vmem_limit_bytes=mebibytes * MIB)


def project_kernel(groups, limit_ref, place_ref, x_ref, clock_ref, gain_ref, *refs):
    w_refs, (mixed_ref, n_turn_ref, wide) = refs[:-3], refs[-3:]
    step = pl.program_id(0)

    @pl.when(step == 0)
    def _():
        for part, w_ref in enumerate(w_refs):
            width = w_ref.shape[1]
            columns = slice(part * width, (part + 1) * width)
            place_rows(groups, place_ref, 0, w_ref, [(wide, columns, slice(0, width))])

    @pl.when(step * ROWS < limit_ref[0])
    def _():
        begin = join_tokens(x_ref) + clock_ref[...]
        unit, _ = norm_parts(begin)
        normed = (unit * gain_ref[...]).astype(BF16)
        n_turn_ref[...] = normed.T
        mixed_ref[...] = mul(normed, wide[...]).astype(BF16)

    @pl.when(step * ROWS >= limit_ref[0])
    def _():
        n_turn_ref[...] = jnp.zeros_like(n_turn_ref)
        mixed_ref[...] = jnp.zeros_like(mixed_ref)


def project(limit, place, groups, x_blocks, clock, gain, w_parts):
    senders, feature_parts, tall, width = x_blocks.shape
    tokens = tall - SPARE
    length = senders * tokens
    features = feature_parts * width
    parts, columns = len(w_parts), w_parts[0].shape[1]
    take = ROWS // tokens
    return pl.pallas_call(
        functools.partial(project_kernel, groups),
        grid_spec=pltpu.PrefetchScalarGridSpec(
            num_scalar_prefetch=2,
            grid=(length // ROWS,),
            in_specs=[
                pl.BlockSpec((take, feature_parts, tall, width), lambda i, *s: (i, 0, 0, 0)),
                pl.BlockSpec((1, features), lambda i, *s: (0, 0)),
                pl.BlockSpec((1, features), lambda i, *s: (0, 0)),
            ]
            + [pl.BlockSpec((features, columns), lambda i, *s: (0, 0))] * parts,
            out_specs=[
                pl.BlockSpec((ROWS, parts * columns), lambda i, *s: (i, 0)),
                pl.BlockSpec((features, ROWS), lambda i, *s: (0, i)),
                pl.BlockSpec((features, parts * columns), lambda i, *s: (0, 0)),
            ],
        ),
        out_shape=[
            jax.ShapeDtypeStruct((length, parts * columns), BF16),
            pltpu.HBM((features, length), BF16),
            pltpu.HBM((features, parts * columns), BF16),
        ],
        compiler_params=params(20),
        cost_estimate=cost(5),
        name="project",
    )(limit, place, x_blocks, clock, gain, *w_parts)


def head_lanes(shape, head):
    lane = lax.broadcasted_iota(jnp.int32, shape, 1)
    return (lane >= head * HEAD_DIM) & (lane < (head + 1) * HEAD_DIM)


def spare_lane(shape, head):
    lane = lax.broadcasted_iota(jnp.int32, shape, 1)
    return lane == (1 - head) * HEAD_DIM


def masked_keys(keys, head, limit):
    row = lax.broadcasted_iota(jnp.int32, keys.shape, 0)
    spare = jnp.where(
        spare_lane(keys.shape, head) & (row >= limit), jnp.asarray(-1e30, F32), jnp.asarray(0.0, F32)
    )
    return jnp.where(head_lanes(keys.shape, head), keys.astype(F32), spare).astype(BF16)


def own_lanes(values, head):
    return jnp.where(head_lanes(values.shape, head), values.astype(F32), 0.0).astype(BF16)


def masked_queries(queries, head):
    spare = jnp.where(spare_lane(queries.shape, head), jnp.asarray(1.0, F32), jnp.asarray(0.0, F32))
    return jnp.where(head_lanes(queries.shape, head), queries.astype(F32), spare).astype(BF16)


def attend_kernel(limit_ref, q_ref, k_ref, v_ref, ctx_ref, turn_ref, lse_ref, keys_s, q_s, vt_s, sc_s):
    length = q_ref.shape[0]
    vt_s[...] = v_ref[...].astype(F32).T.astype(BF16)
    for head in range(2):
        keys_s[head] = masked_keys(k_ref[...], head, limit_ref[0])
        q_s[head] = masked_queries(q_ref[...], head)
    factor = SCORE_SCALE * LOG2E
    spans = [slice(at, at + KEYS) for at in range(0, length, KEYS)]
    outs = []
    for head in range(2):
        feats = slice(head * HEAD_DIM, (head + 1) * HEAD_DIM)
        peak = None
        for span in spans:
            scores = mul(keys_s[head, span], q_s[head], NT)
            sc_s[head, span] = scores
            high = jnp.max(scores, axis=0, keepdims=True)
            peak = high if peak is None else jnp.maximum(peak, high)
        peak = peak * factor
        total = jnp.zeros_like(peak)
        gathered = jnp.zeros((HEAD_DIM, length), F32)
        for span in spans:
            expo = jnp.exp2(sc_s[head, span] * factor - peak)
            total += jnp.sum(expo, axis=0, keepdims=True)
            gathered += mul(vt_s[feats, span], expo.astype(BF16))
        outs.append(gathered / total)
        lse_ref[0, head : head + 1, :] = peak + jnp.log2(total)
    both = jnp.concatenate(outs, axis=0)
    turn_ref[...] = both.astype(BF16)
    ctx_ref[...] = both.T.astype(BF16)


def attend(limit, mixed, pairs):
    length = mixed.shape[0]
    column = lambda c: pl.BlockSpec((length, PAIR), lambda i, s: (0, i * 3 + c))
    return pl.pallas_call(
        attend_kernel,
        grid_spec=pltpu.PrefetchScalarGridSpec(
            num_scalar_prefetch=1,
            grid=(pairs,),
            in_specs=[column(0), column(1), column(2)],
            out_specs=[
                pl.BlockSpec((length, PAIR), lambda i, s: (0, i)),
                pl.BlockSpec((PAIR, length), lambda i, s: (i, 0)),
                pl.BlockSpec((1, 2, length), lambda i, s: (i, 0, 0)),
            ],
            scratch_shapes=[
                pltpu.VMEM((2, length, PAIR), BF16),
                pltpu.VMEM((2, length, PAIR), BF16),
                pltpu.VMEM((PAIR, length), BF16),
                pltpu.VMEM((2, length, length), F32),
            ],
        ),
        out_shape=[
            pltpu.HBM((length, pairs * PAIR), BF16),
            pltpu.HBM((pairs * PAIR, length), BF16),
            jax.ShapeDtypeStruct((pairs, 2, length), F32),
        ],
        compiler_params=params(28),
        cost_estimate=cost(15),
        name="attend",
    )(limit, mixed, mixed, mixed)


def gelu_both(values):
    root = math.sqrt(2.0 / math.pi)
    scaled = root * values
    inner = scaled * (1.0 + 0.044715 * (values * values))
    tanh = jnp.tanh(inner)
    half = 0.5 + 0.5 * tanh
    slope = half + (1.0 - tanh * tanh) * (1.5 * inner - scaled)
    return values * half, slope


def middle_kernel(
    groups, limit_ref, place_ref, x_ref, clock_ref, gain_ref, ctx_ref, og_ref, *refs
):
    weight_refs, refs = refs[:-17], refs[-17:]
    out_ref, cg_ref, mg_ref, gg_ref, up_send, down_send, up_keep, down_keep = refs[:8]
    wide, units, active_s, ug_s, n_turn, fg_turn, ag_turn, ctx_s, sems = refs[8:]
    step = pl.program_id(0)
    parts, _, hidden = active_s.shape
    blocks = pl.num_programs(0) - parts
    each = len(weight_refs) // parts

    def fetch(part, kind):
        target, wide_, own = (
            (wide, PAIR, slice(0, PAIR)),
            (units, 2 * hidden, slice(PAIR, PAIR + 2 * hidden)),
        )[kind]
        columns = slice(part * wide_, (part + 1) * wide_)
        copies = []
        for at, w_ref in enumerate(weight_refs[part * each : (part + 1) * each]):
            count = 1 if groups is None else groups // each
            rows = w_ref.shape[0] // count
            for group in range(count):
                index = at * count + group
                spot = pl.ds(0, rows)
                if groups is not None:
                    spot = pl.ds(pl.multiple_of(place_ref[index] * rows, rows), rows)
                copies.append(
                    pltpu.make_async_copy(
                        w_ref.at[pl.ds(group * rows, rows), own],
                        target.at[spot, columns],
                        sems.at[kind, part, index],
                    )
                )
        return copies

    @pl.when(step == 0)
    def _():
        gg_ref[...] = jnp.zeros_like(gg_ref)
        for part in range(parts):
            for copy in fetch(part, 0) + fetch(part, 1):
                copy.start()
        for part in range(parts):
            for copy in fetch(part, 0) + fetch(part, 1):
                copy.wait()

    dead = (step < blocks) & (step * ROWS >= limit_ref[0])

    @pl.when((step < blocks) & jnp.logical_not(dead))
    def _():
        spot = pl.ds(pl.multiple_of(step * ROWS, ROWS), ROWS)
        gain = gain_ref[...]
        live = step * ROWS + lax.broadcasted_iota(jnp.int32, (ROWS, 1), 0) < limit_ref[0]
        begin = join_tokens(x_ref) + clock_ref[...]
        middle = begin + mul(ctx_ref[...], wide[...], NT)
        unit, inverse = norm_parts(middle)
        normed = (unit * gain).astype(BF16)
        n_turn[:, spot] = normed.T
        res_grad = jnp.where(live, og_ref[0].astype(F32), 0.0)
        feed_grad = res_grad.astype(BF16)
        fg_turn[:, spot] = feed_grad.T
        feed = jnp.zeros_like(middle)
        two_grad = jnp.zeros_like(middle)
        for part in range(parts):
            up = slice(2 * part * hidden, (2 * part + 1) * hidden)
            down = slice((2 * part + 1) * hidden, (2 * part + 2) * hidden)
            upper = mul(normed, units[:, up])
            active, slope = gelu_both(upper)
            active = active.astype(BF16)
            active_s[part, spot] = active
            feed += mul(active, units[:, down], NT)
            upper_grad = (mul(feed_grad, units[:, down]) * slope).astype(BF16)
            ug_s[part, spot] = upper_grad
            two_grad += mul(upper_grad, units[:, up], NT)
        out_ref[0] = jnp.where(live, middle + feed, 0.0).astype(BF16)
        gg_ref[...] += jnp.sum(two_grad * unit, axis=0, keepdims=True)
        middle_grad = res_grad + norm_back(two_grad, gain, unit, inverse)
        mg_ref[...] = middle_grad
        att_grad = middle_grad.astype(BF16)
        ag_turn[:, spot] = att_grad.T
        cg_ref[...] = mul(att_grad, wide[...]).astype(BF16)
        for part in range(parts):
            ctx_s[part, spot] = ctx_ref[:, part * PAIR : (part + 1) * PAIR]

    @pl.when(dead)
    def _():
        spot = pl.ds(pl.multiple_of(step * ROWS, ROWS), ROWS)
        for ref in (out_ref, cg_ref, mg_ref):
            ref[...] = jnp.zeros_like(ref)
        for ref in (active_s, ug_s, ctx_s):
            ref[:, spot] = jnp.zeros((ref.shape[0], ROWS, ref.shape[2]), BF16)
        for ref in (n_turn, fg_turn, ag_turn):
            ref[:, spot] = jnp.zeros((ref.shape[0], ROWS), BF16)

    @pl.when(step >= blocks)
    def _():
        turn = step - blocks
        part = jnp.where(turn < 2, 3 - 2 * turn, 6 - 2 * turn)
        grads = (
            mul(ag_turn[...], ctx_s[part]).astype(BF16),
            mul(n_turn[...], ug_s[part]).astype(BF16),
            mul(fg_turn[...], active_s[part]).astype(BF16),
        )

        def into(up_ref, down_ref):
            up_ref[0, :, 0:PAIR], up_ref[0, :, PAIR:], down_ref[0] = grads

        pl.when(turn < 2)(lambda: into(up_send, down_send))
        pl.when(turn >= 2)(lambda: into(up_keep, down_keep))


def middle_block(limit, place, groups, x_blocks, clock, gain, ctx, w_parts, out_grad):
    senders, feature_parts, tall, width = x_blocks.shape
    tokens = tall - SPARE
    length = senders * tokens
    features = feature_parts * width
    parts = len(w_parts)
    weights = [in_hbm(w) for part in w_parts for w in part]
    columns = weights[0].shape[1]
    hidden = (columns - PAIR) // 2
    take = ROWS // tokens
    blocks = length // ROWS
    row = lambda i: jnp.minimum(i, blocks - 1)
    whole = lambda array: pl.BlockSpec(
        array.shape, lambda i, *s: (0,) * array.ndim, pipeline_mode=pl.Buffered(1)
    )
    rows = lambda n: pl.BlockSpec((ROWS, n), lambda i, *s: (row(i), 0))
    one = pl.BlockSpec((1, ROWS, features), lambda i, *s: (0, row(i), 0))
    grads = lambda first, n: pl.BlockSpec(
        (1, features, n), lambda i, *s: (jnp.clip(i - blocks - first, 0, 1), 0, 0)
    )
    up_shape = pltpu.HBM((2, features, PAIR + hidden), BF16)
    down_shape = pltpu.HBM((2, features, hidden), BF16)
    return pl.pallas_call(
        functools.partial(middle_kernel, groups),
        grid_spec=pltpu.PrefetchScalarGridSpec(
            num_scalar_prefetch=2,
            grid=(blocks + parts,),
            in_specs=[
                pl.BlockSpec(
                    (take, feature_parts, tall, width), lambda i, *s: (row(i), 0, 0, 0)
                ),
                whole(clock),
                whole(gain),
                rows(features),
                one,
            ]
            + [pl.BlockSpec(memory_space=pltpu.HBM)] * len(weights),
            out_specs=[
                one, rows(features), rows(features),
                pl.BlockSpec((1, features), lambda i, *s: (0, 0)),
                grads(0, PAIR + hidden), grads(0, hidden), grads(2, PAIR + hidden), grads(2, hidden),
            ],
            scratch_shapes=[
                pltpu.VMEM((features, parts * PAIR), BF16),
                pltpu.VMEM((features, parts * 2 * hidden), BF16),
                pltpu.VMEM((parts, length, hidden), BF16),
                pltpu.VMEM((parts, length, hidden), BF16),
                pltpu.VMEM((features, length), BF16),
                pltpu.VMEM((features, length), BF16),
                pltpu.VMEM((features, length), BF16),
                pltpu.VMEM((parts, length, PAIR), BF16),
                pltpu.SemaphoreType.DMA((2, parts, groups or 1)),
            ],
        ),
        out_shape=[
            jax.ShapeDtypeStruct((1, length, features), BF16),
            pltpu.HBM((length, features), BF16),
            pltpu.HBM((length, features), F32),
            jax.ShapeDtypeStruct((1, features), F32),
            up_shape, down_shape, up_shape, down_shape,
        ],
        compiler_params=params(48),
        cost_estimate=cost(25),
        name="middle",
    )(limit, place, x_blocks, clock, gain, in_hbm(ctx), in_hbm(out_grad), *weights)


def attend_back_kernel(
    limit_ref, q_ref, k_ref, v_ref, turn_ref, lse_ref, cg_ref, n_turn_ref,
    dm_ref, first_ref, second_ref, keys_s, q_s, qz_s, do_s, kt_s, delta_s,
):
    limit = limit_ref[0]
    length = q_ref.shape[0]
    kt_s[...] = k_ref[...].astype(F32).T.astype(BF16)
    along = cg_ref[...].astype(F32).T * turn_ref[...].astype(F32)
    for head in range(2):
        feats = slice(head * HEAD_DIM, (head + 1) * HEAD_DIM)
        delta_s[head : head + 1, :] = jnp.sum(along[feats, :], axis=0, keepdims=True)
        keys_s[head] = masked_keys(k_ref[...], head, limit)
        q_s[head] = masked_queries(q_ref[...], head)
        qz_s[head] = own_lanes(q_ref[...], head)
        do_s[head] = own_lanes(cg_ref[...], head)
    factor = SCORE_SCALE * LOG2E
    turned = [jnp.zeros((HEAD_DIM, length), F32)] * 2
    for at in range(0, length, BACK_KEYS):
        span = slice(at, at + BACK_KEYS)
        key_grad = jnp.zeros((BACK_KEYS, PAIR), F32)
        value_grad = jnp.zeros((BACK_KEYS, PAIR), F32)
        for head in range(2):
            feats = slice(head * HEAD_DIM, (head + 1) * HEAD_DIM)
            scores = mul(keys_s[head, span], q_s[head], NT)
            prob = jnp.exp2(scores * factor - lse_ref[0, head : head + 1, :])
            prob_grad = mul(v_ref[span, :], do_s[head], NT)
            score_grad = (prob * (prob_grad - delta_s[head : head + 1, :])).astype(BF16)
            value_grad += mul(prob.astype(BF16), do_s[head])
            key_grad += mul(score_grad, qz_s[head])
            turned[head] += mul(kt_s[feats, span], score_grad)
        dm_ref[span, PAIR : 2 * PAIR] = (key_grad * SCORE_SCALE).astype(BF16)
        dm_ref[span, 2 * PAIR : 3 * PAIR] = value_grad.astype(BF16)
    query_grad = jnp.concatenate(turned, axis=0) * SCORE_SCALE
    dm_ref[:, 0:PAIR] = query_grad.T.astype(BF16)
    grad = mul(n_turn_ref[...], dm_ref[...]).astype(BF16)

    @pl.when(pl.program_id(0) == 0)
    def _():
        first_ref[...] = grad

    @pl.when(pl.program_id(0) == 1)
    def _():
        second_ref[...] = grad


def attend_back(limit, mixed, ctx_turn, lse, context_grad, n_turn, first):
    length = mixed.shape[0]
    features = n_turn.shape[0]
    pair = lambda i: first - i
    column = lambda c: pl.BlockSpec((length, PAIR), lambda i, s: (0, pair(i) * 3 + c))
    return pl.pallas_call(
        attend_back_kernel,
        grid_spec=pltpu.PrefetchScalarGridSpec(
            num_scalar_prefetch=1,
            grid=(2,),
            in_specs=[
                column(0), column(1), column(2),
                pl.BlockSpec((PAIR, length), lambda i, s: (pair(i), 0)),
                pl.BlockSpec((1, 2, length), lambda i, s: (pair(i), 0, 0)),
                pl.BlockSpec((length, PAIR), lambda i, s: (0, pair(i))),
                pl.BlockSpec((features, length), lambda i, s: (0, 0)),
            ],
            out_specs=[
                pl.BlockSpec((length, 3 * PAIR), lambda i, s: (0, i)),
                pl.BlockSpec((features, 3 * PAIR), lambda i, s: (0, 0)),
                pl.BlockSpec((features, 3 * PAIR), lambda i, s: (0, 0)),
            ],
            scratch_shapes=[
                pltpu.VMEM((2, length, PAIR), BF16),
                pltpu.VMEM((2, length, PAIR), BF16),
                pltpu.VMEM((2, length, PAIR), BF16),
                pltpu.VMEM((2, length, PAIR), BF16),
                pltpu.VMEM((PAIR, length), BF16),
                pltpu.VMEM((8, length), F32),
            ],
        ),
        out_shape=[
            jax.ShapeDtypeStruct((length, 2 * 3 * PAIR), BF16),
            jax.ShapeDtypeStruct((features, 3 * PAIR), BF16),
            jax.ShapeDtypeStruct((features, 3 * PAIR), BF16),
        ],
        compiler_params=params(28),
        cost_estimate=cost(16),
        name="attend_back",
    )(limit, mixed, mixed, mixed, ctx_turn, lse, context_grad, n_turn)


def begin_kernel(
    limit_ref, x_ref, clock_ref, gain_ref, gg_two_ref, mg_ref, w_ref, high_ref, low_ref, bg_ref, gg_s
):
    step = pl.program_id(0)
    _, parts, tall, width = bg_ref.shape
    tokens = tall - SPARE
    blocks = ROWS // tokens
    spot = pl.ds(step * blocks, blocks)

    @pl.when(step == 0)
    def _():
        gg_s[...] = jnp.zeros_like(gg_s)

    @pl.when(step * ROWS < limit_ref[0])
    def _():
        begin = join_tokens(x_ref) + clock_ref[...]
        unit, inverse = norm_parts(begin)
        one_grad = jnp.zeros_like(begin)
        for part, (d_ref, at) in enumerate(((low_ref, 1), (low_ref, 0), (high_ref, 1), (high_ref, 0))):
            columns = slice(part * 3 * PAIR, (part + 1) * 3 * PAIR)
            own = slice(at * 3 * PAIR, (at + 1) * 3 * PAIR)
            one_grad += mul(d_ref[:, own], w_ref[:, columns], NT)
        gg_s[...] += jnp.sum(one_grad * unit, axis=0, keepdims=True)
        total = (mg_ref[...] + norm_back(one_grad, gain_ref[...], unit, inverse)).astype(BF16)
        for part in range(parts):
            piece = total[:, part * width : (part + 1) * width]
            bg_ref[spot, part, 0:tokens] = piece.reshape(blocks, tokens, width)

    @pl.when(step * ROWS >= limit_ref[0])
    def _():
        bg_ref[spot] = jnp.zeros((blocks,) + bg_ref.shape[1:], BF16)

    @pl.when(step == pl.num_programs(0) - 1)
    def _():
        rows = []
        for ref in (gg_s, gg_two_ref):
            for part in range(parts):
                rows.append(ref[:, part * width : (part + 1) * width])
        bg_ref[:, :, tokens:tall] = jnp.broadcast_to(
            jnp.concatenate(rows, axis=0).astype(BF16), bg_ref.shape[:2] + (SPARE, width)
        )


def begin_block(limit, x_blocks, clock, gain, two_grad, w_wide, middle_grad, high, low):
    senders, feature_parts, tall, width = x_blocks.shape
    tokens = tall - SPARE
    length = senders * tokens
    features = feature_parts * width
    take = ROWS // tokens
    whole = lambda array: pl.BlockSpec(array.shape, lambda i, s: (0,) * array.ndim)
    rows = lambda n: pl.BlockSpec((ROWS, n), lambda i, s: (i, 0))
    return pl.pallas_call(
        begin_kernel,
        grid_spec=pltpu.PrefetchScalarGridSpec(
            num_scalar_prefetch=1,
            grid=(length // ROWS,),
            in_specs=[
                pl.BlockSpec((take, feature_parts, tall, width), lambda i, s: (i, 0, 0, 0)),
                whole(clock), whole(gain), whole(two_grad), rows(features), whole(w_wide),
            ]
            + [rows(6 * PAIR)] * 2,
            out_specs=whole(x_blocks),
            scratch_shapes=[pltpu.VMEM((1, features), F32)],
        ),
        out_shape=jax.ShapeDtypeStruct(x_blocks.shape, BF16),
        compiler_params=params(20),
        cost_estimate=cost(7),
        name="begin_back",
    )(limit, x_blocks, clock, gain, two_grad, middle_grad, w_wide, high, low)


DIRECT = 8


def clock_rows(step_ids, features):
    half_width = features // 2
    ladder = jnp.arange(half_width, dtype=F32) / half_width
    rate_rows = jnp.exp(-math.log(10000.0) * ladder)
    angles = step_ids.astype(F32)[:, None] * rate_rows[None, :]
    return jnp.concatenate([jnp.sin(angles), jnp.cos(angles)], axis=-1)


def swap(value, apart):
    count = lax.axis_size("tensor")
    return lax.ppermute(value, "tensor", [(i, i ^ apart) for i in range(count)])


def along_dp(value, move):
    count = lax.axis_size("dp")
    return lax.ppermute(value, "dp", [(i, move(i)) for i in range(count)])


def across(value):
    return ahead(value, 0, 1)


def ahead(value, step, flip=0):
    count = lax.axis_size("dp") // 2
    return along_dp(value, lambda i: (i // 2 + step) % count * 2 + (i + flip) % 2)


def places():
    count = lax.axis_size("dp") // 2
    own = lax.axis_index("dp")
    coarse = (own // 2 - jnp.arange(count, dtype=jnp.int32)) % count
    return jnp.concatenate([coarse * 2 + own % 2, coarse * 2 + 1 - own % 2])


def collect_coarse(shard):
    count = lax.axis_size("dp") // 2
    return [shard] + [ahead(shard, step) for step in range(1, count)]


def collect_rows(shard):
    count = lax.axis_size("dp")
    rows = lax.all_to_all(
        jnp.broadcast_to(shard[None], (count,) + shard.shape), "dp", 0, 0, tiled=True
    )
    return rows.reshape(count * shard.shape[0], shard.shape[1])


def collect_columns(rows):
    far = swap(rows, 2)
    return rows, swap(rows, 1), far, swap(far, 1)


def add(*values):
    return add_wide(*values).astype(BF16)


def fold_pair(values):
    own = lax.axis_index("dp") % 2
    pick = lambda value, which: lax.dynamic_index_in_dim(value, which, value.ndim - 3, keepdims=False)
    sent = add(*[pick(value, 1 - own) for value in values])
    return sent, lambda: [pick(value, own) for value in values] + [across(sent)]


def fold_far(values):
    sent = add(*[value[0] for value in values])
    return sent, lambda: [value[1] for value in values] + [swap(sent, 2)]


def fold_coarse(values):
    count = lax.axis_size("dp") // 2
    own = lax.axis_index("dp") // 2
    pick = lambda value, which: lax.dynamic_index_in_dim(value, which % count, 0, keepdims=False)
    value = add(*values)
    came = [ahead(pick(value, own + step), step) for step in range(1, count)]
    return value, [pick(value, own)] + came


def add_wide(*values):
    total = values[0].astype(F32)
    for value in values[1:]:
        total += value.astype(F32)
    return total


def grouped(value):
    count = lax.axis_size("dp")
    two, rows, columns = value.shape
    return value.reshape(two, count // 2, 2, rows // count, columns)


def exchange_rows(value):
    count = lax.axis_size("dp")
    groups = value.reshape(count, value.shape[0] // count, value.shape[1])
    return jnp.sum(lax.all_to_all(groups, "dp", 0, 0, tiled=True).astype(F32), axis=0)


def three_terms(values):
    terms = []
    for _ in range(3):
        term = lax.reduce_precision(values, 8, 7)
        terms.append(term.astype(BF16))
        values = values - term
    return terms


def together(*values):
    return lax.optimization_barrier(values)


def after(value, *others):
    return lax.optimization_barrier((value,) + others)[0]


def on_device(
    states, timesteps, lengths, deal_order, w_qkv, w_out, w_up, w_down, gain_attn, gain_ffn, out_grad
):
    both = ("dp", "tensor")
    dp_count = lax.axis_size("dp")
    tensor_count = lax.axis_size("tensor")
    devices = dp_count * tensor_count
    total_seqs, tokens, width = states.shape
    assert tensor_count == 4 and total_seqs == devices
    features = width * tensor_count
    own = lax.axis_index("dp") * tensor_count + lax.axis_index("tensor")
    per = gain_attn.shape[0]
    rows = w_qkv.shape[0]
    hidden = w_up.shape[1]

    rest = jnp.concatenate([w_out.T, w_up, w_down.T], axis=1)
    qkv = w_qkv.reshape(rows, -1)
    direct = dp_count <= DIRECT
    if direct:
        place, groups = places(), dp_count
        wide = qkv.shape[1]
        pieces = collect_coarse(jnp.concatenate([qkv, across(qkv)], axis=1))
        qkv_rows = jnp.concatenate(
            [piece[:, :wide] for piece in pieces] + [piece[:, wide:] for piece in pieces], axis=0
        )
        mine = jnp.concatenate(collect_coarse(rest), axis=0)
        far_rows, other, far_mine = together(
            swap(qkv_rows, 2), in_hbm(across(mine)), in_hbm(swap(mine, 2))
        )
        qkv_parts = (qkv_rows, swap(qkv_rows, 1), far_rows, swap(far_rows, 1))
    else:
        place, groups = jnp.zeros((1,), jnp.int32), None
        qkv_parts = collect_columns(collect_rows(qkv))
        rest_parts = [(part,) for part in collect_columns(collect_rows(rest))]

    deal_later = after(deal_order, pieces[1]) if direct else deal_order
    own_id = lax.dynamic_slice_in_dim(deal_later, own, 1)
    limit = lengths[own_id]
    clock = clock_rows(timesteps[own_id], features)
    spare = jnp.stack(three_terms(gain_attn) + three_terms(gain_ffn)).reshape(1, 6 * per)
    spare = jnp.pad(spare, ((0, SPARE - 1), (0, width - 6 * per)))
    arranged = jnp.concatenate(
        [states[deal_order], jnp.broadcast_to(spare[None], (devices, SPARE, width))], axis=1
    )
    x_blocks = lax.all_to_all(arranged, both, 0, 0, tiled=True)
    gains = jnp.sum(x_blocks[:, tokens, : 6 * per].reshape(devices, 2, 3, per).astype(F32), axis=2)
    gain_one = gains[:, 0].reshape(1, features)
    gain_two = gains[:, 1].reshape(1, features)
    x_blocks = x_blocks.reshape(dp_count, tensor_count, tokens + SPARE, width)

    mixed, n_one_turn, qkv_wide = project(
        limit, place, groups, x_blocks, clock, gain_one, qkv_parts
    )
    if direct:
        near_mine, near_other = in_hbm(swap(mine, 1)), in_hbm(swap(other, 1))
        last_mine, far_other = in_hbm(swap(far_mine, 1)), in_hbm(swap(other, 2))
    ctx, ctx_turn, lse = attend(limit, mixed, tensor_count)
    if direct:
        ctx, near_mine, near_other, last_mine, far_other = together(
            ctx, near_mine, near_other, last_mine, far_other
        )
        last_other = swap(far_other, 1)
        rest_parts = (
            (mine, other), (near_mine, near_other), (far_mine, far_other), (last_mine, last_other)
        )
    output, context_grad, middle_grad, two_grad, up_send, down_send, up_keep, down_keep = middle_block(
        limit, place, groups, x_blocks, clock, gain_two, ctx, rest_parts, out_grad
    )
    up_came, down_came = swap(up_send, 1), swap(down_send, 1)

    back = functools.partial(attend_back, limit, mixed, ctx_turn, lse)
    if direct:
        down_sent, down_rest = fold_far([grouped(value) for value in (down_keep, down_came)])
        up_sent, up_rest = fold_pair([grouped(value) for value in (up_keep, up_came)])
        context_grad = after(context_grad, down_sent, up_sent)
    high, three, two = back(in_hbm(context_grad), n_one_turn, 3)
    if direct:
        *down_rest, down_came = down_rest()
        *up_rest, up_came = up_rest()
        high, three, two, down_came, up_came = together(high, three, two, down_came, up_came)
        down_value, down_pieces = fold_coarse([*down_rest, down_came])
        up_sent, up_rest = fold_far([add(*up_rest, up_came)])
        context_grad = after(context_grad, down_value, up_sent)
    far = add(two, swap(three, 1))
    came_far = swap(far, 2)
    low, one, own_part = back(after(context_grad, high, far), n_one_turn, 1)
    if direct:
        *up_rest, up_came = up_rest()
        low, one, own_part, up_came, came_far, *down_pieces = together(
            low, one, own_part, up_came, came_far, *down_pieces
        )
        up_value, up_pieces = fold_coarse([*up_rest, up_came])
        down_sent, down_rest = fold_pair([add_wide(*down_pieces)[..., None, :, :, :]])
        middle_grad = after(middle_grad, up_value, down_sent)
    came_one = swap(one, 1)
    begin_grad = begin_block(
        limit, x_blocks, clock, gain_one, two_grad, qkv_wide, middle_grad, high, low
    )
    if direct:
        begin_grad, came_one, up_pieces[2] = together(begin_grad, came_one, up_pieces[2])
        near = [grouped(value[None])[0] for value in (own_part, came_one, came_far)]
        qkv_value, qkv_pieces = fold_coarse(fold_pair(near)[1]())
        down_total = add_wide(*down_rest())[0]
        pieces = together(*up_pieces, *qkv_pieces)
        up_total = add_wide(*pieces[: len(up_pieces)])
        qkv_total = add_wide(*pieces[len(up_pieces) :])
    else:
        up_total = exchange_rows(add(*fold_far([up_keep, up_came])[1]()))
        down_total = exchange_rows(add(*fold_far([down_keep, down_came])[1]()))
        qkv_total = exchange_rows(add(own_part, came_one, came_far))
    returned = lax.all_to_all(
        begin_grad.reshape(devices, tokens + SPARE, width), both, 0, 0, tiled=True
    )
    inverse = (
        jnp.zeros((total_seqs,), jnp.int32)
        .at[deal_order]
        .set(jnp.arange(total_seqs, dtype=jnp.int32))
    )
    states_grad = returned[inverse][:, :tokens]
    gain_grads = jnp.sum(returned[:, tokens:].astype(F32), axis=0).reshape(2, devices, per)
    gain_grads = lax.dynamic_index_in_dim(gain_grads, own, 1, keepdims=False)
    return (
        output,
        states_grad,
        qkv_total.reshape(w_qkv.shape),
        up_total[:, :PAIR].T,
        up_total[:, PAIR:],
        down_total.T,
        gain_grads[0],
        gain_grads[1],
    )


def solution(mesh):
    in_specs = (
        P(None, "dp", "tensor"),
        P(),
        P(),
        P(),
        P("dp", None, "tensor"),
        P("tensor", "dp"),
        P("dp", "tensor"),
        P("tensor", "dp"),
        P(("dp", "tensor")),
        P(("dp", "tensor")),
        P(("dp", "tensor"), None, None),
    )
    out_specs = (
        P(("dp", "tensor"), None, None),
        P(None, "dp", "tensor"),
        P("dp", None, "tensor"),
        P("tensor", "dp"),
        P("dp", "tensor"),
        P("tensor", "dp"),
        P(("dp", "tensor")),
        P(("dp", "tensor")),
    )
    return jax.shard_map(
        on_device, mesh=mesh, in_specs=in_specs, out_specs=out_specs, check_vma=False
    )
```

```python
import functools
import math

import jax
import jax.numpy as jnp
from jax import lax
from jax.experimental import pallas as pl
from jax.experimental.pallas import tpu as pltpu
from jax.sharding import PartitionSpec as P

HEAD_DIM = 64
PAIR = 2 * HEAD_DIM
ROWS = 512
KEYS = 256
BACK_KEYS = 512
SPARE = 8
UNITS = 2048
SCORE_SCALE = 1.0 / math.sqrt(HEAD_DIM)
LOG2E = math.log2(math.e)
F32 = jnp.float32
BF16 = jnp.bfloat16
NN = (((1,), (0,)), ((), ()))
NT = (((1,), (1,)), ((), ()))
MIB = 1024 * 1024


def mul(lhs, rhs, dims=NN):
    return lax.dot_general(lhs, rhs, dims, preferred_element_type=F32)


def join_tokens(ref):
    blocks, parts, tall, width = ref.shape
    tokens = tall - SPARE
    return jnp.concatenate(
        [ref[:, part, 0:tokens].reshape(blocks * tokens, width) for part in range(parts)], axis=-1
    ).astype(F32)


def place_rows(groups, place_ref, first, source, targets):
    if groups is None:
        for target, columns, own in targets:
            target[:, columns] = source[:, own]
        return
    rows = source.shape[0] // groups
    for group in range(groups):
        spot = pl.ds(pl.multiple_of(place_ref[first + group] * rows, rows), rows)
        for target, columns, own in targets:
            target[spot, columns] = source[group * rows : (group + 1) * rows, own]


def norm_parts(values):
    center = values - jnp.mean(values, axis=-1, keepdims=True)
    spread = jnp.mean(center * center, axis=-1, keepdims=True)
    inverse = lax.rsqrt(spread + 1e-05)
    return center * inverse, inverse


def norm_back(grad, gain, unit, inverse):
    scaled = grad * gain
    mean_scaled = jnp.mean(scaled, axis=-1, keepdims=True)
    mean_along = jnp.mean(scaled * unit, axis=-1, keepdims=True)
    return inverse * (scaled - mean_scaled - unit * mean_along)


def in_hbm(value):
    return pltpu.with_memory_space_constraint(value, pltpu.HBM)


def cost(microseconds):
    return pl.CostEstimate(
        flops=int(microseconds * 1.15e9), bytes_accessed=1 << 20, transcendentals=0
    )


def params(mebibytes):
    return pltpu.CompilerParams(vmem_limit_bytes=mebibytes * MIB)


def project_kernel(groups, limit_ref, place_ref, x_ref, clock_ref, gain_ref, *refs):
    w_refs, (mixed_ref, n_turn_ref, wide) = refs[:-3], refs[-3:]
    step = pl.program_id(0)

    @pl.when(step == 0)
    def _():
        for part, w_ref in enumerate(w_refs):
            width = w_ref.shape[1]
            columns = slice(part * width, (part + 1) * width)
            place_rows(groups, place_ref, 0, w_ref, [(wide, columns, slice(0, width))])

    @pl.when(step * ROWS < limit_ref[0])
    def _():
        begin = join_tokens(x_ref) + clock_ref[...]
        unit, _ = norm_parts(begin)
        normed = (unit * gain_ref[...]).astype(BF16)
        n_turn_ref[...] = normed.T
        mixed_ref[...] = mul(normed, wide[...]).astype(BF16)

    @pl.when(step * ROWS >= limit_ref[0])
    def _():
        n_turn_ref[...] = jnp.zeros_like(n_turn_ref)
        mixed_ref[...] = jnp.zeros_like(mixed_ref)


def project(limit, place, groups, x_blocks, clock, gain, w_parts):
    senders, feature_parts, tall, width = x_blocks.shape
    tokens = tall - SPARE
    length = senders * tokens
    features = feature_parts * width
    parts, columns = len(w_parts), w_parts[0].shape[1]
    take = ROWS // tokens
    return pl.pallas_call(
        functools.partial(project_kernel, groups),
        grid_spec=pltpu.PrefetchScalarGridSpec(
            num_scalar_prefetch=2,
            grid=(length // ROWS,),
            in_specs=[
                pl.BlockSpec((take, feature_parts, tall, width), lambda i, *s: (i, 0, 0, 0)),
                pl.BlockSpec((1, features), lambda i, *s: (0, 0)),
                pl.BlockSpec((1, features), lambda i, *s: (0, 0)),
            ]
            + [pl.BlockSpec((features, columns), lambda i, *s: (0, 0))] * parts,
            out_specs=[
                pl.BlockSpec((ROWS, parts * columns), lambda i, *s: (i, 0)),
                pl.BlockSpec((features, ROWS), lambda i, *s: (0, i)),
                pl.BlockSpec((features, parts * columns), lambda i, *s: (0, 0)),
            ],
        ),
        out_shape=[
            jax.ShapeDtypeStruct((length, parts * columns), BF16),
            pltpu.HBM((features, length), BF16),
            pltpu.HBM((features, parts * columns), BF16),
        ],
        compiler_params=params(20),
        cost_estimate=cost(5),
        name="project",
    )(limit, place, x_blocks, clock, gain, *w_parts)


def head_lanes(shape, head):
    lane = lax.broadcasted_iota(jnp.int32, shape, 1)
    return (lane >= head * HEAD_DIM) & (lane < (head + 1) * HEAD_DIM)


def spare_lane(shape, head):
    lane = lax.broadcasted_iota(jnp.int32, shape, 1)
    return lane == (1 - head) * HEAD_DIM


def masked_keys(keys, head, limit):
    row = lax.broadcasted_iota(jnp.int32, keys.shape, 0)
    spare = jnp.where(
        spare_lane(keys.shape, head) & (row >= limit), jnp.asarray(-1e30, F32), jnp.asarray(0.0, F32)
    )
    return jnp.where(head_lanes(keys.shape, head), keys.astype(F32), spare).astype(BF16)


def own_lanes(values, head):
    return jnp.where(head_lanes(values.shape, head), values.astype(F32), 0.0).astype(BF16)


def masked_queries(queries, head):
    spare = jnp.where(spare_lane(queries.shape, head), jnp.asarray(1.0, F32), jnp.asarray(0.0, F32))
    return jnp.where(head_lanes(queries.shape, head), queries.astype(F32), spare).astype(BF16)


def attend_kernel(limit_ref, q_ref, k_ref, v_ref, ctx_ref, turn_ref, lse_ref, keys_s, q_s, vt_s, sc_s):
    length = q_ref.shape[0]
    vt_s[...] = v_ref[...].astype(F32).T.astype(BF16)
    for head in range(2):
        keys_s[head] = masked_keys(k_ref[...], head, limit_ref[0])
        q_s[head] = masked_queries(q_ref[...], head)
    factor = SCORE_SCALE * LOG2E
    spans = [slice(at, at + KEYS) for at in range(0, length, KEYS)]
    outs = []
    for head in range(2):
        feats = slice(head * HEAD_DIM, (head + 1) * HEAD_DIM)
        peak = None
        for span in spans:
            scores = mul(keys_s[head, span], q_s[head], NT)
            sc_s[head, span] = scores
            high = jnp.max(scores, axis=0, keepdims=True)
            peak = high if peak is None else jnp.maximum(peak, high)
        peak = peak * factor
        total = jnp.zeros_like(peak)
        gathered = jnp.zeros((HEAD_DIM, length), F32)
        for span in spans:
            expo = jnp.exp2(sc_s[head, span] * factor - peak)
            total += jnp.sum(expo, axis=0, keepdims=True)
            gathered += mul(vt_s[feats, span], expo.astype(BF16))
        outs.append(gathered / total)
        lse_ref[0, head : head + 1, :] = peak + jnp.log2(total)
    both = jnp.concatenate(outs, axis=0)
    turn_ref[...] = both.astype(BF16)
    ctx_ref[...] = both.T.astype(BF16)


def attend(limit, mixed, pairs):
    length = mixed.shape[0]
    column = lambda c: pl.BlockSpec((length, PAIR), lambda i, s: (0, i * 3 + c))
    return pl.pallas_call(
        attend_kernel,
        grid_spec=pltpu.PrefetchScalarGridSpec(
            num_scalar_prefetch=1,
            grid=(pairs,),
            in_specs=[column(0), column(1), column(2)],
            out_specs=[
                pl.BlockSpec((length, PAIR), lambda i, s: (0, i)),
                pl.BlockSpec((PAIR, length), lambda i, s: (i, 0)),
                pl.BlockSpec((1, 2, length), lambda i, s: (i, 0, 0)),
            ],
            scratch_shapes=[
                pltpu.VMEM((2, length, PAIR), BF16),
                pltpu.VMEM((2, length, PAIR), BF16),
                pltpu.VMEM((PAIR, length), BF16),
                pltpu.VMEM((2, length, length), F32),
            ],
        ),
        out_shape=[
            pltpu.HBM((length, pairs * PAIR), BF16),
            pltpu.HBM((pairs * PAIR, length), BF16),
            jax.ShapeDtypeStruct((pairs, 2, length), F32),
        ],
        compiler_params=params(28),
        cost_estimate=cost(15),
        name="attend",
    )(limit, mixed, mixed, mixed)


def gelu_both(values):
    root = math.sqrt(2.0 / math.pi)
    scaled = root * values
    inner = scaled * (1.0 + 0.044715 * (values * values))
    tanh = jnp.tanh(inner)
    half = 0.5 + 0.5 * tanh
    slope = half + (1.0 - tanh * tanh) * (1.5 * inner - scaled)
    return values * half, slope


def middle_kernel(
    groups, limit_ref, place_ref, x_ref, clock_ref, gain_ref, ctx_ref, og_ref, *refs
):
    weight_refs, refs = refs[:-18], refs[-18:]
    out_ref, cg_ref, mg_ref, gg_ref, up_send, down_send, up_keep, down_keep = refs[:8]
    wide, ups, downs, active_s, ug_s, n_turn, fg_turn, ag_turn, ctx_s, sems = refs[8:]
    step = pl.program_id(0)
    parts = ctx_s.shape[0]
    hidden = active_s.shape[1] // parts
    blocks = pl.num_programs(0) - parts
    each = len(weight_refs) // parts

    def fetch(part, kind):
        target, width, first = ((wide, PAIR, 0), (ups, hidden, PAIR), (downs, hidden, PAIR + hidden))[kind]
        own = slice(first, first + width)
        columns = slice(part * width, (part + 1) * width)
        copies = []
        for at, w_ref in enumerate(weight_refs[part * each : (part + 1) * each]):
            count = 1 if groups is None else groups // each
            rows = w_ref.shape[0] // count
            for group in range(count):
                index = at * count + group
                spot = pl.ds(0, rows)
                if groups is not None:
                    spot = pl.ds(pl.multiple_of(place_ref[index] * rows, rows), rows)
                copies.append(
                    pltpu.make_async_copy(
                        w_ref.at[pl.ds(group * rows, rows), own],
                        target.at[spot, columns],
                        sems.at[kind, part, index],
                    )
                )
        return copies

    @pl.when(step == 0)
    def _():
        gg_ref[...] = jnp.zeros_like(gg_ref)
        for part in range(parts):
            for copy in fetch(part, 0) + fetch(part, 1) + fetch(part, 2):
                copy.start()
        for part in range(parts):
            for copy in fetch(part, 0) + fetch(part, 1) + fetch(part, 2):
                copy.wait()

    dead = (step < blocks) & (step * ROWS >= limit_ref[0])

    @pl.when((step < blocks) & jnp.logical_not(dead))
    def _():
        spot = pl.ds(pl.multiple_of(step * ROWS, ROWS), ROWS)
        gain = gain_ref[...]
        live = step * ROWS + lax.broadcasted_iota(jnp.int32, (ROWS, 1), 0) < limit_ref[0]
        begin = join_tokens(x_ref) + clock_ref[...]
        middle = begin + mul(ctx_ref[...], wide[...], NT)
        unit, inverse = norm_parts(middle)
        normed = (unit * gain).astype(BF16)
        n_turn[:, spot] = normed.T
        res_grad = jnp.where(live, og_ref[0].astype(F32), 0.0)
        feed_grad = res_grad.astype(BF16)
        fg_turn[:, spot] = feed_grad.T
        feed = jnp.zeros_like(middle)
        two_grad = jnp.zeros_like(middle)
        for at in range(0, parts * hidden, UNITS):
            some = slice(at, at + UNITS)
            active, slope = gelu_both(mul(normed, ups[:, some]))
            active = active.astype(BF16)
            active_s[spot, some] = active
            feed += mul(active, downs[:, some], NT)
            upper_grad = (mul(feed_grad, downs[:, some]) * slope).astype(BF16)
            ug_s[spot, some] = upper_grad
            two_grad += mul(upper_grad, ups[:, some], NT)
        out_ref[0] = jnp.where(live, middle + feed, 0.0).astype(BF16)
        gg_ref[...] += jnp.sum(two_grad * unit, axis=0, keepdims=True)
        middle_grad = res_grad + norm_back(two_grad, gain, unit, inverse)
        mg_ref[...] = middle_grad
        att_grad = middle_grad.astype(BF16)
        ag_turn[:, spot] = att_grad.T
        cg_ref[...] = mul(att_grad, wide[...]).astype(BF16)
        for part in range(parts):
            ctx_s[part, spot] = ctx_ref[:, part * PAIR : (part + 1) * PAIR]

    @pl.when(dead)
    def _():
        spot = pl.ds(pl.multiple_of(step * ROWS, ROWS), ROWS)
        for ref in (out_ref, cg_ref, mg_ref):
            ref[...] = jnp.zeros_like(ref)
        for ref in (active_s, ug_s):
            ref[spot] = jnp.zeros((ROWS, ref.shape[1]), BF16)
        ctx_s[:, spot] = jnp.zeros((parts, ROWS, PAIR), BF16)
        for ref in (n_turn, fg_turn, ag_turn):
            ref[:, spot] = jnp.zeros((ref.shape[0], ROWS), BF16)

    @pl.when(step >= blocks)
    def _():
        turn = step - blocks
        part = jnp.where(turn < 2, 3 - 2 * turn, 6 - 2 * turn)
        own = pl.ds(pl.multiple_of(part * hidden, hidden), hidden)
        grads = (
            mul(ag_turn[...], ctx_s[part]).astype(BF16),
            mul(n_turn[...], ug_s[:, own]).astype(BF16),
            mul(fg_turn[...], active_s[:, own]).astype(BF16),
        )

        def into(up_ref, down_ref):
            up_ref[0, :, 0:PAIR], up_ref[0, :, PAIR:], down_ref[0] = grads

        pl.when(turn < 2)(lambda: into(up_send, down_send))
        pl.when(turn >= 2)(lambda: into(up_keep, down_keep))


def middle_block(limit, place, groups, x_blocks, clock, gain, ctx, w_parts, out_grad):
    senders, feature_parts, tall, width = x_blocks.shape
    tokens = tall - SPARE
    length = senders * tokens
    features = feature_parts * width
    parts = len(w_parts)
    weights = [in_hbm(w) for part in w_parts for w in part]
    columns = weights[0].shape[1]
    hidden = (columns - PAIR) // 2
    take = ROWS // tokens
    blocks = length // ROWS
    row = lambda i: jnp.minimum(i, blocks - 1)
    whole = lambda array: pl.BlockSpec(
        array.shape, lambda i, *s: (0,) * array.ndim, pipeline_mode=pl.Buffered(1)
    )
    rows = lambda n: pl.BlockSpec((ROWS, n), lambda i, *s: (row(i), 0))
    one = pl.BlockSpec((1, ROWS, features), lambda i, *s: (0, row(i), 0))
    grads = lambda first, n: pl.BlockSpec(
        (1, features, n), lambda i, *s: (jnp.clip(i - blocks - first, 0, 1), 0, 0)
    )
    up_shape = pltpu.HBM((2, features, PAIR + hidden), BF16)
    down_shape = pltpu.HBM((2, features, hidden), BF16)
    return pl.pallas_call(
        functools.partial(middle_kernel, groups),
        grid_spec=pltpu.PrefetchScalarGridSpec(
            num_scalar_prefetch=2,
            grid=(blocks + parts,),
            in_specs=[
                pl.BlockSpec(
                    (take, feature_parts, tall, width), lambda i, *s: (row(i), 0, 0, 0)
                ),
                whole(clock),
                whole(gain),
                rows(features),
                one,
            ]
            + [pl.BlockSpec(memory_space=pltpu.HBM)] * len(weights),
            out_specs=[
                one, rows(features), rows(features),
                pl.BlockSpec((1, features), lambda i, *s: (0, 0)),
                grads(0, PAIR + hidden), grads(0, hidden), grads(2, PAIR + hidden), grads(2, hidden),
            ],
            scratch_shapes=[
                pltpu.VMEM((features, parts * PAIR), BF16),
                pltpu.VMEM((features, parts * hidden), BF16),
                pltpu.VMEM((features, parts * hidden), BF16),
                pltpu.VMEM((length, parts * hidden), BF16),
                pltpu.VMEM((length, parts * hidden), BF16),
                pltpu.VMEM((features, length), BF16),
                pltpu.VMEM((features, length), BF16),
                pltpu.VMEM((features, length), BF16),
                pltpu.VMEM((parts, length, PAIR), BF16),
                pltpu.SemaphoreType.DMA((3, parts, groups or 1)),
            ],
        ),
        out_shape=[
            jax.ShapeDtypeStruct((1, length, features), BF16),
            pltpu.HBM((length, features), BF16),
            pltpu.HBM((length, features), F32),
            jax.ShapeDtypeStruct((1, features), F32),
            up_shape, down_shape, up_shape, down_shape,
        ],
        compiler_params=params(48),
        cost_estimate=cost(25),
        name="middle",
    )(limit, place, x_blocks, clock, gain, in_hbm(ctx), in_hbm(out_grad), *weights)


def attend_back_kernel(
    limit_ref, q_ref, k_ref, v_ref, turn_ref, lse_ref, cg_ref, n_turn_ref,
    dm_ref, first_ref, second_ref, keys_s, q_s, qz_s, do_s, kt_s, delta_s,
):
    limit = limit_ref[0]
    length = q_ref.shape[0]
    kt_s[...] = k_ref[...].astype(F32).T.astype(BF16)
    along = cg_ref[...].astype(F32).T * turn_ref[...].astype(F32)
    for head in range(2):
        feats = slice(head * HEAD_DIM, (head + 1) * HEAD_DIM)
        delta_s[head : head + 1, :] = jnp.sum(along[feats, :], axis=0, keepdims=True)
        keys_s[head] = masked_keys(k_ref[...], head, limit)
        q_s[head] = masked_queries(q_ref[...], head)
        qz_s[head] = own_lanes(q_ref[...], head)
        do_s[head] = own_lanes(cg_ref[...], head)
    factor = SCORE_SCALE * LOG2E
    turned = [jnp.zeros((HEAD_DIM, length), F32)] * 2
    for at in range(0, length, BACK_KEYS):
        span = slice(at, at + BACK_KEYS)
        key_grad = jnp.zeros((BACK_KEYS, PAIR), F32)
        value_grad = jnp.zeros((BACK_KEYS, PAIR), F32)
        for head in range(2):
            feats = slice(head * HEAD_DIM, (head + 1) * HEAD_DIM)
            scores = mul(keys_s[head, span], q_s[head], NT)
            prob = jnp.exp2(scores * factor - lse_ref[0, head : head + 1, :])
            prob_grad = mul(v_ref[span, :], do_s[head], NT)
            score_grad = (prob * (prob_grad - delta_s[head : head + 1, :])).astype(BF16)
            value_grad += mul(prob.astype(BF16), do_s[head])
            key_grad += mul(score_grad, qz_s[head])
            turned[head] += mul(kt_s[feats, span], score_grad)
        dm_ref[span, PAIR : 2 * PAIR] = (key_grad * SCORE_SCALE).astype(BF16)
        dm_ref[span, 2 * PAIR : 3 * PAIR] = value_grad.astype(BF16)
    query_grad = jnp.concatenate(turned, axis=0) * SCORE_SCALE
    dm_ref[:, 0:PAIR] = query_grad.T.astype(BF16)
    grad = mul(n_turn_ref[...], dm_ref[...]).astype(BF16)

    @pl.when(pl.program_id(0) == 0)
    def _():
        first_ref[...] = grad

    @pl.when(pl.program_id(0) == 1)
    def _():
        second_ref[...] = grad


def attend_back(limit, mixed, ctx_turn, lse, context_grad, n_turn, first):
    length = mixed.shape[0]
    features = n_turn.shape[0]
    pair = lambda i: first - i
    column = lambda c: pl.BlockSpec((length, PAIR), lambda i, s: (0, pair(i) * 3 + c))
    return pl.pallas_call(
        attend_back_kernel,
        grid_spec=pltpu.PrefetchScalarGridSpec(
            num_scalar_prefetch=1,
            grid=(2,),
            in_specs=[
                column(0), column(1), column(2),
                pl.BlockSpec((PAIR, length), lambda i, s: (pair(i), 0)),
                pl.BlockSpec((1, 2, length), lambda i, s: (pair(i), 0, 0)),
                pl.BlockSpec((length, PAIR), lambda i, s: (0, pair(i))),
                pl.BlockSpec((features, length), lambda i, s: (0, 0)),
            ],
            out_specs=[
                pl.BlockSpec((length, 3 * PAIR), lambda i, s: (0, i)),
                pl.BlockSpec((features, 3 * PAIR), lambda i, s: (0, 0)),
                pl.BlockSpec((features, 3 * PAIR), lambda i, s: (0, 0)),
            ],
            scratch_shapes=[
                pltpu.VMEM((2, length, PAIR), BF16),
                pltpu.VMEM((2, length, PAIR), BF16),
                pltpu.VMEM((2, length, PAIR), BF16),
                pltpu.VMEM((2, length, PAIR), BF16),
                pltpu.VMEM((PAIR, length), BF16),
                pltpu.VMEM((8, length), F32),
            ],
        ),
        out_shape=[
            jax.ShapeDtypeStruct((length, 2 * 3 * PAIR), BF16),
            jax.ShapeDtypeStruct((features, 3 * PAIR), BF16),
            jax.ShapeDtypeStruct((features, 3 * PAIR), BF16),
        ],
        compiler_params=params(28),
        cost_estimate=cost(16),
        name="attend_back",
    )(limit, mixed, mixed, mixed, ctx_turn, lse, context_grad, n_turn)


def begin_kernel(
    limit_ref, x_ref, clock_ref, gain_ref, gg_two_ref, mg_ref, w_ref, high_ref, low_ref, bg_ref, gg_s
):
    step = pl.program_id(0)
    _, parts, tall, width = bg_ref.shape
    tokens = tall - SPARE
    blocks = ROWS // tokens
    spot = pl.ds(step * blocks, blocks)

    @pl.when(step == 0)
    def _():
        gg_s[...] = jnp.zeros_like(gg_s)

    @pl.when(step * ROWS < limit_ref[0])
    def _():
        begin = join_tokens(x_ref) + clock_ref[...]
        unit, inverse = norm_parts(begin)
        one_grad = jnp.zeros_like(begin)
        for part, (d_ref, at) in enumerate(((low_ref, 1), (low_ref, 0), (high_ref, 1), (high_ref, 0))):
            columns = slice(part * 3 * PAIR, (part + 1) * 3 * PAIR)
            own = slice(at * 3 * PAIR, (at + 1) * 3 * PAIR)
            one_grad += mul(d_ref[:, own], w_ref[:, columns], NT)
        gg_s[...] += jnp.sum(one_grad * unit, axis=0, keepdims=True)
        total = (mg_ref[...] + norm_back(one_grad, gain_ref[...], unit, inverse)).astype(BF16)
        for part in range(parts):
            piece = total[:, part * width : (part + 1) * width]
            bg_ref[spot, part, 0:tokens] = piece.reshape(blocks, tokens, width)

    @pl.when(step * ROWS >= limit_ref[0])
    def _():
        bg_ref[spot] = jnp.zeros((blocks,) + bg_ref.shape[1:], BF16)

    @pl.when(step == pl.num_programs(0) - 1)
    def _():
        rows = []
        for ref in (gg_s, gg_two_ref):
            for part in range(parts):
                rows.append(ref[:, part * width : (part + 1) * width])
        bg_ref[:, :, tokens:tall] = jnp.broadcast_to(
            jnp.concatenate(rows, axis=0).astype(BF16), bg_ref.shape[:2] + (SPARE, width)
        )


def begin_block(limit, x_blocks, clock, gain, two_grad, w_wide, middle_grad, high, low):
    senders, feature_parts, tall, width = x_blocks.shape
    tokens = tall - SPARE
    length = senders * tokens
    features = feature_parts * width
    take = ROWS // tokens
    whole = lambda array: pl.BlockSpec(array.shape, lambda i, s: (0,) * array.ndim)
    rows = lambda n: pl.BlockSpec((ROWS, n), lambda i, s: (i, 0))
    return pl.pallas_call(
        begin_kernel,
        grid_spec=pltpu.PrefetchScalarGridSpec(
            num_scalar_prefetch=1,
            grid=(length // ROWS,),
            in_specs=[
                pl.BlockSpec((take, feature_parts, tall, width), lambda i, s: (i, 0, 0, 0)),
                whole(clock), whole(gain), whole(two_grad), rows(features), whole(w_wide),
            ]
            + [rows(6 * PAIR)] * 2,
            out_specs=whole(x_blocks),
            scratch_shapes=[pltpu.VMEM((1, features), F32)],
        ),
        out_shape=jax.ShapeDtypeStruct(x_blocks.shape, BF16),
        compiler_params=params(20),
        cost_estimate=cost(7),
        name="begin_back",
    )(limit, x_blocks, clock, gain, two_grad, middle_grad, w_wide, high, low)


DIRECT = 8


def clock_rows(step_ids, features):
    half_width = features // 2
    ladder = jnp.arange(half_width, dtype=F32) / half_width
    rate_rows = jnp.exp(-math.log(10000.0) * ladder)
    angles = step_ids.astype(F32)[:, None] * rate_rows[None, :]
    return jnp.concatenate([jnp.sin(angles), jnp.cos(angles)], axis=-1)


def swap(value, apart):
    count = lax.axis_size("tensor")
    return lax.ppermute(value, "tensor", [(i, i ^ apart) for i in range(count)])


def along_dp(value, move):
    count = lax.axis_size("dp")
    return lax.ppermute(value, "dp", [(i, move(i)) for i in range(count)])


def across(value):
    return ahead(value, 0, 1)


def ahead(value, step, flip=0):
    count = lax.axis_size("dp") // 2
    return along_dp(value, lambda i: (i // 2 + step) % count * 2 + (i + flip) % 2)


def places():
    count = lax.axis_size("dp") // 2
    own = lax.axis_index("dp")
    coarse = (own // 2 - jnp.arange(count, dtype=jnp.int32)) % count
    return jnp.concatenate([coarse * 2 + own % 2, coarse * 2 + 1 - own % 2])


def collect_coarse(shard):
    count = lax.axis_size("dp") // 2
    return [shard] + [ahead(shard, step) for step in range(1, count)]


def collect_rows(shard):
    count = lax.axis_size("dp")
    rows = lax.all_to_all(
        jnp.broadcast_to(shard[None], (count,) + shard.shape), "dp", 0, 0, tiled=True
    )
    return rows.reshape(count * shard.shape[0], shard.shape[1])


def collect_columns(rows):
    far = swap(rows, 2)
    return rows, swap(rows, 1), far, swap(far, 1)


def add(*values):
    return add_wide(*values).astype(BF16)


def fold_pair(values):
    own = lax.axis_index("dp") % 2
    pick = lambda value, which: lax.dynamic_index_in_dim(value, which, value.ndim - 3, keepdims=False)
    sent = add(*[pick(value, 1 - own) for value in values])
    return sent, lambda: [pick(value, own) for value in values] + [across(sent)]


def fold_far(values):
    sent = add(*[value[0] for value in values])
    return sent, lambda: [value[1] for value in values] + [swap(sent, 2)]


def fold_coarse(values):
    count = lax.axis_size("dp") // 2
    own = lax.axis_index("dp") // 2
    pick = lambda value, which: lax.dynamic_index_in_dim(value, which % count, 0, keepdims=False)
    value = add(*values)
    came = [ahead(pick(value, own + step), step) for step in range(1, count)]
    return value, [pick(value, own)] + came


def add_wide(*values):
    total = values[0].astype(F32)
    for value in values[1:]:
        total += value.astype(F32)
    return total


def grouped(value):
    count = lax.axis_size("dp")
    two, rows, columns = value.shape
    return value.reshape(two, count // 2, 2, rows // count, columns)


def exchange_rows(value):
    count = lax.axis_size("dp")
    groups = value.reshape(count, value.shape[0] // count, value.shape[1])
    return jnp.sum(lax.all_to_all(groups, "dp", 0, 0, tiled=True).astype(F32), axis=0)


def three_terms(values):
    terms = []
    for _ in range(3):
        term = lax.reduce_precision(values, 8, 7)
        terms.append(term.astype(BF16))
        values = values - term
    return terms


def together(*values):
    return lax.optimization_barrier(values)


def after(value, *others):
    return lax.optimization_barrier((value,) + others)[0]


def on_device(
    states, timesteps, lengths, deal_order, w_qkv, w_out, w_up, w_down, gain_attn, gain_ffn, out_grad
):
    both = ("dp", "tensor")
    dp_count = lax.axis_size("dp")
    tensor_count = lax.axis_size("tensor")
    devices = dp_count * tensor_count
    total_seqs, tokens, width = states.shape
    assert tensor_count == 4 and total_seqs == devices
    features = width * tensor_count
    own = lax.axis_index("dp") * tensor_count + lax.axis_index("tensor")
    per = gain_attn.shape[0]
    rows = w_qkv.shape[0]
    hidden = w_up.shape[1]

    rest = jnp.concatenate([w_out.T, w_up, w_down.T], axis=1)
    qkv = w_qkv.reshape(rows, -1)
    direct = dp_count <= DIRECT
    if direct:
        place, groups = places(), dp_count
        wide = qkv.shape[1]
        pieces = collect_coarse(jnp.concatenate([qkv, across(qkv)], axis=1))
        qkv_rows = jnp.concatenate(
            [piece[:, :wide] for piece in pieces] + [piece[:, wide:] for piece in pieces], axis=0
        )
        mine = jnp.concatenate(collect_coarse(rest), axis=0)
        far_rows, other, far_mine = together(
            swap(qkv_rows, 2), in_hbm(across(mine)), in_hbm(swap(mine, 2))
        )
        qkv_parts = (qkv_rows, swap(qkv_rows, 1), far_rows, swap(far_rows, 1))
    else:
        place, groups = jnp.zeros((1,), jnp.int32), None
        qkv_parts = collect_columns(collect_rows(qkv))
        rest_parts = [(part,) for part in collect_columns(collect_rows(rest))]

    deal_later = after(deal_order, pieces[1]) if direct else deal_order
    own_id = lax.dynamic_slice_in_dim(deal_later, own, 1)
    limit = lengths[own_id]
    clock = clock_rows(timesteps[own_id], features)
    spare = jnp.stack(three_terms(gain_attn) + three_terms(gain_ffn)).reshape(1, 6 * per)
    spare = jnp.pad(spare, ((0, SPARE - 1), (0, width - 6 * per)))
    arranged = jnp.concatenate(
        [states[deal_order], jnp.broadcast_to(spare[None], (devices, SPARE, width))], axis=1
    )
    x_blocks = lax.all_to_all(arranged, both, 0, 0, tiled=True)
    gains = jnp.sum(x_blocks[:, tokens, : 6 * per].reshape(devices, 2, 3, per).astype(F32), axis=2)
    gain_one = gains[:, 0].reshape(1, features)
    gain_two = gains[:, 1].reshape(1, features)
    x_blocks = x_blocks.reshape(dp_count, tensor_count, tokens + SPARE, width)

    mixed, n_one_turn, qkv_wide = project(
        limit, place, groups, x_blocks, clock, gain_one, qkv_parts
    )
    if direct:
        near_mine, near_other = in_hbm(swap(mine, 1)), in_hbm(swap(other, 1))
        last_mine, far_other = in_hbm(swap(far_mine, 1)), in_hbm(swap(other, 2))
    ctx, ctx_turn, lse = attend(limit, mixed, tensor_count)
    if direct:
        ctx, near_mine, near_other, last_mine, far_other = together(
            ctx, near_mine, near_other, last_mine, far_other
        )
        last_other = swap(far_other, 1)
        rest_parts = (
            (mine, other), (near_mine, near_other), (far_mine, far_other), (last_mine, last_other)
        )
    output, context_grad, middle_grad, two_grad, up_send, down_send, up_keep, down_keep = middle_block(
        limit, place, groups, x_blocks, clock, gain_two, ctx, rest_parts, out_grad
    )
    up_came, down_came = swap(up_send, 1), swap(down_send, 1)

    back = functools.partial(attend_back, limit, mixed, ctx_turn, lse)
    if direct:
        down_sent, down_rest = fold_far([grouped(value) for value in (down_keep, down_came)])
        up_sent, up_rest = fold_pair([grouped(value) for value in (up_keep, up_came)])
        context_grad = after(context_grad, down_sent, up_sent)
    high, three, two = back(in_hbm(context_grad), n_one_turn, 3)
    if direct:
        *down_rest, down_came = down_rest()
        *up_rest, up_came = up_rest()
        high, three, two, down_came, up_came = together(high, three, two, down_came, up_came)
        down_value, down_pieces = fold_coarse([*down_rest, down_came])
        up_sent, up_rest = fold_far([add(*up_rest, up_came)])
        context_grad = after(context_grad, down_value, up_sent)
    far = add(two, swap(three, 1))
    came_far = swap(far, 2)
    low, one, own_part = back(after(context_grad, high, far), n_one_turn, 1)
    if direct:
        *up_rest, up_came = up_rest()
        low, one, own_part, up_came, came_far, *down_pieces = together(
            low, one, own_part, up_came, came_far, *down_pieces
        )
        up_value, up_pieces = fold_coarse([*up_rest, up_came])
        down_sent, down_rest = fold_pair([add_wide(*down_pieces)[..., None, :, :, :]])
        middle_grad = after(middle_grad, up_value, down_sent)
    came_one = swap(one, 1)
    begin_grad = begin_block(
        limit, x_blocks, clock, gain_one, two_grad, qkv_wide, middle_grad, high, low
    )
    if direct:
        begin_grad, came_one, up_pieces[2] = together(begin_grad, came_one, up_pieces[2])
        near = [grouped(value[None])[0] for value in (own_part, came_one, came_far)]
        qkv_value, qkv_pieces = fold_coarse(fold_pair(near)[1]())
        down_total = add_wide(*down_rest())[0]
        pieces = together(*up_pieces, *qkv_pieces)
        up_total = add_wide(*pieces[: len(up_pieces)])
        qkv_total = add_wide(*pieces[len(up_pieces) :])
    else:
        up_total = exchange_rows(add(*fold_far([up_keep, up_came])[1]()))
        down_total = exchange_rows(add(*fold_far([down_keep, down_came])[1]()))
        qkv_total = exchange_rows(add(own_part, came_one, came_far))
    returned = lax.all_to_all(
        begin_grad.reshape(devices, tokens + SPARE, width), both, 0, 0, tiled=True
    )
    inverse = (
        jnp.zeros((total_seqs,), jnp.int32)
        .at[deal_order]
        .set(jnp.arange(total_seqs, dtype=jnp.int32))
    )
    states_grad = returned[inverse][:, :tokens]
    gain_grads = jnp.sum(returned[:, tokens:].astype(F32), axis=0).reshape(2, devices, per)
    gain_grads = lax.dynamic_index_in_dim(gain_grads, own, 1, keepdims=False)
    return (
        output,
        states_grad,
        qkv_total.reshape(w_qkv.shape),
        up_total[:, :PAIR].T,
        up_total[:, PAIR:],
        down_total.T,
        gain_grads[0],
        gain_grads[1],
    )


def solution(mesh):
    in_specs = (
        P(None, "dp", "tensor"),
        P(),
        P(),
        P(),
        P("dp", None, "tensor"),
        P("tensor", "dp"),
        P("dp", "tensor"),
        P("tensor", "dp"),
        P(("dp", "tensor")),
        P(("dp", "tensor")),
        P(("dp", "tensor"), None, None),
    )
    out_specs = (
        P(("dp", "tensor"), None, None),
        P(None, "dp", "tensor"),
        P("dp", None, "tensor"),
        P("tensor", "dp"),
        P("dp", "tensor"),
        P("tensor", "dp"),
        P(("dp", "tensor")),
        P(("dp", "tensor")),
    )
    return jax.shard_map(
        on_device, mesh=mesh, in_specs=in_specs, out_specs=out_specs, check_vma=False
    )
```

```python
import functools
import math

import jax
import jax.numpy as jnp
from jax import lax
from jax.experimental import pallas as pl
from jax.experimental.pallas import tpu as pltpu
from jax.sharding import PartitionSpec as P

HEAD_DIM = 64
PAIR = 2 * HEAD_DIM
ROWS = 512
KEYS = 256
BACK_KEYS = 512
SPARE = 8
UNITS = 2048
SCORE_SCALE = 1.0 / math.sqrt(HEAD_DIM)
LOG2E = math.log2(math.e)
F32 = jnp.float32
BF16 = jnp.bfloat16
NN = (((1,), (0,)), ((), ()))
NT = (((1,), (1,)), ((), ()))
MIB = 1024 * 1024


def mul(lhs, rhs, dims=NN):
    return lax.dot_general(lhs, rhs, dims, preferred_element_type=F32)


def join_tokens(ref):
    blocks, parts, tall, width = ref.shape
    tokens = tall - SPARE
    return jnp.concatenate(
        [ref[:, part, 0:tokens].reshape(blocks * tokens, width) for part in range(parts)], axis=-1
    ).astype(F32)


def place_rows(groups, place_ref, first, source, targets):
    if groups is None:
        for target, columns, own in targets:
            target[:, columns] = source[:, own]
        return
    rows = source.shape[0] // groups
    for group in range(groups):
        spot = pl.ds(pl.multiple_of(place_ref[first + group] * rows, rows), rows)
        for target, columns, own in targets:
            target[spot, columns] = source[group * rows : (group + 1) * rows, own]


def norm_parts(values):
    center = values - jnp.mean(values, axis=-1, keepdims=True)
    spread = jnp.mean(center * center, axis=-1, keepdims=True)
    inverse = lax.rsqrt(spread + 1e-05)
    return center * inverse, inverse


def norm_back(grad, gain, unit, inverse):
    scaled = grad * gain
    mean_scaled = jnp.mean(scaled, axis=-1, keepdims=True)
    mean_along = jnp.mean(scaled * unit, axis=-1, keepdims=True)
    return inverse * (scaled - mean_scaled - unit * mean_along)


def in_hbm(value):
    return pltpu.with_memory_space_constraint(value, pltpu.HBM)


def cost(microseconds):
    return pl.CostEstimate(
        flops=int(microseconds * 1.15e9), bytes_accessed=1 << 20, transcendentals=0
    )


def params(mebibytes):
    return pltpu.CompilerParams(vmem_limit_bytes=mebibytes * MIB)


def project_kernel(groups, limit_ref, place_ref, x_ref, clock_ref, gain_ref, *refs):
    w_refs, (mixed_ref, n_turn_ref, wide) = refs[:-3], refs[-3:]
    step = pl.program_id(0)

    @pl.when(step == 0)
    def _():
        for part, w_ref in enumerate(w_refs):
            width = w_ref.shape[1]
            columns = slice(part * width, (part + 1) * width)
            place_rows(groups, place_ref, 0, w_ref, [(wide, columns, slice(0, width))])

    @pl.when(step * ROWS < limit_ref[0])
    def _():
        begin = join_tokens(x_ref) + clock_ref[...]
        unit, _ = norm_parts(begin)
        normed = (unit * gain_ref[...]).astype(BF16)
        n_turn_ref[...] = normed.T
        mixed_ref[...] = mul(normed, wide[...]).astype(BF16)

    @pl.when(step * ROWS >= limit_ref[0])
    def _():
        n_turn_ref[...] = jnp.zeros_like(n_turn_ref)
        mixed_ref[...] = jnp.zeros_like(mixed_ref)


def project(limit, place, groups, x_blocks, clock, gain, w_parts):
    senders, feature_parts, tall, width = x_blocks.shape
    tokens = tall - SPARE
    length = senders * tokens
    features = feature_parts * width
    parts, columns = len(w_parts), w_parts[0].shape[1]
    take = ROWS // tokens
    return pl.pallas_call(
        functools.partial(project_kernel, groups),
        grid_spec=pltpu.PrefetchScalarGridSpec(
            num_scalar_prefetch=2,
            grid=(length // ROWS,),
            in_specs=[
                pl.BlockSpec((take, feature_parts, tall, width), lambda i, *s: (i, 0, 0, 0)),
                pl.BlockSpec((1, features), lambda i, *s: (0, 0)),
                pl.BlockSpec((1, features), lambda i, *s: (0, 0)),
            ]
            + [pl.BlockSpec((features, columns), lambda i, *s: (0, 0))] * parts,
            out_specs=[
                pl.BlockSpec((ROWS, parts * columns), lambda i, *s: (i, 0)),
                pl.BlockSpec((features, ROWS), lambda i, *s: (0, i)),
                pl.BlockSpec((features, parts * columns), lambda i, *s: (0, 0)),
            ],
        ),
        out_shape=[
            jax.ShapeDtypeStruct((length, parts * columns), BF16),
            pltpu.HBM((features, length), BF16),
            pltpu.HBM((features, parts * columns), BF16),
        ],
        compiler_params=params(20),
        cost_estimate=cost(5),
        name="project",
    )(limit, place, x_blocks, clock, gain, *w_parts)


def head_lanes(shape, head):
    lane = lax.broadcasted_iota(jnp.int32, shape, 1)
    return (lane >= head * HEAD_DIM) & (lane < (head + 1) * HEAD_DIM)


def spare_lane(shape, head):
    lane = lax.broadcasted_iota(jnp.int32, shape, 1)
    return lane == (1 - head) * HEAD_DIM


def masked_keys(keys, head, limit):
    row = lax.broadcasted_iota(jnp.int32, keys.shape, 0)
    spare = jnp.where(
        spare_lane(keys.shape, head) & (row >= limit), jnp.asarray(-1e30, F32), jnp.asarray(0.0, F32)
    )
    return jnp.where(head_lanes(keys.shape, head), keys.astype(F32), spare).astype(BF16)


def own_lanes(values, head):
    return jnp.where(head_lanes(values.shape, head), values.astype(F32), 0.0).astype(BF16)


def masked_queries(queries, head):
    spare = jnp.where(spare_lane(queries.shape, head), jnp.asarray(1.0, F32), jnp.asarray(0.0, F32))
    return jnp.where(head_lanes(queries.shape, head), queries.astype(F32), spare).astype(BF16)


def attend_kernel(limit_ref, q_ref, k_ref, v_ref, ctx_ref, turn_ref, lse_ref, keys_s, q_s, vt_s, sc_s):
    length = q_ref.shape[0]
    vt_s[...] = v_ref[...].astype(F32).T.astype(BF16)
    for head in range(2):
        keys_s[head] = masked_keys(k_ref[...], head, limit_ref[0])
        q_s[head] = masked_queries(q_ref[...], head)
    factor = SCORE_SCALE * LOG2E
    spans = [slice(at, at + KEYS) for at in range(0, length, KEYS)]
    outs = []
    for head in range(2):
        feats = slice(head * HEAD_DIM, (head + 1) * HEAD_DIM)
        peak = None
        for span in spans:
            scores = mul(keys_s[head, span], q_s[head], NT)
            sc_s[head, span] = scores
            high = jnp.max(scores, axis=0, keepdims=True)
            peak = high if peak is None else jnp.maximum(peak, high)
        peak = peak * factor
        total = jnp.zeros_like(peak)
        gathered = jnp.zeros((HEAD_DIM, length), F32)
        for span in spans:
            expo = jnp.exp2(sc_s[head, span] * factor - peak)
            total += jnp.sum(expo, axis=0, keepdims=True)
            gathered += mul(vt_s[feats, span], expo.astype(BF16))
        outs.append(gathered / total)
        lse_ref[0, head : head + 1, :] = peak + jnp.log2(total)
    both = jnp.concatenate(outs, axis=0)
    turn_ref[...] = both.astype(BF16)
    ctx_ref[...] = both.T.astype(BF16)


def attend(limit, mixed, pairs):
    length = mixed.shape[0]
    column = lambda c: pl.BlockSpec((length, PAIR), lambda i, s: (0, i * 3 + c))
    return pl.pallas_call(
        attend_kernel,
        grid_spec=pltpu.PrefetchScalarGridSpec(
            num_scalar_prefetch=1,
            grid=(pairs,),
            in_specs=[column(0), column(1), column(2)],
            out_specs=[
                pl.BlockSpec((length, PAIR), lambda i, s: (0, i)),
                pl.BlockSpec((PAIR, length), lambda i, s: (i, 0)),
                pl.BlockSpec((1, 2, length), lambda i, s: (i, 0, 0)),
            ],
            scratch_shapes=[
                pltpu.VMEM((2, length, PAIR), BF16),
                pltpu.VMEM((2, length, PAIR), BF16),
                pltpu.VMEM((PAIR, length), BF16),
                pltpu.VMEM((2, length, length), F32),
            ],
        ),
        out_shape=[
            pltpu.HBM((length, pairs * PAIR), BF16),
            pltpu.HBM((pairs * PAIR, length), BF16),
            jax.ShapeDtypeStruct((pairs, 2, length), F32),
        ],
        compiler_params=params(28),
        cost_estimate=cost(15),
        name="attend",
    )(limit, mixed, mixed, mixed)


def gelu_both(values):
    root = math.sqrt(2.0 / math.pi)
    scaled = root * values
    inner = scaled * (1.0 + 0.044715 * (values * values))
    tanh = jnp.tanh(inner)
    half = 0.5 + 0.5 * tanh
    slope = half + (1.0 - tanh * tanh) * (1.5 * inner - scaled)
    return values * half, slope


def middle_kernel(
    groups, limit_ref, place_ref, x_ref, clock_ref, gain_ref, ctx_ref, og_ref, *refs
):
    weight_refs, refs = refs[:-18], refs[-18:]
    out_ref, cg_ref, mg_ref, gg_ref, up_send, down_send, up_keep, down_keep = refs[:8]
    wide, ups, downs, active_s, ug_s, n_turn, fg_turn, ag_turn, ctx_s, sems = refs[8:]
    step = pl.program_id(0)
    parts = ctx_s.shape[0]
    hidden = active_s.shape[1] // parts
    blocks = pl.num_programs(0) - parts
    each = len(weight_refs) // parts

    def fetch(part, kind):
        target, width, first = ((wide, PAIR, 0), (ups, hidden, PAIR), (downs, hidden, PAIR + hidden))[kind]
        own = slice(first, first + width)
        columns = slice(part * width, (part + 1) * width)
        copies = []
        for at, w_ref in enumerate(weight_refs[part * each : (part + 1) * each]):
            count = 1 if groups is None else groups // each
            rows = w_ref.shape[0] // count
            for group in range(count):
                index = at * count + group
                spot = pl.ds(0, rows)
                if groups is not None:
                    spot = pl.ds(pl.multiple_of(place_ref[index] * rows, rows), rows)
                copies.append(
                    pltpu.make_async_copy(
                        w_ref.at[pl.ds(group * rows, rows), own],
                        target.at[spot, columns],
                        sems.at[kind, part, index],
                    )
                )
        return copies

    @pl.when(step == 0)
    def _():
        gg_ref[...] = jnp.zeros_like(gg_ref)
        for part in range(parts):
            for copy in fetch(part, 0) + fetch(part, 1) + fetch(part, 2):
                copy.start()
        for part in range(parts):
            for copy in fetch(part, 0) + fetch(part, 1) + fetch(part, 2):
                copy.wait()

    dead = (step < blocks) & (step * ROWS >= limit_ref[0])

    @pl.when((step < blocks) & jnp.logical_not(dead))
    def _():
        spot = pl.ds(pl.multiple_of(step * ROWS, ROWS), ROWS)
        gain = gain_ref[...]
        live = step * ROWS + lax.broadcasted_iota(jnp.int32, (ROWS, 1), 0) < limit_ref[0]
        begin = join_tokens(x_ref) + clock_ref[...]
        middle = begin + mul(ctx_ref[...], wide[...], NT)
        unit, inverse = norm_parts(middle)
        normed = (unit * gain).astype(BF16)
        n_turn[:, spot] = normed.T
        res_grad = jnp.where(live, og_ref[0].astype(F32), 0.0)
        feed_grad = res_grad.astype(BF16)
        fg_turn[:, spot] = feed_grad.T
        feed = jnp.zeros_like(middle)
        two_grad = jnp.zeros_like(middle)
        for at in range(0, parts * hidden, UNITS):
            some = slice(at, at + UNITS)
            active, slope = gelu_both(mul(normed, ups[:, some]))
            active = active.astype(BF16)
            active_s[spot, some] = active
            feed += mul(active, downs[:, some], NT)
            upper_grad = (mul(feed_grad, downs[:, some]) * slope).astype(BF16)
            ug_s[spot, some] = upper_grad
            two_grad += mul(upper_grad, ups[:, some], NT)
        out_ref[0] = jnp.where(live, middle + feed, 0.0).astype(BF16)
        gg_ref[...] += jnp.sum(two_grad * unit, axis=0, keepdims=True)
        middle_grad = res_grad + norm_back(two_grad, gain, unit, inverse)
        mg_ref[...] = middle_grad
        att_grad = middle_grad.astype(BF16)
        ag_turn[:, spot] = att_grad.T
        cg_ref[...] = mul(att_grad, wide[...]).astype(BF16)
        for part in range(parts):
            ctx_s[part, spot] = ctx_ref[:, part * PAIR : (part + 1) * PAIR]

    @pl.when(dead)
    def _():
        spot = pl.ds(pl.multiple_of(step * ROWS, ROWS), ROWS)
        for ref in (out_ref, cg_ref, mg_ref):
            ref[...] = jnp.zeros_like(ref)
        for ref in (active_s, ug_s):
            ref[spot] = jnp.zeros((ROWS, ref.shape[1]), BF16)
        ctx_s[:, spot] = jnp.zeros((parts, ROWS, PAIR), BF16)
        for ref in (n_turn, fg_turn, ag_turn):
            ref[:, spot] = jnp.zeros((ref.shape[0], ROWS), BF16)

    @pl.when(step >= blocks)
    def _():
        turn = step - blocks
        part = jnp.where(turn < 2, 3 - 2 * turn, 6 - 2 * turn)
        own = pl.ds(pl.multiple_of(part * hidden, hidden), hidden)
        grads = (
            mul(ag_turn[...], ctx_s[part]).astype(BF16),
            mul(n_turn[...], ug_s[:, own]).astype(BF16),
            mul(fg_turn[...], active_s[:, own]).astype(BF16),
        )

        def into(up_ref, down_ref):
            up_ref[0, :, 0:PAIR], up_ref[0, :, PAIR:], down_ref[0] = grads

        pl.when(turn < 2)(lambda: into(up_send, down_send))
        pl.when(turn >= 2)(lambda: into(up_keep, down_keep))


def middle_block(limit, place, groups, x_blocks, clock, gain, ctx, w_parts, out_grad):
    senders, feature_parts, tall, width = x_blocks.shape
    tokens = tall - SPARE
    length = senders * tokens
    features = feature_parts * width
    parts = len(w_parts)
    weights = [in_hbm(w) for part in w_parts for w in part]
    columns = weights[0].shape[1]
    hidden = (columns - PAIR) // 2
    take = ROWS // tokens
    blocks = length // ROWS
    row = lambda i: jnp.minimum(i, blocks - 1)
    whole = lambda array: pl.BlockSpec(
        array.shape, lambda i, *s: (0,) * array.ndim, pipeline_mode=pl.Buffered(1)
    )
    rows = lambda n: pl.BlockSpec((ROWS, n), lambda i, *s: (row(i), 0))
    one = pl.BlockSpec((1, ROWS, features), lambda i, *s: (0, row(i), 0))
    grads = lambda first, n: pl.BlockSpec(
        (1, features, n), lambda i, *s: (jnp.clip(i - blocks - first, 0, 1), 0, 0)
    )
    up_shape = pltpu.HBM((2, features, PAIR + hidden), BF16)
    down_shape = pltpu.HBM((2, features, hidden), BF16)
    return pl.pallas_call(
        functools.partial(middle_kernel, groups),
        grid_spec=pltpu.PrefetchScalarGridSpec(
            num_scalar_prefetch=2,
            grid=(blocks + parts,),
            in_specs=[
                pl.BlockSpec(
                    (take, feature_parts, tall, width), lambda i, *s: (row(i), 0, 0, 0)
                ),
                whole(clock),
                whole(gain),
                rows(features),
                one,
            ]
            + [pl.BlockSpec(memory_space=pltpu.HBM)] * len(weights),
            out_specs=[
                one, rows(features), rows(features),
                pl.BlockSpec((1, features), lambda i, *s: (0, 0)),
                grads(0, PAIR + hidden), grads(0, hidden), grads(2, PAIR + hidden), grads(2, hidden),
            ],
            scratch_shapes=[
                pltpu.VMEM((features, parts * PAIR), BF16),
                pltpu.VMEM((features, parts * hidden), BF16),
                pltpu.VMEM((features, parts * hidden), BF16),
                pltpu.VMEM((length, parts * hidden), BF16),
                pltpu.VMEM((length, parts * hidden), BF16),
                pltpu.VMEM((features, length), BF16),
                pltpu.VMEM((features, length), BF16),
                pltpu.VMEM((features, length), BF16),
                pltpu.VMEM((parts, length, PAIR), BF16),
                pltpu.SemaphoreType.DMA((3, parts, groups or 1)),
            ],
        ),
        out_shape=[
            jax.ShapeDtypeStruct((1, length, features), BF16),
            pltpu.HBM((length, features), BF16),
            pltpu.HBM((length, features), F32),
            jax.ShapeDtypeStruct((1, features), F32),
            up_shape, down_shape, up_shape, down_shape,
        ],
        compiler_params=params(48),
        cost_estimate=cost(25),
        name="middle",
    )(limit, place, x_blocks, clock, gain, in_hbm(ctx), in_hbm(out_grad), *weights)


def attend_back_kernel(
    limit_ref, q_ref, k_ref, v_ref, turn_ref, lse_ref, cg_ref, n_turn_ref,
    dm_ref, first_ref, second_ref, keys_s, q_s, qz_s, do_s, kt_s, delta_s,
):
    limit = limit_ref[0]
    length = q_ref.shape[0]
    kt_s[...] = k_ref[...].astype(F32).T.astype(BF16)
    along = cg_ref[...].astype(F32).T * turn_ref[...].astype(F32)
    for head in range(2):
        feats = slice(head * HEAD_DIM, (head + 1) * HEAD_DIM)
        delta_s[head : head + 1, :] = jnp.sum(along[feats, :], axis=0, keepdims=True)
        keys_s[head] = masked_keys(k_ref[...], head, limit)
        q_s[head] = masked_queries(q_ref[...], head)
        qz_s[head] = own_lanes(q_ref[...], head)
        do_s[head] = own_lanes(cg_ref[...], head)
    factor = SCORE_SCALE * LOG2E
    turned = [jnp.zeros((HEAD_DIM, length), F32)] * 2
    for at in range(0, length, BACK_KEYS):
        span = slice(at, at + BACK_KEYS)
        key_grad = jnp.zeros((BACK_KEYS, PAIR), F32)
        value_grad = jnp.zeros((BACK_KEYS, PAIR), F32)
        for head in range(2):
            feats = slice(head * HEAD_DIM, (head + 1) * HEAD_DIM)
            scores = mul(keys_s[head, span], q_s[head], NT)
            prob = jnp.exp2(scores * factor - lse_ref[0, head : head + 1, :])
            prob_grad = mul(v_ref[span, :], do_s[head], NT)
            score_grad = (prob * (prob_grad - delta_s[head : head + 1, :])).astype(BF16)
            value_grad += mul(prob.astype(BF16), do_s[head])
            key_grad += mul(score_grad, qz_s[head])
            turned[head] += mul(kt_s[feats, span], score_grad)
        dm_ref[span, PAIR : 2 * PAIR] = (key_grad * SCORE_SCALE).astype(BF16)
        dm_ref[span, 2 * PAIR : 3 * PAIR] = value_grad.astype(BF16)
    query_grad = jnp.concatenate(turned, axis=0) * SCORE_SCALE
    dm_ref[:, 0:PAIR] = query_grad.T.astype(BF16)
    grad = mul(n_turn_ref[...], dm_ref[...]).astype(BF16)

    @pl.when(pl.program_id(0) == 0)
    def _():
        first_ref[...] = grad

    @pl.when(pl.program_id(0) == 1)
    def _():
        second_ref[...] = grad


def attend_back(limit, mixed, ctx_turn, lse, context_grad, n_turn, first):
    length = mixed.shape[0]
    features = n_turn.shape[0]
    pair = lambda i: first - i
    column = lambda c: pl.BlockSpec((length, PAIR), lambda i, s: (0, pair(i) * 3 + c))
    return pl.pallas_call(
        attend_back_kernel,
        grid_spec=pltpu.PrefetchScalarGridSpec(
            num_scalar_prefetch=1,
            grid=(2,),
            in_specs=[
                column(0), column(1), column(2),
                pl.BlockSpec((PAIR, length), lambda i, s: (pair(i), 0)),
                pl.BlockSpec((1, 2, length), lambda i, s: (pair(i), 0, 0)),
                pl.BlockSpec((length, PAIR), lambda i, s: (0, pair(i))),
                pl.BlockSpec((features, length), lambda i, s: (0, 0)),
            ],
            out_specs=[
                pl.BlockSpec((length, 3 * PAIR), lambda i, s: (0, i)),
                pl.BlockSpec((features, 3 * PAIR), lambda i, s: (0, 0)),
                pl.BlockSpec((features, 3 * PAIR), lambda i, s: (0, 0)),
            ],
            scratch_shapes=[
                pltpu.VMEM((2, length, PAIR), BF16),
                pltpu.VMEM((2, length, PAIR), BF16),
                pltpu.VMEM((2, length, PAIR), BF16),
                pltpu.VMEM((2, length, PAIR), BF16),
                pltpu.VMEM((PAIR, length), BF16),
                pltpu.VMEM((8, length), F32),
            ],
        ),
        out_shape=[
            jax.ShapeDtypeStruct((length, 2 * 3 * PAIR), BF16),
            jax.ShapeDtypeStruct((features, 3 * PAIR), BF16),
            jax.ShapeDtypeStruct((features, 3 * PAIR), BF16),
        ],
        compiler_params=params(28),
        cost_estimate=cost(16),
        name="attend_back",
    )(limit, mixed, mixed, mixed, ctx_turn, lse, context_grad, n_turn)


def begin_kernel(
    limit_ref, x_ref, clock_ref, gain_ref, gg_two_ref, mg_ref, w_ref, high_ref, low_ref, bg_ref, gg_s
):
    step = pl.program_id(0)
    _, parts, tall, width = bg_ref.shape
    tokens = tall - SPARE
    blocks = ROWS // tokens
    spot = pl.ds(step * blocks, blocks)

    @pl.when(step == 0)
    def _():
        gg_s[...] = jnp.zeros_like(gg_s)

    @pl.when(step * ROWS < limit_ref[0])
    def _():
        begin = join_tokens(x_ref) + clock_ref[...]
        unit, inverse = norm_parts(begin)
        one_grad = jnp.zeros_like(begin)
        for part, (d_ref, at) in enumerate(((low_ref, 1), (low_ref, 0), (high_ref, 1), (high_ref, 0))):
            columns = slice(part * 3 * PAIR, (part + 1) * 3 * PAIR)
            own = slice(at * 3 * PAIR, (at + 1) * 3 * PAIR)
            one_grad += mul(d_ref[:, own], w_ref[:, columns], NT)
        gg_s[...] += jnp.sum(one_grad * unit, axis=0, keepdims=True)
        total = (mg_ref[...] + norm_back(one_grad, gain_ref[...], unit, inverse)).astype(BF16)
        for part in range(parts):
            piece = total[:, part * width : (part + 1) * width]
            bg_ref[spot, part, 0:tokens] = piece.reshape(blocks, tokens, width)

    @pl.when(step * ROWS >= limit_ref[0])
    def _():
        bg_ref[spot] = jnp.zeros((blocks,) + bg_ref.shape[1:], BF16)

    @pl.when(step == pl.num_programs(0) - 1)
    def _():
        rows = []
        for ref in (gg_s, gg_two_ref):
            for part in range(parts):
                rows.append(ref[:, part * width : (part + 1) * width])
        bg_ref[:, :, tokens:tall] = jnp.broadcast_to(
            jnp.concatenate(rows, axis=0).astype(BF16), bg_ref.shape[:2] + (SPARE, width)
        )


def begin_block(limit, x_blocks, clock, gain, two_grad, w_wide, middle_grad, high, low):
    senders, feature_parts, tall, width = x_blocks.shape
    tokens = tall - SPARE
    length = senders * tokens
    features = feature_parts * width
    take = ROWS // tokens
    whole = lambda array: pl.BlockSpec(array.shape, lambda i, s: (0,) * array.ndim)
    rows = lambda n: pl.BlockSpec((ROWS, n), lambda i, s: (i, 0))
    return pl.pallas_call(
        begin_kernel,
        grid_spec=pltpu.PrefetchScalarGridSpec(
            num_scalar_prefetch=1,
            grid=(length // ROWS,),
            in_specs=[
                pl.BlockSpec((take, feature_parts, tall, width), lambda i, s: (i, 0, 0, 0)),
                whole(clock), whole(gain), whole(two_grad), rows(features), whole(w_wide),
            ]
            + [rows(6 * PAIR)] * 2,
            out_specs=whole(x_blocks),
            scratch_shapes=[pltpu.VMEM((1, features), F32)],
        ),
        out_shape=jax.ShapeDtypeStruct(x_blocks.shape, BF16),
        compiler_params=params(20),
        cost_estimate=cost(7),
        name="begin_back",
    )(limit, x_blocks, clock, gain, two_grad, middle_grad, w_wide, high, low)


DIRECT = 8


def clock_rows(step_ids, features):
    half_width = features // 2
    ladder = jnp.arange(half_width, dtype=F32) / half_width
    rate_rows = jnp.exp(-math.log(10000.0) * ladder)
    angles = step_ids.astype(F32)[:, None] * rate_rows[None, :]
    return jnp.concatenate([jnp.sin(angles), jnp.cos(angles)], axis=-1)


def swap(value, apart):
    count = lax.axis_size("tensor")
    return lax.ppermute(value, "tensor", [(i, i ^ apart) for i in range(count)])


def along_dp(value, move):
    count = lax.axis_size("dp")
    return lax.ppermute(value, "dp", [(i, move(i)) for i in range(count)])


def across(value):
    return ahead(value, 0, 1)


def ahead(value, step, flip=0):
    count = lax.axis_size("dp") // 2
    return along_dp(value, lambda i: (i // 2 + step) % count * 2 + (i + flip) % 2)


def places():
    count = lax.axis_size("dp") // 2
    own = lax.axis_index("dp")
    coarse = (own // 2 - jnp.arange(count, dtype=jnp.int32)) % count
    return jnp.concatenate([coarse * 2 + own % 2, coarse * 2 + 1 - own % 2])


def collect_coarse(shard):
    count = lax.axis_size("dp") // 2
    return [shard] + [ahead(shard, step) for step in range(1, count)]


def collect_rows(shard):
    count = lax.axis_size("dp")
    rows = lax.all_to_all(
        jnp.broadcast_to(shard[None], (count,) + shard.shape), "dp", 0, 0, tiled=True
    )
    return rows.reshape(count * shard.shape[0], shard.shape[1])


def collect_columns(rows):
    far = swap(rows, 2)
    return rows, swap(rows, 1), far, swap(far, 1)


def add(*values):
    return add_wide(*values).astype(BF16)


def fold_pair(values):
    own = lax.axis_index("dp") % 2
    pick = lambda value, which: lax.dynamic_index_in_dim(value, which, value.ndim - 3, keepdims=False)
    sent = add(*[pick(value, 1 - own) for value in values])
    return sent, lambda: [pick(value, own) for value in values] + [across(sent)]


def fold_far(values):
    sent = add(*[value[0] for value in values])
    return sent, lambda: [value[1] for value in values] + [swap(sent, 2)]


def fold_coarse(values):
    count = lax.axis_size("dp") // 2
    own = lax.axis_index("dp") // 2
    pick = lambda value, which: lax.dynamic_index_in_dim(value, which % count, 0, keepdims=False)
    value = add(*values)
    came = [ahead(pick(value, own + step), step) for step in range(1, count)]
    return value, [pick(value, own)] + came


def add_wide(*values):
    total = values[0].astype(F32)
    for value in values[1:]:
        total += value.astype(F32)
    return total


def grouped(value):
    count = lax.axis_size("dp")
    two, rows, columns = value.shape
    return value.reshape(two, count // 2, 2, rows // count, columns)


def exchange_rows(value):
    count = lax.axis_size("dp")
    groups = value.reshape(count, value.shape[0] // count, value.shape[1])
    return jnp.sum(lax.all_to_all(groups, "dp", 0, 0, tiled=True).astype(F32), axis=0)


def three_terms(values):
    terms = []
    for _ in range(3):
        term = lax.reduce_precision(values, 8, 7)
        terms.append(term.astype(BF16))
        values = values - term
    return terms


def together(*values):
    return lax.optimization_barrier(values)


def after(value, *others):
    return lax.optimization_barrier((value,) + others)[0]


def on_device(
    states, timesteps, lengths, deal_order, w_qkv, w_out, w_up, w_down, gain_attn, gain_ffn, out_grad
):
    both = ("dp", "tensor")
    dp_count = lax.axis_size("dp")
    tensor_count = lax.axis_size("tensor")
    devices = dp_count * tensor_count
    total_seqs, tokens, width = states.shape
    assert tensor_count == 4 and total_seqs == devices
    features = width * tensor_count
    own = lax.axis_index("dp") * tensor_count + lax.axis_index("tensor")
    per = gain_attn.shape[0]
    rows = w_qkv.shape[0]
    hidden = w_up.shape[1]

    rest = jnp.concatenate([w_out.T, w_up, w_down.T], axis=1)
    qkv = w_qkv.reshape(rows, -1)
    direct = dp_count <= DIRECT
    if direct:
        place, groups = places(), dp_count
        wide = qkv.shape[1]
        pieces = collect_coarse(jnp.concatenate([qkv, across(qkv)], axis=1))
        qkv_rows = jnp.concatenate(
            [piece[:, :wide] for piece in pieces] + [piece[:, wide:] for piece in pieces], axis=0
        )
        mine = jnp.concatenate(collect_coarse(rest), axis=0)
        far_rows, other, far_mine = together(
            swap(qkv_rows, 2), in_hbm(across(mine)), in_hbm(swap(mine, 2))
        )
        qkv_parts = (qkv_rows, swap(qkv_rows, 1), far_rows, swap(far_rows, 1))
    else:
        place, groups = jnp.zeros((1,), jnp.int32), None
        qkv_parts = collect_columns(collect_rows(qkv))
        rest_parts = [(part,) for part in collect_columns(collect_rows(rest))]

    deal_later = after(deal_order, pieces[1]) if direct else deal_order
    own_id = lax.dynamic_slice_in_dim(deal_later, own, 1)
    limit = lengths[own_id]
    clock = clock_rows(timesteps[own_id], features)
    spare = jnp.stack(three_terms(gain_attn) + three_terms(gain_ffn)).reshape(1, 6 * per)
    spare = jnp.pad(spare, ((0, SPARE - 1), (0, width - 6 * per)))
    arranged = jnp.concatenate(
        [states[deal_order], jnp.broadcast_to(spare[None], (devices, SPARE, width))], axis=1
    )
    x_blocks = lax.all_to_all(arranged, both, 0, 0, tiled=True)
    gains = jnp.sum(x_blocks[:, tokens, : 6 * per].reshape(devices, 2, 3, per).astype(F32), axis=2)
    gain_one = gains[:, 0].reshape(1, features)
    gain_two = gains[:, 1].reshape(1, features)
    x_blocks = x_blocks.reshape(dp_count, tensor_count, tokens + SPARE, width)

    mixed, n_one_turn, qkv_wide = project(
        limit, place, groups, x_blocks, clock, gain_one, qkv_parts
    )
    if direct:
        near_mine, near_other = in_hbm(swap(mine, 1)), in_hbm(swap(other, 1))
        last_mine, far_other = in_hbm(swap(far_mine, 1)), in_hbm(swap(other, 2))
    ctx, ctx_turn, lse = attend(limit, mixed, tensor_count)
    if direct:
        ctx, near_mine, near_other, last_mine, far_other = together(
            ctx, near_mine, near_other, last_mine, far_other
        )
        last_other = swap(far_other, 1)
        rest_parts = (
            (mine, other), (near_mine, near_other), (far_mine, far_other), (last_mine, last_other)
        )
    output, context_grad, middle_grad, two_grad, up_send, down_send, up_keep, down_keep = middle_block(
        limit, place, groups, x_blocks, clock, gain_two, ctx, rest_parts, out_grad
    )
    up_came, down_came = swap(up_send, 1), swap(down_send, 1)

    back = functools.partial(attend_back, limit, mixed, ctx_turn, lse)
    if direct:
        down_sent, down_rest = fold_far([grouped(value) for value in (down_keep, down_came)])
        up_sent, up_rest = fold_pair([grouped(value) for value in (up_keep, up_came)])
        context_grad = after(context_grad, down_sent, up_sent)
    high, three, two = back(in_hbm(context_grad), n_one_turn, 3)
    if direct:
        *down_rest, down_came = down_rest()
        *up_rest, up_came = up_rest()
        high, three, two, down_came, up_came = together(high, three, two, down_came, up_came)
        down_value, down_pieces = fold_coarse([*down_rest, down_came])
        up_sent, up_rest = fold_far([add(*up_rest, up_came)])
        context_grad = after(context_grad, down_value, up_sent)
    far = add(two, swap(three, 1))
    came_far = swap(far, 2)
    low, one, own_part = back(after(context_grad, high, far), n_one_turn, 1)
    if direct:
        *up_rest, up_came = up_rest()
        low, one, own_part, up_came, came_far, *down_pieces = together(
            low, one, own_part, up_came, came_far, *down_pieces
        )
        up_value, up_pieces = fold_coarse([*up_rest, up_came])
        down_sent, down_rest = fold_pair([add_wide(*down_pieces)[..., None, :, :, :]])
        middle_grad = after(middle_grad, up_value, down_sent)
    came_one = swap(one, 1)
    begin_grad = begin_block(
        limit, x_blocks, clock, gain_one, two_grad, qkv_wide, middle_grad, high, low
    )
    if direct:
        begin_grad, came_one, up_pieces[1], up_pieces[2] = together(
            begin_grad, came_one, up_pieces[1], up_pieces[2]
        )
        near = [grouped(value[None])[0] for value in (own_part, came_one, came_far)]
        qkv_value, qkv_pieces = fold_coarse(fold_pair(near)[1]())
        down_total = add_wide(*down_rest())[0]
        pieces = together(*up_pieces, *qkv_pieces)
        up_total = add_wide(*pieces[: len(up_pieces)])
        qkv_total = add_wide(*pieces[len(up_pieces) :])
    else:
        up_total = exchange_rows(add(*fold_far([up_keep, up_came])[1]()))
        down_total = exchange_rows(add(*fold_far([down_keep, down_came])[1]()))
        qkv_total = exchange_rows(add(own_part, came_one, came_far))
    returned = lax.all_to_all(
        begin_grad.reshape(devices, tokens + SPARE, width), both, 0, 0, tiled=True
    )
    inverse = (
        jnp.zeros((total_seqs,), jnp.int32)
        .at[deal_order]
        .set(jnp.arange(total_seqs, dtype=jnp.int32))
    )
    states_grad = returned[inverse][:, :tokens]
    gain_grads = jnp.sum(returned[:, tokens:].astype(F32), axis=0).reshape(2, devices, per)
    gain_grads = lax.dynamic_index_in_dim(gain_grads, own, 1, keepdims=False)
    return (
        output,
        states_grad,
        qkv_total.reshape(w_qkv.shape),
        up_total[:, :PAIR].T,
        up_total[:, PAIR:],
        down_total.T,
        gain_grads[0],
        gain_grads[1],
    )


def solution(mesh):
    in_specs = (
        P(None, "dp", "tensor"),
        P(),
        P(),
        P(),
        P("dp", None, "tensor"),
        P("tensor", "dp"),
        P("dp", "tensor"),
        P("tensor", "dp"),
        P(("dp", "tensor")),
        P(("dp", "tensor")),
        P(("dp", "tensor"), None, None),
    )
    out_specs = (
        P(("dp", "tensor"), None, None),
        P(None, "dp", "tensor"),
        P("dp", None, "tensor"),
        P("tensor", "dp"),
        P("dp", "tensor"),
        P("tensor", "dp"),
        P(("dp", "tensor")),
        P(("dp", "tensor")),
    )
    return jax.shard_map(
        on_device, mesh=mesh, in_specs=in_specs, out_specs=out_specs, check_vma=False
    )
```

```python
import functools
import math

import jax
import jax.numpy as jnp
from jax import lax
from jax.experimental import pallas as pl
from jax.experimental.pallas import tpu as pltpu
from jax.sharding import PartitionSpec as P

HEAD_DIM = 64
PAIR = 2 * HEAD_DIM
ROWS = 512
KEYS = 256
BACK_KEYS = 512
SPARE = 8
UNITS = 2048
SCORE_SCALE = 1.0 / math.sqrt(HEAD_DIM)
LOG2E = math.log2(math.e)
F32 = jnp.float32
BF16 = jnp.bfloat16
NN = (((1,), (0,)), ((), ()))
NT = (((1,), (1,)), ((), ()))
MIB = 1024 * 1024


def mul(lhs, rhs, dims=NN):
    return lax.dot_general(lhs, rhs, dims, preferred_element_type=F32)


def join_tokens(ref):
    blocks, parts, tall, width = ref.shape
    tokens = tall - SPARE
    return jnp.concatenate(
        [ref[:, part, 0:tokens].reshape(blocks * tokens, width) for part in range(parts)], axis=-1
    ).astype(F32)


def place_rows(groups, place_ref, first, source, targets):
    if groups is None:
        for target, columns, own in targets:
            target[:, columns] = source[:, own]
        return
    rows = source.shape[0] // groups
    for group in range(groups):
        spot = pl.ds(pl.multiple_of(place_ref[first + group] * rows, rows), rows)
        for target, columns, own in targets:
            target[spot, columns] = source[group * rows : (group + 1) * rows, own]


def norm_parts(values):
    center = values - jnp.mean(values, axis=-1, keepdims=True)
    spread = jnp.mean(center * center, axis=-1, keepdims=True)
    inverse = lax.rsqrt(spread + 1e-05)
    return center * inverse, inverse


def norm_back(grad, gain, unit, inverse):
    scaled = grad * gain
    mean_scaled = jnp.mean(scaled, axis=-1, keepdims=True)
    mean_along = jnp.mean(scaled * unit, axis=-1, keepdims=True)
    return inverse * (scaled - mean_scaled - unit * mean_along)


def in_hbm(value):
    return pltpu.with_memory_space_constraint(value, pltpu.HBM)


def cost(microseconds):
    return pl.CostEstimate(
        flops=int(microseconds * 1.15e9), bytes_accessed=1 << 20, transcendentals=0
    )


def params(mebibytes):
    return pltpu.CompilerParams(vmem_limit_bytes=mebibytes * MIB)


def project_kernel(groups, limit_ref, place_ref, x_ref, clock_ref, gain_ref, *refs):
    w_refs, (mixed_ref, n_turn_ref, wide) = refs[:-3], refs[-3:]
    step = pl.program_id(0)

    @pl.when(step == 0)
    def _():
        for part, w_ref in enumerate(w_refs):
            width = w_ref.shape[1]
            columns = slice(part * width, (part + 1) * width)
            place_rows(groups, place_ref, 0, w_ref, [(wide, columns, slice(0, width))])

    @pl.when(step * ROWS < limit_ref[0])
    def _():
        begin = join_tokens(x_ref) + clock_ref[...]
        unit, _ = norm_parts(begin)
        normed = (unit * gain_ref[...]).astype(BF16)
        n_turn_ref[...] = normed.T
        mixed_ref[...] = mul(normed, wide[...]).astype(BF16)

    @pl.when(step * ROWS >= limit_ref[0])
    def _():
        n_turn_ref[...] = jnp.zeros_like(n_turn_ref)
        mixed_ref[...] = jnp.zeros_like(mixed_ref)


def project(limit, place, groups, x_blocks, clock, gain, w_parts):
    senders, feature_parts, tall, width = x_blocks.shape
    tokens = tall - SPARE
    length = senders * tokens
    features = feature_parts * width
    parts, columns = len(w_parts), w_parts[0].shape[1]
    take = ROWS // tokens
    return pl.pallas_call(
        functools.partial(project_kernel, groups),
        grid_spec=pltpu.PrefetchScalarGridSpec(
            num_scalar_prefetch=2,
            grid=(length // ROWS,),
            in_specs=[
                pl.BlockSpec((take, feature_parts, tall, width), lambda i, *s: (i, 0, 0, 0)),
                pl.BlockSpec((1, features), lambda i, *s: (0, 0)),
                pl.BlockSpec((1, features), lambda i, *s: (0, 0)),
            ]
            + [pl.BlockSpec((features, columns), lambda i, *s: (0, 0))] * parts,
            out_specs=[
                pl.BlockSpec((ROWS, parts * columns), lambda i, *s: (i, 0)),
                pl.BlockSpec((features, ROWS), lambda i, *s: (0, i)),
                pl.BlockSpec((features, parts * columns), lambda i, *s: (0, 0)),
            ],
        ),
        out_shape=[
            jax.ShapeDtypeStruct((length, parts * columns), BF16),
            pltpu.HBM((features, length), BF16),
            pltpu.HBM((features, parts * columns), BF16),
        ],
        compiler_params=params(20),
        cost_estimate=cost(5),
        name="project",
    )(limit, place, x_blocks, clock, gain, *w_parts)


def head_lanes(shape, head):
    lane = lax.broadcasted_iota(jnp.int32, shape, 1)
    return (lane >= head * HEAD_DIM) & (lane < (head + 1) * HEAD_DIM)


def spare_lane(shape, head):
    lane = lax.broadcasted_iota(jnp.int32, shape, 1)
    return lane == (1 - head) * HEAD_DIM


def masked_keys(keys, head, limit):
    row = lax.broadcasted_iota(jnp.int32, keys.shape, 0)
    spare = jnp.where(
        spare_lane(keys.shape, head) & (row >= limit), jnp.asarray(-1e30, F32), jnp.asarray(0.0, F32)
    )
    return jnp.where(head_lanes(keys.shape, head), keys.astype(F32), spare).astype(BF16)


def own_lanes(values, head):
    return jnp.where(head_lanes(values.shape, head), values.astype(F32), 0.0).astype(BF16)


def masked_queries(queries, head):
    spare = jnp.where(spare_lane(queries.shape, head), jnp.asarray(1.0, F32), jnp.asarray(0.0, F32))
    return jnp.where(head_lanes(queries.shape, head), queries.astype(F32), spare).astype(BF16)


def attend_kernel(limit_ref, q_ref, k_ref, v_ref, ctx_ref, turn_ref, lse_ref, keys_s, q_s, vt_s, sc_s):
    length = q_ref.shape[0]
    vt_s[...] = v_ref[...].astype(F32).T.astype(BF16)
    for head in range(2):
        keys_s[head] = masked_keys(k_ref[...], head, limit_ref[0])
        q_s[head] = masked_queries(q_ref[...], head)
    factor = SCORE_SCALE * LOG2E
    spans = [slice(at, at + KEYS) for at in range(0, length, KEYS)]
    outs = []
    for head in range(2):
        feats = slice(head * HEAD_DIM, (head + 1) * HEAD_DIM)
        peak = None
        for span in spans:
            scores = mul(keys_s[head, span], q_s[head], NT)
            sc_s[head, span] = scores
            high = jnp.max(scores, axis=0, keepdims=True)
            peak = high if peak is None else jnp.maximum(peak, high)
        peak = peak * factor
        total = jnp.zeros_like(peak)
        gathered = jnp.zeros((HEAD_DIM, length), F32)
        for span in spans:
            expo = jnp.exp2(sc_s[head, span] * factor - peak)
            total += jnp.sum(expo, axis=0, keepdims=True)
            gathered += mul(vt_s[feats, span], expo.astype(BF16))
        outs.append(gathered / total)
        lse_ref[0, head : head + 1, :] = peak + jnp.log2(total)
    both = jnp.concatenate(outs, axis=0)
    turn_ref[...] = both.astype(BF16)
    ctx_ref[...] = both.T.astype(BF16)


def attend(limit, mixed, pairs):
    length = mixed.shape[0]
    column = lambda c: pl.BlockSpec((length, PAIR), lambda i, s: (0, i * 3 + c))
    return pl.pallas_call(
        attend_kernel,
        grid_spec=pltpu.PrefetchScalarGridSpec(
            num_scalar_prefetch=1,
            grid=(pairs,),
            in_specs=[column(0), column(1), column(2)],
            out_specs=[
                pl.BlockSpec((length, PAIR), lambda i, s: (0, i)),
                pl.BlockSpec((PAIR, length), lambda i, s: (i, 0)),
                pl.BlockSpec((1, 2, length), lambda i, s: (i, 0, 0)),
            ],
            scratch_shapes=[
                pltpu.VMEM((2, length, PAIR), BF16),
                pltpu.VMEM((2, length, PAIR), BF16),
                pltpu.VMEM((PAIR, length), BF16),
                pltpu.VMEM((2, length, length), F32),
            ],
        ),
        out_shape=[
            pltpu.HBM((length, pairs * PAIR), BF16),
            pltpu.HBM((pairs * PAIR, length), BF16),
            jax.ShapeDtypeStruct((pairs, 2, length), F32),
        ],
        compiler_params=params(28),
        cost_estimate=cost(15),
        name="attend",
    )(limit, mixed, mixed, mixed)


def gelu_both(values):
    root = math.sqrt(2.0 / math.pi)
    scaled = root * values
    inner = scaled * (1.0 + 0.044715 * (values * values))
    tanh = jnp.tanh(inner)
    half = 0.5 + 0.5 * tanh
    slope = half + (1.0 - tanh * tanh) * (1.5 * inner - scaled)
    return values * half, slope


def middle_kernel(
    groups, limit_ref, place_ref, x_ref, clock_ref, gain_ref, ctx_ref, og_ref, *refs
):
    weight_refs, refs = refs[:-18], refs[-18:]
    out_ref, cg_ref, mg_ref, gg_ref, up_send, down_send, up_keep, down_keep = refs[:8]
    wide, ups, downs, active_s, ug_s, n_turn, fg_turn, ag_turn, ctx_s, sems = refs[8:]
    step = pl.program_id(0)
    parts = ctx_s.shape[0]
    hidden = active_s.shape[1] // parts
    blocks = pl.num_programs(0) - parts
    each = len(weight_refs) // parts

    def fetch(part, kind):
        target, width, first = ((wide, PAIR, 0), (ups, hidden, PAIR), (downs, hidden, PAIR + hidden))[kind]
        own = slice(first, first + width)
        columns = slice(part * width, (part + 1) * width)
        copies = []
        for at, w_ref in enumerate(weight_refs[part * each : (part + 1) * each]):
            count = 1 if groups is None else groups // each
            rows = w_ref.shape[0] // count
            for group in range(count):
                index = at * count + group
                spot = pl.ds(0, rows)
                if groups is not None:
                    spot = pl.ds(pl.multiple_of(place_ref[index] * rows, rows), rows)
                copies.append(
                    pltpu.make_async_copy(
                        w_ref.at[pl.ds(group * rows, rows), own],
                        target.at[spot, columns],
                        sems.at[kind, part, index],
                    )
                )
        return copies

    @pl.when(step == 0)
    def _():
        gg_ref[...] = jnp.zeros_like(gg_ref)
        for part in range(parts):
            for copy in fetch(part, 0) + fetch(part, 1) + fetch(part, 2):
                copy.start()
        for part in range(parts):
            for copy in fetch(part, 0) + fetch(part, 1) + fetch(part, 2):
                copy.wait()

    dead = (step < blocks) & (step * ROWS >= limit_ref[0])

    @pl.when((step < blocks) & jnp.logical_not(dead))
    def _():
        spot = pl.ds(pl.multiple_of(step * ROWS, ROWS), ROWS)
        gain = gain_ref[...]
        live = step * ROWS + lax.broadcasted_iota(jnp.int32, (ROWS, 1), 0) < limit_ref[0]
        begin = join_tokens(x_ref) + clock_ref[...]
        middle = begin + mul(ctx_ref[...], wide[...], NT)
        unit, inverse = norm_parts(middle)
        normed = (unit * gain).astype(BF16)
        n_turn[:, spot] = normed.T
        res_grad = jnp.where(live, og_ref[0].astype(F32), 0.0)
        feed_grad = res_grad.astype(BF16)
        fg_turn[:, spot] = feed_grad.T
        feed = jnp.zeros_like(middle)
        two_grad = jnp.zeros_like(middle)
        for at in range(0, parts * hidden, UNITS):
            some = slice(at, at + UNITS)
            active, slope = gelu_both(mul(normed, ups[:, some]))
            active = active.astype(BF16)
            active_s[spot, some] = active
            feed += mul(active, downs[:, some], NT)
            upper_grad = (mul(feed_grad, downs[:, some]) * slope).astype(BF16)
            ug_s[spot, some] = upper_grad
            two_grad += mul(upper_grad, ups[:, some], NT)
        out_ref[0] = jnp.where(live, middle + feed, 0.0).astype(BF16)
        gg_ref[...] += jnp.sum(two_grad * unit, axis=0, keepdims=True)
        middle_grad = res_grad + norm_back(two_grad, gain, unit, inverse)
        mg_ref[...] = middle_grad
        att_grad = middle_grad.astype(BF16)
        ag_turn[:, spot] = att_grad.T
        cg_ref[...] = mul(att_grad, wide[...]).astype(BF16)
        for part in range(parts):
            ctx_s[part, spot] = ctx_ref[:, part * PAIR : (part + 1) * PAIR]

    @pl.when(dead)
    def _():
        spot = pl.ds(pl.multiple_of(step * ROWS, ROWS), ROWS)
        for ref in (out_ref, cg_ref, mg_ref):
            ref[...] = jnp.zeros_like(ref)
        for ref in (active_s, ug_s):
            ref[spot] = jnp.zeros((ROWS, ref.shape[1]), BF16)
        ctx_s[:, spot] = jnp.zeros((parts, ROWS, PAIR), BF16)
        for ref in (n_turn, fg_turn, ag_turn):
            ref[:, spot] = jnp.zeros((ref.shape[0], ROWS), BF16)

    @pl.when(step >= blocks)
    def _():
        turn = step - blocks
        part = jnp.where(turn < 2, 3 - 2 * turn, 6 - 2 * turn)
        own = pl.ds(pl.multiple_of(part * hidden, hidden), hidden)
        grads = (
            mul(ag_turn[...], ctx_s[part]).astype(BF16),
            mul(n_turn[...], ug_s[:, own]).astype(BF16),
            mul(fg_turn[...], active_s[:, own]).astype(BF16),
        )

        def into(up_ref, down_ref):
            up_ref[0, :, 0:PAIR], up_ref[0, :, PAIR:], down_ref[0] = grads

        pl.when(turn < 2)(lambda: into(up_send, down_send))
        pl.when(turn >= 2)(lambda: into(up_keep, down_keep))


def middle_block(limit, place, groups, x_blocks, clock, gain, ctx, w_parts, out_grad):
    senders, feature_parts, tall, width = x_blocks.shape
    tokens = tall - SPARE
    length = senders * tokens
    features = feature_parts * width
    parts = len(w_parts)
    weights = [in_hbm(w) for part in w_parts for w in part]
    columns = weights[0].shape[1]
    hidden = (columns - PAIR) // 2
    take = ROWS // tokens
    blocks = length // ROWS
    row = lambda i: jnp.minimum(i, blocks - 1)
    whole = lambda array: pl.BlockSpec(
        array.shape, lambda i, *s: (0,) * array.ndim, pipeline_mode=pl.Buffered(1)
    )
    rows = lambda n: pl.BlockSpec((ROWS, n), lambda i, *s: (row(i), 0))
    one = pl.BlockSpec((1, ROWS, features), lambda i, *s: (0, row(i), 0))
    grads = lambda first, n: pl.BlockSpec(
        (1, features, n), lambda i, *s: (jnp.clip(i - blocks - first, 0, 1), 0, 0)
    )
    up_shape = pltpu.HBM((2, features, PAIR + hidden), BF16)
    down_shape = pltpu.HBM((2, features, hidden), BF16)
    return pl.pallas_call(
        functools.partial(middle_kernel, groups),
        grid_spec=pltpu.PrefetchScalarGridSpec(
            num_scalar_prefetch=2,
            grid=(blocks + parts,),
            in_specs=[
                pl.BlockSpec(
                    (take, feature_parts, tall, width), lambda i, *s: (row(i), 0, 0, 0)
                ),
                whole(clock),
                whole(gain),
                rows(features),
                one,
            ]
            + [pl.BlockSpec(memory_space=pltpu.HBM)] * len(weights),
            out_specs=[
                one, rows(features), rows(features),
                pl.BlockSpec((1, features), lambda i, *s: (0, 0)),
                grads(0, PAIR + hidden), grads(0, hidden), grads(2, PAIR + hidden), grads(2, hidden),
            ],
            scratch_shapes=[
                pltpu.VMEM((features, parts * PAIR), BF16),
                pltpu.VMEM((features, parts * hidden), BF16),
                pltpu.VMEM((features, parts * hidden), BF16),
                pltpu.VMEM((length, parts * hidden), BF16),
                pltpu.VMEM((length, parts * hidden), BF16),
                pltpu.VMEM((features, length), BF16),
                pltpu.VMEM((features, length), BF16),
                pltpu.VMEM((features, length), BF16),
                pltpu.VMEM((parts, length, PAIR), BF16),
                pltpu.SemaphoreType.DMA((3, parts, groups or 1)),
            ],
        ),
        out_shape=[
            jax.ShapeDtypeStruct((1, length, features), BF16),
            pltpu.HBM((length, features), BF16),
            pltpu.HBM((length, features), F32),
            jax.ShapeDtypeStruct((1, features), F32),
            up_shape, down_shape, up_shape, down_shape,
        ],
        compiler_params=params(48),
        cost_estimate=cost(25),
        name="middle",
    )(limit, place, x_blocks, clock, gain, in_hbm(ctx), in_hbm(out_grad), *weights)


def attend_back_kernel(
    limit_ref, q_ref, k_ref, v_ref, turn_ref, lse_ref, cg_ref, n_turn_ref,
    dm_ref, first_ref, second_ref, keys_s, q_s, qz_s, do_s, kt_s, delta_s,
):
    limit = limit_ref[0]
    length = q_ref.shape[0]
    kt_s[...] = k_ref[...].astype(F32).T.astype(BF16)
    along = cg_ref[...].astype(F32).T * turn_ref[...].astype(F32)
    for head in range(2):
        feats = slice(head * HEAD_DIM, (head + 1) * HEAD_DIM)
        delta_s[head : head + 1, :] = jnp.sum(along[feats, :], axis=0, keepdims=True)
        keys_s[head] = masked_keys(k_ref[...], head, limit)
        q_s[head] = masked_queries(q_ref[...], head)
        qz_s[head] = own_lanes(q_ref[...], head)
        do_s[head] = own_lanes(cg_ref[...], head)
    factor = SCORE_SCALE * LOG2E
    turned = [jnp.zeros((HEAD_DIM, length), F32)] * 2
    for at in range(0, length, BACK_KEYS):
        span = slice(at, at + BACK_KEYS)
        key_grad = jnp.zeros((BACK_KEYS, PAIR), F32)
        value_grad = jnp.zeros((BACK_KEYS, PAIR), F32)
        for head in range(2):
            feats = slice(head * HEAD_DIM, (head + 1) * HEAD_DIM)
            scores = mul(keys_s[head, span], q_s[head], NT)
            prob = jnp.exp2(scores * factor - lse_ref[0, head : head + 1, :])
            prob_grad = mul(v_ref[span, :], do_s[head], NT)
            score_grad = (prob * (prob_grad - delta_s[head : head + 1, :])).astype(BF16)
            value_grad += mul(prob.astype(BF16), do_s[head])
            key_grad += mul(score_grad, qz_s[head])
            turned[head] += mul(kt_s[feats, span], score_grad)
        dm_ref[span, PAIR : 2 * PAIR] = (key_grad * SCORE_SCALE).astype(BF16)
        dm_ref[span, 2 * PAIR : 3 * PAIR] = value_grad.astype(BF16)
    query_grad = jnp.concatenate(turned, axis=0) * SCORE_SCALE
    dm_ref[:, 0:PAIR] = query_grad.T.astype(BF16)
    grad = mul(n_turn_ref[...], dm_ref[...]).astype(BF16)

    @pl.when(pl.program_id(0) == 0)
    def _():
        first_ref[...] = grad

    @pl.when(pl.program_id(0) == 1)
    def _():
        second_ref[...] = grad


def attend_back(limit, mixed, ctx_turn, lse, context_grad, n_turn, first):
    length = mixed.shape[0]
    features = n_turn.shape[0]
    pair = lambda i: first - i
    column = lambda c: pl.BlockSpec((length, PAIR), lambda i, s: (0, pair(i) * 3 + c))
    return pl.pallas_call(
        attend_back_kernel,
        grid_spec=pltpu.PrefetchScalarGridSpec(
            num_scalar_prefetch=1,
            grid=(2,),
            in_specs=[
                column(0), column(1), column(2),
                pl.BlockSpec((PAIR, length), lambda i, s: (pair(i), 0)),
                pl.BlockSpec((1, 2, length), lambda i, s: (pair(i), 0, 0)),
                pl.BlockSpec((length, PAIR), lambda i, s: (0, pair(i))),
                pl.BlockSpec((features, length), lambda i, s: (0, 0)),
            ],
            out_specs=[
                pl.BlockSpec((length, 3 * PAIR), lambda i, s: (0, i)),
                pl.BlockSpec((features, 3 * PAIR), lambda i, s: (0, 0)),
                pl.BlockSpec((features, 3 * PAIR), lambda i, s: (0, 0)),
            ],
            scratch_shapes=[
                pltpu.VMEM((2, length, PAIR), BF16),
                pltpu.VMEM((2, length, PAIR), BF16),
                pltpu.VMEM((2, length, PAIR), BF16),
                pltpu.VMEM((2, length, PAIR), BF16),
                pltpu.VMEM((PAIR, length), BF16),
                pltpu.VMEM((8, length), F32),
            ],
        ),
        out_shape=[
            jax.ShapeDtypeStruct((length, 2 * 3 * PAIR), BF16),
            jax.ShapeDtypeStruct((features, 3 * PAIR), BF16),
            jax.ShapeDtypeStruct((features, 3 * PAIR), BF16),
        ],
        compiler_params=params(28),
        cost_estimate=cost(16),
        name="attend_back",
    )(limit, mixed, mixed, mixed, ctx_turn, lse, context_grad, n_turn)


def begin_kernel(
    limit_ref, x_ref, clock_ref, gain_ref, gg_two_ref, mg_ref, w_ref, high_ref, low_ref, bg_ref, gg_s
):
    step = pl.program_id(0)
    _, parts, tall, width = bg_ref.shape
    tokens = tall - SPARE
    blocks = ROWS // tokens
    spot = pl.ds(step * blocks, blocks)

    @pl.when(step == 0)
    def _():
        gg_s[...] = jnp.zeros_like(gg_s)

    @pl.when(step * ROWS < limit_ref[0])
    def _():
        begin = join_tokens(x_ref) + clock_ref[...]
        unit, inverse = norm_parts(begin)
        one_grad = jnp.zeros_like(begin)
        for part, (d_ref, at) in enumerate(((low_ref, 1), (low_ref, 0), (high_ref, 1), (high_ref, 0))):
            columns = slice(part * 3 * PAIR, (part + 1) * 3 * PAIR)
            own = slice(at * 3 * PAIR, (at + 1) * 3 * PAIR)
            one_grad += mul(d_ref[:, own], w_ref[:, columns], NT)
        gg_s[...] += jnp.sum(one_grad * unit, axis=0, keepdims=True)
        total = (mg_ref[...] + norm_back(one_grad, gain_ref[...], unit, inverse)).astype(BF16)
        for part in range(parts):
            piece = total[:, part * width : (part + 1) * width]
            bg_ref[spot, part, 0:tokens] = piece.reshape(blocks, tokens, width)

    @pl.when(step * ROWS >= limit_ref[0])
    def _():
        bg_ref[spot] = jnp.zeros((blocks,) + bg_ref.shape[1:], BF16)

    @pl.when(step == pl.num_programs(0) - 1)
    def _():
        rows = []
        for ref in (gg_s, gg_two_ref):
            for part in range(parts):
                rows.append(ref[:, part * width : (part + 1) * width])
        bg_ref[:, :, tokens:tall] = jnp.broadcast_to(
            jnp.concatenate(rows, axis=0).astype(BF16), bg_ref.shape[:2] + (SPARE, width)
        )


def begin_block(limit, x_blocks, clock, gain, two_grad, w_wide, middle_grad, high, low):
    senders, feature_parts, tall, width = x_blocks.shape
    tokens = tall - SPARE
    length = senders * tokens
    features = feature_parts * width
    take = ROWS // tokens
    whole = lambda array: pl.BlockSpec(array.shape, lambda i, s: (0,) * array.ndim)
    rows = lambda n: pl.BlockSpec((ROWS, n), lambda i, s: (i, 0))
    return pl.pallas_call(
        begin_kernel,
        grid_spec=pltpu.PrefetchScalarGridSpec(
            num_scalar_prefetch=1,
            grid=(length // ROWS,),
            in_specs=[
                pl.BlockSpec((take, feature_parts, tall, width), lambda i, s: (i, 0, 0, 0)),
                whole(clock), whole(gain), whole(two_grad), rows(features), whole(w_wide),
            ]
            + [rows(6 * PAIR)] * 2,
            out_specs=whole(x_blocks),
            scratch_shapes=[pltpu.VMEM((1, features), F32)],
        ),
        out_shape=jax.ShapeDtypeStruct(x_blocks.shape, BF16),
        compiler_params=params(20),
        cost_estimate=cost(7),
        name="begin_back",
    )(limit, x_blocks, clock, gain, two_grad, middle_grad, w_wide, high, low)


DIRECT = 8


def clock_rows(step_ids, features):
    half_width = features // 2
    ladder = jnp.arange(half_width, dtype=F32) / half_width
    rate_rows = jnp.exp(-math.log(10000.0) * ladder)
    angles = step_ids.astype(F32)[:, None] * rate_rows[None, :]
    return jnp.concatenate([jnp.sin(angles), jnp.cos(angles)], axis=-1)


def swap(value, apart):
    count = lax.axis_size("tensor")
    return lax.ppermute(value, "tensor", [(i, i ^ apart) for i in range(count)])


def along_dp(value, move):
    count = lax.axis_size("dp")
    return lax.ppermute(value, "dp", [(i, move(i)) for i in range(count)])


def across(value):
    return ahead(value, 0, 1)


def ahead(value, step, flip=0):
    count = lax.axis_size("dp") // 2
    return along_dp(value, lambda i: (i // 2 + step) % count * 2 + (i + flip) % 2)


def places():
    count = lax.axis_size("dp") // 2
    own = lax.axis_index("dp")
    coarse = (own // 2 - jnp.arange(count, dtype=jnp.int32)) % count
    return jnp.concatenate([coarse * 2 + own % 2, coarse * 2 + 1 - own % 2])


def collect_coarse(shard):
    count = lax.axis_size("dp") // 2
    return [shard] + [ahead(shard, step) for step in range(1, count)]


def collect_rows(shard):
    count = lax.axis_size("dp")
    rows = lax.all_to_all(
        jnp.broadcast_to(shard[None], (count,) + shard.shape), "dp", 0, 0, tiled=True
    )
    return rows.reshape(count * shard.shape[0], shard.shape[1])


def collect_columns(rows):
    far = swap(rows, 2)
    return rows, swap(rows, 1), far, swap(far, 1)


def add(*values):
    return add_wide(*values).astype(BF16)


def fold_pair(values):
    own = lax.axis_index("dp") % 2
    pick = lambda value, which: lax.dynamic_index_in_dim(value, which, value.ndim - 3, keepdims=False)
    sent = add(*[pick(value, 1 - own) for value in values])
    return sent, lambda: [pick(value, own) for value in values] + [across(sent)]


def fold_far(values):
    sent = add(*[value[0] for value in values])
    return sent, lambda: [value[1] for value in values] + [swap(sent, 2)]


def fold_coarse(values):
    count = lax.axis_size("dp") // 2
    own = lax.axis_index("dp") // 2
    pick = lambda value, which: lax.dynamic_index_in_dim(value, which % count, 0, keepdims=False)
    value = add(*values)
    came = [ahead(pick(value, own + step), step) for step in range(1, count)]
    return value, [pick(value, own)] + came


def add_wide(*values):
    total = values[0].astype(F32)
    for value in values[1:]:
        total += value.astype(F32)
    return total


def grouped(value):
    count = lax.axis_size("dp")
    two, rows, columns = value.shape
    return value.reshape(two, count // 2, 2, rows // count, columns)


def exchange_rows(value):
    count = lax.axis_size("dp")
    groups = value.reshape(count, value.shape[0] // count, value.shape[1])
    return jnp.sum(lax.all_to_all(groups, "dp", 0, 0, tiled=True).astype(F32), axis=0)


def three_terms(values):
    terms = []
    for _ in range(3):
        term = lax.reduce_precision(values, 8, 7)
        terms.append(term.astype(BF16))
        values = values - term
    return terms


def together(*values):
    return lax.optimization_barrier(values)


def after(value, *others):
    return lax.optimization_barrier((value,) + others)[0]


def on_device(
    states, timesteps, lengths, deal_order, w_qkv, w_out, w_up, w_down, gain_attn, gain_ffn, out_grad
):
    both = ("dp", "tensor")
    dp_count = lax.axis_size("dp")
    tensor_count = lax.axis_size("tensor")
    devices = dp_count * tensor_count
    total_seqs, tokens, width = states.shape
    assert tensor_count == 4 and total_seqs == devices
    features = width * tensor_count
    own = lax.axis_index("dp") * tensor_count + lax.axis_index("tensor")
    per = gain_attn.shape[0]
    rows = w_qkv.shape[0]
    hidden = w_up.shape[1]

    rest = jnp.concatenate([w_out.T, w_up, w_down.T], axis=1)
    qkv = w_qkv.reshape(rows, -1)
    direct = dp_count <= DIRECT
    if direct:
        place, groups = places(), dp_count
        wide = qkv.shape[1]
        pieces = collect_coarse(jnp.concatenate([qkv, across(qkv)], axis=1))
        qkv_rows = jnp.concatenate(
            [piece[:, :wide] for piece in pieces] + [piece[:, wide:] for piece in pieces], axis=0
        )
        mine = jnp.concatenate(collect_coarse(rest), axis=0)
        far_rows, other, far_mine = together(
            swap(qkv_rows, 2), in_hbm(across(mine)), in_hbm(swap(mine, 2))
        )
        qkv_parts = (qkv_rows, swap(qkv_rows, 1), far_rows, swap(far_rows, 1))
    else:
        place, groups = jnp.zeros((1,), jnp.int32), None
        qkv_parts = collect_columns(collect_rows(qkv))
        rest_parts = [(part,) for part in collect_columns(collect_rows(rest))]

    deal_later = after(deal_order, pieces[1]) if direct else deal_order
    own_id = lax.dynamic_slice_in_dim(deal_later, own, 1)
    limit = lengths[own_id]
    clock = clock_rows(timesteps[own_id], features)
    spare = jnp.stack(three_terms(gain_attn) + three_terms(gain_ffn)).reshape(1, 6 * per)
    spare = jnp.pad(spare, ((0, SPARE - 1), (0, width - 6 * per)))
    arranged = jnp.concatenate(
        [states[deal_order], jnp.broadcast_to(spare[None], (devices, SPARE, width))], axis=1
    )
    x_blocks = lax.all_to_all(arranged, both, 0, 0, tiled=True)
    gains = jnp.sum(x_blocks[:, tokens, : 6 * per].reshape(devices, 2, 3, per).astype(F32), axis=2)
    gain_one = gains[:, 0].reshape(1, features)
    gain_two = gains[:, 1].reshape(1, features)
    x_blocks = x_blocks.reshape(dp_count, tensor_count, tokens + SPARE, width)

    mixed, n_one_turn, qkv_wide = project(
        limit, place, groups, x_blocks, clock, gain_one, qkv_parts
    )
    if direct:
        near_mine, near_other = in_hbm(swap(mine, 1)), in_hbm(swap(other, 1))
        last_mine, far_other = in_hbm(swap(far_mine, 1)), in_hbm(swap(other, 2))
    ctx, ctx_turn, lse = attend(limit, mixed, tensor_count)
    if direct:
        ctx, near_mine, near_other, last_mine, far_other = together(
            ctx, near_mine, near_other, last_mine, far_other
        )
        last_other = swap(far_other, 1)
        rest_parts = (
            (mine, other), (near_mine, near_other), (far_mine, far_other), (last_mine, last_other)
        )
    output, context_grad, middle_grad, two_grad, up_send, down_send, up_keep, down_keep = middle_block(
        limit, place, groups, x_blocks, clock, gain_two, ctx, rest_parts, out_grad
    )
    up_came, down_came = swap(up_send, 1), swap(down_send, 1)

    back = functools.partial(attend_back, limit, mixed, ctx_turn, lse)
    if direct:
        down_sent, down_rest = fold_far([grouped(value) for value in (down_keep, down_came)])
        up_sent, up_rest = fold_pair([grouped(value) for value in (up_keep, up_came)])
        context_grad = after(context_grad, down_sent, up_sent)
    high, three, two = back(in_hbm(context_grad), n_one_turn, 3)
    if direct:
        *down_rest, down_came = down_rest()
        *up_rest, up_came = up_rest()
        high, three, two, down_came, up_came = together(high, three, two, down_came, up_came)
        down_value, down_pieces = fold_coarse([*down_rest, down_came])
        up_sent, up_rest = fold_far([add(*up_rest, up_came)])
        context_grad = after(context_grad, down_value, up_sent)
    far = add(two, swap(three, 1))
    came_far = swap(far, 2)
    low, one, own_part = back(after(context_grad, high, far), n_one_turn, 1)
    if direct:
        *up_rest, up_came = up_rest()
        low, one, own_part, up_came, came_far, *down_pieces = together(
            low, one, own_part, up_came, came_far, *down_pieces
        )
        up_value, up_pieces = fold_coarse([*up_rest, up_came])
        down_sent, down_rest = fold_pair([add_wide(*down_pieces)[..., None, :, :, :]])
        middle_grad = after(middle_grad, up_value, down_sent)
    came_one = swap(one, 1)
    begin_grad = begin_block(
        limit, x_blocks, clock, gain_one, two_grad, qkv_wide, middle_grad, high, low
    )
    if direct:
        begin_grad, came_one, up_pieces[2] = together(begin_grad, came_one, up_pieces[2])
        near = [grouped(value[None])[0] for value in (own_part, came_one, came_far)]
        qkv_value, qkv_pieces = fold_coarse(fold_pair(near)[1]())
        down_total = add_wide(*down_rest())[0]
        *up_pieces, qkv_pieces[1] = together(*up_pieces, qkv_pieces[1])
        up_total = add_wide(*up_pieces)
    else:
        up_total = exchange_rows(add(*fold_far([up_keep, up_came])[1]()))
        down_total = exchange_rows(add(*fold_far([down_keep, down_came])[1]()))
        qkv_total = exchange_rows(add(own_part, came_one, came_far))
    returned = lax.all_to_all(
        begin_grad.reshape(devices, tokens + SPARE, width), both, 0, 0, tiled=True
    )
    inverse = (
        jnp.zeros((total_seqs,), jnp.int32)
        .at[deal_order]
        .set(jnp.arange(total_seqs, dtype=jnp.int32))
    )
    states_grad = returned[inverse][:, :tokens]
    if direct:
        *qkv_pieces, states_grad = together(*qkv_pieces, states_grad)
        qkv_total = add_wide(*qkv_pieces)
    gain_grads = jnp.sum(returned[:, tokens:].astype(F32), axis=0).reshape(2, devices, per)
    gain_grads = lax.dynamic_index_in_dim(gain_grads, own, 1, keepdims=False)
    return (
        output,
        states_grad,
        qkv_total.reshape(w_qkv.shape),
        up_total[:, :PAIR].T,
        up_total[:, PAIR:],
        down_total.T,
        gain_grads[0],
        gain_grads[1],
    )


def solution(mesh):
    in_specs = (
        P(None, "dp", "tensor"),
        P(),
        P(),
        P(),
        P("dp", None, "tensor"),
        P("tensor", "dp"),
        P("dp", "tensor"),
        P("tensor", "dp"),
        P(("dp", "tensor")),
        P(("dp", "tensor")),
        P(("dp", "tensor"), None, None),
    )
    out_specs = (
        P(("dp", "tensor"), None, None),
        P(None, "dp", "tensor"),
        P("dp", None, "tensor"),
        P("tensor", "dp"),
        P("dp", "tensor"),
        P("tensor", "dp"),
        P(("dp", "tensor")),
        P(("dp", "tensor")),
    )
    return jax.shard_map(
        on_device, mesh=mesh, in_specs=in_specs, out_specs=out_specs, check_vma=False
    )
```

```python
import functools
import math

import jax
import jax.numpy as jnp
from jax import lax
from jax.experimental import pallas as pl
from jax.experimental.pallas import tpu as pltpu
from jax.sharding import PartitionSpec as P

HEAD_DIM = 64
PAIR = 2 * HEAD_DIM
ROWS = 512
KEYS = 256
BACK_KEYS = 512
SPARE = 8
UNITS = 2048
SCORE_SCALE = 1.0 / math.sqrt(HEAD_DIM)
LOG2E = math.log2(math.e)
F32 = jnp.float32
BF16 = jnp.bfloat16
NN = (((1,), (0,)), ((), ()))
NT = (((1,), (1,)), ((), ()))
MIB = 1024 * 1024


def mul(lhs, rhs, dims=NN):
    return lax.dot_general(lhs, rhs, dims, preferred_element_type=F32)


def join_tokens(ref):
    blocks, parts, tall, width = ref.shape
    tokens = tall - SPARE
    return jnp.concatenate(
        [ref[:, part, 0:tokens].reshape(blocks * tokens, width) for part in range(parts)], axis=-1
    ).astype(F32)


def place_rows(groups, place_ref, first, source, targets):
    if groups is None:
        for target, columns, own in targets:
            target[:, columns] = source[:, own]
        return
    rows = source.shape[0] // groups
    for group in range(groups):
        spot = pl.ds(pl.multiple_of(place_ref[first + group] * rows, rows), rows)
        for target, columns, own in targets:
            target[spot, columns] = source[group * rows : (group + 1) * rows, own]


def norm_parts(values):
    center = values - jnp.mean(values, axis=-1, keepdims=True)
    spread = jnp.mean(center * center, axis=-1, keepdims=True)
    inverse = lax.rsqrt(spread + 1e-05)
    return center * inverse, inverse


def norm_back(grad, gain, unit, inverse):
    scaled = grad * gain
    mean_scaled = jnp.mean(scaled, axis=-1, keepdims=True)
    mean_along = jnp.mean(scaled * unit, axis=-1, keepdims=True)
    return inverse * (scaled - mean_scaled - unit * mean_along)


def in_hbm(value):
    return pltpu.with_memory_space_constraint(value, pltpu.HBM)


def cost(microseconds):
    return pl.CostEstimate(
        flops=int(microseconds * 1.15e9), bytes_accessed=1 << 20, transcendentals=0
    )


def params(mebibytes):
    return pltpu.CompilerParams(vmem_limit_bytes=mebibytes * MIB)


def project_kernel(groups, limit_ref, place_ref, x_ref, clock_ref, gain_ref, *refs):
    w_refs, (mixed_ref, n_turn_ref, wide) = refs[:-3], refs[-3:]
    step = pl.program_id(0)

    @pl.when(step == 0)
    def _():
        for part, w_ref in enumerate(w_refs):
            width = w_ref.shape[1]
            columns = slice(part * width, (part + 1) * width)
            place_rows(groups, place_ref, 0, w_ref, [(wide, columns, slice(0, width))])

    @pl.when(step * ROWS < limit_ref[0])
    def _():
        begin = join_tokens(x_ref) + clock_ref[...]
        unit, _ = norm_parts(begin)
        normed = (unit * gain_ref[...]).astype(BF16)
        n_turn_ref[...] = normed.T
        mixed_ref[...] = mul(normed, wide[...]).astype(BF16)

    @pl.when(step * ROWS >= limit_ref[0])
    def _():
        n_turn_ref[...] = jnp.zeros_like(n_turn_ref)
        mixed_ref[...] = jnp.zeros_like(mixed_ref)


def project(limit, place, groups, x_blocks, clock, gain, w_parts):
    senders, feature_parts, tall, width = x_blocks.shape
    tokens = tall - SPARE
    length = senders * tokens
    features = feature_parts * width
    parts, columns = len(w_parts), w_parts[0].shape[1]
    take = ROWS // tokens
    return pl.pallas_call(
        functools.partial(project_kernel, groups),
        grid_spec=pltpu.PrefetchScalarGridSpec(
            num_scalar_prefetch=2,
            grid=(length // ROWS,),
            in_specs=[
                pl.BlockSpec((take, feature_parts, tall, width), lambda i, *s: (i, 0, 0, 0)),
                pl.BlockSpec((1, features), lambda i, *s: (0, 0)),
                pl.BlockSpec((1, features), lambda i, *s: (0, 0)),
            ]
            + [pl.BlockSpec((features, columns), lambda i, *s: (0, 0))] * parts,
            out_specs=[
                pl.BlockSpec((ROWS, parts * columns), lambda i, *s: (i, 0)),
                pl.BlockSpec((features, ROWS), lambda i, *s: (0, i)),
                pl.BlockSpec((features, parts * columns), lambda i, *s: (0, 0)),
            ],
        ),
        out_shape=[
            jax.ShapeDtypeStruct((length, parts * columns), BF16),
            pltpu.HBM((features, length), BF16),
            pltpu.HBM((features, parts * columns), BF16),
        ],
        compiler_params=params(20),
        cost_estimate=cost(5),
        name="project",
    )(limit, place, x_blocks, clock, gain, *w_parts)


def head_lanes(shape, head):
    lane = lax.broadcasted_iota(jnp.int32, shape, 1)
    return (lane >= head * HEAD_DIM) & (lane < (head + 1) * HEAD_DIM)


def spare_lane(shape, head):
    lane = lax.broadcasted_iota(jnp.int32, shape, 1)
    return lane == (1 - head) * HEAD_DIM


def masked_keys(keys, head, limit):
    row = lax.broadcasted_iota(jnp.int32, keys.shape, 0)
    spare = jnp.where(
        spare_lane(keys.shape, head) & (row >= limit), jnp.asarray(-1e30, F32), jnp.asarray(0.0, F32)
    )
    return jnp.where(head_lanes(keys.shape, head), keys.astype(F32), spare).astype(BF16)


def own_lanes(values, head):
    return jnp.where(head_lanes(values.shape, head), values.astype(F32), 0.0).astype(BF16)


def masked_queries(queries, head):
    spare = jnp.where(spare_lane(queries.shape, head), jnp.asarray(1.0, F32), jnp.asarray(0.0, F32))
    return jnp.where(head_lanes(queries.shape, head), queries.astype(F32), spare).astype(BF16)


def attend_kernel(limit_ref, q_ref, k_ref, v_ref, ctx_ref, turn_ref, lse_ref, keys_s, q_s, vt_s, sc_s):
    length = q_ref.shape[0]
    vt_s[...] = v_ref[...].astype(F32).T.astype(BF16)
    for head in range(2):
        keys_s[head] = masked_keys(k_ref[...], head, limit_ref[0])
        q_s[head] = masked_queries(q_ref[...], head)
    factor = SCORE_SCALE * LOG2E
    spans = [slice(at, at + KEYS) for at in range(0, length, KEYS)]
    outs = []
    for head in range(2):
        feats = slice(head * HEAD_DIM, (head + 1) * HEAD_DIM)
        peak = None
        for span in spans:
            scores = mul(keys_s[head, span], q_s[head], NT)
            sc_s[head, span] = scores
            high = jnp.max(scores, axis=0, keepdims=True)
            peak = high if peak is None else jnp.maximum(peak, high)
        peak = peak * factor
        total = jnp.zeros_like(peak)
        gathered = jnp.zeros((HEAD_DIM, length), F32)
        for span in spans:
            expo = jnp.exp2(sc_s[head, span] * factor - peak)
            total += jnp.sum(expo, axis=0, keepdims=True)
            gathered += mul(vt_s[feats, span], expo.astype(BF16))
        outs.append(gathered / total)
        lse_ref[0, head : head + 1, :] = peak + jnp.log2(total)
    both = jnp.concatenate(outs, axis=0)
    turn_ref[...] = both.astype(BF16)
    ctx_ref[...] = both.T.astype(BF16)


def attend(limit, mixed, pairs):
    length = mixed.shape[0]
    column = lambda c: pl.BlockSpec((length, PAIR), lambda i, s: (0, i * 3 + c))
    return pl.pallas_call(
        attend_kernel,
        grid_spec=pltpu.PrefetchScalarGridSpec(
            num_scalar_prefetch=1,
            grid=(pairs,),
            in_specs=[column(0), column(1), column(2)],
            out_specs=[
                pl.BlockSpec((length, PAIR), lambda i, s: (0, i)),
                pl.BlockSpec((PAIR, length), lambda i, s: (i, 0)),
                pl.BlockSpec((1, 2, length), lambda i, s: (i, 0, 0)),
            ],
            scratch_shapes=[
                pltpu.VMEM((2, length, PAIR), BF16),
                pltpu.VMEM((2, length, PAIR), BF16),
                pltpu.VMEM((PAIR, length), BF16),
                pltpu.VMEM((2, length, length), F32),
            ],
        ),
        out_shape=[
            pltpu.HBM((length, pairs * PAIR), BF16),
            pltpu.HBM((pairs * PAIR, length), BF16),
            jax.ShapeDtypeStruct((pairs, 2, length), F32),
        ],
        compiler_params=params(28),
        cost_estimate=cost(15),
        name="attend",
    )(limit, mixed, mixed, mixed)


def gelu_both(values):
    root = math.sqrt(2.0 / math.pi)
    scaled = root * values
    inner = scaled * (1.0 + 0.044715 * (values * values))
    tanh = jnp.tanh(inner)
    half = 0.5 + 0.5 * tanh
    slope = half + (1.0 - tanh * tanh) * (1.5 * inner - scaled)
    return values * half, slope


def middle_kernel(
    groups, limit_ref, place_ref, x_ref, clock_ref, gain_ref, ctx_ref, og_ref, *refs
):
    weight_refs, refs = refs[:-18], refs[-18:]
    out_ref, cg_ref, mg_ref, gg_ref, up_send, down_send, up_keep, down_keep = refs[:8]
    wide, ups, downs, active_s, ug_s, n_turn, fg_turn, ag_turn, ctx_s, sems = refs[8:]
    step = pl.program_id(0)
    parts = ctx_s.shape[0]
    hidden = active_s.shape[1] // parts
    blocks = pl.num_programs(0) - parts
    each = len(weight_refs) // parts

    def fetch(part, kind):
        target, width, first = ((wide, PAIR, 0), (ups, hidden, PAIR), (downs, hidden, PAIR + hidden))[kind]
        own = slice(first, first + width)
        columns = slice(part * width, (part + 1) * width)
        copies = []
        for at, w_ref in enumerate(weight_refs[part * each : (part + 1) * each]):
            count = 1 if groups is None else groups // each
            rows = w_ref.shape[0] // count
            for group in range(count):
                index = at * count + group
                spot = pl.ds(0, rows)
                if groups is not None:
                    spot = pl.ds(pl.multiple_of(place_ref[index] * rows, rows), rows)
                copies.append(
                    pltpu.make_async_copy(
                        w_ref.at[pl.ds(group * rows, rows), own],
                        target.at[spot, columns],
                        sems.at[kind, part, index],
                    )
                )
        return copies

    @pl.when(step == 0)
    def _():
        gg_ref[...] = jnp.zeros_like(gg_ref)
        for part in range(parts):
            for copy in fetch(part, 0) + fetch(part, 1) + fetch(part, 2):
                copy.start()
        for part in range(parts):
            for copy in fetch(part, 0) + fetch(part, 1) + fetch(part, 2):
                copy.wait()

    dead = (step < blocks) & (step * ROWS >= limit_ref[0])

    @pl.when((step < blocks) & jnp.logical_not(dead))
    def _():
        spot = pl.ds(pl.multiple_of(step * ROWS, ROWS), ROWS)
        gain = gain_ref[...]
        live = step * ROWS + lax.broadcasted_iota(jnp.int32, (ROWS, 1), 0) < limit_ref[0]
        begin = join_tokens(x_ref) + clock_ref[...]
        middle = begin + mul(ctx_ref[...], wide[...], NT)
        unit, inverse = norm_parts(middle)
        normed = (unit * gain).astype(BF16)
        n_turn[:, spot] = normed.T
        res_grad = jnp.where(live, og_ref[0].astype(F32), 0.0)
        feed_grad = res_grad.astype(BF16)
        fg_turn[:, spot] = feed_grad.T
        feed = jnp.zeros_like(middle)
        two_grad = jnp.zeros_like(middle)
        for at in range(0, parts * hidden, UNITS):
            some = slice(at, at + UNITS)
            active, slope = gelu_both(mul(normed, ups[:, some]))
            active = active.astype(BF16)
            active_s[spot, some] = active
            feed += mul(active, downs[:, some], NT)
            upper_grad = (mul(feed_grad, downs[:, some]) * slope).astype(BF16)
            ug_s[spot, some] = upper_grad
            two_grad += mul(upper_grad, ups[:, some], NT)
        out_ref[0] = jnp.where(live, middle + feed, 0.0).astype(BF16)
        gg_ref[...] += jnp.sum(two_grad * unit, axis=0, keepdims=True)
        middle_grad = res_grad + norm_back(two_grad, gain, unit, inverse)
        mg_ref[...] = middle_grad
        att_grad = middle_grad.astype(BF16)
        ag_turn[:, spot] = att_grad.T
        cg_ref[...] = mul(att_grad, wide[...]).astype(BF16)
        for part in range(parts):
            ctx_s[part, spot] = ctx_ref[:, part * PAIR : (part + 1) * PAIR]

    @pl.when(dead)
    def _():
        spot = pl.ds(pl.multiple_of(step * ROWS, ROWS), ROWS)
        for ref in (out_ref, cg_ref, mg_ref):
            ref[...] = jnp.zeros_like(ref)
        for ref in (active_s, ug_s):
            ref[spot] = jnp.zeros((ROWS, ref.shape[1]), BF16)
        ctx_s[:, spot] = jnp.zeros((parts, ROWS, PAIR), BF16)
        for ref in (n_turn, fg_turn, ag_turn):
            ref[:, spot] = jnp.zeros((ref.shape[0], ROWS), BF16)

    @pl.when(step >= blocks)
    def _():
        turn = step - blocks
        part = jnp.where(turn < 2, 3 - 2 * turn, 6 - 2 * turn)
        own = pl.ds(pl.multiple_of(part * hidden, hidden), hidden)
        grads = (
            mul(ag_turn[...], ctx_s[part]).astype(BF16),
            mul(n_turn[...], ug_s[:, own]).astype(BF16),
            mul(fg_turn[...], active_s[:, own]).astype(BF16),
        )

        def into(up_ref, down_ref):
            up_ref[0, :, 0:PAIR], up_ref[0, :, PAIR:], down_ref[0] = grads

        pl.when(turn < 2)(lambda: into(up_send, down_send))
        pl.when(turn >= 2)(lambda: into(up_keep, down_keep))


def middle_block(limit, place, groups, x_blocks, clock, gain, ctx, w_parts, out_grad):
    senders, feature_parts, tall, width = x_blocks.shape
    tokens = tall - SPARE
    length = senders * tokens
    features = feature_parts * width
    parts = len(w_parts)
    weights = [in_hbm(w) for part in w_parts for w in part]
    columns = weights[0].shape[1]
    hidden = (columns - PAIR) // 2
    take = ROWS // tokens
    blocks = length // ROWS
    row = lambda i: jnp.minimum(i, blocks - 1)
    whole = lambda array: pl.BlockSpec(
        array.shape, lambda i, *s: (0,) * array.ndim, pipeline_mode=pl.Buffered(1)
    )
    rows = lambda n: pl.BlockSpec((ROWS, n), lambda i, *s: (row(i), 0))
    one = pl.BlockSpec((1, ROWS, features), lambda i, *s: (0, row(i), 0))
    grads = lambda first, n: pl.BlockSpec(
        (1, features, n), lambda i, *s: (jnp.clip(i - blocks - first, 0, 1), 0, 0)
    )
    up_shape = pltpu.HBM((2, features, PAIR + hidden), BF16)
    down_shape = pltpu.HBM((2, features, hidden), BF16)
    return pl.pallas_call(
        functools.partial(middle_kernel, groups),
        grid_spec=pltpu.PrefetchScalarGridSpec(
            num_scalar_prefetch=2,
            grid=(blocks + parts,),
            in_specs=[
                pl.BlockSpec(
                    (take, feature_parts, tall, width), lambda i, *s: (row(i), 0, 0, 0)
                ),
                whole(clock),
                whole(gain),
                rows(features),
                one,
            ]
            + [pl.BlockSpec(memory_space=pltpu.HBM)] * len(weights),
            out_specs=[
                one, rows(features), rows(features),
                pl.BlockSpec((1, features), lambda i, *s: (0, 0)),
                grads(0, PAIR + hidden), grads(0, hidden), grads(2, PAIR + hidden), grads(2, hidden),
            ],
            scratch_shapes=[
                pltpu.VMEM((features, parts * PAIR), BF16),
                pltpu.VMEM((features, parts * hidden), BF16),
                pltpu.VMEM((features, parts * hidden), BF16),
                pltpu.VMEM((length, parts * hidden), BF16),
                pltpu.VMEM((length, parts * hidden), BF16),
                pltpu.VMEM((features, length), BF16),
                pltpu.VMEM((features, length), BF16),
                pltpu.VMEM((features, length), BF16),
                pltpu.VMEM((parts, length, PAIR), BF16),
                pltpu.SemaphoreType.DMA((3, parts, groups or 1)),
            ],
        ),
        out_shape=[
            jax.ShapeDtypeStruct((1, length, features), BF16),
            pltpu.HBM((length, features), BF16),
            pltpu.HBM((length, features), F32),
            jax.ShapeDtypeStruct((1, features), F32),
            up_shape, down_shape, up_shape, down_shape,
        ],
        compiler_params=params(48),
        cost_estimate=cost(25),
        name="middle",
    )(limit, place, x_blocks, clock, gain, in_hbm(ctx), in_hbm(out_grad), *weights)


def attend_back_kernel(
    limit_ref, q_ref, k_ref, v_ref, turn_ref, lse_ref, cg_ref, n_turn_ref,
    dm_ref, first_ref, second_ref, keys_s, q_s, qz_s, do_s, kt_s, delta_s,
):
    limit = limit_ref[0]
    length = q_ref.shape[0]
    kt_s[...] = k_ref[...].astype(F32).T.astype(BF16)
    along = cg_ref[...].astype(F32).T * turn_ref[...].astype(F32)
    for head in range(2):
        feats = slice(head * HEAD_DIM, (head + 1) * HEAD_DIM)
        delta_s[head : head + 1, :] = jnp.sum(along[feats, :], axis=0, keepdims=True)
        keys_s[head] = masked_keys(k_ref[...], head, limit)
        q_s[head] = masked_queries(q_ref[...], head)
        qz_s[head] = own_lanes(q_ref[...], head)
        do_s[head] = own_lanes(cg_ref[...], head)
    factor = SCORE_SCALE * LOG2E
    turned = [jnp.zeros((HEAD_DIM, length), F32)] * 2
    for at in range(0, length, BACK_KEYS):
        span = slice(at, at + BACK_KEYS)
        key_grad = jnp.zeros((BACK_KEYS, PAIR), F32)
        value_grad = jnp.zeros((BACK_KEYS, PAIR), F32)
        for head in range(2):
            feats = slice(head * HEAD_DIM, (head + 1) * HEAD_DIM)
            scores = mul(keys_s[head, span], q_s[head], NT)
            prob = jnp.exp2(scores * factor - lse_ref[0, head : head + 1, :])
            prob_grad = mul(v_ref[span, :], do_s[head], NT)
            score_grad = (prob * (prob_grad - delta_s[head : head + 1, :])).astype(BF16)
            value_grad += mul(prob.astype(BF16), do_s[head])
            key_grad += mul(score_grad, qz_s[head])
            turned[head] += mul(kt_s[feats, span], score_grad)
        dm_ref[span, PAIR : 2 * PAIR] = (key_grad * SCORE_SCALE).astype(BF16)
        dm_ref[span, 2 * PAIR : 3 * PAIR] = value_grad.astype(BF16)
    query_grad = jnp.concatenate(turned, axis=0) * SCORE_SCALE
    dm_ref[:, 0:PAIR] = query_grad.T.astype(BF16)
    grad = mul(n_turn_ref[...], dm_ref[...]).astype(BF16)

    @pl.when(pl.program_id(0) == 0)
    def _():
        first_ref[...] = grad

    @pl.when(pl.program_id(0) == 1)
    def _():
        second_ref[...] = grad


def attend_back(limit, mixed, ctx_turn, lse, context_grad, n_turn, first):
    length = mixed.shape[0]
    features = n_turn.shape[0]
    pair = lambda i: first - i
    column = lambda c: pl.BlockSpec((length, PAIR), lambda i, s: (0, pair(i) * 3 + c))
    return pl.pallas_call(
        attend_back_kernel,
        grid_spec=pltpu.PrefetchScalarGridSpec(
            num_scalar_prefetch=1,
            grid=(2,),
            in_specs=[
                column(0), column(1), column(2),
                pl.BlockSpec((PAIR, length), lambda i, s: (pair(i), 0)),
                pl.BlockSpec((1, 2, length), lambda i, s: (pair(i), 0, 0)),
                pl.BlockSpec((length, PAIR), lambda i, s: (0, pair(i))),
                pl.BlockSpec((features, length), lambda i, s: (0, 0)),
            ],
            out_specs=[
                pl.BlockSpec((length, 3 * PAIR), lambda i, s: (0, i)),
                pl.BlockSpec((features, 3 * PAIR), lambda i, s: (0, 0)),
                pl.BlockSpec((features, 3 * PAIR), lambda i, s: (0, 0)),
            ],
            scratch_shapes=[
                pltpu.VMEM((2, length, PAIR), BF16),
                pltpu.VMEM((2, length, PAIR), BF16),
                pltpu.VMEM((2, length, PAIR), BF16),
                pltpu.VMEM((2, length, PAIR), BF16),
                pltpu.VMEM((PAIR, length), BF16),
                pltpu.VMEM((8, length), F32),
            ],
        ),
        out_shape=[
            jax.ShapeDtypeStruct((length, 2 * 3 * PAIR), BF16),
            jax.ShapeDtypeStruct((features, 3 * PAIR), BF16),
            jax.ShapeDtypeStruct((features, 3 * PAIR), BF16),
        ],
        compiler_params=params(28),
        cost_estimate=cost(16),
        name="attend_back",
    )(limit, mixed, mixed, mixed, ctx_turn, lse, context_grad, n_turn)


def begin_kernel(
    limit_ref, x_ref, clock_ref, gain_ref, gg_two_ref, mg_ref, w_ref, high_ref, low_ref, bg_ref, gg_s
):
    step = pl.program_id(0)
    _, parts, tall, width = bg_ref.shape
    tokens = tall - SPARE
    blocks = ROWS // tokens
    spot = pl.ds(step * blocks, blocks)

    @pl.when(step == 0)
    def _():
        gg_s[...] = jnp.zeros_like(gg_s)

    @pl.when(step * ROWS < limit_ref[0])
    def _():
        begin = join_tokens(x_ref) + clock_ref[...]
        unit, inverse = norm_parts(begin)
        one_grad = jnp.zeros_like(begin)
        for part, (d_ref, at) in enumerate(((low_ref, 1), (low_ref, 0), (high_ref, 1), (high_ref, 0))):
            columns = slice(part * 3 * PAIR, (part + 1) * 3 * PAIR)
            own = slice(at * 3 * PAIR, (at + 1) * 3 * PAIR)
            one_grad += mul(d_ref[:, own], w_ref[:, columns], NT)
        gg_s[...] += jnp.sum(one_grad * unit, axis=0, keepdims=True)
        total = (mg_ref[...] + norm_back(one_grad, gain_ref[...], unit, inverse)).astype(BF16)
        for part in range(parts):
            piece = total[:, part * width : (part + 1) * width]
            bg_ref[spot, part, 0:tokens] = piece.reshape(blocks, tokens, width)

    @pl.when(step * ROWS >= limit_ref[0])
    def _():
        bg_ref[spot] = jnp.zeros((blocks,) + bg_ref.shape[1:], BF16)

    @pl.when(step == pl.num_programs(0) - 1)
    def _():
        rows = []
        for ref in (gg_s, gg_two_ref):
            for part in range(parts):
                rows.append(ref[:, part * width : (part + 1) * width])
        bg_ref[:, :, tokens:tall] = jnp.broadcast_to(
            jnp.concatenate(rows, axis=0).astype(BF16), bg_ref.shape[:2] + (SPARE, width)
        )


def begin_block(limit, x_blocks, clock, gain, two_grad, w_wide, middle_grad, high, low):
    senders, feature_parts, tall, width = x_blocks.shape
    tokens = tall - SPARE
    length = senders * tokens
    features = feature_parts * width
    take = ROWS // tokens
    whole = lambda array: pl.BlockSpec(array.shape, lambda i, s: (0,) * array.ndim)
    rows = lambda n: pl.BlockSpec((ROWS, n), lambda i, s: (i, 0))
    return pl.pallas_call(
        begin_kernel,
        grid_spec=pltpu.PrefetchScalarGridSpec(
            num_scalar_prefetch=1,
            grid=(length // ROWS,),
            in_specs=[
                pl.BlockSpec((take, feature_parts, tall, width), lambda i, s: (i, 0, 0, 0)),
                whole(clock), whole(gain), whole(two_grad), rows(features), whole(w_wide),
            ]
            + [rows(6 * PAIR)] * 2,
            out_specs=whole(x_blocks),
            scratch_shapes=[pltpu.VMEM((1, features), F32)],
        ),
        out_shape=jax.ShapeDtypeStruct(x_blocks.shape, BF16),
        compiler_params=params(20),
        cost_estimate=cost(7),
        name="begin_back",
    )(limit, x_blocks, clock, gain, two_grad, middle_grad, w_wide, high, low)


DIRECT = 8


def clock_rows(step_ids, features):
    half_width = features // 2
    ladder = jnp.arange(half_width, dtype=F32) / half_width
    rate_rows = jnp.exp(-math.log(10000.0) * ladder)
    angles = step_ids.astype(F32)[:, None] * rate_rows[None, :]
    return jnp.concatenate([jnp.sin(angles), jnp.cos(angles)], axis=-1)


def swap(value, apart):
    count = lax.axis_size("tensor")
    return lax.ppermute(value, "tensor", [(i, i ^ apart) for i in range(count)])


def along_dp(value, move):
    count = lax.axis_size("dp")
    return lax.ppermute(value, "dp", [(i, move(i)) for i in range(count)])


def across(value):
    return ahead(value, 0, 1)


def ahead(value, step, flip=0):
    count = lax.axis_size("dp") // 2
    return along_dp(value, lambda i: (i // 2 + step) % count * 2 + (i + flip) % 2)


def places():
    count = lax.axis_size("dp") // 2
    own = lax.axis_index("dp")
    coarse = (own // 2 - jnp.arange(count, dtype=jnp.int32)) % count
    return jnp.concatenate([coarse * 2 + own % 2, coarse * 2 + 1 - own % 2])


def collect_coarse(shard):
    count = lax.axis_size("dp") // 2
    return [shard] + [ahead(shard, step) for step in range(1, count)]


def collect_rows(shard):
    count = lax.axis_size("dp")
    rows = lax.all_to_all(
        jnp.broadcast_to(shard[None], (count,) + shard.shape), "dp", 0, 0, tiled=True
    )
    return rows.reshape(count * shard.shape[0], shard.shape[1])


def collect_columns(rows):
    far = swap(rows, 2)
    return rows, swap(rows, 1), far, swap(far, 1)


def add(*values):
    return add_wide(*values).astype(BF16)


def fold_pair(values):
    own = lax.axis_index("dp") % 2
    pick = lambda value, which: lax.dynamic_index_in_dim(value, which, value.ndim - 3, keepdims=False)
    sent = add(*[pick(value, 1 - own) for value in values])
    return sent, lambda: [pick(value, own) for value in values] + [across(sent)]


def fold_far(values):
    sent = add(*[value[0] for value in values])
    return sent, lambda: [value[1] for value in values] + [swap(sent, 2)]


def fold_coarse(values):
    count = lax.axis_size("dp") // 2
    own = lax.axis_index("dp") // 2
    pick = lambda value, which: lax.dynamic_index_in_dim(value, which % count, 0, keepdims=False)
    value = add(*values)
    came = [ahead(pick(value, own + step), step) for step in range(1, count)]
    return value, [pick(value, own)] + came


def add_wide(*values):
    total = values[0].astype(F32)
    for value in values[1:]:
        total += value.astype(F32)
    return total


def grouped(value):
    count = lax.axis_size("dp")
    two, rows, columns = value.shape
    return value.reshape(two, count // 2, 2, rows // count, columns)


def exchange_rows(value):
    count = lax.axis_size("dp")
    groups = value.reshape(count, value.shape[0] // count, value.shape[1])
    return jnp.sum(lax.all_to_all(groups, "dp", 0, 0, tiled=True).astype(F32), axis=0)


def three_terms(values):
    terms = []
    for _ in range(3):
        term = lax.reduce_precision(values, 8, 7)
        terms.append(term.astype(BF16))
        values = values - term
    return terms


def together(*values):
    return lax.optimization_barrier(values)


def after(value, *others):
    return lax.optimization_barrier((value,) + others)[0]


def on_device(
    states, timesteps, lengths, deal_order, w_qkv, w_out, w_up, w_down, gain_attn, gain_ffn, out_grad
):
    both = ("dp", "tensor")
    dp_count = lax.axis_size("dp")
    tensor_count = lax.axis_size("tensor")
    devices = dp_count * tensor_count
    total_seqs, tokens, width = states.shape
    assert tensor_count == 4 and total_seqs == devices
    features = width * tensor_count
    own = lax.axis_index("dp") * tensor_count + lax.axis_index("tensor")
    per = gain_attn.shape[0]
    rows = w_qkv.shape[0]
    hidden = w_up.shape[1]

    rest = jnp.concatenate([w_out.T, w_up, w_down.T], axis=1)
    qkv = w_qkv.reshape(rows, -1)
    direct = dp_count <= DIRECT
    if direct:
        place, groups = places(), dp_count
        wide = qkv.shape[1]
        pieces = collect_coarse(jnp.concatenate([qkv, across(qkv)], axis=1))
        qkv_rows = jnp.concatenate(
            [piece[:, :wide] for piece in pieces] + [piece[:, wide:] for piece in pieces], axis=0
        )
        mine = jnp.concatenate(collect_coarse(rest), axis=0)
        far_rows, other, far_mine = together(
            swap(qkv_rows, 2), in_hbm(across(mine)), in_hbm(swap(mine, 2))
        )
        qkv_parts = (qkv_rows, swap(qkv_rows, 1), far_rows, swap(far_rows, 1))
    else:
        place, groups = jnp.zeros((1,), jnp.int32), None
        qkv_parts = collect_columns(collect_rows(qkv))
        rest_parts = [(part,) for part in collect_columns(collect_rows(rest))]

    deal_later = after(deal_order, pieces[1]) if direct else deal_order
    own_id = lax.dynamic_slice_in_dim(deal_later, own, 1)
    limit = lengths[own_id]
    clock = clock_rows(timesteps[own_id], features)
    spare = jnp.stack(three_terms(gain_attn) + three_terms(gain_ffn)).reshape(1, 6 * per)
    spare = jnp.pad(spare, ((0, SPARE - 1), (0, width - 6 * per)))
    arranged = jnp.concatenate(
        [states[deal_order], jnp.broadcast_to(spare[None], (devices, SPARE, width))], axis=1
    )
    x_blocks = lax.all_to_all(arranged, both, 0, 0, tiled=True)
    gains = jnp.sum(x_blocks[:, tokens, : 6 * per].reshape(devices, 2, 3, per).astype(F32), axis=2)
    gain_one = gains[:, 0].reshape(1, features)
    gain_two = gains[:, 1].reshape(1, features)
    x_blocks = x_blocks.reshape(dp_count, tensor_count, tokens + SPARE, width)

    mixed, n_one_turn, qkv_wide = project(
        limit, place, groups, x_blocks, clock, gain_one, qkv_parts
    )
    if direct:
        near_mine, near_other = in_hbm(swap(mine, 1)), in_hbm(swap(other, 1))
        last_mine, far_other = in_hbm(swap(far_mine, 1)), in_hbm(swap(other, 2))
    ctx, ctx_turn, lse = attend(limit, mixed, tensor_count)
    if direct:
        ctx, near_mine, near_other, last_mine, far_other = together(
            ctx, near_mine, near_other, last_mine, far_other
        )
        last_other = in_hbm(swap(far_other, 1))
        rest_parts = (
            (mine, other), (near_mine, near_other), (far_mine, far_other), (last_mine, last_other)
        )
    output, context_grad, middle_grad, two_grad, up_send, down_send, up_keep, down_keep = middle_block(
        limit, place, groups, x_blocks, clock, gain_two, ctx, rest_parts, out_grad
    )
    up_came, down_came = swap(up_send, 1), swap(down_send, 1)

    back = functools.partial(attend_back, limit, mixed, ctx_turn, lse)
    if direct:
        down_sent, down_rest = fold_far([grouped(value) for value in (down_keep, down_came)])
        up_sent, up_rest = fold_pair([grouped(value) for value in (up_keep, up_came)])
        context_grad = after(context_grad, down_sent, up_sent)
    high, three, two = back(in_hbm(context_grad), n_one_turn, 3)
    if direct:
        *down_rest, down_came = down_rest()
        *up_rest, up_came = up_rest()
        high, three, two, down_came, up_came = together(high, three, two, down_came, up_came)
        down_value, down_pieces = fold_coarse([*down_rest, down_came])
        up_sent, up_rest = fold_far([add(*up_rest, up_came)])
        context_grad = after(context_grad, down_value, up_sent)
    far = add(two, swap(three, 1))
    came_far = swap(far, 2)
    low, one, own_part = back(after(context_grad, high, far), n_one_turn, 1)
    if direct:
        *up_rest, up_came = up_rest()
        low, one, own_part, up_came, came_far, *down_pieces = together(
            low, one, own_part, up_came, came_far, *down_pieces
        )
        up_value, up_pieces = fold_coarse([*up_rest, up_came])
        down_sent, down_rest = fold_pair([add_wide(*down_pieces)[..., None, :, :, :]])
        middle_grad = after(middle_grad, up_value, down_sent)
    came_one = swap(one, 1)
    begin_grad = begin_block(
        limit, x_blocks, clock, gain_one, two_grad, qkv_wide, middle_grad, high, low
    )
    if direct:
        begin_grad, came_one, up_pieces[2] = together(begin_grad, came_one, up_pieces[2])
        near = [grouped(value[None])[0] for value in (own_part, came_one, came_far)]
        qkv_value, qkv_pieces = fold_coarse(fold_pair(near)[1]())
        down_total = add_wide(*down_rest())[0]
        pieces = together(*up_pieces, *qkv_pieces)
        up_total = add_wide(*pieces[: len(up_pieces)])
        qkv_total = add_wide(*pieces[len(up_pieces) :])
    else:
        up_total = exchange_rows(add(*fold_far([up_keep, up_came])[1]()))
        down_total = exchange_rows(add(*fold_far([down_keep, down_came])[1]()))
        qkv_total = exchange_rows(add(own_part, came_one, came_far))
    returned = lax.all_to_all(
        begin_grad.reshape(devices, tokens + SPARE, width), both, 0, 0, tiled=True
    )
    inverse = (
        jnp.zeros((total_seqs,), jnp.int32)
        .at[deal_order]
        .set(jnp.arange(total_seqs, dtype=jnp.int32))
    )
    states_grad = returned[inverse][:, :tokens]
    gain_grads = jnp.sum(returned[:, tokens:].astype(F32), axis=0).reshape(2, devices, per)
    gain_grads = lax.dynamic_index_in_dim(gain_grads, own, 1, keepdims=False)
    return (
        output,
        states_grad,
        qkv_total.reshape(w_qkv.shape),
        up_total[:, :PAIR].T,
        up_total[:, PAIR:],
        down_total.T,
        gain_grads[0],
        gain_grads[1],
    )


def solution(mesh):
    in_specs = (
        P(None, "dp", "tensor"),
        P(),
        P(),
        P(),
        P("dp", None, "tensor"),
        P("tensor", "dp"),
        P("dp", "tensor"),
        P("tensor", "dp"),
        P(("dp", "tensor")),
        P(("dp", "tensor")),
        P(("dp", "tensor"), None, None),
    )
    out_specs = (
        P(("dp", "tensor"), None, None),
        P(None, "dp", "tensor"),
        P("dp", None, "tensor"),
        P("tensor", "dp"),
        P("dp", "tensor"),
        P("tensor", "dp"),
        P(("dp", "tensor")),
        P(("dp", "tensor")),
    )
    return jax.shard_map(
        on_device, mesh=mesh, in_specs=in_specs, out_specs=out_specs, check_vma=False
    )
```
